32 devices in a mesh: seq: 8 (over y, x, core), row: 4 (over z).
Axes of the slice: x: 2, y: 2, z: 4, core: 2. Of those that a mesh axis runs over, the one named last changes fastest.
Arguments:
- tokens: bfloat16 [32, 1024, 768], P('row', 'seq'), may hold values from -6 to 6
- segment_ids: int32 [32, 1024], P('row'), may hold values from 0 to 1023, as said below
- w_in: bfloat16 [768, 3840], replicated, may hold values from -0.21875 to 0.21875
- w_out: bfloat16 [768, 768], replicated, may hold values from -3 to 3
- w_up: bfloat16 [768, 3072], replicated, may hold values from -0.21875 to 0.21875
- w_down: bfloat16 [3072, 768], replicated, may hold values from -0.109375 to 0.109375
- conv_kernel: float32 [5, 768], replicated, may hold values from -2.5 to 2.5
- norm_gain: float32 [2, 768], replicated, may hold values from 0.5 to 1.5
- norm_bias: float32 [2, 768], replicated, may hold values from -1.5 to 1.5
- cotangent: bfloat16 [32, 1024, 768], P('row', 'seq'), may hold values from -6 to 6
Outputs:
- layer_out: bfloat16 [32, 1024, 768], P('row', 'seq')
- token_grad: float32 [32, 1024, 768], P('row', 'seq')
- w_in_grad: float32 [768, 3840], P('seq', 'row')
- w_out_grad: float32 [768, 768], P('seq', 'row')
- w_up_grad: float32 [768, 3072], P('seq', 'row')
- w_down_grad: float32 [3072, 768], P('seq', 'row')
- conv_kernel_grad: float32 [5, 768], replicated
- norm_gain_grad: float32 [2, 768], replicated
- norm_bias_grad: float32 [2, 768], replicated
The draws below stay inside these ranges and needn't reach their ends.
Inputs may be any that keep to these rules, and one draw needn't show every extreme that they name: `segment_ids`: each token's id is the position in its row at which its document begins, so ids never fall along a row and equal ids mark one document.
All inputs are finite; a program needn't handle non-finite values.
Results may differ from the reference program's by a relative error of at most 0.015.
Values may be sent and summed in bfloat16 or wider, within the bound.
A program may use at most 384 MiB of HBM per device.

```python
import jax
import jax.numpy as jnp
from jax import lax

D = 768
HEADS = 12
HEAD = 64
FF = 3072
WIN = 128
KER = 5
STR = 4
SEQ_DEV = 128
ROWS_DEV = 8
SEQ_LEN = 1024
ROWS = 32


def draw_segment_ids(key, part):
    key_flags = jax.random.fold_in(key, 11)
    key_chosen = jax.random.fold_in(key, 12)
    starts = jax.random.randint(key_flags, (ROWS, SEQ_LEN), 0, 3 * SEQ_DEV) == 0
    position = jnp.arange(SEQ_LEN, dtype=jnp.int32)[None, :]
    chosen = jax.random.randint(key_chosen, (ROWS // ROWS_DEV,), 0, ROWS_DEV)
    row_index = jnp.arange(ROWS, dtype=jnp.int32)
    is_long = row_index % ROWS_DEV == jnp.repeat(chosen, ROWS_DEV)
    edge_zone = (position < SEQ_DEV // 2) | (position >= SEQ_LEN - SEQ_DEV // 2)
    starts = starts & (edge_zone | jnp.logical_not(is_long)[:, None])
    starts = starts | (position == 0)
    marked = jnp.where(starts, position, 0)
    return lax.cummax(marked, axis=1).astype(jnp.int32)


def level_of(rng, dims, cuts, smallest, largest):
    def one(dim, shards_of):
        heights = jax.random.uniform(jax.random.fold_in(jax.random.fold_in(rng, 6), dim), (shards_of,), jnp.float32, smallest / len(cuts), largest / len(cuts))
        return jnp.repeat(jnp.exp(heights), dims[dim] // shards_of).reshape((-1,) + (1,) * (len(dims) - dim - 1))

    level = one(*cuts[0])
    for cut in cuts[1:]:
        level = level * one(*cut)
    return level


def gaussian(key, extent, width, reach, shards=(), kind=jnp.bfloat16):
    gain = level_of(key, extent, shards, -0.22, 0.18) if shards else 1.0
    result = jax.random.normal(key, extent, jnp.float32) * width * gain
    return jnp.minimum(jnp.maximum(result, -reach), reach).astype(kind)


def setup_inputs(seed: int = 0) -> dict:
    splits = jax.random.split(jax.random.key(seed), 11)
    tokens = gaussian(splits[0], (ROWS, SEQ_LEN, D), 1.0, 6.0, ((0, 4), (1, 8)))
    segment_ids = draw_segment_ids(jax.random.fold_in(splits[10], 71), 0)
    w_in = gaussian(splits[2], (D, 5 * D), D ** -0.5, 0.21875)
    w_out = gaussian(splits[3], (D, D), (max(D // 192, 1)) ** -0.5, 3.0)
    w_up = gaussian(splits[4], (D, FF), D ** -0.5, 0.21875)
    w_down = gaussian(splits[5], (FF, D), FF ** -0.5, 0.109375)
    conv_kernel = gaussian(splits[6], (KER, D), KER ** -0.5, 2.5, (), jnp.float32)
    norm_gain = jnp.clip(1.0 + 0.1 * jax.random.normal(splits[7], (2, D), jnp.float32), 0.5, 1.5)
    norm_bias = gaussian(splits[8], (2, D), 0.3, 1.5, (), jnp.float32)
    cotangent = gaussian(splits[9], (ROWS, SEQ_LEN, D), 1.0, 6.0, ((0, 4), (1, 8)))
    return {"tokens": tokens, "segment_ids": segment_ids, "w_in": w_in, "w_out": w_out, "w_up": w_up, "w_down": w_down, "conv_kernel": conv_kernel, "norm_gain": norm_gain, "norm_bias": norm_bias, "cotangent": cotangent}


@jax.custom_vjp
def low(v):
    return lax.optimization_barrier(v.astype(jnp.bfloat16)).astype(jnp.float32)

@jax.custom_vjp
def low_back(v):
    return v

def low_keep(v):
    return (low(v), None)

def low_pass(kept, grad):
    return (grad,)

def back_keep(v):
    return (v, None)

def back_low(kept, grad):
    return (low(grad),)
low.defvjp(low_keep, low_pass)
low_back.defvjp(back_keep, back_low)
EPSILON = 1e-05
ROOT_HALF = 0.7071067811865476
NEG_LARGE = -1e+30

def highest(left_mat, right_mat):
    return jnp.dot(left_mat, right_mat, precision=lax.Precision.HIGHEST)

def layer_norm(values, gain_row, offset):
    centred = values - lax.optimization_barrier(jnp.mean(values, axis=-1, keepdims=True))
    spread = lax.optimization_barrier(jnp.mean(centred * centred, axis=-1, keepdims=True))
    return centred * lax.rsqrt(spread + EPSILON) * gain_row + offset

def gelu_exact(values):
    return 0.5 * values * (1.0 + jax.scipy.special.erf(values * ROOT_HALF))

def attend_row(queries, near_keys, near_values, far_keys, far_values, segment_row):
    seq_len = queries.shape[0]
    half_win = WIN // 2
    block_len = min(512, seq_len)
    near_len = block_len + 2 * half_win
    head_scale = HEAD ** (-0.5)
    query_heads = queries.reshape(seq_len, HEADS, HEAD)
    key_pad = jnp.pad(near_keys, ((half_win, half_win), (0, 0))).reshape(seq_len + 2 * half_win, HEADS, HEAD)
    value_pad = jnp.pad(near_values, ((half_win, half_win), (0, 0))).reshape(seq_len + 2 * half_win, HEADS, HEAD)
    seg_pad = jnp.pad(segment_row, (half_win, half_win), constant_values=-1)
    far_seg = segment_row[::STR]
    far_key_heads = far_keys.reshape(far_keys.shape[0], HEADS, HEAD)
    far_value_heads = far_values.reshape(far_values.shape[0], HEADS, HEAD)
    offsets = jnp.arange(near_len)[None, :] - jnp.arange(block_len)[:, None]
    near_ok = (offsets >= 0) & (offsets <= 2 * half_win)

    def one_block(block_index):
        block_start = (block_index * block_len).astype(jnp.int32)
        block_query = lax.dynamic_slice_in_dim(query_heads, block_start, block_len, 0)
        block_key = lax.dynamic_slice_in_dim(key_pad, block_start, near_len, 0)
        block_value = lax.dynamic_slice_in_dim(value_pad, block_start, near_len, 0)
        block_seg = lax.dynamic_slice_in_dim(segment_row, block_start, block_len, 0)
        key_seg = lax.dynamic_slice_in_dim(seg_pad, block_start, near_len, 0)
        near_scores = jnp.einsum('qhd,khd->hqk', block_query, block_key, precision=lax.Precision.HIGHEST)
        far_scores = jnp.einsum('qhd,khd->hqk', block_query, far_key_heads, precision=lax.Precision.HIGHEST)
        scores = low_back(jnp.concatenate([near_scores, far_scores], axis=-1) * head_scale)
        allowed = jnp.concatenate([near_ok & (block_seg[:, None] == key_seg[None, :]), block_seg[:, None] == far_seg[None, :]], axis=-1)
        scores = jnp.where(allowed[None], scores, NEG_LARGE)
        row_top = lax.optimization_barrier(jnp.max(scores, axis=-1, keepdims=True))
        exp_terms = jnp.exp(scores - row_top)
        weighting = low(exp_terms / lax.optimization_barrier(jnp.sum(exp_terms, axis=-1, keepdims=True)))
        near_part = jnp.einsum('hqk,khd->qhd', weighting[..., :near_len], block_value, precision=lax.Precision.HIGHEST)
        far_part = jnp.einsum('hqk,khd->qhd', weighting[..., near_len:], far_value_heads, precision=lax.Precision.HIGHEST)
        return near_part + far_part
    blocks = lax.map(jax.checkpoint(one_block), jnp.arange(seq_len // block_len, dtype=jnp.int32))
    return blocks.reshape(seq_len, HEADS * HEAD)

def layer_row(tokens, segment_row, w_in, w_out, w_up, w_down, conv_kernel, norm_gain, norm_bias):
    seq_len, model_width = tokens.shape
    edge_len = KER // 2
    pooled_len = seq_len // STR
    projected = highest(tokens, w_in[:, :3 * model_width])
    queries = low_back(low(projected[:, :model_width]))
    near_keys = low_back(low(projected[:, model_width:2 * model_width]))
    near_values = low_back(low(projected[:, 2 * model_width:]))
    seg_ext = jnp.pad(segment_row, (edge_len, edge_len), constant_values=-1)
    tok_ext = jnp.pad(tokens, ((edge_len, edge_len), (0, 0)))
    centre_seg = segment_row[::STR]
    pooled = jnp.zeros((pooled_len, model_width), jnp.float32)
    for tap_index in range(KER):
        tap_rows = tok_ext[tap_index:tap_index + seq_len].reshape(pooled_len, STR, model_width)[:, 0]
        same_doc = (seg_ext[tap_index:tap_index + seq_len].reshape(pooled_len, STR)[:, 0] == centre_seg).astype(jnp.float32)
        pooled = pooled + tap_rows * conv_kernel[tap_index] * same_doc[:, None]
    pooled = low(pooled)
    far_proj = highest(pooled, w_in[:, 3 * model_width:])
    far_keys = low_back(low(far_proj[:, :model_width]))
    far_values = low_back(low(far_proj[:, model_width:]))
    attended = low_back(low(attend_row(queries, near_keys, near_values, far_keys, far_values, segment_row)))
    attn_proj = low_back(highest(attended, w_out))
    normed_one = layer_norm(tokens + attn_proj, norm_gain[0], norm_bias[0])
    up_value = low_back(highest(low(normed_one), w_up))
    activated = low(gelu_exact(up_value))
    down_value = low_back(highest(activated, w_down))
    return layer_norm(normed_one + down_value, norm_gain[1], norm_bias[1])

def reference(tokens, segment_ids, w_in, w_out, w_up, w_down, conv_kernel, norm_gain, norm_bias, cotangent):
    w_in_f = w_in.astype(jnp.float32)
    w_out_f = w_out.astype(jnp.float32)
    w_up_f = w_up.astype(jnp.float32)
    w_down_f = w_down.astype(jnp.float32)
    kernel_f = conv_kernel.astype(jnp.float32)
    gain_f = norm_gain.astype(jnp.float32)
    bias_f = norm_bias.astype(jnp.float32)

    def one_row(totals, row_data):
        token_row, seg_row, cot_row = row_data

        def run(token_f, w_in_p, w_out_p, w_up_p, w_down_p, kernel_p, gain_p, bias_p):
            return layer_row(token_f, seg_row, w_in_p, w_out_p, w_up_p, w_down_p, kernel_p, gain_p, bias_p)
        out_row, pullback = jax.vjp(run, token_row.astype(jnp.float32), w_in_f, w_out_f, w_up_f, w_down_f, kernel_f, gain_f, bias_f)
        grads = pullback(cot_row.astype(jnp.float32))
        new_totals = tuple((total_sum + grad_part for total_sum, grad_part in zip(totals, grads[1:])))
        return (new_totals, (out_row.astype(jnp.bfloat16), grads[0]))
    zero_sums = (jnp.zeros(w_in_f.shape, jnp.float32), jnp.zeros(w_out_f.shape, jnp.float32), jnp.zeros(w_up_f.shape, jnp.float32), jnp.zeros(w_down_f.shape, jnp.float32), jnp.zeros(kernel_f.shape, jnp.float32), jnp.zeros(gain_f.shape, jnp.float32), jnp.zeros(bias_f.shape, jnp.float32))
    totals, outputs = lax.scan(one_row, zero_sums, (tokens, segment_ids, cotangent))
    return (outputs[0], outputs[1], totals[0], totals[1], totals[2], totals[3], totals[4], totals[5], totals[6])
```

```python
import functools

import jax
import jax.numpy as jnp
from jax import lax
from jax.experimental import pallas as pl
from jax.experimental.pallas import tpu as pltpu
from jax.sharding import PartitionSpec as P

HEADS = 12
HEAD = 64
WIN = 128
KER = 5
STR = 4
PAIRS = HEADS // 2

EPSILON = 1e-05
ROOT_HALF = 0.7071067811865476
INV_ROOT_2PI = 0.3989422804014327
NEG_LARGE = -1e30
BF = jnp.bfloat16
F32 = jnp.float32
MB = 1 << 20


def dot(a, b, ca=1, cb=0):
    return lax.dot_general(a, b, (((ca,), (cb,)), ((), ())), preferred_element_type=F32)


def passed_along(block, axis, distance):
    devices = range(lax.axis_size(axis))
    route = [(i - distance, i) for i in devices if i - distance in devices]
    return lax.ppermute(block, axis, route)


def tap_select(seg_row, half, pooled_local):
    width = seg_row.shape[1]
    shape = (KER * pooled_local, width)
    rows = lax.broadcasted_iota(jnp.int32, shape, 0)
    cols = lax.broadcasted_iota(jnp.int32, shape, 1)
    tap = rows // pooled_local
    centre = half + STR * (rows - tap * pooled_local)
    seg = jnp.broadcast_to(seg_row, shape)
    centre_seg = jnp.sum(jnp.where(cols == centre, seg, 0), axis=1, keepdims=True)
    hit = (cols == centre + tap - KER // 2) & (seg == centre_seg)
    return jnp.where(hit, 1.0, 0.0).astype(BF)


def pool_kernel(half, tok_ref, seg_ref, ker_ref, out_ref):
    pooled_local = out_ref.shape[1]
    picked = dot(tap_select(seg_ref[0], half, pooled_local), tok_ref[0])
    total = picked[:pooled_local] * ker_ref[0:1]
    for t in range(1, KER):
        total = total + picked[t * pooled_local : (t + 1) * pooled_local] * ker_ref[t : t + 1]
    out_ref[0] = total.astype(BF)


def attend_kernel(half, tok_ref, pool_ref, qseg_ref, kseg_ref, w_ref, q_ref, k_ref, v_ref, p_ref, att_ref):
    shard = q_ref.shape[1]
    width = tok_ref.shape[2]
    near = shard + 2 * half
    keys = k_ref.shape[1]
    tok = tok_ref[0]
    own = tok_ref[0, half : half + shard]
    q_ref[0] = (dot(own, w_ref[:, :width]) * HEAD ** (-0.5)).astype(BF)
    k_ref[0, :near] = dot(tok, w_ref[:, width : 2 * width]).astype(BF)
    v_ref[0, :near] = dot(tok, w_ref[:, 2 * width : 3 * width]).astype(BF)
    k_ref[0, near:] = dot(pool_ref[0], w_ref[:, 3 * width : 4 * width]).astype(BF)
    v_ref[0, near:] = dot(pool_ref[0], w_ref[:, 4 * width :]).astype(BF)

    key_seg = jnp.transpose(jnp.broadcast_to(kseg_ref[0], (shard, keys)))
    shape = (keys, shard)
    row = lax.broadcasted_iota(jnp.int32, shape, 0)
    col = lax.broadcasted_iota(jnp.int32, shape, 1)
    inside = (row >= near) | ((row >= col) & (row - col <= 2 * half))
    kept = inside & (key_seg == jnp.broadcast_to(qseg_ref[0], shape))
    bias = jnp.where(kept, 0.0, NEG_LARGE)
    bias = jnp.concatenate([bias, bias], axis=1)
    lane = lax.broadcasted_iota(jnp.int32, (shard, 2 * HEAD), 1)
    even = lane < HEAD
    for j in range(PAIRS):
        cols = slice(2 * HEAD * j, 2 * HEAD * (j + 1))
        qp = q_ref[0, :, cols]
        zero = jnp.zeros_like(qp)
        stacked = jnp.concatenate([jnp.where(even, qp, zero), jnp.where(even, zero, qp)], axis=0)
        scores = dot(k_ref[0, :, cols], stacked, 1, 1) + bias
        top = jnp.max(scores, axis=0, keepdims=True)
        terms = jnp.exp(scores - top)
        prob = (terms * (1.0 / jnp.sum(terms, axis=0, keepdims=True))).astype(BF)
        p_ref[0, j] = prob
        mixed = dot(v_ref[0, :, cols], prob, 0, 0)
        mixed = jnp.concatenate([mixed[:HEAD, :shard], mixed[HEAD:, shard:]], axis=0)
        att_ref[0, :, cols] = jnp.transpose(mixed).astype(BF)


def mlp_kernel(
    tok_ref, att_ref, cot_ref, wo_ref, wu_ref, wd_ref, gain_ref, bias_ref,
    out_ref, act_ref, upg_ref, n1_ref, r2_ref, g1_ref, g1b_ref, da_ref, dsum_ref, small_ref,
    slope,
):
    hidden = wu_ref.shape[1]
    chunk = 512
    gain_a, gain_b = gain_ref[0:1], gain_ref[1:2]

    def mean(x):
        return jnp.mean(x, axis=-1, keepdims=True)

    resid = tok_ref[...].astype(F32) + dot(att_ref[...], wo_ref[...])
    centred = resid - mean(resid)
    rstd_a = lax.rsqrt(mean(centred * centred) + EPSILON)
    hat_a = centred * rstd_a
    normed = hat_a * gain_a + bias_ref[0:1]
    low = normed.astype(BF)
    n1_ref[...] = low
    total = normed
    for c in range(0, hidden, chunk):
        up = dot(low, wu_ref[:, c : c + chunk])
        half_cdf = 0.5 * (1.0 + lax.erf(up * ROOT_HALF))
        act = (up * half_cdf).astype(BF)
        act_ref[:, c : c + chunk] = act
        slope[:, c : c + chunk] = half_cdf + up * (INV_ROOT_2PI * jnp.exp(-0.5 * up * up))
        total = total + dot(act, wd_ref[c : c + chunk, :])
    centred = total - mean(total)
    rstd_b = lax.rsqrt(mean(centred * centred) + EPSILON)
    hat_b = centred * rstd_b
    out_ref[...] = (hat_b * gain_b + bias_ref[1:2]).astype(BF)
    g = cot_ref[...].astype(F32)
    gain_two = jnp.sum(g * hat_b, axis=0, keepdims=True)
    bias_two = jnp.sum(g, axis=0, keepdims=True)
    e = g * gain_b
    grad = rstd_b * (e - mean(e) - hat_b * mean(e * hat_b))
    grad_low = grad.astype(BF)
    r2_ref[...] = grad_low
    for c in range(0, hidden, chunk):
        up_grad = (dot(grad_low, wd_ref[c : c + chunk, :], 1, 1) * slope[:, c : c + chunk]).astype(BF)
        upg_ref[:, c : c + chunk] = up_grad
        grad = grad + dot(up_grad, wu_ref[:, c : c + chunk], 1, 1)
    gain_one = jnp.sum(grad * hat_a, axis=0, keepdims=True)
    bias_one = jnp.sum(grad, axis=0, keepdims=True)
    e = grad * gain_a
    resid_grad = rstd_a * (e - mean(e) - hat_a * mean(e * hat_a))
    g1_ref[...] = resid_grad
    resid_low = resid_grad.astype(BF)
    g1b_ref[...] = resid_low
    att_grad = dot(resid_low, wo_ref[...], 1, 1).astype(BF)
    da_ref[...] = att_grad
    prod = att_grad.astype(F32) * att_ref[...].astype(F32)
    high = prod.astype(BF)
    rest = (prod - high.astype(F32)).astype(BF)
    heads = dsum_ref.shape[0]
    width = prod.shape[1]
    head_row = lax.broadcasted_iota(jnp.int32, (heads, width), 0)
    head_col = lax.broadcasted_iota(jnp.int32, (heads, width), 1) // HEAD
    pick = jnp.where(head_row == head_col, 1.0, 0.0).astype(BF)
    dsum_ref[...] = dot(pick, high, 1, 1) + dot(pick, rest, 1, 1)

    @pl.when(pl.program_id(0) == 0)
    def _():
        small_ref[...] = jnp.zeros_like(small_ref)

    small_ref[0:4] += jnp.concatenate([gain_one, gain_two, bias_one, bias_two], axis=0)


def attend_back_kernel(
    half, q_ref, k_ref, v_ref, p_ref, da_ref, dsum_ref, w_ref,
    dq_ref, dk_ref, dv_ref, dtok_ref, dpool_ref,
):
    shard = q_ref.shape[1]
    width = q_ref.shape[2]
    near = shard + 2 * half
    lane = lax.broadcasted_iota(jnp.int32, (shard, 2 * HEAD), 1)
    even = lane < HEAD

    def stack(pair):
        zero = jnp.zeros_like(pair)
        return jnp.concatenate([jnp.where(even, pair, zero), jnp.where(even, zero, pair)], axis=0)

    for j in range(PAIRS):
        cols = slice(2 * HEAD * j, 2 * HEAD * (j + 1))
        queries = stack(q_ref[0, :, cols])
        grads = stack(da_ref[0, :, cols])
        keys = k_ref[0, :, cols]
        prob = p_ref[0, j]
        dprob = dot(v_ref[0, :, cols], grads, 1, 1)
        row_dot = jnp.concatenate([dsum_ref[2 * j : 2 * j + 1], dsum_ref[2 * j + 1 : 2 * j + 2]], axis=1)
        dscore = (prob.astype(F32) * (dprob - row_dot)).astype(BF)
        dv_ref[0, :, cols] = dot(prob, grads).astype(BF)
        dk_ref[0, :, cols] = dot(dscore, queries).astype(BF)
        mixed = dot(keys, dscore, 0, 0)
        mixed = jnp.concatenate([mixed[:HEAD, :shard], mixed[HEAD:, shard:]], axis=0)
        dq_ref[0, :, cols] = (jnp.transpose(mixed) * HEAD ** (-0.5)).astype(BF)
    dtok_ref[0] = dot(dk_ref[0, :near], w_ref[:, width : 2 * width], 1, 1) + dot(
        dv_ref[0, :near], w_ref[:, 2 * width : 3 * width], 1, 1
    )
    dtok_ref[0, half : half + shard] += dot(dq_ref[0], w_ref[:, :width], 1, 1)
    dpool_ref[0] = (
        dot(dk_ref[0, near:], w_ref[:, 3 * width : 4 * width], 1, 1)
        + dot(dv_ref[0, near:], w_ref[:, 4 * width :], 1, 1)
    ).astype(BF)


def pool_back_kernel(half, tok_ref, seg_ref, ker_ref, dpool_ref, dtok_ref, g1_ref, left_ref, right_ref, out_ref, rim_ref, small_ref):
    shard = out_ref.shape[1]
    pooled_local = dpool_ref.shape[1]
    select = tap_select(seg_ref[0], half, pooled_local)
    picked = dot(select, tok_ref[0])
    grad = dpool_ref[0].astype(F32)
    terms, kernel_rows = [], []
    for t in range(KER):
        terms.append((grad * ker_ref[t : t + 1]).astype(BF))
        kernel_rows.append(
            jnp.sum(grad * picked[t * pooled_local : (t + 1) * pooled_local], axis=0, keepdims=True)
        )
    spread = dot(select, jnp.concatenate(terms, axis=0), 0, 0)
    rim_ref[0] = spread[half - 8 : half].astype(BF)
    total = g1_ref[0] + dtok_ref[0, half : half + shard] + spread[half : half + shard]
    out_ref[0] = total
    out_ref[0, :half] += left_ref[0].astype(F32)
    out_ref[0, shard - half :] += right_ref[0].astype(F32)

    @pl.when(pl.program_id(0) == 0)
    def _():
        small_ref[...] = jnp.zeros_like(small_ref)

    small_ref[0:KER] += jnp.concatenate(kernel_rows, axis=0)


def tile_order(grad, seq_count, row_count):
    first, second = grad.shape
    tiles = grad.reshape(seq_count, first // seq_count, row_count, second // row_count)
    tiles = tiles.transpose(0, 2, 1, 3)
    return tiles.reshape(seq_count * row_count * (first // seq_count), second // row_count)


def body(tokens, segment_ids, w_in, w_out, w_up, w_down, conv_kernel, norm_gain, norm_bias, cotangent):
    rows, shard, width = tokens.shape
    half = WIN // 2
    pooled_local = shard // STR
    near = shard + 2 * half
    count = rows * shard
    hidden = w_up.shape[1]
    seq_count = lax.axis_size("seq")
    row_count = lax.axis_size("row")
    seq_start = lax.axis_index("seq") * shard
    keys = near + pooled_local * seq_count

    own_seg = lax.dynamic_slice_in_dim(segment_ids, seq_start, shard, 1)
    padded_seg = jnp.pad(segment_ids, ((0, 0), (half, half)), constant_values=-1)
    window_seg = lax.dynamic_slice_in_dim(padded_seg, seq_start, near, 1)
    key_seg = jnp.concatenate([window_seg, segment_ids[:, ::STR]], axis=1)
    own_seg = own_seg[:, None]
    key_seg = key_seg[:, None]
    window_seg = window_seg[:, None]

    before = passed_along(tokens[:, shard - half :], "seq", 1)
    after = passed_along(tokens[:, :half], "seq", -1)
    tok_ext = jnp.concatenate([before, tokens, after], axis=1)

    def row_spec(*tail):
        return pl.BlockSpec((1,) + tail, lambda r: (r,) + (0,) * len(tail))

    def whole_spec(*dims):
        return pl.BlockSpec(dims, lambda r: (0,) * len(dims), pipeline_mode=pl.Buffered(1))

    def struct(*dims, dtype=BF):
        return jax.ShapeDtypeStruct(dims, dtype)

    def params(limit):
        return pltpu.CompilerParams(dimension_semantics=("arbitrary",), vmem_limit_bytes=limit * MB)

    pooled = pl.pallas_call(
        functools.partial(pool_kernel, half),
        out_shape=struct(rows, pooled_local, width),
        grid=(rows,),
        in_specs=[row_spec(near, width), row_spec(1, near), whole_spec(KER, width)],
        out_specs=row_spec(pooled_local, width),
        compiler_params=params(32),
        name="pool",
    )(tok_ext, window_seg, conv_kernel)
    pooled_all = lax.all_gather(pooled, "seq", axis=1, tiled=True)
    far = pooled_all.shape[1]

    q, k_all, v_all, prob, attended = pl.pallas_call(
        functools.partial(attend_kernel, half),
        out_shape=(
            struct(rows, shard, width), struct(rows, keys, width), struct(rows, keys, width),
            struct(rows, PAIRS, keys, 2 * shard), struct(rows, shard, width),
        ),
        grid=(rows,),
        in_specs=[
            row_spec(near, width), row_spec(far, width), row_spec(1, shard), row_spec(1, keys),
            whole_spec(*w_in.shape),
        ],
        out_specs=(
            row_spec(shard, width), row_spec(keys, width), row_spec(keys, width),
            row_spec(PAIRS, keys, 2 * shard), row_spec(shard, width),
        ),
        compiler_params=params(56),
        name="attend",
    )(tok_ext, pooled_all, own_seg, key_seg, w_in)

    block = 256
    flat_tokens = tokens.reshape(count, width)
    att_flat = attended.reshape(count, width)
    cot_flat = cotangent.reshape(count, width)

    def tok_spec(cols):
        return pl.BlockSpec((block, cols), lambda i: (i, 0))

    layer_out, act, upg, n1, r2, g1, g1b, att_grad, dsum, norm_sums = pl.pallas_call(
        mlp_kernel,
        out_shape=(
            struct(count, width), struct(count, hidden), struct(count, hidden), struct(count, width),
            struct(count, width), struct(count, width, dtype=F32), struct(count, width), struct(count, width),
            struct(16, count, dtype=F32), struct(8, width, dtype=F32),
        ),
        grid=(count // block,),
        in_specs=[
            tok_spec(width), tok_spec(width), tok_spec(width), whole_spec(*w_out.shape),
            whole_spec(*w_up.shape), whole_spec(*w_down.shape), whole_spec(2, width), whole_spec(2, width),
        ],
        out_specs=(
            tok_spec(width), tok_spec(hidden), tok_spec(hidden), tok_spec(width), tok_spec(width),
            tok_spec(width), tok_spec(width), tok_spec(width),
            pl.BlockSpec((16, block), lambda i: (0, i)), pl.BlockSpec((8, width), lambda i: (0, 0)),
        ),
        scratch_shapes=[pltpu.VMEM((block, hidden), F32)],
        compiler_params=params(56),
        name="mlp",
    )(flat_tokens, att_flat, cot_flat, w_out, w_up, w_down, norm_gain, norm_bias)

    dq, dk, dv, dtok, dpool = pl.pallas_call(
        functools.partial(attend_back_kernel, half),
        out_shape=(
            struct(rows, shard, width), struct(rows, keys, width), struct(rows, keys, width),
            struct(rows, near, width, dtype=F32), struct(rows, far, width),
        ),
        grid=(rows,),
        in_specs=[
            row_spec(shard, width), row_spec(keys, width), row_spec(keys, width),
            row_spec(PAIRS, keys, 2 * shard), row_spec(shard, width),
            pl.BlockSpec((16, shard), lambda r: (0, r)), whole_spec(*w_in.shape),
        ],
        out_specs=(
            row_spec(shard, width), row_spec(keys, width), row_spec(keys, width),
            row_spec(near, width), row_spec(far, width),
        ),
        compiler_params=params(56),
        name="attend_back",
    )(q, k_all, v_all, prob, att_grad.reshape(rows, shard, width), dsum, w_in)

    dpool_own = lax.psum_scatter(dpool, "seq", scatter_dimension=1, tiled=True)
    from_right = passed_along(dtok[:, :half].astype(BF), "seq", -1)
    from_left = passed_along(dtok[:, shard + half :].astype(BF), "seq", 1)

    token_grad, rim, ker_sums = pl.pallas_call(
        functools.partial(pool_back_kernel, half),
        out_shape=(
            struct(rows, shard, width, dtype=F32), struct(rows, 8, width), struct(8, width, dtype=F32),
        ),
        grid=(rows,),
        in_specs=[
            row_spec(near, width), row_spec(1, near), whole_spec(KER, width), row_spec(pooled_local, width),
            row_spec(near, width), row_spec(shard, width), row_spec(half, width), row_spec(half, width),
        ],
        out_specs=(
            row_spec(shard, width), row_spec(8, width), pl.BlockSpec((8, width), lambda r: (0, 0)),
        ),
        compiler_params=params(48),
        name="pool_back",
    )(tok_ext, window_seg, conv_kernel, dpool_own, dtok, g1.reshape(rows, shard, width), from_left, from_right)
    rim_back = passed_along(rim, "seq", -1).astype(F32)
    token_grad = token_grad.at[:, shard - 8 :].add(rim_back)

    def product(a, b):
        return lax.dot_general(
            a.reshape(-1, a.shape[-1]), b.reshape(-1, b.shape[-1]), (((0,), (0,)), ((), ())),
            preferred_element_type=F32,
        ).astype(BF)

    w_in_grad = jnp.concatenate(
        [
            product(tokens, dq), product(tok_ext, dk[:, :near]), product(tok_ext, dv[:, :near]),
            product(pooled_all, dk[:, near:]), product(pooled_all, dv[:, near:]),
        ],
        axis=1,
    )

    def reduced(grad):
        first, second = grad.shape
        tiles = tile_order(grad, seq_count, row_count)
        out = lax.psum_scatter(tiles, ("seq", "row"), scatter_dimension=0, tiled=True)
        return out.astype(F32)

    small_sum = lax.psum(jnp.concatenate([ker_sums[:KER], norm_sums[:4]], axis=0), ("seq", "row"))
    return (
        layer_out.reshape(rows, shard, width),
        token_grad,
        reduced(w_in_grad),
        reduced(product(attended, g1b)),
        reduced(product(n1, upg)),
        reduced(product(act, r2)),
        small_sum[:KER],
        small_sum[KER : KER + 2],
        small_sum[KER + 2 : KER + 4],
    )


def solution(mesh):
    placed = (
        P("row", "seq", None), P("row", None), P(), P(), P(), P(), P(), P(), P(), P("row", "seq", None),
    )
    return jax.shard_map(
        body,
        mesh=mesh,
        in_specs=placed,
        out_specs=(
            P("row", "seq", None), P("row", "seq", None), P("seq", "row"), P("seq", "row"),
            P("seq", "row"), P("seq", "row"), P(), P(), P(),
        ),
        check_vma=False,
    )
```

```python
import functools

import jax
import jax.numpy as jnp
from jax import lax
from jax.experimental import pallas as pl
from jax.experimental.pallas import tpu as pltpu
from jax.sharding import PartitionSpec as P

HEADS = 12
HEAD = 64
WIN = 128
KER = 5
STR = 4
PAIRS = HEADS // 2

EPSILON = 1e-05
ROOT_HALF = 0.7071067811865476
INV_ROOT_2PI = 0.3989422804014327
NEG_LARGE = -1e30
BF = jnp.bfloat16
F32 = jnp.float32
MB = 1 << 20
MESH = pl.DeviceIdType.MESH


def dot(a, b, ca=1, cb=0):
    return lax.dot_general(a, b, (((ca,), (cb,)), ((), ())), preferred_element_type=F32)


def passed_along(block, axis, distance):
    devices = range(lax.axis_size(axis))
    route = [(i - distance, i) for i in devices if i - distance in devices]
    return lax.ppermute(block, axis, route)


def tap_select(seg_row, half, pooled_local):
    width = seg_row.shape[1]
    shape = (KER * pooled_local, width)
    rows = lax.broadcasted_iota(jnp.int32, shape, 0)
    cols = lax.broadcasted_iota(jnp.int32, shape, 1)
    tap = rows // pooled_local
    centre = half + STR * (rows - tap * pooled_local)
    seg = jnp.broadcast_to(seg_row, shape)
    centre_seg = jnp.sum(jnp.where(cols == centre, seg, 0), axis=1, keepdims=True)
    hit = (cols == centre + tap - KER // 2) & (seg == centre_seg)
    return jnp.where(hit, 1.0, 0.0).astype(BF)


def pool_kernel(half, tok_ref, seg_ref, ker_ref, out_ref):
    pooled_local = out_ref.shape[1]
    picked = dot(tap_select(seg_ref[0], half, pooled_local), tok_ref[0])
    total = picked[:pooled_local] * ker_ref[0:1]
    for t in range(1, KER):
        total = total + picked[t * pooled_local : (t + 1) * pooled_local] * ker_ref[t : t + 1]
    out_ref[0] = total.astype(BF)


def attend_kernel(half, tok_ref, pool_ref, qseg_ref, kseg_ref, w_ref, q_ref, k_ref, v_ref, p_ref, att_ref):
    shard = q_ref.shape[1]
    width = tok_ref.shape[2]
    near = shard + 2 * half
    keys = k_ref.shape[1]
    tok = tok_ref[0]
    own = tok_ref[0, half : half + shard]
    q_ref[0] = (dot(own, w_ref[:, :width]) * HEAD ** (-0.5)).astype(BF)
    k_ref[0, :near] = dot(tok, w_ref[:, width : 2 * width]).astype(BF)
    v_ref[0, :near] = dot(tok, w_ref[:, 2 * width : 3 * width]).astype(BF)
    k_ref[0, near:] = dot(pool_ref[0], w_ref[:, 3 * width : 4 * width]).astype(BF)
    v_ref[0, near:] = dot(pool_ref[0], w_ref[:, 4 * width :]).astype(BF)

    key_seg = jnp.transpose(jnp.broadcast_to(kseg_ref[0], (shard, keys)))
    shape = (keys, shard)
    row = lax.broadcasted_iota(jnp.int32, shape, 0)
    col = lax.broadcasted_iota(jnp.int32, shape, 1)
    inside = (row >= near) | ((row >= col) & (row - col <= 2 * half))
    kept = inside & (key_seg == jnp.broadcast_to(qseg_ref[0], shape))
    bias = jnp.where(kept, 0.0, NEG_LARGE)
    bias = jnp.concatenate([bias, bias], axis=1)
    lane = lax.broadcasted_iota(jnp.int32, (shard, 2 * HEAD), 1)
    even = lane < HEAD
    for j in range(PAIRS):
        cols = slice(2 * HEAD * j, 2 * HEAD * (j + 1))
        qp = q_ref[0, :, cols]
        zero = jnp.zeros_like(qp)
        stacked = jnp.concatenate([jnp.where(even, qp, zero), jnp.where(even, zero, qp)], axis=0)
        scores = dot(k_ref[0, :, cols], stacked, 1, 1) + bias
        top = jnp.max(scores, axis=0, keepdims=True)
        terms = jnp.exp(scores - top)
        prob = (terms * (1.0 / jnp.sum(terms, axis=0, keepdims=True))).astype(BF)
        p_ref[0, j] = prob
        mixed = dot(v_ref[0, :, cols], prob, 0, 0)
        mixed = jnp.concatenate([mixed[:HEAD, :shard], mixed[HEAD:, shard:]], axis=0)
        att_ref[0, :, cols] = jnp.transpose(mixed).astype(BF)


def mlp_kernel(
    tok_ref, att_ref, cot_ref, wo_ref, wu_ref, wd_ref, gain_ref, bias_ref,
    out_ref, act_ref, upg_ref, n1_ref, r2_ref, g1_ref, g1b_ref, da_ref, dsum_ref, small_ref,
    slope,
):
    hidden = wu_ref.shape[1]
    chunk = 512
    gain_a, gain_b = gain_ref[0:1], gain_ref[1:2]

    def mean(x):
        return jnp.mean(x, axis=-1, keepdims=True)

    resid = tok_ref[...].astype(F32) + dot(att_ref[...], wo_ref[...])
    centred = resid - mean(resid)
    rstd_a = lax.rsqrt(mean(centred * centred) + EPSILON)
    hat_a = centred * rstd_a
    normed = hat_a * gain_a + bias_ref[0:1]
    low = normed.astype(BF)
    n1_ref[...] = low
    total = normed
    for c in range(0, hidden, chunk):
        up = dot(low, wu_ref[:, c : c + chunk])
        half_cdf = 0.5 * (1.0 + lax.erf(up * ROOT_HALF))
        act = (up * half_cdf).astype(BF)
        act_ref[:, c : c + chunk] = act
        slope[:, c : c + chunk] = half_cdf + up * (INV_ROOT_2PI * jnp.exp(-0.5 * up * up))
        total = total + dot(act, wd_ref[c : c + chunk, :])
    centred = total - mean(total)
    rstd_b = lax.rsqrt(mean(centred * centred) + EPSILON)
    hat_b = centred * rstd_b
    out_ref[...] = (hat_b * gain_b + bias_ref[1:2]).astype(BF)
    g = cot_ref[...].astype(F32)
    gain_two = jnp.sum(g * hat_b, axis=0, keepdims=True)
    bias_two = jnp.sum(g, axis=0, keepdims=True)
    e = g * gain_b
    grad = rstd_b * (e - mean(e) - hat_b * mean(e * hat_b))
    grad_low = grad.astype(BF)
    r2_ref[...] = grad_low
    for c in range(0, hidden, chunk):
        up_grad = (dot(grad_low, wd_ref[c : c + chunk, :], 1, 1) * slope[:, c : c + chunk]).astype(BF)
        upg_ref[:, c : c + chunk] = up_grad
        grad = grad + dot(up_grad, wu_ref[:, c : c + chunk], 1, 1)
    gain_one = jnp.sum(grad * hat_a, axis=0, keepdims=True)
    bias_one = jnp.sum(grad, axis=0, keepdims=True)
    e = grad * gain_a
    resid_grad = rstd_a * (e - mean(e) - hat_a * mean(e * hat_a))
    g1_ref[...] = resid_grad
    resid_low = resid_grad.astype(BF)
    g1b_ref[...] = resid_low
    att_grad = dot(resid_low, wo_ref[...], 1, 1).astype(BF)
    da_ref[...] = att_grad
    prod = att_grad.astype(F32) * att_ref[...].astype(F32)
    high = prod.astype(BF)
    rest = (prod - high.astype(F32)).astype(BF)
    heads = dsum_ref.shape[0]
    width = prod.shape[1]
    head_row = lax.broadcasted_iota(jnp.int32, (heads, width), 0)
    head_col = lax.broadcasted_iota(jnp.int32, (heads, width), 1) // HEAD
    pick = jnp.where(head_row == head_col, 1.0, 0.0).astype(BF)
    dsum_ref[...] = dot(pick, high, 1, 1) + dot(pick, rest, 1, 1)

    @pl.when(pl.program_id(0) == 0)
    def _():
        small_ref[...] = jnp.zeros_like(small_ref)

    small_ref[0:4] += jnp.concatenate([gain_one, gain_two, bias_one, bias_two], axis=0)


def attend_back_kernel(
    half, q_ref, k_ref, v_ref, p_ref, da_ref, dsum_ref, w_ref,
    dq_ref, dk_ref, dv_ref, dtok_ref, dpool_ref,
):
    shard = q_ref.shape[1]
    width = q_ref.shape[2]
    near = shard + 2 * half
    lane = lax.broadcasted_iota(jnp.int32, (shard, 2 * HEAD), 1)
    even = lane < HEAD

    def stack(pair):
        zero = jnp.zeros_like(pair)
        return jnp.concatenate([jnp.where(even, pair, zero), jnp.where(even, zero, pair)], axis=0)

    for j in range(PAIRS):
        cols = slice(2 * HEAD * j, 2 * HEAD * (j + 1))
        queries = stack(q_ref[0, :, cols])
        grads = stack(da_ref[0, :, cols])
        keys = k_ref[0, :, cols]
        prob = p_ref[0, j]
        dprob = dot(v_ref[0, :, cols], grads, 1, 1)
        row_dot = jnp.concatenate([dsum_ref[2 * j : 2 * j + 1], dsum_ref[2 * j + 1 : 2 * j + 2]], axis=1)
        dscore = (prob.astype(F32) * (dprob - row_dot)).astype(BF)
        dv_ref[0, :, cols] = dot(prob, grads).astype(BF)
        dk_ref[0, :, cols] = dot(dscore, queries).astype(BF)
        mixed = dot(keys, dscore, 0, 0)
        mixed = jnp.concatenate([mixed[:HEAD, :shard], mixed[HEAD:, shard:]], axis=0)
        dq_ref[0, :, cols] = (jnp.transpose(mixed) * HEAD ** (-0.5)).astype(BF)
    dtok_ref[0] = dot(dk_ref[0, :near], w_ref[:, width : 2 * width], 1, 1) + dot(
        dv_ref[0, :near], w_ref[:, 2 * width : 3 * width], 1, 1
    )
    dtok_ref[0, half : half + shard] += dot(dq_ref[0], w_ref[:, :width], 1, 1)
    dpool_ref[0] = (
        dot(dk_ref[0, near:], w_ref[:, 3 * width : 4 * width], 1, 1)
        + dot(dv_ref[0, near:], w_ref[:, 4 * width :], 1, 1)
    ).astype(BF)


def pool_back_kernel(half, tok_ref, seg_ref, ker_ref, dpool_ref, dtok_ref, g1_ref, left_ref, right_ref, out_ref, rim_ref, small_ref):
    shard = out_ref.shape[1]
    pooled_local = dpool_ref.shape[1]
    select = tap_select(seg_ref[0], half, pooled_local)
    picked = dot(select, tok_ref[0])
    grad = dpool_ref[0].astype(F32)
    terms, kernel_rows = [], []
    for t in range(KER):
        terms.append((grad * ker_ref[t : t + 1]).astype(BF))
        kernel_rows.append(
            jnp.sum(grad * picked[t * pooled_local : (t + 1) * pooled_local], axis=0, keepdims=True)
        )
    spread = dot(select, jnp.concatenate(terms, axis=0), 0, 0)
    rim_ref[0] = spread[half - 8 : half].astype(BF)
    total = g1_ref[0] + dtok_ref[0, half : half + shard] + spread[half : half + shard]
    out_ref[0] = total
    out_ref[0, :half] += left_ref[0].astype(F32)
    out_ref[0, shard - half :] += right_ref[0].astype(F32)

    @pl.when(pl.program_id(0) == 0)
    def _():
        small_ref[...] = jnp.zeros_like(small_ref)

    small_ref[0:KER] += jnp.concatenate(kernel_rows, axis=0)


def stage_orders(bits):
    rest = list(range(bits - 1))
    cut = len(rest) // 2
    return (
        [bits - 1] + rest[::-1],
        [bits - 1] + rest[:cut][::-1] + rest[cut:][::-1],
    )


class Reducer:
    def __init__(self, seq_count, row_count, units, dest, held, bufs, zsend, zrecv, sems):
        self.bits = seq_count.bit_length() - 1
        self.row_count = row_count
        self.units = units
        self.dest = dest
        self.held, self.bufs, self.zsend, self.zrecv = held, bufs, zsend, zrecv
        self.send_sem, self.recv_sem, self.zsend_sem, self.zrecv_sem = sems
        self.seq = lax.axis_index("seq")
        self.row = lax.axis_index("row")
        self.orders = stage_orders(self.bits)

    def bit(self, dim):
        weight = 1 << (self.bits - 1 - dim)
        value = (self.seq // weight) % 2
        return value, self.seq + (1 - 2 * value) * weight

    def barrier(self):
        sem = pltpu.get_barrier_semaphore()
        for dim in range(self.bits):
            pl.semaphore_signal(sem, inc=1, device_id={"seq": self.bit(dim)[1]}, device_id_type=MESH)
        for k in range(1, self.row_count):
            other = (self.row + k) % self.row_count
            pl.semaphore_signal(sem, inc=1, device_id={"row": other}, device_id_type=MESH)
        pl.semaphore_wait(sem, self.bits + self.row_count - 1)

    def position(self, unit, stage):
        order = self.orders[unit % 2]
        left = sorted(order[stage:])
        return order[stage], left.index(order[stage])

    def source(self, unit, stage, value):
        pos = self.position(unit, stage)[1]
        base, slot = (self.held, unit % self.held.shape[0]) if stage == 0 else (self.bufs[stage - 1], unit)
        return base, (slot,) + (slice(None),) * pos + (value,)

    def copy(self, unit, stage):
        value, partner = self.bit(self.position(unit, stage)[0])
        base, index = self.source(unit, stage, 1 - value)
        return pltpu.make_async_remote_copy(
            src_ref=base.at[index],
            dst_ref=self.bufs[stage].at[unit],
            send_sem=self.send_sem.at[unit, stage],
            recv_sem=self.recv_sem.at[unit, stage],
            device_id={"seq": partner},
            device_id_type=MESH,
        )

    def start(self, unit):
        self.copy(unit, 0).start()

    def advance(self, unit, stage):
        self.copy(unit, stage - 1).wait()
        dim, pos = self.position(unit, stage - 1)
        value = self.bit(dim)[0]
        buf = self.bufs[stage - 1]
        base, _ = self.source(unit, stage - 1, value)
        slot = unit % self.held.shape[0] if stage == 1 else unit
        lead = self.bits - stage
        total = None
        for flat in range(1 << lead):
            index = tuple((flat >> (lead - 1 - d)) & 1 for d in range(lead))
            own = base[(slot,) + index[:pos] + (value,) + index[pos:]]
            total = own.astype(F32) + buf[(unit,) + index].astype(F32)
            if stage < self.bits:
                buf[(unit,) + index] = total.astype(BF)
        if stage < self.bits:
            self.copy(unit, stage).start()
            return
        cols = total.shape[1] // self.row_count
        for i in range(self.row_count):
            self.zsend[unit, i] = total[:, i * cols : (i + 1) * cols].astype(BF)
        for i in range(self.row_count):
            target, slot = self.dest(unit, i)

            @pl.when(self.row != target)
            def _():
                self.row_copy(unit, i, target, slot).start()

    def row_copy(self, unit, i, target, slot):
        return pltpu.make_async_remote_copy(
            src_ref=self.zsend.at[unit, i],
            dst_ref=self.zrecv.at[slot, self.row],
            send_sem=self.zsend_sem.at[unit, i],
            recv_sem=self.zrecv_sem.at[slot, self.row],
            device_id={"row": target},
            device_id_type=MESH,
        )

    def tick(self, unit):
        if unit < self.units:
            self.start(unit)
        for stage in range(1, self.bits + 1):
            if 0 <= unit - stage < self.units:
                self.advance(unit - stage, stage)

    def arrived(self, slot, unit, i):
        total = self.zsend[unit, i].astype(F32)
        for k in range(1, self.row_count):
            other = (self.row + k) % self.row_count
            pltpu.make_async_remote_copy(
                src_ref=self.zsend.at[0, 0],
                dst_ref=self.zrecv.at[slot, other],
                send_sem=self.zsend_sem.at[0, 0],
                recv_sem=self.zrecv_sem.at[slot, other],
                device_id={"row": other},
                device_id_type=MESH,
            ).wait_recv()
            total = total + self.zrecv[slot, other].astype(F32)
        return total

    def sent(self):
        for unit in range(self.units):
            for i in range(self.row_count):
                target, slot = self.dest(unit, i)

                @pl.when(self.row != target)
                def _():
                    self.row_copy(unit, i, target, slot).wait_send()


def grads_kernel(
    seq_count, row_count, half,
    n1_ref, r2_ref, att_ref, g1_ref, tok_ref, pool_hbm, upg_hbm, act_hbm, dq_hbm, dk_hbm, dv_hbm,
    win_ref, wout_ref, wup_ref, wdown_ref,
    held, *rest,
):
    bits = seq_count.bit_length() - 1
    bufs = rest[:bits]
    zsend, zrecv, slots, pool_ref, partial, send_sem, recv_sem, zsend_sem, zrecv_sem, load_sem, pool_sem = rest[bits:]
    rows, shard, width = n1_ref.shape
    near = tok_ref.shape[1]
    part = width // seq_count
    up_units = upg_hbm.shape[2] // width
    in_base = 2 * up_units + 1
    units = in_base + 5
    tall = width // 2

    def dest(unit, i):
        if unit < up_units:
            g = unit * row_count + i
            return g // up_units, g % up_units
        if unit < in_base:
            return i, unit
        g = (unit - in_base) * row_count + i
        return g // 5, in_base + g % 5

    red = Reducer(
        seq_count, row_count, units, dest, held, bufs, zsend, zrecv, (send_sem, recv_sem, zsend_sem, zrecv_sem)
    )

    acts = up_units * 2
    piece = pool_ref.shape[1]
    pieces = (dk_hbm.shape[1] - near) // piece
    steps = up_units + acts + 3 + 2 * pieces

    def load(k):
        buf = slots.at[k % 2]
        if k < up_units:
            src, dst = upg_hbm.at[:, :, width * k : width * (k + 1)], buf.at[:, :shard]
        elif k < up_units + acts:
            c = k - up_units
            src, dst = act_hbm.at[:, :, tall * c : tall * (c + 1)], buf.at[:, :shard, :tall]
        elif k == up_units + acts:
            src, dst = dq_hbm, buf.at[:, :shard]
        elif k < up_units + acts + 3:
            src, dst = (dk_hbm, dv_hbm)[k - up_units - acts - 1].at[:, :near], buf
        else:
            c = k - up_units - acts - 3
            first = near + (c % pieces) * piece
            src, dst = (dk_hbm, dv_hbm)[c // pieces].at[:, first : first + piece], buf.at[:, :piece]
        return pltpu.make_async_copy(src, dst, load_sem.at[k % 2])

    def taken(k):
        load(k).wait()
        if k + 1 < steps:
            load(k + 1).start()

    def pool_load(n):
        return pltpu.make_async_copy(pool_hbm.at[:, n * piece : (n + 1) * piece], pool_ref, pool_sem)

    load(0).start()
    pool_load(0).start()
    red.barrier()
    group = seq_count // 2
    lead = (2,) * (bits - 1)

    def product(unit, left, right, first=True, last=True):
        for m in range(2):
            total = dot(left(m), right, 0, 0)
            if not first:
                total = total + partial[m]
            if not last:
                partial[m] = total
                continue
            held[unit % held.shape[0], m] = total.reshape(lead + (part, width)).astype(BF)

    def columns(ref, keep=slice(None)):
        return lambda m: ref[:, keep, tall * m : tall * (m + 1)].reshape(-1, tall)

    def whole(k, length):
        return slots[k % 2, :, :length].reshape(-1, width)

    for u in range(up_units):
        taken(u)
        product(u, columns(n1_ref), whole(u, shard))
        red.tick(u)
    product(up_units, columns(att_ref), g1_ref[...].reshape(-1, width))
    red.tick(up_units)
    for c in range(acts):
        k = up_units + c
        taken(k)
        left = slots[k % 2, :, :shard, :tall].reshape(-1, tall)
        total = dot(left, r2_ref[...].reshape(-1, width), 0, 0)
        blocked = total.reshape(tall // part, part, width).astype(BF)
        for n in range(tall // part):
            flat = (c * tall + n * part) // part
            owner, sub = flat // up_units, flat % up_units
            index = tuple((owner >> (bits - 1 - d)) & 1 for d in range(bits))
            held[(up_units + 1 + sub,) + index] = blocked[n]
    for u in range(up_units + 1, in_base):
        red.tick(u)
    own = slice(half, half + shard)
    base = up_units + acts
    sources = [(columns(tok_ref, own), shard), (columns(tok_ref), near), (columns(tok_ref), near)]
    for n, (left, length) in enumerate(sources):
        taken(base + n)
        product(in_base + n, left, whole(base + n, length))
        red.tick(in_base + n)
    for n in range(2):
        for c in range(pieces):
            k = base + 3 + n * pieces + c
            if pieces > 1 and (n or c):
                pool_load(c).start()
            if pieces > 1 or n == 0:
                pool_load(c).wait()
            taken(k)
            product(in_base + 3 + n, columns(pool_ref), whole(k, piece), c == 0, c == pieces - 1)
        red.tick(in_base + 3 + n)
    for u in range(units, units + bits):
        red.tick(u)
    row = red.row
    for n in range(up_units):
        g = row * up_units + n
        cols = width // row_count
        wup_ref[:, n * cols : (n + 1) * cols] = red.arrived(n, g // row_count, g % row_count)
    wout_ref[...] = red.arrived(up_units, up_units, row)
    for n in range(up_units):
        wdown_ref[n * part : (n + 1) * part] = red.arrived(up_units + 1 + n, up_units + 1 + n, row)
    for n in range(5):
        g = row * 5 + n
        win_ref[:, n * cols : (n + 1) * cols] = red.arrived(in_base + n, in_base + g // row_count, g % row_count)
    red.sent()


def body(tokens, segment_ids, w_in, w_out, w_up, w_down, conv_kernel, norm_gain, norm_bias, cotangent):
    rows, shard, width = tokens.shape
    half = WIN // 2
    pooled_local = shard // STR
    near = shard + 2 * half
    count = rows * shard
    hidden = w_up.shape[1]
    seq_count = lax.axis_size("seq")
    row_count = lax.axis_size("row")
    seq_start = lax.axis_index("seq") * shard
    keys = near + pooled_local * seq_count

    own_seg = lax.dynamic_slice_in_dim(segment_ids, seq_start, shard, 1)
    padded_seg = jnp.pad(segment_ids, ((0, 0), (half, half)), constant_values=-1)
    window_seg = lax.dynamic_slice_in_dim(padded_seg, seq_start, near, 1)
    key_seg = jnp.concatenate([window_seg, segment_ids[:, ::STR]], axis=1)
    own_seg = own_seg[:, None]
    key_seg = key_seg[:, None]
    window_seg = window_seg[:, None]

    before = passed_along(tokens[:, shard - half :], "seq", 1)
    after = passed_along(tokens[:, :half], "seq", -1)
    tok_ext = jnp.concatenate([before, tokens, after], axis=1)

    def row_spec(*tail):
        return pl.BlockSpec((1,) + tail, lambda r: (r,) + (0,) * len(tail))

    def whole_spec(*dims):
        return pl.BlockSpec(dims, lambda r: (0,) * len(dims), pipeline_mode=pl.Buffered(1))

    def struct(*dims, dtype=BF):
        return jax.ShapeDtypeStruct(dims, dtype)

    def params(limit):
        return pltpu.CompilerParams(dimension_semantics=("arbitrary",), vmem_limit_bytes=limit * MB)

    pooled = pl.pallas_call(
        functools.partial(pool_kernel, half),
        out_shape=struct(rows, pooled_local, width),
        grid=(rows,),
        in_specs=[row_spec(near, width), row_spec(1, near), whole_spec(KER, width)],
        out_specs=row_spec(pooled_local, width),
        compiler_params=params(32),
        name="pool",
    )(tok_ext, window_seg, conv_kernel)
    pooled_all = lax.all_gather(pooled, "seq", axis=1, tiled=True)
    far = pooled_all.shape[1]

    q, k_all, v_all, prob, attended = pl.pallas_call(
        functools.partial(attend_kernel, half),
        out_shape=(
            struct(rows, shard, width), struct(rows, keys, width), struct(rows, keys, width),
            struct(rows, PAIRS, keys, 2 * shard), struct(rows, shard, width),
        ),
        grid=(rows,),
        in_specs=[
            row_spec(near, width), row_spec(far, width), row_spec(1, shard), row_spec(1, keys),
            whole_spec(*w_in.shape),
        ],
        out_specs=(
            row_spec(shard, width), row_spec(keys, width), row_spec(keys, width),
            row_spec(PAIRS, keys, 2 * shard), row_spec(shard, width),
        ),
        compiler_params=params(56),
        name="attend",
    )(tok_ext, pooled_all, own_seg, key_seg, w_in)

    block = 256
    flat_tokens = tokens.reshape(count, width)
    att_flat = attended.reshape(count, width)
    cot_flat = cotangent.reshape(count, width)

    def tok_spec(cols):
        return pl.BlockSpec((block, cols), lambda i: (i, 0))

    layer_out, act, upg, n1, r2, g1, g1b, att_grad, dsum, norm_sums = pl.pallas_call(
        mlp_kernel,
        out_shape=(
            struct(count, width), struct(count, hidden), struct(count, hidden), struct(count, width),
            struct(count, width), struct(count, width, dtype=F32), struct(count, width), struct(count, width),
            struct(16, count, dtype=F32), struct(8, width, dtype=F32),
        ),
        grid=(count // block,),
        in_specs=[
            tok_spec(width), tok_spec(width), tok_spec(width), whole_spec(*w_out.shape),
            whole_spec(*w_up.shape), whole_spec(*w_down.shape), whole_spec(2, width), whole_spec(2, width),
        ],
        out_specs=(
            tok_spec(width), tok_spec(hidden), tok_spec(hidden), tok_spec(width), tok_spec(width),
            tok_spec(width), tok_spec(width), tok_spec(width),
            pl.BlockSpec((16, block), lambda i: (0, i)), pl.BlockSpec((8, width), lambda i: (0, 0)),
        ),
        scratch_shapes=[pltpu.VMEM((block, hidden), F32)],
        compiler_params=params(56),
        name="mlp",
    )(flat_tokens, att_flat, cot_flat, w_out, w_up, w_down, norm_gain, norm_bias)

    dq, dk, dv, dtok, dpool = pl.pallas_call(
        functools.partial(attend_back_kernel, half),
        out_shape=(
            struct(rows, shard, width), struct(rows, keys, width), struct(rows, keys, width),
            struct(rows, near, width, dtype=F32), struct(rows, far, width),
        ),
        grid=(rows,),
        in_specs=[
            row_spec(shard, width), row_spec(keys, width), row_spec(keys, width),
            row_spec(PAIRS, keys, 2 * shard), row_spec(shard, width),
            pl.BlockSpec((16, shard), lambda r: (0, r)), whole_spec(*w_in.shape),
        ],
        out_specs=(
            row_spec(shard, width), row_spec(keys, width), row_spec(keys, width),
            row_spec(near, width), row_spec(far, width),
        ),
        compiler_params=params(56),
        name="attend_back",
    )(q, k_all, v_all, prob, att_grad.reshape(rows, shard, width), dsum, w_in)

    dpool_own = lax.psum_scatter(dpool, "seq", scatter_dimension=1, tiled=True)
    from_right = passed_along(dtok[:, :half].astype(BF), "seq", -1)
    from_left = passed_along(dtok[:, shard + half :].astype(BF), "seq", 1)

    token_grad, rim, ker_sums = pl.pallas_call(
        functools.partial(pool_back_kernel, half),
        out_shape=(
            struct(rows, shard, width, dtype=F32), struct(rows, 8, width), struct(8, width, dtype=F32),
        ),
        grid=(rows,),
        in_specs=[
            row_spec(near, width), row_spec(1, near), whole_spec(KER, width), row_spec(pooled_local, width),
            row_spec(near, width), row_spec(shard, width), row_spec(half, width), row_spec(half, width),
        ],
        out_specs=(
            row_spec(shard, width), row_spec(8, width), pl.BlockSpec((8, width), lambda r: (0, 0)),
        ),
        compiler_params=params(48),
        name="pool_back",
    )(tok_ext, window_seg, conv_kernel, dpool_own, dtok, g1.reshape(rows, shard, width), from_left, from_right)
    rim_back = passed_along(rim, "seq", -1).astype(F32)
    token_grad = token_grad.at[:, shard - 8 :].add(rim_back)

    def deep(x):
        return x.reshape(rows, shard, -1)

    bits = seq_count.bit_length() - 1
    part = width // seq_count
    up_units = hidden // width
    units = 2 * up_units + 6
    cols = width // row_count
    vmem = pl.BlockSpec(memory_space=pltpu.VMEM)
    hbm = pl.BlockSpec(memory_space=pl.ANY)
    w_in_grad, w_out_grad, w_up_grad, w_down_grad = pl.pallas_call(
        functools.partial(grads_kernel, seq_count, row_count, half),
        out_shape=(
            struct(part, 5 * cols, dtype=F32), struct(part, cols, dtype=F32),
            struct(part, up_units * cols, dtype=F32), struct(up_units * part, cols, dtype=F32),
        ),
        in_specs=[vmem] * 5 + [hbm] * 6,
        out_specs=(vmem,) * 4,
        scratch_shapes=[pltpu.VMEM((2 * up_units + 1,) + (2,) * bits + (part, width), BF)]
        + [pltpu.VMEM((units,) + (2,) * (bits - 1 - i) + (part, width), BF) for i in range(bits)]
        + [
            pltpu.VMEM((units, row_count, part, cols), BF),
            pltpu.VMEM((units, row_count, part, cols), BF),
            pltpu.VMEM((2, rows, near, width), BF),
            pltpu.VMEM((rows, min(near, far), width), BF),
            pltpu.VMEM((2, width // 2, width) if far > near else (8, 128), F32),
            pltpu.SemaphoreType.DMA((units, bits)),
            pltpu.SemaphoreType.DMA((units, bits)),
            pltpu.SemaphoreType.DMA((units, row_count)),
            pltpu.SemaphoreType.DMA((units, row_count)),
            pltpu.SemaphoreType.DMA((2,)),
            pltpu.SemaphoreType.DMA,
        ],
        compiler_params=pltpu.CompilerParams(collective_id=0, has_side_effects=True, vmem_limit_bytes=60 * MB),
        name="grads",
    )(
        deep(n1), deep(r2), attended, deep(g1b), tok_ext, pooled_all, deep(upg), deep(act), dq, dk, dv,
    )

    small_sum = lax.psum(jnp.concatenate([ker_sums[:KER], norm_sums[:4]], axis=0), ("seq", "row"))
    return (
        layer_out.reshape(rows, shard, width),
        token_grad,
        w_in_grad,
        w_out_grad,
        w_up_grad,
        w_down_grad,
        small_sum[:KER],
        small_sum[KER : KER + 2],
        small_sum[KER + 2 : KER + 4],
    )


def solution(mesh):
    placed = (
        P("row", "seq", None), P("row", None), P(), P(), P(), P(), P(), P(), P(), P("row", "seq", None),
    )
    return jax.shard_map(
        body,
        mesh=mesh,
        in_specs=placed,
        out_specs=(
            P("row", "seq", None), P("row", "seq", None), P("seq", "row"), P("seq", "row"),
            P("seq", "row"), P("seq", "row"), P(), P(), P(),
        ),
        check_vma=False,
    )
```

```python
import functools

import jax
import jax.numpy as jnp
from jax import lax
from jax.experimental import pallas as pl
from jax.experimental.pallas import tpu as pltpu
from jax.sharding import PartitionSpec as P

HEADS = 12
HEAD = 64
WIN = 128
KER = 5
STR = 4
PAIRS = HEADS // 2

EPSILON = 1e-05
ROOT_HALF = 0.7071067811865476
INV_ROOT_2PI = 0.3989422804014327
NEG_LARGE = -1e30
BF = jnp.bfloat16
F32 = jnp.float32
MB = 1 << 20
MESH = pl.DeviceIdType.MESH


def dot(a, b, ca=1, cb=0):
    return lax.dot_general(a, b, (((ca,), (cb,)), ((), ())), preferred_element_type=F32)


def passed_along(block, axis, distance):
    devices = range(lax.axis_size(axis))
    route = [(i - distance, i) for i in devices if i - distance in devices]
    return lax.ppermute(block, axis, route)


def tap_select(seg_row, half, pooled_local):
    width = seg_row.shape[1]
    shape = (KER * pooled_local, width)
    rows = lax.broadcasted_iota(jnp.int32, shape, 0)
    cols = lax.broadcasted_iota(jnp.int32, shape, 1)
    tap = rows // pooled_local
    centre = half + STR * (rows - tap * pooled_local)
    seg = jnp.broadcast_to(seg_row, shape)
    centre_seg = jnp.sum(jnp.where(cols == centre, seg, 0), axis=1, keepdims=True)
    hit = (cols == centre + tap - KER // 2) & (seg == centre_seg)
    return jnp.where(hit, 1.0, 0.0).astype(BF)


def pool_kernel(half, tok_ref, seg_ref, ker_ref, out_ref):
    pooled_local = out_ref.shape[1]
    picked = dot(tap_select(seg_ref[0], half, pooled_local), tok_ref[0])
    total = picked[:pooled_local] * ker_ref[0:1]
    for t in range(1, KER):
        total = total + picked[t * pooled_local : (t + 1) * pooled_local] * ker_ref[t : t + 1]
    out_ref[0] = total.astype(BF)


def attend_kernel(half, tok_ref, pool_ref, qseg_ref, kseg_ref, w_ref, q_ref, k_ref, v_ref, p_ref, att_ref):
    shard = q_ref.shape[1]
    width = tok_ref.shape[2]
    near = shard + 2 * half
    keys = k_ref.shape[1]
    tok = tok_ref[0]
    own = tok_ref[0, half : half + shard]
    q_ref[0] = (dot(own, w_ref[:, :width]) * HEAD ** (-0.5)).astype(BF)
    k_ref[0, :near] = dot(tok, w_ref[:, width : 2 * width]).astype(BF)
    v_ref[0, :near] = dot(tok, w_ref[:, 2 * width : 3 * width]).astype(BF)
    k_ref[0, near:] = dot(pool_ref[0], w_ref[:, 3 * width : 4 * width]).astype(BF)
    v_ref[0, near:] = dot(pool_ref[0], w_ref[:, 4 * width :]).astype(BF)

    key_seg = jnp.transpose(jnp.broadcast_to(kseg_ref[0], (shard, keys)))
    shape = (keys, shard)
    row = lax.broadcasted_iota(jnp.int32, shape, 0)
    col = lax.broadcasted_iota(jnp.int32, shape, 1)
    inside = (row >= near) | ((row >= col) & (row - col <= 2 * half))
    kept = inside & (key_seg == jnp.broadcast_to(qseg_ref[0], shape))
    bias = jnp.where(kept, 0.0, NEG_LARGE)
    bias = jnp.concatenate([bias, bias], axis=1)
    lane = lax.broadcasted_iota(jnp.int32, (shard, 2 * HEAD), 1)
    even = lane < HEAD
    for j in range(PAIRS):
        cols = slice(2 * HEAD * j, 2 * HEAD * (j + 1))
        qp = q_ref[0, :, cols]
        zero = jnp.zeros_like(qp)
        stacked = jnp.concatenate([jnp.where(even, qp, zero), jnp.where(even, zero, qp)], axis=0)
        scores = dot(k_ref[0, :, cols], stacked, 1, 1) + bias
        top = jnp.max(scores, axis=0, keepdims=True)
        terms = jnp.exp(scores - top)
        prob = (terms * (1.0 / jnp.sum(terms, axis=0, keepdims=True))).astype(BF)
        p_ref[0, j] = prob
        mixed = dot(v_ref[0, :, cols], prob, 0, 0)
        mixed = jnp.concatenate([mixed[:HEAD, :shard], mixed[HEAD:, shard:]], axis=0)
        att_ref[0, :, cols] = jnp.transpose(mixed).astype(BF)


def mlp_kernel(
    tok_ref, att_ref, cot_ref, wo_ref, wu_ref, wd_ref, gain_ref, bias_ref,
    out_ref, act_ref, upg_ref, n1_ref, r2_ref, g1_ref, g1b_ref, da_ref, dsum_ref, small_ref,
    slope,
):
    hidden = wu_ref.shape[1]
    chunk = 512
    gain_a, gain_b = gain_ref[0:1], gain_ref[1:2]

    def mean(x):
        return jnp.mean(x, axis=-1, keepdims=True)

    resid = tok_ref[...].astype(F32) + dot(att_ref[...], wo_ref[...])
    centred = resid - mean(resid)
    rstd_a = lax.rsqrt(mean(centred * centred) + EPSILON)
    hat_a = centred * rstd_a
    normed = hat_a * gain_a + bias_ref[0:1]
    low = normed.astype(BF)
    n1_ref[...] = low
    total = normed
    for c in range(0, hidden, chunk):
        up = dot(low, wu_ref[:, c : c + chunk])
        half_cdf = 0.5 * (1.0 + lax.erf(up * ROOT_HALF))
        act = (up * half_cdf).astype(BF)
        act_ref[:, c : c + chunk] = act
        slope[:, c : c + chunk] = half_cdf + up * (INV_ROOT_2PI * jnp.exp(-0.5 * up * up))
        total = total + dot(act, wd_ref[c : c + chunk, :])
    centred = total - mean(total)
    rstd_b = lax.rsqrt(mean(centred * centred) + EPSILON)
    hat_b = centred * rstd_b
    out_ref[...] = (hat_b * gain_b + bias_ref[1:2]).astype(BF)
    g = cot_ref[...].astype(F32)
    gain_two = jnp.sum(g * hat_b, axis=0, keepdims=True)
    bias_two = jnp.sum(g, axis=0, keepdims=True)
    e = g * gain_b
    grad = rstd_b * (e - mean(e) - hat_b * mean(e * hat_b))
    grad_low = grad.astype(BF)
    r2_ref[...] = grad_low
    for c in range(0, hidden, chunk):
        up_grad = (dot(grad_low, wd_ref[c : c + chunk, :], 1, 1) * slope[:, c : c + chunk]).astype(BF)
        upg_ref[:, c : c + chunk] = up_grad
        grad = grad + dot(up_grad, wu_ref[:, c : c + chunk], 1, 1)
    gain_one = jnp.sum(grad * hat_a, axis=0, keepdims=True)
    bias_one = jnp.sum(grad, axis=0, keepdims=True)
    e = grad * gain_a
    resid_grad = rstd_a * (e - mean(e) - hat_a * mean(e * hat_a))
    g1_ref[...] = resid_grad
    resid_low = resid_grad.astype(BF)
    g1b_ref[...] = resid_low
    att_grad = dot(resid_low, wo_ref[...], 1, 1).astype(BF)
    da_ref[...] = att_grad
    prod = att_grad.astype(F32) * att_ref[...].astype(F32)
    high = prod.astype(BF)
    rest = (prod - high.astype(F32)).astype(BF)
    heads = dsum_ref.shape[0]
    width = prod.shape[1]
    head_row = lax.broadcasted_iota(jnp.int32, (heads, width), 0)
    head_col = lax.broadcasted_iota(jnp.int32, (heads, width), 1) // HEAD
    pick = jnp.where(head_row == head_col, 1.0, 0.0).astype(BF)
    dsum_ref[...] = dot(pick, high, 1, 1) + dot(pick, rest, 1, 1)

    @pl.when(pl.program_id(0) == 0)
    def _():
        small_ref[...] = jnp.zeros_like(small_ref)

    small_ref[0:4] += jnp.concatenate([gain_one, gain_two, bias_one, bias_two], axis=0)


def stage_orders(bits):
    rest = list(range(bits - 1))
    cut = len(rest) // 2
    return (
        [bits - 1] + rest[::-1],
        [bits - 1] + rest[:cut][::-1] + rest[cut:][::-1],
    )


class Reducer:
    def __init__(self, seq_count, row_count, units, dest, held, bufs, zsend, zrecv, sems, take=None):
        self.take = take
        self.bits = seq_count.bit_length() - 1
        self.row_count = row_count
        self.units = units
        self.dest = dest
        self.held, self.bufs, self.zsend, self.zrecv = held, bufs, zsend, zrecv
        self.send_sem, self.recv_sem, self.zsend_sem, self.zrecv_sem = sems
        self.seq = lax.axis_index("seq")
        self.row = lax.axis_index("row")
        self.orders = stage_orders(self.bits)

    def bit(self, dim):
        weight = 1 << (self.bits - 1 - dim)
        value = (self.seq // weight) % 2
        return value, self.seq + (1 - 2 * value) * weight

    def barrier(self, line=False):
        sem = pltpu.get_barrier_semaphore()
        count = 1 << self.bits
        peers = [{"seq": self.bit(dim)[1]} for dim in range(self.bits)]
        peers += [{"row": (self.row + k) % self.row_count} for k in range(1, self.row_count)]
        if line:
            peers += [{"seq": (self.seq + 1) % count}, {"seq": (self.seq + count - 1) % count}]
        for peer in peers:
            pl.semaphore_signal(sem, inc=1, device_id=peer, device_id_type=MESH)
        pl.semaphore_wait(sem, len(peers))

    def position(self, unit, stage):
        order = self.orders[unit % 2]
        left = sorted(order[stage:])
        return order[stage], left.index(order[stage])

    def source(self, unit, stage, value):
        pos = self.position(unit, stage)[1]
        base, slot = (self.held, unit % self.held.shape[0]) if stage == 0 else (self.bufs[stage - 1], unit)
        return base, (slot,) + (slice(None),) * pos + (value,)

    def copy(self, unit, stage):
        value, partner = self.bit(self.position(unit, stage)[0])
        base, index = self.source(unit, stage, 1 - value)
        return pltpu.make_async_remote_copy(
            src_ref=base.at[index],
            dst_ref=self.bufs[stage].at[unit],
            send_sem=self.send_sem.at[unit, stage],
            recv_sem=self.recv_sem.at[unit, stage],
            device_id={"seq": partner},
            device_id_type=MESH,
        )

    def start(self, unit):
        self.copy(unit, 0).start()

    def advance(self, unit, stage):
        self.copy(unit, stage - 1).wait()
        dim, pos = self.position(unit, stage - 1)
        value = self.bit(dim)[0]
        buf = self.bufs[stage - 1]
        base, _ = self.source(unit, stage - 1, value)
        slot = unit % self.held.shape[0] if stage == 1 else unit
        lead = self.bits - stage
        total = None
        for flat in range(1 << lead):
            index = tuple((flat >> (lead - 1 - d)) & 1 for d in range(lead))
            own = base[(slot,) + index[:pos] + (value,) + index[pos:]]
            total = own.astype(F32) + buf[(unit,) + index].astype(F32)
            if stage < self.bits:
                buf[(unit,) + index] = total.astype(BF)
        if stage < self.bits:
            self.copy(unit, stage).start()
            return
        if self.take is not None:
            self.take(unit, total)
            return
        cols = total.shape[1] // self.row_count
        for i in range(self.row_count):
            self.zsend[unit, i] = total[:, i * cols : (i + 1) * cols].astype(BF)
        for i in range(self.row_count):
            target, slot = self.dest(unit, i)

            @pl.when(self.row != target)
            def _():
                self.row_copy(unit, i, target, slot).start()

    def row_copy(self, unit, i, target, slot):
        return pltpu.make_async_remote_copy(
            src_ref=self.zsend.at[unit, i],
            dst_ref=self.zrecv.at[slot, self.row],
            send_sem=self.zsend_sem.at[unit, i],
            recv_sem=self.zrecv_sem.at[slot, self.row],
            device_id={"row": target},
            device_id_type=MESH,
        )

    def tick(self, unit, start=True):
        if start and unit < self.units:
            self.start(unit)
        for stage in range(1, self.bits + 1):
            if 0 <= unit - (2 * stage - 1) < self.units:
                self.advance(unit - (2 * stage - 1), stage)

    def ticks(self):
        return self.units + 2 * self.bits - 1

    def arrived(self, slot, unit, i):
        total = self.zsend[unit, i].astype(F32)
        for k in range(1, self.row_count):
            other = (self.row + k) % self.row_count
            pltpu.make_async_remote_copy(
                src_ref=self.zsend.at[0, 0],
                dst_ref=self.zrecv.at[slot, other],
                send_sem=self.zsend_sem.at[0, 0],
                recv_sem=self.zrecv_sem.at[slot, other],
                device_id={"row": other},
                device_id_type=MESH,
            ).wait_recv()
            total = total + self.zrecv[slot, other].astype(F32)
        return total

    def sent(self):
        for unit in range(self.units):
            for i in range(self.row_count):
                target, slot = self.dest(unit, i)

                @pl.when(self.row != target)
                def _():
                    self.row_copy(unit, i, target, slot).wait_send()


def split_index(flat, bits):
    return tuple((flat >> (bits - 1 - d)) & 1 for d in range(bits))


def mid_kernel(
    seq_count, row_count, half, buffers,
    n1_hbm, r2_hbm, att_hbm, g1b_hbm, upg_hbm, act_hbm, w_hbm, dsum_ref,
    q_hbm, k_hbm, v_hbm, p_hbm, da_hbm, g1_hbm,
    wout_ref, wup_ref, wdown_ref, dq_hbm, dk_hbm, dv_hbm, dpool_hbm, own_hbm, left_hbm, right_hbm,
    held, *rest,
):
    bits = seq_count.bit_length() - 1
    bufs = rest[:bits]
    (
        zsend, zrecv, slots, n1_ref, r2_ref, att_ref, g1b_ref, w_ref,
        qb, kb, vb, pb, dab, g1_buf, dqb, dkb, dvb, dpb, owb, lfb, rtb,
        send_sem, recv_sem, zsend_sem, zrecv_sem, load_sem, once_sem, in_sem, out_sem,
    ) = rest[bits:]
    rows, shard, width = n1_ref.shape
    near = shard + 2 * half
    part = width // seq_count
    up_units = upg_hbm.shape[2] // width
    units = 2 * up_units + 1
    tall = width // 2
    acts = up_units * 2
    steps = up_units + acts

    def dest(unit, i):
        if unit < up_units:
            g = unit * row_count + i
            return g // up_units, g % up_units
        return i, unit

    red = Reducer(
        seq_count, row_count, units, dest, held, bufs, zsend, zrecv, (send_sem, recv_sem, zsend_sem, zrecv_sem)
    )
    once = [
        pltpu.make_async_copy(src, dst, once_sem.at[n])
        for n, (src, dst) in enumerate(
            [(n1_hbm, n1_ref), (att_hbm, att_ref), (g1b_hbm, g1b_ref), (r2_hbm, r2_ref), (w_hbm, w_ref)]
        )
    ]

    def load(k):
        buf = slots.at[k % 2]
        if k < up_units:
            src, dst = upg_hbm.at[:, :, width * k : width * (k + 1)], buf
        else:
            c = k - up_units
            src, dst = act_hbm.at[:, :, tall * c : tall * (c + 1)], buf.at[:, :, :tall]
        return pltpu.make_async_copy(src, dst, load_sem.at[k % 2])

    def taken(k):
        load(k).wait()
        if k + 1 < steps:
            load(k + 1).start()

    def row_loads(r, slot):
        pairs = [(q_hbm, qb), (k_hbm, kb), (v_hbm, vb), (p_hbm, pb), (da_hbm, dab), (g1_hbm, g1_buf)]
        return [
            pltpu.make_async_copy(src.at[r], dst.at[slot], in_sem.at[n, slot])
            for n, (src, dst) in enumerate(pairs)
        ]

    def row_stores(r, slot):
        pairs = [
            (dqb, dq_hbm), (dkb, dk_hbm), (dvb, dv_hbm), (dpb, dpool_hbm), (owb, own_hbm),
            (lfb, left_hbm), (rtb, right_hbm),
        ]
        return [
            pltpu.make_async_copy(src.at[slot], dst.at[r], out_sem.at[n, slot])
            for n, (src, dst) in enumerate(pairs)
        ]

    once[0].start()
    load(0).start()
    for copy in once[1:]:
        copy.start()
    if buffers > 1:
        for copy in row_loads(0, 0):
            copy.start()
    red.barrier()
    lead = (2,) * (bits - 1)

    def product(unit, left_ref, right):
        for m in range(2):
            left = left_ref[:, :, tall * m : tall * (m + 1)].reshape(-1, tall)
            held[unit, m] = dot(left, right, 0, 0).reshape(lead + (part, width)).astype(BF)

    once[0].wait()
    for u in range(up_units):
        taken(u)
        product(u, n1_ref, slots[u % 2].reshape(-1, width))
        red.tick(u)
    once[1].wait()
    once[2].wait()
    product(up_units, att_ref, g1b_ref[...].reshape(-1, width))
    red.tick(up_units)
    once[3].wait()
    for c in range(acts):
        k = up_units + c
        taken(k)
        left = slots[k % 2, :, :, :tall].reshape(-1, tall)
        total = dot(left, r2_ref[...].reshape(-1, width), 0, 0)
        blocked = total.reshape(tall // part, part, width).astype(BF)
        for n in range(tall // part):
            flat = (c * tall + n * part) // part
            held[(up_units + 1 + flat % up_units,) + split_index(flat // up_units, bits)] = blocked[n]
    for u in range(up_units + 1, units):
        red.start(u)
    once[4].wait()

    lane = lax.broadcasted_iota(jnp.int32, (shard, 2 * HEAD), 1)
    even = lane < HEAD

    def stack(pair):
        zero = jnp.zeros_like(pair)
        return jnp.concatenate([jnp.where(even, pair, zero), jnp.where(even, zero, pair)], axis=0)

    def row_step(r, carry):
        slot = r % buffers
        if buffers > 1:

            @pl.when(r + 1 < rows)
            def _():
                for copy in row_loads(r + 1, (r + 1) % buffers):
                    copy.start()

        else:
            for copy in row_loads(r, slot):
                copy.start()
        for t in range(rows):

            @pl.when(r == t)
            def _():
                red.tick(up_units + 1 + t, start=False)

        for copy in row_loads(r, slot):
            copy.wait()

        @pl.when(r >= buffers)
        def _():
            for copy in row_stores(r - buffers, slot):
                copy.wait()

        row_sums = dsum_ref[:, pl.ds(pl.multiple_of(r * shard, shard), shard)]
        for j in range(PAIRS):
            cols = slice(2 * HEAD * j, 2 * HEAD * (j + 1))
            queries = stack(qb[slot, :, cols])
            grads = stack(dab[slot, :, cols])
            prob = pb[slot, j]
            dprob = dot(vb[slot, :, cols], grads, 1, 1)
            row_dot = jnp.concatenate([row_sums[2 * j : 2 * j + 1], row_sums[2 * j + 1 : 2 * j + 2]], axis=1)
            dscore = (prob.astype(F32) * (dprob - row_dot)).astype(BF)
            dvb[slot, :, cols] = dot(prob, grads).astype(BF)
            dkb[slot, :, cols] = dot(dscore, queries).astype(BF)
            mixed = dot(kb[slot, :, cols], dscore, 0, 0)
            mixed = jnp.concatenate([mixed[:HEAD, :shard], mixed[HEAD:, shard:]], axis=0)
            dqb[slot, :, cols] = (jnp.transpose(mixed) * HEAD ** (-0.5)).astype(BF)
        back = dot(dkb[slot, :near], w_ref[:, width : 2 * width], 1, 1) + dot(
            dvb[slot, :near], w_ref[:, 2 * width : 3 * width], 1, 1
        )
        lfb[slot] = back[:half].astype(BF)
        rtb[slot] = back[half + shard :].astype(BF)
        owb[slot] = g1_buf[slot] + back[half : half + shard] + dot(dqb[slot], w_ref[:, :width], 1, 1)
        dpb[slot] = (
            dot(dkb[slot, near:], w_ref[:, 3 * width : 4 * width], 1, 1)
            + dot(dvb[slot, near:], w_ref[:, 4 * width :], 1, 1)
        ).astype(BF)
        for copy in row_stores(r, slot):
            copy.start()
        return carry

    lax.fori_loop(0, rows, row_step, 0)
    for t in range(up_units + 1 + rows, red.ticks()):
        red.tick(t, start=False)
    for n in range(buffers):
        r = rows - buffers + n
        for copy in row_stores(r, r % buffers):
            copy.wait()
    row = red.row
    cols = width // row_count
    for n in range(up_units):
        g = row * up_units + n
        wup_ref[:, n * cols : (n + 1) * cols] = red.arrived(n, g // row_count, g % row_count)
    wout_ref[...] = red.arrived(up_units, up_units, row)
    for n in range(up_units):
        wdown_ref[n * part : (n + 1) * part] = red.arrived(up_units + 1 + n, up_units + 1 + n, row)
    red.sent()


def tail_kernel(
    seq_count, row_count, half,
    tok_ref, pool_hbm, dq_hbm, dk_hbm, dv_hbm, dpool_hbm, own_hbm, left_hbm, right_hbm,
    seg_ref, ker_ref, norm_ref,
    win_ref, out_hbm, small_ref,
    held, *rest,
):
    bits = seq_count.bit_length() - 1
    bufs, rest = rest[:bits], rest[bits:]
    pheld, pbufs, rest = rest[0], rest[1 : 1 + bits], rest[1 + bits :]
    (
        zsend, zrecv, slots, pool_ref, partial, dpool_own, from_left, from_right, rim_out, rim_in, ownb, outb,
        ssum, srecv, zsum,
        send_sem, recv_sem, zsend_sem, zrecv_sem, psend_sem, precv_sem, load_sem, pool_sem, ploads_sem,
        line_sem, own_sem, out_sem, small_sem, zsmall_sem,
    ) = rest
    rows, near, width = tok_ref.shape
    shard = near - 2 * half
    part = width // seq_count
    units = 5
    tall = width // 2
    piece = pool_ref.shape[1]
    pieces = (dk_hbm.shape[1] - near) // piece
    steps = 3 + 2 * pieces
    pooled_local = dpool_own.shape[1]
    wide = width // 2

    def dest(unit, i):
        g = unit * row_count + i
        return g // 5, g % 5

    red = Reducer(
        seq_count, row_count, units, dest, held, bufs, zsend, zrecv, (send_sem, recv_sem, zsend_sem, zrecv_sem)
    )

    def take(unit, total):
        dpool_own[:, :, unit * wide : (unit + 1) * wide] = total

    pred = Reducer(
        seq_count, row_count, 2, None, pheld, pbufs, None, None, (psend_sem, precv_sem, None, None), take
    )

    def load(k):
        buf = slots.at[k % 2]
        if k == 0:
            src, dst = dq_hbm, buf.at[:, :shard]
        elif k < 3:
            src, dst = (dk_hbm, dv_hbm)[k - 1].at[:, :near], buf
        else:
            c = k - 3
            first = near + (c % pieces) * piece
            src, dst = (dk_hbm, dv_hbm)[c // pieces].at[:, first : first + piece], buf.at[:, :piece]
        return pltpu.make_async_copy(src, dst, load_sem.at[k % 2])

    def taken(k):
        load(k).wait()
        if k + 1 < steps:
            load(k + 1).start()

    def pool_load(n):
        return pltpu.make_async_copy(pool_hbm.at[:, n * piece : (n + 1) * piece], pool_ref, pool_sem)

    def grad_load(unit, owner):
        src = dpool_hbm.at[:, owner * pooled_local : (owner + 1) * pooled_local, unit * wide : (unit + 1) * wide]
        return pltpu.make_async_copy(
            src, pheld.at[(unit,) + split_index(owner, bits)], ploads_sem.at[unit, owner]
        )

    def line(n, src, dst, step):
        return pltpu.make_async_remote_copy(
            src_ref=src, dst_ref=dst, send_sem=line_sem.at[n, 0], recv_sem=line_sem.at[n, 1],
            device_id={"seq": red.seq + step}, device_id_type=MESH,
        )

    to_prev = line(0, left_hbm, from_right, -1)
    to_next = line(1, right_hbm, from_left, 1)
    rim = line(2, rim_out, rim_in, -1)
    has_prev = red.seq > 0
    has_next = red.seq < seq_count - 1

    for unit in range(2):
        for owner in range(seq_count):
            grad_load(unit, owner).start()
    load(0).start()
    pool_load(0).start()
    red.barrier(line=True)
    for unit in range(2):
        for owner in range(seq_count):
            grad_load(unit, owner).wait()
        pred.start(unit)

    @pl.when(has_prev)
    def _():
        to_prev.start()

    @pl.when(has_next)
    def _():
        to_next.start()

    lead = (2,) * (bits - 1)

    def product(unit, left, right, first=True, last=True):
        for m in range(2):
            total = dot(left(m), right, 0, 0)
            if not first:
                total = total + partial[m]
            if not last:
                partial[m] = total
                continue
            held[unit, m] = total.reshape(lead + (part, width)).astype(BF)

    def columns(ref, keep=slice(None)):
        return lambda m: ref[:, keep, tall * m : tall * (m + 1)].reshape(-1, tall)

    def whole(k, length):
        return slots[k % 2, :, :length].reshape(-1, width)

    own = slice(half, half + shard)
    sources = [(columns(tok_ref, own), shard), (columns(tok_ref), near), (columns(tok_ref), near)]
    for n, (left, length) in enumerate(sources):
        taken(n)
        product(n, left, whole(n, length))
        if n == 0:
            pred.advance(0, 1)
            pred.advance(1, 1)
        red.tick(n)
    for n in range(2):
        for c in range(pieces):
            k = 3 + n * pieces + c
            if pieces > 1 and (n or c):
                pool_load(c).start()
            if pieces > 1 or n == 0:
                pool_load(c).wait()
            taken(k)
            product(3 + n, columns(pool_ref), whole(k, piece), c == 0, c == pieces - 1)
        red.tick(3 + n)
        if n == 0:
            pred.advance(0, 2)
            pred.advance(1, 2)
    for stage in range(3, bits + 1):
        pred.advance(0, stage)
        pred.advance(1, stage)

    ssum[...] = jnp.zeros_like(ssum)
    ssum[8:12] = norm_ref[0:4]

    def own_load(r, slot):
        return pltpu.make_async_copy(own_hbm.at[r], ownb.at[slot], own_sem.at[slot])

    def out_store(r, slot):
        return pltpu.make_async_copy(outb.at[slot], out_hbm.at[r], out_sem.at[slot])

    @pl.when(has_next)
    def _():
        to_prev.wait_recv()

    @pl.when(has_prev)
    def _():
        to_next.wait_recv()

    own_load(0, 0).start()

    def pool_step(r, carry):
        slot = r % 2

        @pl.when(r + 1 < rows)
        def _():
            own_load(r + 1, (r + 1) % 2).start()

        select = tap_select(seg_ref[r], half, pooled_local)
        picked = dot(select, tok_ref[r])
        grad = dpool_own[r]
        terms, sums = [], []
        for t in range(KER):
            terms.append((grad * ker_ref[t : t + 1]).astype(BF))
            sums.append(jnp.sum(grad * picked[t * pooled_local : (t + 1) * pooled_local], axis=0, keepdims=True))
        ssum[0:KER] += jnp.concatenate(sums, axis=0)
        spread = dot(select, jnp.concatenate(terms, axis=0), 0, 0)
        rim_out[r] = spread[half - 16 : half].astype(BF)
        own_load(r, slot).wait()

        @pl.when(r >= 2)
        def _():
            out_store(r - 2, slot).wait()

        outb[slot] = ownb[slot] + spread[half : half + shard]

        @pl.when(has_prev)
        def _():
            outb[slot, :half] += from_left[r].astype(F32)

        @pl.when(has_next)
        def _():
            outb[slot, shard - half :] += from_right[r].astype(F32)

        out_store(r, slot).start()
        return carry

    lax.fori_loop(0, rows, pool_step, 0)

    @pl.when(has_prev)
    def _():
        rim.start()

    for t in range(units, red.ticks()):
        red.tick(t)
    for n in range(2):
        out_store(rows - 2 + n, n).wait()

    def edge(load):
        pairs = (out_hbm.at[:, shard - 16 :], outb.at[0, : rows * 16].reshape(rows, 16, width))
        return pltpu.make_async_copy(*(pairs if load else pairs[::-1]), own_sem.at[0])

    edge(True).start()
    edge(True).wait()

    @pl.when(has_next)
    def _():
        rim.wait_recv()
        outb[0, : rows * 16] += rim_in[...].reshape(rows * 16, width).astype(F32)

    edge(False).start()

    for stage in range(bits):
        dim = bits - 1 - stage
        copy = pltpu.make_async_remote_copy(
            src_ref=ssum, dst_ref=srecv.at[stage], send_sem=small_sem.at[stage, 0], recv_sem=small_sem.at[stage, 1],
            device_id={"seq": red.bit(dim)[1]}, device_id_type=MESH,
        )
        copy.start()
        copy.wait()
        ssum[...] += srecv[stage]

    def small_row(k):
        other = (red.row + k) % row_count
        return pltpu.make_async_remote_copy(
            src_ref=ssum, dst_ref=zsum.at[row_count - k], send_sem=zsmall_sem.at[k, 0],
            recv_sem=zsmall_sem.at[row_count - k, 1], device_id={"row": other}, device_id_type=MESH,
        )

    for k in range(1, row_count):
        small_row(k).start()
    zsum[0] = ssum[...]
    cols = width // row_count
    for n in range(5):
        g = red.row * 5 + n
        win_ref[:, n * cols : (n + 1) * cols] = red.arrived(n, g // row_count, g % row_count)
    total = None
    for k in range(1, row_count):
        small_row(row_count - k).wait_recv()
    for owner in range(row_count):
        term = zsum[(owner - red.row + row_count) % row_count]
        total = term if total is None else total + term
    small_ref[...] = total
    for k in range(1, row_count):
        small_row(k).wait_send()
    red.sent()
    edge(False).wait()

    @pl.when(has_prev)
    def _():
        to_prev.wait_send()
        rim.wait_send()

    @pl.when(has_next)
    def _():
        to_next.wait_send()


def body(tokens, segment_ids, w_in, w_out, w_up, w_down, conv_kernel, norm_gain, norm_bias, cotangent):
    rows, shard, width = tokens.shape
    half = WIN // 2
    pooled_local = shard // STR
    near = shard + 2 * half
    count = rows * shard
    hidden = w_up.shape[1]
    seq_count = lax.axis_size("seq")
    row_count = lax.axis_size("row")
    seq_start = lax.axis_index("seq") * shard
    keys = near + pooled_local * seq_count

    own_seg = lax.dynamic_slice_in_dim(segment_ids, seq_start, shard, 1)
    padded_seg = jnp.pad(segment_ids, ((0, 0), (half, half)), constant_values=-1)
    window_seg = lax.dynamic_slice_in_dim(padded_seg, seq_start, near, 1)
    key_seg = jnp.concatenate([window_seg, segment_ids[:, ::STR]], axis=1)
    own_seg = own_seg[:, None]
    key_seg = key_seg[:, None]
    window_seg = window_seg[:, None]

    before = passed_along(tokens[:, shard - half :], "seq", 1)
    after = passed_along(tokens[:, :half], "seq", -1)
    tok_ext = jnp.concatenate([before, tokens, after], axis=1)

    def row_spec(*tail):
        return pl.BlockSpec((1,) + tail, lambda r: (r,) + (0,) * len(tail))

    def whole_spec(*dims):
        return pl.BlockSpec(dims, lambda r: (0,) * len(dims), pipeline_mode=pl.Buffered(1))

    def struct(*dims, dtype=BF):
        return jax.ShapeDtypeStruct(dims, dtype)

    def params(limit):
        return pltpu.CompilerParams(dimension_semantics=("arbitrary",), vmem_limit_bytes=limit * MB)

    pooled = pl.pallas_call(
        functools.partial(pool_kernel, half),
        out_shape=struct(rows, pooled_local, width),
        grid=(rows,),
        in_specs=[row_spec(near, width), row_spec(1, near), whole_spec(KER, width)],
        out_specs=row_spec(pooled_local, width),
        compiler_params=params(32),
        name="pool",
    )(tok_ext, window_seg, conv_kernel)
    pooled_all = lax.all_gather(pooled, "seq", axis=1, tiled=True)
    far = pooled_all.shape[1]

    q, k_all, v_all, prob, attended = pl.pallas_call(
        functools.partial(attend_kernel, half),
        out_shape=(
            struct(rows, shard, width), struct(rows, keys, width), struct(rows, keys, width),
            struct(rows, PAIRS, keys, 2 * shard), struct(rows, shard, width),
        ),
        grid=(rows,),
        in_specs=[
            row_spec(near, width), row_spec(far, width), row_spec(1, shard), row_spec(1, keys),
            whole_spec(*w_in.shape),
        ],
        out_specs=(
            row_spec(shard, width), row_spec(keys, width), row_spec(keys, width),
            row_spec(PAIRS, keys, 2 * shard), row_spec(shard, width),
        ),
        compiler_params=params(56),
        name="attend",
    )(tok_ext, pooled_all, own_seg, key_seg, w_in)

    block = 256
    flat_tokens = tokens.reshape(count, width)
    att_flat = attended.reshape(count, width)
    cot_flat = cotangent.reshape(count, width)

    def tok_spec(cols):
        return pl.BlockSpec((block, cols), lambda i: (i, 0))

    layer_out, act, upg, n1, r2, g1, g1b, att_grad, dsum, norm_sums = pl.pallas_call(
        mlp_kernel,
        out_shape=(
            struct(count, width), struct(count, hidden), struct(count, hidden), struct(count, width),
            struct(count, width), struct(count, width, dtype=F32), struct(count, width), struct(count, width),
            struct(16, count, dtype=F32), struct(8, width, dtype=F32),
        ),
        grid=(count // block,),
        in_specs=[
            tok_spec(width), tok_spec(width), tok_spec(width), whole_spec(*w_out.shape),
            whole_spec(*w_up.shape), whole_spec(*w_down.shape), whole_spec(2, width), whole_spec(2, width),
        ],
        out_specs=(
            tok_spec(width), tok_spec(hidden), tok_spec(hidden), tok_spec(width), tok_spec(width),
            tok_spec(width), tok_spec(width), tok_spec(width),
            pl.BlockSpec((16, block), lambda i: (0, i)), pl.BlockSpec((8, width), lambda i: (0, 0)),
        ),
        scratch_shapes=[pltpu.VMEM((block, hidden), F32)],
        compiler_params=params(56),
        name="mlp",
    )(flat_tokens, att_flat, cot_flat, w_out, w_up, w_down, norm_gain, norm_bias)

    def deep(x):
        return x.reshape(rows, shard, -1)

    bits = seq_count.bit_length() - 1
    part = width // seq_count
    up_units = hidden // width
    cols = width // row_count
    buffers = 2 if keys <= 2 * near else 1
    vmem = pl.BlockSpec(memory_space=pltpu.VMEM)
    hbm = pl.BlockSpec(memory_space=pl.ANY)
    dma = pltpu.SemaphoreType.DMA

    def halves(units, *tail, dtype=BF):
        return [pltpu.VMEM((units,) + (2,) * (bits - i) + tail, dtype) for i in range(bits + 1)]

    def scratch(*dims, dtype=BF):
        return pltpu.VMEM(dims, dtype)

    units = 2 * up_units + 1
    (
        w_out_grad, w_up_grad, w_down_grad, dq, dk, dv, dpool, own_grad, left_grad, right_grad,
    ) = pl.pallas_call(
        functools.partial(mid_kernel, seq_count, row_count, half, buffers),
        out_shape=(
            struct(part, cols, dtype=F32), struct(part, up_units * cols, dtype=F32),
            struct(up_units * part, cols, dtype=F32),
            struct(rows, shard, width), struct(rows, keys, width), struct(rows, keys, width),
            struct(rows, far, width), struct(rows, shard, width, dtype=F32),
            struct(rows, half, width), struct(rows, half, width),
        ),
        in_specs=[hbm] * 7 + [vmem] + [hbm] * 6,
        out_specs=(vmem,) * 3 + (hbm,) * 7,
        scratch_shapes=halves(units, part, width)
        + [scratch(units, row_count, part, cols), scratch(units, row_count, part, cols)]
        + [scratch(2, rows, shard, width)] + [scratch(rows, shard, width)] * 4 + [scratch(*w_in.shape)]
        + [
            scratch(buffers, shard, width), scratch(buffers, keys, width), scratch(buffers, keys, width),
            scratch(buffers, PAIRS, keys, 2 * shard), scratch(buffers, shard, width),
            scratch(buffers, shard, width, dtype=F32),
            scratch(buffers, shard, width), scratch(buffers, keys, width), scratch(buffers, keys, width),
            scratch(buffers, far, width), scratch(buffers, shard, width, dtype=F32),
            scratch(buffers, half, width), scratch(buffers, half, width),
        ]
        + [
            dma((units, bits)), dma((units, bits)), dma((units, row_count)), dma((units, row_count)),
            dma((2,)), dma((5,)), dma((6, buffers)), dma((7, buffers)),
        ],
        compiler_params=pltpu.CompilerParams(collective_id=0, has_side_effects=True, vmem_limit_bytes=60 * MB),
        name="mid",
    )(
        deep(n1), deep(r2), attended, deep(g1b), deep(upg), deep(act), w_in, dsum,
        q, k_all, v_all, prob, deep(att_grad), deep(g1),
    )

    w_in_grad, token_grad, small_sum = pl.pallas_call(
        functools.partial(tail_kernel, seq_count, row_count, half),
        out_shape=(
            struct(part, 5 * cols, dtype=F32), struct(rows, shard, width, dtype=F32), struct(16, width, dtype=F32),
        ),
        in_specs=[vmem] + [hbm] * 8 + [vmem] * 3,
        out_specs=(vmem, hbm, vmem),
        scratch_shapes=halves(5, part, width) + halves(2, rows, pooled_local, width // 2)
        + [scratch(5, row_count, part, cols), scratch(5, row_count, part, cols)]
        + [
            scratch(2, rows, near, width), scratch(rows, min(near, far), width),
            scratch(*((2, width // 2, width) if far > near else (8, 128)), dtype=F32),
            scratch(rows, pooled_local, width, dtype=F32), scratch(rows, half, width), scratch(rows, half, width),
            scratch(rows, 16, width), scratch(rows, 16, width),
            scratch(2, shard, width, dtype=F32), scratch(2, shard, width, dtype=F32),
            scratch(16, width, dtype=F32), scratch(bits, 16, width, dtype=F32), scratch(row_count, 16, width, dtype=F32),
        ]
        + [
            dma((5, bits)), dma((5, bits)), dma((5, row_count)), dma((5, row_count)), dma((2, bits)), dma((2, bits)),
            dma((2,)), dma, dma((2, seq_count)), dma((3, 2)), dma((2,)), dma((2,)), dma((bits, 2)), dma((row_count, 2)),
        ],
        compiler_params=pltpu.CompilerParams(collective_id=1, has_side_effects=True, vmem_limit_bytes=60 * MB),
        name="tail",
    )(
        tok_ext, pooled_all, dq, dk, dv, dpool, own_grad, left_grad, right_grad,
        window_seg, conv_kernel, norm_sums,
    )
    return (
        layer_out.reshape(rows, shard, width),
        token_grad,
        w_in_grad,
        w_out_grad,
        w_up_grad,
        w_down_grad,
        small_sum[:KER],
        small_sum[8:10],
        small_sum[10:12],
    )


def solution(mesh):
    placed = (
        P("row", "seq", None), P("row", None), P(), P(), P(), P(), P(), P(), P(), P("row", "seq", None),
    )
    return jax.shard_map(
        body,
        mesh=mesh,
        in_specs=placed,
        out_specs=(
            P("row", "seq", None), P("row", "seq", None), P("seq", "row"), P("seq", "row"),
            P("seq", "row"), P("seq", "row"), P(), P(), P(),
        ),
        check_vma=False,
    )
```

```python
import functools

import jax
import jax.numpy as jnp
from jax import lax
from jax.experimental import pallas as pl
from jax.experimental.pallas import tpu as pltpu
from jax.sharding import PartitionSpec as P

HEADS = 12
HEAD = 64
WIN = 128
KER = 5
STR = 4
PAIRS = HEADS // 2

EPSILON = 1e-05
ROOT_HALF = 0.7071067811865476
INV_ROOT_2PI = 0.3989422804014327
NEG_LARGE = -1e30
BF = jnp.bfloat16
F32 = jnp.float32
MB = 1 << 20
MESH = pl.DeviceIdType.MESH


def dot(a, b, ca=1, cb=0):
    return lax.dot_general(a, b, (((ca,), (cb,)), ((), ())), preferred_element_type=F32)


def tap_select(seg_row, half, pooled_local):
    width = seg_row.shape[1]
    shape = (KER * pooled_local, width)
    rows = lax.broadcasted_iota(jnp.int32, shape, 0)
    cols = lax.broadcasted_iota(jnp.int32, shape, 1)
    tap = rows // pooled_local
    centre = half + STR * (rows - tap * pooled_local)
    seg = jnp.broadcast_to(seg_row, shape)
    centre_seg = jnp.sum(jnp.where(cols == centre, seg, 0), axis=1, keepdims=True)
    hit = (cols == centre + tap - KER // 2) & (seg == centre_seg)
    return jnp.where(hit, 1.0, 0.0).astype(BF)


def front_kernel(
    seq_count, half, buffers,
    tok_hbm, w_hbm, wseg_ref, qseg_ref, kseg_ref, ker_ref,
    ext_hbm, pool_hbm, q_hbm, k_hbm, v_hbm, p_hbm, att_hbm,
    tokx, rim_in, pool_ref, w_ref, qb, knb, vnb, kfb, vfb, pb, attb,
    load_sem, line_sem, gather_sem, near_sem, far_sem, ext_sem, pool_sem,
):
    bits = seq_count.bit_length() - 1
    rows, near, width = tokx.shape
    shard = near - 2 * half
    keys = k_hbm.shape[1]
    pooled_local = pool_ref.shape[bits + 1]
    seq = lax.axis_index("seq")
    has_prev = seq > 0
    has_next = seq < seq_count - 1
    edge = 16

    def flipped(dim):
        weight = 1 << (bits - 1 - dim)
        return seq + (1 - 2 * ((seq // weight) % 2)) * weight

    def line(n, src, dst, step):
        return pltpu.make_async_remote_copy(
            src_ref=src, dst_ref=dst, send_sem=line_sem.at[n, 0], recv_sem=line_sem.at[n, 1],
            device_id={"seq": seq + step}, device_id_type=MESH,
        )

    rim = line(0, tok_hbm.at[:, shard - edge :], rim_in, 1)
    to_next = line(1, tok_hbm.at[:, shard - half :], tokx.at[:, :half], 1)
    to_prev = line(2, tok_hbm.at[:, :half], tokx.at[:, half + shard :], -1)

    rest = list(range(bits - 1))
    cut = len(rest) // 2
    orders = (rest[::-1] + [bits - 1], rest[:cut][::-1] + rest[cut:][::-1] + [bits - 1])

    def gather(part, stage):
        order = orders[part]
        done = order[:stage]
        index = tuple(
            slice(None) if d in done else (seq // (1 << (bits - 1 - d))) % 2 for d in range(bits)
        )
        cols = slice(part * (width // 2), (part + 1) * (width // 2))
        block = pool_ref.at[index + (slice(None), slice(None), cols)]
        return pltpu.make_async_remote_copy(
            src_ref=block, dst_ref=block, send_sem=gather_sem.at[part, stage, 0],
            recv_sem=gather_sem.at[part, stage, 1],
            device_id={"seq": flipped(order[stage])}, device_id_type=MESH,
        )

    own = slice(half, half + shard)
    own_load = pltpu.make_async_copy(tok_hbm, tokx.at[:, own], load_sem.at[0])
    w_load = pltpu.make_async_copy(w_hbm, w_ref, load_sem.at[1])
    own_load.start()
    w_load.start()
    sem = pltpu.get_barrier_semaphore()
    peers = [flipped(d) for d in range(bits)] + [(seq + 1) % seq_count, (seq + seq_count - 1) % seq_count]
    for peer in peers:
        pl.semaphore_signal(sem, inc=1, device_id={"seq": peer}, device_id_type=MESH)
    pl.semaphore_wait(sem, len(peers))

    @pl.when(has_next)
    def _():
        rim.start()

    @pl.when(jnp.logical_not(has_prev))
    def _():
        rim_in[...] = jnp.zeros_like(rim_in)
        tokx[:, :half] = jnp.zeros((rows, half, width), BF)

    @pl.when(jnp.logical_not(has_next))
    def _():
        tokx[:, half + shard :] = jnp.zeros((rows, half, width), BF)

    own_load.wait()

    @pl.when(has_prev)
    def _():
        rim.wait_recv()

    mine = tuple((seq // (1 << (bits - 1 - d))) % 2 for d in range(bits))

    def pool_step(r, carry):
        stretch = jnp.concatenate([rim_in[r], tokx[r, own]], axis=0)
        picked = dot(tap_select(wseg_ref[r, :, half - edge : half + shard], edge, pooled_local), stretch)
        total = picked[:pooled_local] * ker_ref[0:1]
        for t in range(1, KER):
            total = total + picked[t * pooled_local : (t + 1) * pooled_local] * ker_ref[t : t + 1]
        pool_ref[mine + (r,)] = total.astype(BF)
        return carry

    lax.fori_loop(0, rows, pool_step, 0)
    for part in range(2):
        gather(part, 0).start()

    @pl.when(has_next)
    def _():
        to_next.start()

    @pl.when(has_prev)
    def _():
        to_prev.start()

    w_load.wait()
    scale = HEAD ** (-0.5)

    def own_step(r, carry):
        x = tokx[pl.ds(2 * r, 2), own].reshape(2 * shard, width)
        qb[pl.ds(2 * r, 2)] = (dot(x, w_ref[:, :width]) * scale).astype(BF).reshape(2, shard, width)
        knb[pl.ds(2 * r, 2), own] = dot(x, w_ref[:, width : 2 * width]).astype(BF).reshape(2, shard, width)
        vnb[pl.ds(2 * r, 2), own] = dot(x, w_ref[:, 2 * width : 3 * width]).astype(BF).reshape(2, shard, width)
        return carry

    lax.fori_loop(0, rows // 2, own_step, 0)
    for stage in range(1, bits):
        for part in range(2):
            gather(part, stage - 1).wait()
            gather(part, stage).start()
        if stage > 1:
            continue

        @pl.when(has_prev)
        def _():
            to_next.wait_recv()

        @pl.when(has_next)
        def _():
            to_prev.wait_recv()

        def halo_step(r, carry):
            x = tokx[pl.ds(2 * r, 2), :half].reshape(2 * half, width)
            y = tokx[pl.ds(2 * r, 2), half + shard :].reshape(2 * half, width)
            x = jnp.concatenate([x, y], axis=0)
            for ref, first in ((knb, width), (vnb, 2 * width)):
                both = dot(x, w_ref[:, first : first + width]).astype(BF)
                ref[pl.ds(2 * r, 2), :half] = both[: 2 * half].reshape(2, half, width)
                ref[pl.ds(2 * r, 2), half + shard :] = both[2 * half :].reshape(2, half, width)
            return carry

        lax.fori_loop(0, rows // 2, halo_step, 0)
    ext_store = pltpu.make_async_copy(tokx, ext_hbm, ext_sem)
    ext_store.start()
    for part in range(2):
        gather(part, bits - 1).wait()

    def pool_store(block):
        index = tuple((block >> (bits - 1 - d)) & 1 for d in range(bits))
        dst = pool_hbm.at[:, block * pooled_local : (block + 1) * pooled_local]
        return pltpu.make_async_copy(pool_ref.at[index], dst, pool_sem.at[block])

    for block in range(seq_count):
        pool_store(block).start()

    def near_stores(r):
        pairs = [(qb.at[r], q_hbm.at[r]), (knb.at[r], k_hbm.at[r, :near]), (vnb.at[r], v_hbm.at[r, :near])]
        return [pltpu.make_async_copy(src, dst, near_sem.at[n, r]) for n, (src, dst) in enumerate(pairs)]

    def far_stores(r, slot):
        pairs = [
            (kfb.at[slot], k_hbm.at[r, near:]), (vfb.at[slot], v_hbm.at[r, near:]),
            (pb.at[slot], p_hbm.at[r]), (attb.at[slot], att_hbm.at[r]),
        ]
        return [pltpu.make_async_copy(src, dst, far_sem.at[n, slot]) for n, (src, dst) in enumerate(pairs)]

    lane = lax.broadcasted_iota(jnp.int32, (shard, 2 * HEAD), 1)
    even = lane < HEAD

    def row_step(r, carry):
        slot = r % buffers
        for copy in near_stores(r):
            copy.start()

        @pl.when(r >= buffers)
        def _():
            for copy in far_stores(r - buffers, slot):
                copy.wait()

        pooled = pool_ref[(slice(None),) * bits + (r,)].reshape(keys - near, width)
        kfb[slot] = dot(pooled, w_ref[:, 3 * width : 4 * width]).astype(BF)
        vfb[slot] = dot(pooled, w_ref[:, 4 * width :]).astype(BF)
        key_seg = jnp.transpose(jnp.broadcast_to(kseg_ref[r], (shard, keys)))
        shape = (keys, shard)
        row = lax.broadcasted_iota(jnp.int32, shape, 0)
        col = lax.broadcasted_iota(jnp.int32, shape, 1)
        inside = (row >= near) | ((row >= col) & (row - col <= 2 * half))
        kept = inside & (key_seg == jnp.broadcast_to(qseg_ref[r], shape))
        bias = jnp.where(kept, 0.0, NEG_LARGE)
        bias = jnp.concatenate([bias, bias], axis=1)
        for j in range(PAIRS):
            cols = slice(2 * HEAD * j, 2 * HEAD * (j + 1))
            qp = qb[r, :, cols]
            zero = jnp.zeros_like(qp)
            stacked = jnp.concatenate([jnp.where(even, qp, zero), jnp.where(even, zero, qp)], axis=0)
            close = dot(knb[r, :, cols], stacked, 1, 1) + bias[:near]
            wide = dot(kfb[slot, :, cols], stacked, 1, 1) + bias[near:]
            top = jnp.maximum(jnp.max(close, axis=0, keepdims=True), jnp.max(wide, axis=0, keepdims=True))
            close = jnp.exp(close - top)
            wide = jnp.exp(wide - top)
            share = 1.0 / (jnp.sum(close, axis=0, keepdims=True) + jnp.sum(wide, axis=0, keepdims=True))
            close = (close * share).astype(BF)
            wide = (wide * share).astype(BF)
            pb[slot, j, :near] = close
            pb[slot, j, near:] = wide
            mixed = dot(vnb[r, :, cols], close, 0, 0) + dot(vfb[slot, :, cols], wide, 0, 0)
            mixed = jnp.concatenate([mixed[:HEAD, :shard], mixed[HEAD:, shard:]], axis=0)
            attb[slot, :, cols] = jnp.transpose(mixed).astype(BF)
        for copy in far_stores(r, slot):
            copy.start()
        return carry

    lax.fori_loop(0, rows, row_step, 0)
    for n in range(buffers):
        r = rows - buffers + n
        for copy in far_stores(r, r % buffers):
            copy.wait()
    for r in range(rows):
        for copy in near_stores(r):
            copy.wait()
    for block in range(seq_count):
        pool_store(block).wait()
    ext_store.wait()

    @pl.when(has_next)
    def _():
        rim.wait_send()
        to_next.wait_send()

    @pl.when(has_prev)
    def _():
        to_prev.wait_send()


def mlp_kernel(
    tok_ref, att_ref, cot_ref, wo_ref, wu_ref, wd_ref, gain_ref, bias_ref,
    out_ref, act_ref, upg_ref, n1_ref, r2_ref, g1_ref, g1b_ref, da_ref, dsum_ref, small_ref,
    slope,
):
    hidden = wu_ref.shape[1]
    chunk = 512
    gain_a, gain_b = gain_ref[0:1], gain_ref[1:2]

    def mean(x):
        return jnp.mean(x, axis=-1, keepdims=True)

    resid = tok_ref[...].astype(F32) + dot(att_ref[...], wo_ref[...])
    centred = resid - mean(resid)
    rstd_a = lax.rsqrt(mean(centred * centred) + EPSILON)
    hat_a = centred * rstd_a
    normed = hat_a * gain_a + bias_ref[0:1]
    low = normed.astype(BF)
    n1_ref[...] = low
    total = normed
    for c in range(0, hidden, chunk):
        up = dot(low, wu_ref[:, c : c + chunk])
        half_cdf = 0.5 * (1.0 + lax.erf(up * ROOT_HALF))
        act = (up * half_cdf).astype(BF)
        act_ref[:, c : c + chunk] = act
        slope[:, c : c + chunk] = half_cdf + up * (INV_ROOT_2PI * jnp.exp(-0.5 * up * up))
        total = total + dot(act, wd_ref[c : c + chunk, :])
    centred = total - mean(total)
    rstd_b = lax.rsqrt(mean(centred * centred) + EPSILON)
    hat_b = centred * rstd_b
    out_ref[...] = (hat_b * gain_b + bias_ref[1:2]).astype(BF)
    g = cot_ref[...].astype(F32)
    gain_two = jnp.sum(g * hat_b, axis=0, keepdims=True)
    bias_two = jnp.sum(g, axis=0, keepdims=True)
    e = g * gain_b
    grad = rstd_b * (e - mean(e) - hat_b * mean(e * hat_b))
    grad_low = grad.astype(BF)
    r2_ref[...] = grad_low
    for c in range(0, hidden, chunk):
        up_grad = (dot(grad_low, wd_ref[c : c + chunk, :], 1, 1) * slope[:, c : c + chunk]).astype(BF)
        upg_ref[:, c : c + chunk] = up_grad
        grad = grad + dot(up_grad, wu_ref[:, c : c + chunk], 1, 1)
    gain_one = jnp.sum(grad * hat_a, axis=0, keepdims=True)
    bias_one = jnp.sum(grad, axis=0, keepdims=True)
    e = grad * gain_a
    resid_grad = rstd_a * (e - mean(e) - hat_a * mean(e * hat_a))
    g1_ref[...] = resid_grad
    resid_low = resid_grad.astype(BF)
    g1b_ref[...] = resid_low
    att_grad = dot(resid_low, wo_ref[...], 1, 1).astype(BF)
    da_ref[...] = att_grad
    prod = att_grad.astype(F32) * att_ref[...].astype(F32)
    high = prod.astype(BF)
    rest = (prod - high.astype(F32)).astype(BF)
    heads = dsum_ref.shape[0]
    width = prod.shape[1]
    head_row = lax.broadcasted_iota(jnp.int32, (heads, width), 0)
    head_col = lax.broadcasted_iota(jnp.int32, (heads, width), 1) // HEAD
    pick = jnp.where(head_row == head_col, 1.0, 0.0).astype(BF)
    dsum_ref[...] = dot(pick, high, 1, 1) + dot(pick, rest, 1, 1)

    @pl.when(pl.program_id(0) == 0)
    def _():
        small_ref[...] = jnp.zeros_like(small_ref)

    small_ref[0:4] += jnp.concatenate([gain_one, gain_two, bias_one, bias_two], axis=0)


def stage_orders(bits):
    rest = list(range(bits - 1))
    cut = len(rest) // 2
    return (
        [bits - 1] + rest[::-1],
        [bits - 1] + rest[:cut][::-1] + rest[cut:][::-1],
    )


class Reducer:
    def __init__(self, seq_count, row_count, units, dest, held, bufs, zsend, zrecv, sems, take=None):
        self.take = take
        self.bits = seq_count.bit_length() - 1
        self.row_count = row_count
        self.units = units
        self.dest = dest
        self.held, self.bufs, self.zsend, self.zrecv = held, bufs, zsend, zrecv
        self.send_sem, self.recv_sem, self.zsend_sem, self.zrecv_sem = sems
        self.seq = lax.axis_index("seq")
        self.row = lax.axis_index("row")
        self.orders = stage_orders(self.bits)

    def bit(self, dim):
        weight = 1 << (self.bits - 1 - dim)
        value = (self.seq // weight) % 2
        return value, self.seq + (1 - 2 * value) * weight

    def barrier(self, line=False):
        sem = pltpu.get_barrier_semaphore()
        count = 1 << self.bits
        peers = [{"seq": self.bit(dim)[1]} for dim in range(self.bits)]
        peers += [{"row": (self.row + k) % self.row_count} for k in range(1, self.row_count)]
        if line:
            peers += [{"seq": (self.seq + 1) % count}, {"seq": (self.seq + count - 1) % count}]
        for peer in peers:
            pl.semaphore_signal(sem, inc=1, device_id=peer, device_id_type=MESH)
        pl.semaphore_wait(sem, len(peers))

    def position(self, unit, stage):
        order = self.orders[unit % 2]
        left = sorted(order[stage:])
        return order[stage], left.index(order[stage])

    def source(self, unit, stage, value):
        pos = self.position(unit, stage)[1]
        base, slot = (self.held, unit % self.held.shape[0]) if stage == 0 else (self.bufs[stage - 1], unit)
        return base, (slot,) + (slice(None),) * pos + (value,)

    def copy(self, unit, stage):
        value, partner = self.bit(self.position(unit, stage)[0])
        base, index = self.source(unit, stage, 1 - value)
        return pltpu.make_async_remote_copy(
            src_ref=base.at[index],
            dst_ref=self.bufs[stage].at[unit],
            send_sem=self.send_sem.at[unit, stage],
            recv_sem=self.recv_sem.at[unit, stage],
            device_id={"seq": partner},
            device_id_type=MESH,
        )

    def start(self, unit):
        self.copy(unit, 0).start()

    def advance(self, unit, stage):
        self.copy(unit, stage - 1).wait()
        dim, pos = self.position(unit, stage - 1)
        value = self.bit(dim)[0]
        buf = self.bufs[stage - 1]
        base, _ = self.source(unit, stage - 1, value)
        slot = unit % self.held.shape[0] if stage == 1 else unit
        lead = self.bits - stage
        total = None
        for flat in range(1 << lead):
            index = tuple((flat >> (lead - 1 - d)) & 1 for d in range(lead))
            own = base[(slot,) + index[:pos] + (value,) + index[pos:]]
            total = own.astype(F32) + buf[(unit,) + index].astype(F32)
            if stage < self.bits:
                buf[(unit,) + index] = total.astype(BF)
        if stage < self.bits:
            self.copy(unit, stage).start()
            return
        if self.take is not None:
            self.take(unit, total)
            return
        cols = total.shape[1] // self.row_count
        for i in range(self.row_count):
            self.zsend[unit, i] = total[:, i * cols : (i + 1) * cols].astype(BF)
        for i in range(self.row_count):
            target, slot = self.dest(unit, i)

            @pl.when(self.row != target)
            def _():
                self.row_copy(unit, i, target, slot).start()

    def row_copy(self, unit, i, target, slot):
        return pltpu.make_async_remote_copy(
            src_ref=self.zsend.at[unit, i],
            dst_ref=self.zrecv.at[slot, self.row],
            send_sem=self.zsend_sem.at[unit, i],
            recv_sem=self.zrecv_sem.at[slot, self.row],
            device_id={"row": target},
            device_id_type=MESH,
        )

    def tick(self, unit, start=True):
        if start and unit < self.units:
            self.start(unit)
        for stage in range(1, self.bits + 1):
            if 0 <= unit - (2 * stage - 1) < self.units:
                self.advance(unit - (2 * stage - 1), stage)

    def ticks(self):
        return self.units + 2 * self.bits - 1

    def arrived(self, slot, unit, i):
        total = self.zsend[unit, i].astype(F32)
        for k in range(1, self.row_count):
            other = (self.row + k) % self.row_count
            pltpu.make_async_remote_copy(
                src_ref=self.zsend.at[0, 0],
                dst_ref=self.zrecv.at[slot, other],
                send_sem=self.zsend_sem.at[0, 0],
                recv_sem=self.zrecv_sem.at[slot, other],
                device_id={"row": other},
                device_id_type=MESH,
            ).wait_recv()
            total = total + self.zrecv[slot, other].astype(F32)
        return total

    def sent(self):
        for unit in range(self.units):
            for i in range(self.row_count):
                target, slot = self.dest(unit, i)

                @pl.when(self.row != target)
                def _():
                    self.row_copy(unit, i, target, slot).wait_send()


def split_index(flat, bits):
    return tuple((flat >> (bits - 1 - d)) & 1 for d in range(bits))


def mid_kernel(
    seq_count, row_count, half, buffers,
    n1_hbm, r2_hbm, att_hbm, g1b_hbm, upg_hbm, act_hbm, w_hbm, dsum_ref,
    q_hbm, k_hbm, v_hbm, p_hbm, da_hbm, g1_hbm,
    wout_ref, wup_ref, wdown_ref, dq_hbm, dk_hbm, dv_hbm, dpool_hbm, own_hbm, left_hbm, right_hbm,
    held, *rest,
):
    bits = seq_count.bit_length() - 1
    bufs = rest[:bits]
    (
        zsend, zrecv, slots, n1_ref, r2_ref, att_ref, g1b_ref, w_ref,
        qb, kb, vb, pb, dab, g1_buf, dqb, dkb, dvb, dpb, owb, lfb, rtb,
        send_sem, recv_sem, zsend_sem, zrecv_sem, load_sem, once_sem, in_sem, out_sem,
    ) = rest[bits:]
    rows, shard, width = n1_ref.shape
    near = shard + 2 * half
    part = width // seq_count
    up_units = upg_hbm.shape[2] // width
    units = 2 * up_units + 1
    tall = width // 2
    acts = up_units * 2
    steps = up_units + acts

    def dest(unit, i):
        if unit < up_units:
            g = unit * row_count + i
            return g // up_units, g % up_units
        return i, unit

    red = Reducer(
        seq_count, row_count, units, dest, held, bufs, zsend, zrecv, (send_sem, recv_sem, zsend_sem, zrecv_sem)
    )
    once = [
        pltpu.make_async_copy(src, dst, once_sem.at[n])
        for n, (src, dst) in enumerate(
            [(n1_hbm, n1_ref), (att_hbm, att_ref), (g1b_hbm, g1b_ref), (r2_hbm, r2_ref), (w_hbm, w_ref)]
        )
    ]

    def load(k):
        buf = slots.at[k % 2]
        if k < up_units:
            src, dst = upg_hbm.at[:, :, width * k : width * (k + 1)], buf
        else:
            c = k - up_units
            src, dst = act_hbm.at[:, :, tall * c : tall * (c + 1)], buf.at[:, :, :tall]
        return pltpu.make_async_copy(src, dst, load_sem.at[k % 2])

    def taken(k):
        load(k).wait()
        if k + 1 < steps:
            load(k + 1).start()

    def row_loads(r, slot):
        pairs = [(q_hbm, qb), (k_hbm, kb), (v_hbm, vb), (p_hbm, pb), (da_hbm, dab), (g1_hbm, g1_buf)]
        return [
            pltpu.make_async_copy(src.at[r], dst.at[slot], in_sem.at[n, slot])
            for n, (src, dst) in enumerate(pairs)
        ]

    def row_stores(r, slot):
        pairs = [
            (dqb, dq_hbm), (dkb, dk_hbm), (dvb, dv_hbm), (dpb, dpool_hbm), (owb, own_hbm),
            (lfb, left_hbm), (rtb, right_hbm),
        ]
        return [
            pltpu.make_async_copy(src.at[slot], dst.at[r], out_sem.at[n, slot])
            for n, (src, dst) in enumerate(pairs)
        ]

    once[0].start()
    load(0).start()
    for copy in once[1:]:
        copy.start()
    if buffers > 1:
        for copy in row_loads(0, 0):
            copy.start()
    red.barrier()
    lead = (2,) * (bits - 1)

    def product(unit, left_ref, right):
        for m in range(2):
            left = left_ref[:, :, tall * m : tall * (m + 1)].reshape(-1, tall)
            held[unit, m] = dot(left, right, 0, 0).reshape(lead + (part, width)).astype(BF)

    once[0].wait()
    for u in range(up_units):
        taken(u)
        product(u, n1_ref, slots[u % 2].reshape(-1, width))
        red.tick(u)
    once[1].wait()
    once[2].wait()
    product(up_units, att_ref, g1b_ref[...].reshape(-1, width))
    red.tick(up_units)
    once[3].wait()
    for c in range(acts):
        k = up_units + c
        taken(k)
        left = slots[k % 2, :, :, :tall].reshape(-1, tall)
        total = dot(left, r2_ref[...].reshape(-1, width), 0, 0)
        blocked = total.reshape(tall // part, part, width).astype(BF)
        for n in range(tall // part):
            flat = (c * tall + n * part) // part
            held[(up_units + 1 + flat % up_units,) + split_index(flat // up_units, bits)] = blocked[n]
    for u in range(up_units + 1, units):
        red.start(u)
    once[4].wait()

    lane = lax.broadcasted_iota(jnp.int32, (shard, 2 * HEAD), 1)
    even = lane < HEAD

    def stack(pair):
        zero = jnp.zeros_like(pair)
        return jnp.concatenate([jnp.where(even, pair, zero), jnp.where(even, zero, pair)], axis=0)

    def row_step(r, carry):
        slot = r % buffers
        if buffers > 1:

            @pl.when(r + 1 < rows)
            def _():
                for copy in row_loads(r + 1, (r + 1) % buffers):
                    copy.start()

        else:
            for copy in row_loads(r, slot):
                copy.start()
        for t in range(rows):

            @pl.when(r == t)
            def _():
                red.tick(up_units + 1 + t, start=False)

        for copy in row_loads(r, slot):
            copy.wait()

        @pl.when(r >= buffers)
        def _():
            for copy in row_stores(r - buffers, slot):
                copy.wait()

        row_sums = dsum_ref[:, pl.ds(pl.multiple_of(r * shard, shard), shard)]
        for j in range(PAIRS):
            cols = slice(2 * HEAD * j, 2 * HEAD * (j + 1))
            queries = stack(qb[slot, :, cols])
            grads = stack(dab[slot, :, cols])
            prob = pb[slot, j]
            dprob = dot(vb[slot, :, cols], grads, 1, 1)
            row_dot = jnp.concatenate([row_sums[2 * j : 2 * j + 1], row_sums[2 * j + 1 : 2 * j + 2]], axis=1)
            dscore = (prob.astype(F32) * (dprob - row_dot)).astype(BF)
            dvb[slot, :, cols] = dot(prob, grads).astype(BF)
            dkb[slot, :, cols] = dot(dscore, queries).astype(BF)
            mixed = dot(kb[slot, :, cols], dscore, 0, 0)
            mixed = jnp.concatenate([mixed[:HEAD, :shard], mixed[HEAD:, shard:]], axis=0)
            dqb[slot, :, cols] = (jnp.transpose(mixed) * HEAD ** (-0.5)).astype(BF)
        back = dot(dkb[slot, :near], w_ref[:, width : 2 * width], 1, 1) + dot(
            dvb[slot, :near], w_ref[:, 2 * width : 3 * width], 1, 1
        )
        lfb[slot] = back[:half].astype(BF)
        rtb[slot] = back[half + shard :].astype(BF)
        owb[slot] = g1_buf[slot] + back[half : half + shard] + dot(dqb[slot], w_ref[:, :width], 1, 1)
        dpb[slot] = (
            dot(dkb[slot, near:], w_ref[:, 3 * width : 4 * width], 1, 1)
            + dot(dvb[slot, near:], w_ref[:, 4 * width :], 1, 1)
        ).astype(BF)
        for copy in row_stores(r, slot):
            copy.start()
        return carry

    lax.fori_loop(0, rows, row_step, 0)
    for t in range(up_units + 1 + rows, red.ticks()):
        red.tick(t, start=False)
    for n in range(buffers):
        r = rows - buffers + n
        for copy in row_stores(r, r % buffers):
            copy.wait()
    row = red.row
    cols = width // row_count
    for n in range(up_units):
        g = row * up_units + n
        wup_ref[:, n * cols : (n + 1) * cols] = red.arrived(n, g // row_count, g % row_count)
    wout_ref[...] = red.arrived(up_units, up_units, row)
    for n in range(up_units):
        wdown_ref[n * part : (n + 1) * part] = red.arrived(up_units + 1 + n, up_units + 1 + n, row)
    red.sent()


def tail_kernel(
    seq_count, row_count, half,
    tok_ref, pool_hbm, dq_hbm, dk_hbm, dv_hbm, dpool_hbm, own_hbm, left_hbm, right_hbm,
    seg_ref, ker_ref, norm_ref,
    win_ref, out_hbm, small_ref,
    held, *rest,
):
    bits = seq_count.bit_length() - 1
    bufs, rest = rest[:bits], rest[bits:]
    pheld, pbufs, rest = rest[0], rest[1 : 1 + bits], rest[1 + bits :]
    (
        zsend, zrecv, slots, pool_ref, partial, dpool_own, from_left, from_right, rim_out, rim_in, ownb, outb,
        ssum, srecv, zsum,
        send_sem, recv_sem, zsend_sem, zrecv_sem, psend_sem, precv_sem, load_sem, pool_sem, ploads_sem,
        line_sem, own_sem, out_sem, small_sem, zsmall_sem,
    ) = rest
    rows, near, width = tok_ref.shape
    shard = near - 2 * half
    part = width // seq_count
    units = 5
    tall = width // 2
    piece = pool_ref.shape[1]
    pieces = (dk_hbm.shape[1] - near) // piece
    steps = 3 + 2 * pieces
    pooled_local = dpool_own.shape[1]
    wide = width // 2

    def dest(unit, i):
        g = unit * row_count + i
        return g // 5, g % 5

    red = Reducer(
        seq_count, row_count, units, dest, held, bufs, zsend, zrecv, (send_sem, recv_sem, zsend_sem, zrecv_sem)
    )

    def take(unit, total):
        dpool_own[:, :, unit * wide : (unit + 1) * wide] = total

    pred = Reducer(
        seq_count, row_count, 2, None, pheld, pbufs, None, None, (psend_sem, precv_sem, None, None), take
    )

    def load(k):
        buf = slots.at[k % 2]
        if k == 0:
            src, dst = dq_hbm, buf.at[:, :shard]
        elif k < 3:
            src, dst = (dk_hbm, dv_hbm)[k - 1].at[:, :near], buf
        else:
            c = k - 3
            first = near + (c % pieces) * piece
            src, dst = (dk_hbm, dv_hbm)[c // pieces].at[:, first : first + piece], buf.at[:, :piece]
        return pltpu.make_async_copy(src, dst, load_sem.at[k % 2])

    def taken(k):
        load(k).wait()
        if k + 1 < steps:
            load(k + 1).start()

    def pool_load(n):
        return pltpu.make_async_copy(pool_hbm.at[:, n * piece : (n + 1) * piece], pool_ref, pool_sem)

    def grad_load(unit, owner):
        src = dpool_hbm.at[:, owner * pooled_local : (owner + 1) * pooled_local, unit * wide : (unit + 1) * wide]
        return pltpu.make_async_copy(
            src, pheld.at[(unit,) + split_index(owner, bits)], ploads_sem.at[unit, owner]
        )

    def line(n, src, dst, step):
        return pltpu.make_async_remote_copy(
            src_ref=src, dst_ref=dst, send_sem=line_sem.at[n, 0], recv_sem=line_sem.at[n, 1],
            device_id={"seq": red.seq + step}, device_id_type=MESH,
        )

    to_prev = line(0, left_hbm, from_right, -1)
    to_next = line(1, right_hbm, from_left, 1)
    rim = line(2, rim_out, rim_in, -1)
    has_prev = red.seq > 0
    has_next = red.seq < seq_count - 1

    for unit in range(2):
        for owner in range(seq_count):
            grad_load(unit, owner).start()
    load(0).start()
    pool_load(0).start()
    red.barrier(line=True)
    for unit in range(2):
        for owner in range(seq_count):
            grad_load(unit, owner).wait()
        pred.start(unit)

    @pl.when(has_prev)
    def _():
        to_prev.start()

    @pl.when(has_next)
    def _():
        to_next.start()

    lead = (2,) * (bits - 1)

    def product(unit, left, right, first=True, last=True):
        for m in range(2):
            total = dot(left(m), right, 0, 0)
            if not first:
                total = total + partial[m]
            if not last:
                partial[m] = total
                continue
            held[unit, m] = total.reshape(lead + (part, width)).astype(BF)

    def columns(ref, keep=slice(None)):
        return lambda m: ref[:, keep, tall * m : tall * (m + 1)].reshape(-1, tall)

    def whole(k, length):
        return slots[k % 2, :, :length].reshape(-1, width)

    own = slice(half, half + shard)
    sources = [(columns(tok_ref, own), shard), (columns(tok_ref), near), (columns(tok_ref), near)]
    for n, (left, length) in enumerate(sources):
        taken(n)
        product(n, left, whole(n, length))
        if n == 0:
            pred.advance(0, 1)
            pred.advance(1, 1)
        red.tick(n)
    for n in range(2):
        for c in range(pieces):
            k = 3 + n * pieces + c
            if pieces > 1 and (n or c):
                pool_load(c).start()
            if pieces > 1 or n == 0:
                pool_load(c).wait()
            taken(k)
            product(3 + n, columns(pool_ref), whole(k, piece), c == 0, c == pieces - 1)
        red.tick(3 + n)
        if n == 0:
            pred.advance(0, 2)
            pred.advance(1, 2)
    for stage in range(3, bits + 1):
        pred.advance(0, stage)
        pred.advance(1, stage)

    ssum[...] = jnp.zeros_like(ssum)
    ssum[8:12] = norm_ref[0:4]

    def own_load(r, slot):
        return pltpu.make_async_copy(own_hbm.at[r], ownb.at[slot], own_sem.at[slot])

    def out_store(r, slot):
        return pltpu.make_async_copy(outb.at[slot], out_hbm.at[r], out_sem.at[slot])

    @pl.when(has_next)
    def _():
        to_prev.wait_recv()

    @pl.when(has_prev)
    def _():
        to_next.wait_recv()

    own_load(0, 0).start()

    def pool_step(r, carry):
        slot = r % 2

        @pl.when(r + 1 < rows)
        def _():
            own_load(r + 1, (r + 1) % 2).start()

        select = tap_select(seg_ref[r], half, pooled_local)
        picked = dot(select, tok_ref[r])
        grad = dpool_own[r]
        terms, sums = [], []
        for t in range(KER):
            terms.append((grad * ker_ref[t : t + 1]).astype(BF))
            sums.append(jnp.sum(grad * picked[t * pooled_local : (t + 1) * pooled_local], axis=0, keepdims=True))
        ssum[0:KER] += jnp.concatenate(sums, axis=0)
        spread = dot(select, jnp.concatenate(terms, axis=0), 0, 0)
        rim_out[r] = spread[half - 16 : half].astype(BF)
        own_load(r, slot).wait()

        @pl.when(r >= 2)
        def _():
            out_store(r - 2, slot).wait()

        outb[slot] = ownb[slot] + spread[half : half + shard]

        @pl.when(has_prev)
        def _():
            outb[slot, :half] += from_left[r].astype(F32)

        @pl.when(has_next)
        def _():
            outb[slot, shard - half :] += from_right[r].astype(F32)

        out_store(r, slot).start()
        return carry

    lax.fori_loop(0, rows, pool_step, 0)

    @pl.when(has_prev)
    def _():
        rim.start()

    for t in range(units, red.ticks()):
        red.tick(t)
    for n in range(2):
        out_store(rows - 2 + n, n).wait()

    def edge(load):
        pairs = (out_hbm.at[:, shard - 16 :], outb.at[0, : rows * 16].reshape(rows, 16, width))
        return pltpu.make_async_copy(*(pairs if load else pairs[::-1]), own_sem.at[0])

    edge(True).start()
    edge(True).wait()

    @pl.when(has_next)
    def _():
        rim.wait_recv()
        outb[0, : rows * 16] += rim_in[...].reshape(rows * 16, width).astype(F32)

    edge(False).start()

    for stage in range(bits):
        dim = bits - 1 - stage
        copy = pltpu.make_async_remote_copy(
            src_ref=ssum, dst_ref=srecv.at[stage], send_sem=small_sem.at[stage, 0], recv_sem=small_sem.at[stage, 1],
            device_id={"seq": red.bit(dim)[1]}, device_id_type=MESH,
        )
        copy.start()
        copy.wait()
        ssum[...] += srecv[stage]

    def small_row(k):
        other = (red.row + k) % row_count
        return pltpu.make_async_remote_copy(
            src_ref=ssum, dst_ref=zsum.at[row_count - k], send_sem=zsmall_sem.at[k, 0],
            recv_sem=zsmall_sem.at[row_count - k, 1], device_id={"row": other}, device_id_type=MESH,
        )

    for k in range(1, row_count):
        small_row(k).start()
    zsum[0] = ssum[...]
    cols = width // row_count
    for n in range(5):
        g = red.row * 5 + n
        win_ref[:, n * cols : (n + 1) * cols] = red.arrived(n, g // row_count, g % row_count)
    total = None
    for k in range(1, row_count):
        small_row(row_count - k).wait_recv()
    for owner in range(row_count):
        term = zsum[(owner - red.row + row_count) % row_count]
        total = term if total is None else total + term
    small_ref[...] = total
    for k in range(1, row_count):
        small_row(k).wait_send()
    red.sent()
    edge(False).wait()

    @pl.when(has_prev)
    def _():
        to_prev.wait_send()
        rim.wait_send()

    @pl.when(has_next)
    def _():
        to_next.wait_send()


def body(tokens, segment_ids, w_in, w_out, w_up, w_down, conv_kernel, norm_gain, norm_bias, cotangent):
    rows, shard, width = tokens.shape
    half = WIN // 2
    pooled_local = shard // STR
    near = shard + 2 * half
    count = rows * shard
    hidden = w_up.shape[1]
    seq_count = lax.axis_size("seq")
    row_count = lax.axis_size("row")
    seq_start = lax.axis_index("seq") * shard
    keys = near + pooled_local * seq_count

    own_seg = lax.dynamic_slice_in_dim(segment_ids, seq_start, shard, 1)
    padded_seg = jnp.pad(segment_ids, ((0, 0), (half, half)), constant_values=-1)
    window_seg = lax.dynamic_slice_in_dim(padded_seg, seq_start, near, 1)
    key_seg = jnp.concatenate([window_seg, segment_ids[:, ::STR]], axis=1)
    own_seg = own_seg[:, None]
    key_seg = key_seg[:, None]
    window_seg = window_seg[:, None]

    def row_spec(*tail):
        return pl.BlockSpec((1,) + tail, lambda r: (r,) + (0,) * len(tail))

    def whole_spec(*dims):
        return pl.BlockSpec(dims, lambda r: (0,) * len(dims), pipeline_mode=pl.Buffered(1))

    def struct(*dims, dtype=BF):
        return jax.ShapeDtypeStruct(dims, dtype)

    def params(limit):
        return pltpu.CompilerParams(dimension_semantics=("arbitrary",), vmem_limit_bytes=limit * MB)

    bits = seq_count.bit_length() - 1
    far = keys - near
    buffers = 2 if keys <= 2 * near else 1
    vmem = pl.BlockSpec(memory_space=pltpu.VMEM)
    hbm = pl.BlockSpec(memory_space=pl.ANY)
    dma = pltpu.SemaphoreType.DMA

    def scratch(*dims, dtype=BF):
        return pltpu.VMEM(dims, dtype)

    tok_ext, pooled_all, q, k_all, v_all, prob, attended = pl.pallas_call(
        functools.partial(front_kernel, seq_count, half, buffers),
        out_shape=(
            struct(rows, near, width), struct(rows, far, width), struct(rows, shard, width),
            struct(rows, keys, width), struct(rows, keys, width), struct(rows, PAIRS, keys, 2 * shard),
            struct(rows, shard, width),
        ),
        in_specs=[hbm] * 2 + [vmem] * 4,
        out_specs=(hbm,) * 7,
        scratch_shapes=[
            scratch(rows, near, width), scratch(rows, 16, width),
            scratch(*((2,) * bits + (rows, pooled_local, width))), scratch(*w_in.shape),
            scratch(rows, shard, width), scratch(rows, near, width), scratch(rows, near, width),
            scratch(buffers, far, width), scratch(buffers, far, width),
            scratch(buffers, PAIRS, keys, 2 * shard), scratch(buffers, shard, width),
            dma((2,)), dma((3, 2)), dma((2, bits, 2)), dma((3, rows)), dma((4, buffers)), dma, dma((seq_count,)),
        ],
        compiler_params=pltpu.CompilerParams(collective_id=2, has_side_effects=True, vmem_limit_bytes=60 * MB),
        name="front",
    )(tokens, w_in, window_seg, own_seg, key_seg, conv_kernel)

    block = 256
    flat_tokens = tokens.reshape(count, width)
    att_flat = attended.reshape(count, width)
    cot_flat = cotangent.reshape(count, width)

    def tok_spec(cols):
        return pl.BlockSpec((block, cols), lambda i: (i, 0))

    layer_out, act, upg, n1, r2, g1, g1b, att_grad, dsum, norm_sums = pl.pallas_call(
        mlp_kernel,
        out_shape=(
            struct(count, width), struct(count, hidden), struct(count, hidden), struct(count, width),
            struct(count, width), struct(count, width, dtype=F32), struct(count, width), struct(count, width),
            struct(16, count, dtype=F32), struct(8, width, dtype=F32),
        ),
        grid=(count // block,),
        in_specs=[
            tok_spec(width), tok_spec(width), tok_spec(width), whole_spec(*w_out.shape),
            whole_spec(*w_up.shape), whole_spec(*w_down.shape), whole_spec(2, width), whole_spec(2, width),
        ],
        out_specs=(
            tok_spec(width), tok_spec(hidden), tok_spec(hidden), tok_spec(width), tok_spec(width),
            tok_spec(width), tok_spec(width), tok_spec(width),
            pl.BlockSpec((16, block), lambda i: (0, i)), pl.BlockSpec((8, width), lambda i: (0, 0)),
        ),
        scratch_shapes=[pltpu.VMEM((block, hidden), F32)],
        compiler_params=params(56),
        name="mlp",
    )(flat_tokens, att_flat, cot_flat, w_out, w_up, w_down, norm_gain, norm_bias)

    def deep(x):
        return x.reshape(rows, shard, -1)

    part = width // seq_count
    up_units = hidden // width
    cols = width // row_count

    def halves(units, *tail, dtype=BF):
        return [pltpu.VMEM((units,) + (2,) * (bits - i) + tail, dtype) for i in range(bits + 1)]

    units = 2 * up_units + 1
    (
        w_out_grad, w_up_grad, w_down_grad, dq, dk, dv, dpool, own_grad, left_grad, right_grad,
    ) = pl.pallas_call(
        functools.partial(mid_kernel, seq_count, row_count, half, buffers),
        out_shape=(
            struct(part, cols, dtype=F32), struct(part, up_units * cols, dtype=F32),
            struct(up_units * part, cols, dtype=F32),
            struct(rows, shard, width), struct(rows, keys, width), struct(rows, keys, width),
            struct(rows, far, width), struct(rows, shard, width, dtype=F32),
            struct(rows, half, width), struct(rows, half, width),
        ),
        in_specs=[hbm] * 7 + [vmem] + [hbm] * 6,
        out_specs=(vmem,) * 3 + (hbm,) * 7,
        scratch_shapes=halves(units, part, width)
        + [scratch(units, row_count, part, cols), scratch(units, row_count, part, cols)]
        + [scratch(2, rows, shard, width)] + [scratch(rows, shard, width)] * 4 + [scratch(*w_in.shape)]
        + [
            scratch(buffers, shard, width), scratch(buffers, keys, width), scratch(buffers, keys, width),
            scratch(buffers, PAIRS, keys, 2 * shard), scratch(buffers, shard, width),
            scratch(buffers, shard, width, dtype=F32),
            scratch(buffers, shard, width), scratch(buffers, keys, width), scratch(buffers, keys, width),
            scratch(buffers, far, width), scratch(buffers, shard, width, dtype=F32),
            scratch(buffers, half, width), scratch(buffers, half, width),
        ]
        + [
            dma((units, bits)), dma((units, bits)), dma((units, row_count)), dma((units, row_count)),
            dma((2,)), dma((5,)), dma((6, buffers)), dma((7, buffers)),
        ],
        compiler_params=pltpu.CompilerParams(collective_id=0, has_side_effects=True, vmem_limit_bytes=60 * MB),
        name="mid",
    )(
        deep(n1), deep(r2), attended, deep(g1b), deep(upg), deep(act), w_in, dsum,
        q, k_all, v_all, prob, deep(att_grad), deep(g1),
    )

    w_in_grad, token_grad, small_sum = pl.pallas_call(
        functools.partial(tail_kernel, seq_count, row_count, half),
        out_shape=(
            struct(part, 5 * cols, dtype=F32), struct(rows, shard, width, dtype=F32), struct(16, width, dtype=F32),
        ),
        in_specs=[vmem] + [hbm] * 8 + [vmem] * 3,
        out_specs=(vmem, hbm, vmem),
        scratch_shapes=halves(5, part, width) + halves(2, rows, pooled_local, width // 2)
        + [scratch(5, row_count, part, cols), scratch(5, row_count, part, cols)]
        + [
            scratch(2, rows, near, width), scratch(rows, min(near, far), width),
            scratch(*((2, width // 2, width) if far > near else (8, 128)), dtype=F32),
            scratch(rows, pooled_local, width, dtype=F32), scratch(rows, half, width), scratch(rows, half, width),
            scratch(rows, 16, width), scratch(rows, 16, width),
            scratch(2, shard, width, dtype=F32), scratch(2, shard, width, dtype=F32),
            scratch(16, width, dtype=F32), scratch(bits, 16, width, dtype=F32), scratch(row_count, 16, width, dtype=F32),
        ]
        + [
            dma((5, bits)), dma((5, bits)), dma((5, row_count)), dma((5, row_count)), dma((2, bits)), dma((2, bits)),
            dma((2,)), dma, dma((2, seq_count)), dma((3, 2)), dma((2,)), dma((2,)), dma((bits, 2)), dma((row_count, 2)),
        ],
        compiler_params=pltpu.CompilerParams(collective_id=1, has_side_effects=True, vmem_limit_bytes=60 * MB),
        name="tail",
    )(
        tok_ext, pooled_all, dq, dk, dv, dpool, own_grad, left_grad, right_grad,
        window_seg, conv_kernel, norm_sums,
    )
    return (
        layer_out.reshape(rows, shard, width),
        token_grad,
        w_in_grad,
        w_out_grad,
        w_up_grad,
        w_down_grad,
        small_sum[:KER],
        small_sum[8:10],
        small_sum[10:12],
    )


def solution(mesh):
    placed = (
        P("row", "seq", None), P("row", None), P(), P(), P(), P(), P(), P(), P(), P("row", "seq", None),
    )
    return jax.shard_map(
        body,
        mesh=mesh,
        in_specs=placed,
        out_specs=(
            P("row", "seq", None), P("row", "seq", None), P("seq", "row"), P("seq", "row"),
            P("seq", "row"), P("seq", "row"), P(), P(), P(),
        ),
        check_vma=False,
    )
```

```python
import functools

import jax
import jax.numpy as jnp
from jax import lax
from jax.experimental import pallas as pl
from jax.experimental.pallas import tpu as pltpu
from jax.sharding import PartitionSpec as P

HEADS = 12
HEAD = 64
WIN = 128
KER = 5
STR = 4
PAIRS = HEADS // 2

EPSILON = 1e-05
ROOT_HALF = 0.7071067811865476
INV_ROOT_2PI = 0.3989422804014327
NEG_LARGE = -1e30
BF = jnp.bfloat16
F32 = jnp.float32
MB = 1 << 20
MESH = pl.DeviceIdType.MESH


def dot(a, b, ca=1, cb=0):
    return lax.dot_general(a, b, (((ca,), (cb,)), ((), ())), preferred_element_type=F32)


def tap_select(seg_row, half, pooled_local):
    width = seg_row.shape[1]
    shape = (KER * pooled_local, width)
    rows = lax.broadcasted_iota(jnp.int32, shape, 0)
    cols = lax.broadcasted_iota(jnp.int32, shape, 1)
    tap = rows // pooled_local
    centre = half + STR * (rows - tap * pooled_local)
    seg = jnp.broadcast_to(seg_row, shape)
    centre_seg = jnp.sum(jnp.where(cols == centre, seg, 0), axis=1, keepdims=True)
    hit = (cols == centre + tap - KER // 2) & (seg == centre_seg)
    return jnp.where(hit, 1.0, 0.0).astype(BF)


def front_kernel(
    seq_count, half, buffers,
    tok_hbm, w_hbm, wseg_ref, qseg_ref, kseg_ref, ker_ref,
    ext_hbm, pool_hbm, q_hbm, k_hbm, v_hbm, p_hbm, att_hbm,
    tokx, rim_in, pool_ref, w_ref, qb, knb, vnb, kfb, vfb, pb, attb,
    load_sem, line_sem, gather_sem, near_sem, far_sem, ext_sem, pool_sem,
):
    bits = seq_count.bit_length() - 1
    rows, near, width = tokx.shape
    shard = near - 2 * half
    keys = k_hbm.shape[1]
    pooled_local = pool_ref.shape[bits + 1]
    seq = lax.axis_index("seq")
    has_prev = seq > 0
    has_next = seq < seq_count - 1
    edge = 16

    def flipped(dim):
        weight = 1 << (bits - 1 - dim)
        return seq + (1 - 2 * ((seq // weight) % 2)) * weight

    def line(n, src, dst, step):
        return pltpu.make_async_remote_copy(
            src_ref=src, dst_ref=dst, send_sem=line_sem.at[n, 0], recv_sem=line_sem.at[n, 1],
            device_id={"seq": seq + step}, device_id_type=MESH,
        )

    rim = line(0, tok_hbm.at[:, shard - edge :], rim_in, 1)
    to_next = line(1, tok_hbm.at[:, shard - half :], tokx.at[:, :half], 1)
    to_prev = line(2, tok_hbm.at[:, :half], tokx.at[:, half + shard :], -1)

    rest = list(range(bits - 1))
    cut = len(rest) // 2
    orders = (rest[::-1] + [bits - 1], rest[:cut][::-1] + rest[cut:][::-1] + [bits - 1])

    def gather(part, stage):
        order = orders[part]
        done = order[:stage]
        index = tuple(
            slice(None) if d in done else (seq // (1 << (bits - 1 - d))) % 2 for d in range(bits)
        )
        cols = slice(part * (width // 2), (part + 1) * (width // 2))
        block = pool_ref.at[index + (slice(None), slice(None), cols)]
        return pltpu.make_async_remote_copy(
            src_ref=block, dst_ref=block, send_sem=gather_sem.at[part, stage, 0],
            recv_sem=gather_sem.at[part, stage, 1],
            device_id={"seq": flipped(order[stage])}, device_id_type=MESH,
        )

    own = slice(half, half + shard)
    own_load = pltpu.make_async_copy(tok_hbm, tokx.at[:, own], load_sem.at[0])
    w_load = pltpu.make_async_copy(w_hbm, w_ref, load_sem.at[1])
    own_load.start()
    w_load.start()
    sem = pltpu.get_barrier_semaphore()
    peers = [flipped(d) for d in range(bits)] + [(seq + 1) % seq_count, (seq + seq_count - 1) % seq_count]
    for peer in peers:
        pl.semaphore_signal(sem, inc=1, device_id={"seq": peer}, device_id_type=MESH)
    pl.semaphore_wait(sem, len(peers))

    @pl.when(has_next)
    def _():
        rim.start()

    @pl.when(jnp.logical_not(has_prev))
    def _():
        rim_in[...] = jnp.zeros_like(rim_in)
        tokx[:, :half] = jnp.zeros((rows, half, width), BF)

    @pl.when(jnp.logical_not(has_next))
    def _():
        tokx[:, half + shard :] = jnp.zeros((rows, half, width), BF)

    own_load.wait()

    @pl.when(has_prev)
    def _():
        rim.wait_recv()

    mine = tuple((seq // (1 << (bits - 1 - d))) % 2 for d in range(bits))

    def pool_step(r, carry):
        stretch = jnp.concatenate([rim_in[r], tokx[r, own]], axis=0)
        picked = dot(tap_select(wseg_ref[r, :, half - edge : half + shard], edge, pooled_local), stretch)
        total = picked[:pooled_local] * ker_ref[0:1]
        for t in range(1, KER):
            total = total + picked[t * pooled_local : (t + 1) * pooled_local] * ker_ref[t : t + 1]
        pool_ref[mine + (r,)] = total.astype(BF)
        return carry

    lax.fori_loop(0, rows, pool_step, 0)
    for part in range(2):
        gather(part, 0).start()

    @pl.when(has_next)
    def _():
        to_next.start()

    @pl.when(has_prev)
    def _():
        to_prev.start()

    w_load.wait()
    scale = HEAD ** (-0.5)

    def own_step(r, carry):
        x = tokx[pl.ds(2 * r, 2), own].reshape(2 * shard, width)
        qb[pl.ds(2 * r, 2)] = (dot(x, w_ref[:, :width]) * scale).astype(BF).reshape(2, shard, width)
        knb[pl.ds(2 * r, 2), own] = dot(x, w_ref[:, width : 2 * width]).astype(BF).reshape(2, shard, width)
        vnb[pl.ds(2 * r, 2), own] = dot(x, w_ref[:, 2 * width : 3 * width]).astype(BF).reshape(2, shard, width)
        return carry

    lax.fori_loop(0, rows // 2, own_step, 0)
    for stage in range(1, bits):
        for part in range(2):
            gather(part, stage - 1).wait()
            gather(part, stage).start()
        if stage > 1:
            continue

        @pl.when(has_prev)
        def _():
            to_next.wait_recv()

        @pl.when(has_next)
        def _():
            to_prev.wait_recv()

        def halo_step(r, carry):
            x = tokx[pl.ds(2 * r, 2), :half].reshape(2 * half, width)
            y = tokx[pl.ds(2 * r, 2), half + shard :].reshape(2 * half, width)
            x = jnp.concatenate([x, y], axis=0)
            for ref, first in ((knb, width), (vnb, 2 * width)):
                both = dot(x, w_ref[:, first : first + width]).astype(BF)
                ref[pl.ds(2 * r, 2), :half] = both[: 2 * half].reshape(2, half, width)
                ref[pl.ds(2 * r, 2), half + shard :] = both[2 * half :].reshape(2, half, width)
            return carry

        lax.fori_loop(0, rows // 2, halo_step, 0)
    ext_store = pltpu.make_async_copy(tokx, ext_hbm, ext_sem)
    ext_store.start()
    for part in range(2):
        gather(part, bits - 1).wait()

    def pool_store(block):
        index = tuple((block >> (bits - 1 - d)) & 1 for d in range(bits))
        dst = pool_hbm.at[:, block * pooled_local : (block + 1) * pooled_local]
        return pltpu.make_async_copy(pool_ref.at[index], dst, pool_sem.at[block])

    for block in range(seq_count):
        pool_store(block).start()

    def near_stores(r):
        pairs = [(qb.at[r], q_hbm.at[r]), (knb.at[r], k_hbm.at[r, :near]), (vnb.at[r], v_hbm.at[r, :near])]
        return [pltpu.make_async_copy(src, dst, near_sem.at[n, r]) for n, (src, dst) in enumerate(pairs)]

    def far_stores(r, slot):
        pairs = [
            (kfb.at[slot], k_hbm.at[r, near:]), (vfb.at[slot], v_hbm.at[r, near:]),
            (pb.at[slot], p_hbm.at[r]), (attb.at[slot], att_hbm.at[r]),
        ]
        return [pltpu.make_async_copy(src, dst, far_sem.at[n, slot]) for n, (src, dst) in enumerate(pairs)]

    lane = lax.broadcasted_iota(jnp.int32, (shard, 2 * HEAD), 1)
    even = lane < HEAD

    def row_step(r, carry):
        slot = r % buffers
        for copy in near_stores(r):
            copy.start()

        @pl.when(r >= buffers)
        def _():
            for copy in far_stores(r - buffers, slot):
                copy.wait()

        pooled = pool_ref[(slice(None),) * bits + (r,)].reshape(keys - near, width)
        kfb[slot] = dot(pooled, w_ref[:, 3 * width : 4 * width]).astype(BF)
        vfb[slot] = dot(pooled, w_ref[:, 4 * width :]).astype(BF)
        key_seg = jnp.transpose(jnp.broadcast_to(kseg_ref[r], (shard, keys)))
        shape = (keys, shard)
        row = lax.broadcasted_iota(jnp.int32, shape, 0)
        col = lax.broadcasted_iota(jnp.int32, shape, 1)
        inside = (row >= near) | ((row >= col) & (row - col <= 2 * half))
        kept = inside & (key_seg == jnp.broadcast_to(qseg_ref[r], shape))
        bias = jnp.where(kept, 0.0, NEG_LARGE)
        bias = jnp.concatenate([bias, bias], axis=1)
        for j in range(PAIRS):
            cols = slice(2 * HEAD * j, 2 * HEAD * (j + 1))
            qp = qb[r, :, cols]
            zero = jnp.zeros_like(qp)
            stacked = jnp.concatenate([jnp.where(even, qp, zero), jnp.where(even, zero, qp)], axis=0)
            close = dot(knb[r, :, cols], stacked, 1, 1) + bias[:near]
            wide = dot(kfb[slot, :, cols], stacked, 1, 1) + bias[near:]
            top = jnp.maximum(jnp.max(close, axis=0, keepdims=True), jnp.max(wide, axis=0, keepdims=True))
            close = jnp.exp(close - top)
            wide = jnp.exp(wide - top)
            share = 1.0 / (jnp.sum(close, axis=0, keepdims=True) + jnp.sum(wide, axis=0, keepdims=True))
            close = (close * share).astype(BF)
            wide = (wide * share).astype(BF)
            pb[slot, j, :near] = close
            pb[slot, j, near:] = wide
            mixed = dot(vnb[r, :, cols], close, 0, 0) + dot(vfb[slot, :, cols], wide, 0, 0)
            mixed = jnp.concatenate([mixed[:HEAD, :shard], mixed[HEAD:, shard:]], axis=0)
            attb[slot, :, cols] = jnp.transpose(mixed).astype(BF)
        for copy in far_stores(r, slot):
            copy.start()
        return carry

    lax.fori_loop(0, rows, row_step, 0)
    for n in range(buffers):
        r = rows - buffers + n
        for copy in far_stores(r, r % buffers):
            copy.wait()
    for r in range(rows):
        for copy in near_stores(r):
            copy.wait()
    for block in range(seq_count):
        pool_store(block).wait()
    ext_store.wait()

    @pl.when(has_next)
    def _():
        rim.wait_send()
        to_next.wait_send()

    @pl.when(has_prev)
    def _():
        to_prev.wait_send()


def mlp_kernel(
    tok_ref, att_ref, cot_ref, wo_ref, wu_ref, wd_ref, gain_ref, bias_ref,
    out_ref, act_ref, upg_ref, n1_ref, r2_ref, g1_ref, g1b_ref, da_ref, dsum_ref, small_ref,
    slope,
):
    hidden = wu_ref.shape[1]
    chunk = 512
    gain_a, gain_b = gain_ref[0:1], gain_ref[1:2]

    def mean(x):
        return jnp.mean(x, axis=-1, keepdims=True)

    resid = tok_ref[...].astype(F32) + dot(att_ref[...], wo_ref[...])
    centred = resid - mean(resid)
    rstd_a = lax.rsqrt(mean(centred * centred) + EPSILON)
    hat_a = centred * rstd_a
    normed = hat_a * gain_a + bias_ref[0:1]
    low = normed.astype(BF)
    n1_ref[...] = low
    total = normed
    for c in range(0, hidden, chunk):
        up = dot(low, wu_ref[:, c : c + chunk])
        half_cdf = 0.5 * (1.0 + lax.erf(up * ROOT_HALF))
        act = (up * half_cdf).astype(BF)
        act_ref[:, c : c + chunk] = act
        slope[:, c : c + chunk] = half_cdf + up * (INV_ROOT_2PI * jnp.exp(-0.5 * up * up))
        total = total + dot(act, wd_ref[c : c + chunk, :])
    centred = total - mean(total)
    rstd_b = lax.rsqrt(mean(centred * centred) + EPSILON)
    hat_b = centred * rstd_b
    out_ref[...] = (hat_b * gain_b + bias_ref[1:2]).astype(BF)
    g = cot_ref[...].astype(F32)
    gain_two = jnp.sum(g * hat_b, axis=0, keepdims=True)
    bias_two = jnp.sum(g, axis=0, keepdims=True)
    e = g * gain_b
    grad = rstd_b * (e - mean(e) - hat_b * mean(e * hat_b))
    grad_low = grad.astype(BF)
    r2_ref[...] = grad_low
    for c in range(0, hidden, chunk):
        up_grad = (dot(grad_low, wd_ref[c : c + chunk, :], 1, 1) * slope[:, c : c + chunk]).astype(BF)
        upg_ref[:, c : c + chunk] = up_grad
        grad = grad + dot(up_grad, wu_ref[:, c : c + chunk], 1, 1)
    gain_one = jnp.sum(grad * hat_a, axis=0, keepdims=True)
    bias_one = jnp.sum(grad, axis=0, keepdims=True)
    e = grad * gain_a
    resid_grad = rstd_a * (e - mean(e) - hat_a * mean(e * hat_a))
    g1_ref[...] = resid_grad
    resid_low = resid_grad.astype(BF)
    g1b_ref[...] = resid_low
    att_grad = dot(resid_low, wo_ref[...], 1, 1).astype(BF)
    da_ref[...] = att_grad
    prod = att_grad.astype(F32) * att_ref[...].astype(F32)
    high = prod.astype(BF)
    rest = (prod - high.astype(F32)).astype(BF)
    heads = dsum_ref.shape[0]
    width = prod.shape[1]
    head_row = lax.broadcasted_iota(jnp.int32, (heads, width), 0)
    head_col = lax.broadcasted_iota(jnp.int32, (heads, width), 1) // HEAD
    pick = jnp.where(head_row == head_col, 1.0, 0.0).astype(BF)
    dsum_ref[...] = dot(pick, high, 1, 1) + dot(pick, rest, 1, 1)

    @pl.when(pl.program_id(0) == 0)
    def _():
        small_ref[...] = jnp.zeros_like(small_ref)

    small_ref[0:4] += jnp.concatenate([gain_one, gain_two, bias_one, bias_two], axis=0)


def stage_orders(bits):
    rest = list(range(bits - 1))
    cut = len(rest) // 2
    return (
        [bits - 1] + rest[::-1],
        [bits - 1] + rest[:cut][::-1] + rest[cut:][::-1],
    )


class Reducer:
    def __init__(self, seq_count, row_count, units, dest, held, bufs, zsend, zrecv, sems, take=None):
        self.take = take
        self.bits = seq_count.bit_length() - 1
        self.row_count = row_count
        self.units = units
        self.dest = dest
        self.held, self.bufs, self.zsend, self.zrecv = held, bufs, zsend, zrecv
        self.send_sem, self.recv_sem, self.zsend_sem, self.zrecv_sem = sems
        self.seq = lax.axis_index("seq")
        self.row = lax.axis_index("row")
        self.orders = stage_orders(self.bits)

    def bit(self, dim):
        weight = 1 << (self.bits - 1 - dim)
        value = (self.seq // weight) % 2
        return value, self.seq + (1 - 2 * value) * weight

    def barrier(self, line=False):
        sem = pltpu.get_barrier_semaphore()
        count = 1 << self.bits
        peers = [{"seq": self.bit(dim)[1]} for dim in range(self.bits)]
        peers += [{"row": (self.row + k) % self.row_count} for k in range(1, self.row_count)]
        if line:
            peers += [{"seq": (self.seq + 1) % count}, {"seq": (self.seq + count - 1) % count}]
        for peer in peers:
            pl.semaphore_signal(sem, inc=1, device_id=peer, device_id_type=MESH)
        pl.semaphore_wait(sem, len(peers))

    def position(self, unit, stage):
        order = self.orders[unit % 2]
        left = sorted(order[stage:])
        return order[stage], left.index(order[stage])

    def source(self, unit, stage, value):
        pos = self.position(unit, stage)[1]
        base, slot = (self.held, unit % self.held.shape[0]) if stage == 0 else (self.bufs[stage - 1], unit)
        return base, (slot,) + (slice(None),) * pos + (value,)

    def copy(self, unit, stage):
        value, partner = self.bit(self.position(unit, stage)[0])
        base, index = self.source(unit, stage, 1 - value)
        return pltpu.make_async_remote_copy(
            src_ref=base.at[index],
            dst_ref=self.bufs[stage].at[unit],
            send_sem=self.send_sem.at[unit, stage],
            recv_sem=self.recv_sem.at[unit, stage],
            device_id={"seq": partner},
            device_id_type=MESH,
        )

    def start(self, unit):
        self.copy(unit, 0).start()

    def advance(self, unit, stage):
        self.copy(unit, stage - 1).wait()
        dim, pos = self.position(unit, stage - 1)
        value = self.bit(dim)[0]
        buf = self.bufs[stage - 1]
        base, _ = self.source(unit, stage - 1, value)
        slot = unit % self.held.shape[0] if stage == 1 else unit
        lead = self.bits - stage
        total = None
        for flat in range(1 << lead):
            index = tuple((flat >> (lead - 1 - d)) & 1 for d in range(lead))
            own = base[(slot,) + index[:pos] + (value,) + index[pos:]]
            total = own.astype(F32) + buf[(unit,) + index].astype(F32)
            if stage < self.bits:
                buf[(unit,) + index] = total.astype(BF)
        if stage < self.bits:
            self.copy(unit, stage).start()
            return
        if self.take is not None:
            self.take(unit, total)
            return
        cols = total.shape[1] // self.row_count
        for i in range(self.row_count):
            self.zsend[unit, i] = total[:, i * cols : (i + 1) * cols].astype(BF)
        for i in range(self.row_count):
            target, slot = self.dest(unit, i)

            @pl.when(self.row != target)
            def _():
                self.row_copy(unit, i, target, slot).start()

    def row_copy(self, unit, i, target, slot):
        return pltpu.make_async_remote_copy(
            src_ref=self.zsend.at[unit, i],
            dst_ref=self.zrecv.at[slot, self.row],
            send_sem=self.zsend_sem.at[unit, i],
            recv_sem=self.zrecv_sem.at[slot, self.row],
            device_id={"row": target},
            device_id_type=MESH,
        )

    def arrived(self, slot, unit, i):
        total = self.zsend[unit, i].astype(F32)
        for k in range(1, self.row_count):
            other = (self.row + k) % self.row_count
            pltpu.make_async_remote_copy(
                src_ref=self.zsend.at[0, 0],
                dst_ref=self.zrecv.at[slot, other],
                send_sem=self.zsend_sem.at[0, 0],
                recv_sem=self.zrecv_sem.at[slot, other],
                device_id={"row": other},
                device_id_type=MESH,
            ).wait_recv()
            total = total + self.zrecv[slot, other].astype(F32)
        return total

    def sent(self):
        for unit in range(self.units):
            for i in range(self.row_count):
                target, slot = self.dest(unit, i)

                @pl.when(self.row != target)
                def _():
                    self.row_copy(unit, i, target, slot).wait_send()


def split_index(flat, bits):
    return tuple((flat >> (bits - 1 - d)) & 1 for d in range(bits))


def mid_kernel(
    seq_count, row_count, half, buffers,
    n1_hbm, r2_hbm, att_hbm, g1b_hbm, upg_hbm, act_hbm, w_hbm, dsum_ref,
    q_hbm, k_hbm, v_hbm, p_hbm, da_hbm, g1_hbm,
    wout_ref, wup_ref, wdown_ref, dq_hbm, dk_hbm, dv_hbm, dpool_hbm, own_hbm, left_hbm, right_hbm,
    held, *rest,
):
    bits = seq_count.bit_length() - 1
    bufs = rest[:bits]
    (
        zsend, zrecv, slots, n1_ref, r2_ref, att_ref, g1b_ref, w_ref,
        qb, kb, vb, pb, dab, g1_buf, dqb, dkb, dvb, dpb, owb, lfb, rtb,
        send_sem, recv_sem, zsend_sem, zrecv_sem, load_sem, once_sem, in_sem, out_sem, line_send, line_recv,
    ) = rest[bits:]
    rows, shard, width = n1_ref.shape
    near = shard + 2 * half
    part = width // seq_count
    up_units = upg_hbm.shape[2] // width
    units = 2 * up_units + 1
    tall = width // 2
    acts = up_units * 2
    steps = up_units + acts

    def dest(unit, i):
        if unit < up_units:
            g = unit * row_count + i
            return g // up_units, g % up_units
        return i, unit

    red = Reducer(
        seq_count, row_count, units, dest, held, bufs, zsend, zrecv, (send_sem, recv_sem, zsend_sem, zrecv_sem)
    )
    once = [
        pltpu.make_async_copy(src, dst, once_sem.at[n])
        for n, (src, dst) in enumerate(
            [(n1_hbm, n1_ref), (att_hbm, att_ref), (g1b_hbm, g1b_ref), (r2_hbm, r2_ref), (w_hbm, w_ref)]
        )
    ]

    def load(k):
        buf = slots.at[k % 2]
        if k < up_units:
            src, dst = upg_hbm.at[:, :, width * k : width * (k + 1)], buf
        else:
            c = k - up_units
            src, dst = act_hbm.at[:, :, tall * c : tall * (c + 1)], buf.at[:, :, :tall]
        return pltpu.make_async_copy(src, dst, load_sem.at[k % 2])

    def taken(k):
        load(k).wait()
        if k + 1 < steps:
            load(k + 1).start()

    def row_loads(r, slot):
        pairs = [(q_hbm, qb), (k_hbm, kb), (v_hbm, vb), (p_hbm, pb), (da_hbm, dab), (g1_hbm, g1_buf)]
        return [
            pltpu.make_async_copy(src.at[r], dst.at[slot], in_sem.at[n, slot])
            for n, (src, dst) in enumerate(pairs)
        ]

    def row_stores(r, slot):
        pairs = [(dqb, dq_hbm), (dkb, dk_hbm), (dvb, dv_hbm), (dpb, dpool_hbm), (owb, own_hbm)]
        return [
            pltpu.make_async_copy(src.at[slot], dst.at[r], out_sem.at[n, slot])
            for n, (src, dst) in enumerate(pairs)
        ]

    has_prev = red.seq > 0
    has_next = red.seq < seq_count - 1

    def line(n, r, slot):
        src, dst = ((lfb, right_hbm), (rtb, left_hbm))[n]
        return pltpu.make_async_remote_copy(
            src_ref=src.at[slot], dst_ref=dst.at[r], send_sem=line_send.at[n, slot], recv_sem=line_recv.at[n, r],
            device_id={"seq": red.seq + 2 * n - 1}, device_id_type=MESH,
        )

    sides = ((0, has_prev, has_next), (1, has_next, has_prev))

    once[0].start()
    load(0).start()
    for copy in once[1:]:
        copy.start()
    if buffers > 1:
        for copy in row_loads(0, 0):
            copy.start()
    red.barrier(line=True)
    lead = (2,) * (bits - 1)
    plan = {}
    if bits == 3 and up_units == 4 and rows == 8:
        plan = {
            ("up", 1): [(0, 1)], ("up", 2): [(1, 1)], ("up", 4): [(2, 1)],
            ("down", 1): [(3, 1), (0, 2)], ("down", 3): [(1, 2)], ("down", 5): [(4, 1)], ("down", 7): [(2, 2), (0, 3)],
            ("row", 0): [(5, 1), (3, 2), (1, 3)], ("row", 1): [(6, 1), (4, 2), (2, 3)],
            ("row", 2): [(7, 1), (5, 2), (3, 3)], ("row", 3): [(8, 1), (6, 2), (4, 3)],
            ("row", 4): [(7, 2), (5, 3)], ("row", 5): [(8, 2), (6, 3)], ("row", 6): [(7, 3)], ("row", 7): [(8, 3)],
        }

    def follow(*place):
        for unit, stage in plan.get(place, ()):
            red.advance(unit, stage)

    def product(unit, left_ref, right):
        for m in range(2):
            left = left_ref[:, :, tall * m : tall * (m + 1)].reshape(-1, tall)
            held[unit, m] = dot(left, right, 0, 0).reshape(lead + (part, width)).astype(BF)

    once[0].wait()
    for u in range(up_units):
        taken(u)
        product(u, n1_ref, slots[u % 2].reshape(-1, width))
        red.start(u)
        follow("up", u)
    once[1].wait()
    once[2].wait()
    product(up_units, att_ref, g1b_ref[...].reshape(-1, width))
    red.start(up_units)
    follow("up", up_units)
    once[3].wait()
    for c in range(acts):
        k = up_units + c
        taken(k)
        left = slots[k % 2, :, :, :tall].reshape(-1, tall)
        total = dot(left, r2_ref[...].reshape(-1, width), 0, 0)
        blocked = total.reshape(tall // part, part, width).astype(BF)
        for n in range(tall // part):
            flat = (c * tall + n * part) // part
            held[(up_units + 1 + flat % up_units,) + split_index(flat // up_units, bits)] = blocked[n]
        follow("down", c)
    for u in range(up_units + 1, units):
        red.start(u)
    once[4].wait()

    lane = lax.broadcasted_iota(jnp.int32, (shard, 2 * HEAD), 1)
    even = lane < HEAD

    def stack(pair):
        zero = jnp.zeros_like(pair)
        return jnp.concatenate([jnp.where(even, pair, zero), jnp.where(even, zero, pair)], axis=0)

    def row_step(r, carry):
        slot = r % buffers
        if buffers > 1:

            @pl.when(r + 1 < rows)
            def _():
                for copy in row_loads(r + 1, (r + 1) % buffers):
                    copy.start()

        else:
            for copy in row_loads(r, slot):
                copy.start()
        for t in range(rows):
            if ("row", t) in plan:

                @pl.when(r == t)
                def _():
                    follow("row", t)

        for copy in row_loads(r, slot):
            copy.wait()

        @pl.when(r >= buffers)
        def _():
            for copy in row_stores(r - buffers, slot):
                copy.wait()

        for n, sends, _ in sides:

            @pl.when((r >= buffers) & sends)
            def _():
                line(n, r - buffers, slot).wait_send()

        row_sums = dsum_ref[:, pl.ds(pl.multiple_of(r * shard, shard), shard)]
        for j in range(PAIRS):
            cols = slice(2 * HEAD * j, 2 * HEAD * (j + 1))
            queries = stack(qb[slot, :, cols])
            grads = stack(dab[slot, :, cols])
            prob = pb[slot, j]
            dprob = dot(vb[slot, :, cols], grads, 1, 1)
            row_dot = jnp.concatenate([row_sums[2 * j : 2 * j + 1], row_sums[2 * j + 1 : 2 * j + 2]], axis=1)
            dscore = (prob.astype(F32) * (dprob - row_dot)).astype(BF)
            dvb[slot, :, cols] = dot(prob, grads).astype(BF)
            dkb[slot, :, cols] = dot(dscore, queries).astype(BF)
            mixed = dot(kb[slot, :, cols], dscore, 0, 0)
            mixed = jnp.concatenate([mixed[:HEAD, :shard], mixed[HEAD:, shard:]], axis=0)
            dqb[slot, :, cols] = (jnp.transpose(mixed) * HEAD ** (-0.5)).astype(BF)
        back = dot(dkb[slot, :near], w_ref[:, width : 2 * width], 1, 1) + dot(
            dvb[slot, :near], w_ref[:, 2 * width : 3 * width], 1, 1
        )
        lfb[slot] = back[:half].astype(BF)
        rtb[slot] = back[half + shard :].astype(BF)
        owb[slot] = g1_buf[slot] + back[half : half + shard] + dot(dqb[slot], w_ref[:, :width], 1, 1)
        dpb[slot] = (
            dot(dkb[slot, near:], w_ref[:, 3 * width : 4 * width], 1, 1)
            + dot(dvb[slot, near:], w_ref[:, 4 * width :], 1, 1)
        ).astype(BF)
        for copy in row_stores(r, slot):
            copy.start()
        for n, sends, _ in sides:

            @pl.when(sends)
            def _():
                line(n, r, slot).start()

        return carry

    lax.fori_loop(0, rows, row_step, 0)
    if not plan:
        for stage in range(1, bits + 1):
            for u in range(units):
                red.advance(u, stage)
    for k in range(buffers):
        r = rows - buffers + k
        for copy in row_stores(r, r % buffers):
            copy.wait()
    for n, sends, takes in sides:

        @pl.when(sends)
        def _():
            for k in range(buffers):
                r = rows - buffers + k
                line(n, r, r % buffers).wait_send()

        @pl.when(takes)
        def _():
            for r in range(rows):
                line(n, r, r % buffers).wait_recv()

    row = red.row
    cols = width // row_count
    for n in range(up_units):
        g = row * up_units + n
        wup_ref[:, n * cols : (n + 1) * cols] = red.arrived(n, g // row_count, g % row_count)
    wout_ref[...] = red.arrived(up_units, up_units, row)
    for n in range(up_units):
        wdown_ref[n * part : (n + 1) * part] = red.arrived(up_units + 1 + n, up_units + 1 + n, row)
    red.sent()


def tail_kernel(
    seq_count, row_count, half,
    tok_hbm, pool_hbm, dq_hbm, dk_hbm, dv_hbm, dpool_hbm, own_hbm, left_hbm, right_hbm,
    seg_ref, ker_ref, norm_ref,
    win_ref, out_hbm, conv_ref, gain_ref, bias_ref,
    held, *rest,
):
    bits = seq_count.bit_length() - 1
    bufs, rest = rest[:bits], rest[bits:]
    pheld, pbufs, rest = rest[0], rest[1 : 1 + bits], rest[1 + bits :]
    (
        zsend, zrecv, slots, tok_ref, pool_ref, partial, dpool_own, rim_out, rim_in, ownb, leftb, rightb, outb, edgeb,
        ssum, srecv, zsum,
        send_sem, recv_sem, zsend_sem, zrecv_sem, psend_sem, precv_sem, load_sem, pool_sem, ploads_sem,
        line_sem, own_sem, out_sem, small_sem, zsmall_sem,
    ) = rest
    rows, near, width = tok_ref.shape
    shard = near - 2 * half
    part = width // seq_count
    units = 5
    tall = width // 2
    piece = pool_ref.shape[1]
    pieces = (dk_hbm.shape[1] - near) // piece
    pooled_local = dpool_own.shape[1]
    wide = width // 2
    edge = 16
    order = (3, 4, 0, 1, 2)

    def dest(unit, i):
        g = order[unit] * row_count + i
        return g // 5, g % 5

    red = Reducer(
        seq_count, row_count, units, dest, held, bufs, zsend, zrecv, (send_sem, recv_sem, zsend_sem, zrecv_sem)
    )

    def take(unit, total):
        dpool_own[:, :, unit * wide : (unit + 1) * wide] = total

    pred = Reducer(
        seq_count, row_count, 2, None, pheld, pbufs, None, None, (psend_sem, precv_sem, None, None), take
    )
    steps = 2 * pieces + 3

    def load(k):
        buf = slots.at[k % 2]
        if k < 2 * pieces:
            first = near + (k % pieces) * piece
            src, dst = (dk_hbm, dv_hbm)[k // pieces].at[:, first : first + piece], buf.at[:, :piece]
        elif k == 2 * pieces:
            src, dst = dq_hbm, buf.at[:, :shard]
        else:
            src, dst = (dk_hbm, dv_hbm)[k - 2 * pieces - 1].at[:, :near], buf
        return pltpu.make_async_copy(src, dst, load_sem.at[k % 2])

    def taken(k):
        load(k).wait()
        if k + 1 < steps:
            load(k + 1).start()

    def pool_load(n):
        return pltpu.make_async_copy(pool_hbm.at[:, n * piece : (n + 1) * piece], pool_ref, pool_sem.at[0])

    tok_load = pltpu.make_async_copy(tok_hbm, tok_ref, pool_sem.at[1])

    def grad_load(unit, owner):
        src = dpool_hbm.at[:, owner * pooled_local : (owner + 1) * pooled_local, unit * wide : (unit + 1) * wide]
        return pltpu.make_async_copy(
            src, pheld.at[(unit,) + split_index(owner, bits)], ploads_sem.at[unit, owner]
        )

    rim = pltpu.make_async_remote_copy(
        src_ref=rim_out, dst_ref=rim_in, send_sem=line_sem.at[0], recv_sem=line_sem.at[1],
        device_id={"seq": red.seq - 1}, device_id_type=MESH,
    )
    has_prev = red.seq > 0
    has_next = red.seq < seq_count - 1

    for unit in range(2):
        for owner in range(seq_count):
            grad_load(unit, owner).start()
    load(0).start()
    pool_load(0).start()
    tok_load.start()
    red.barrier(line=True)
    for unit in range(2):
        for owner in range(seq_count):
            grad_load(unit, owner).wait()
        pred.start(unit)

    lead = (2,) * (bits - 1)

    def product(unit, left, right, first=True, last=True):
        for m in range(2):
            total = dot(left(m), right, 0, 0)
            if not first:
                total = total + partial[m]
            if not last:
                partial[m] = total
                continue
            held[unit, m] = total.reshape(lead + (part, width)).astype(BF)

    def columns(ref, keep=slice(None)):
        return lambda m: ref[:, keep, tall * m : tall * (m + 1)].reshape(-1, tall)

    def whole(k, length):
        return slots[k % 2, :, :length].reshape(-1, width)

    small = bits == 3 and rows == 8

    def forward(*pairs):
        if small:
            for unit, stage in pairs:
                red.advance(unit, stage)

    for n in range(2):
        for c in range(pieces):
            k = n * pieces + c
            if pieces > 1 and (n or c):
                pool_load(c).start()
            if pieces > 1 or n == 0:
                pool_load(c).wait()
            taken(k)
            product(n, columns(pool_ref), whole(k, piece), c == 0, c == pieces - 1)
        red.start(n)
        if n == 0:
            pred.advance(0, 1)
            pred.advance(1, 1)
        else:
            forward((0, 1))
    own = slice(half, half + shard)
    base = 2 * pieces
    tok_load.wait()
    taken(base)
    product(2, columns(tok_ref, own), whole(base, shard))
    red.start(2)
    forward((1, 1))
    taken(base + 1)
    product(3, columns(tok_ref), whole(base + 1, near))
    red.start(3)
    pred.advance(0, 2)
    pred.advance(1, 2)
    forward((2, 1), (0, 2))
    taken(base + 2)
    product(4, columns(tok_ref), whole(base + 2, near))
    red.start(4)
    forward((3, 1), (1, 2))
    for stage in range(3, bits + 1):
        pred.advance(0, stage)
        pred.advance(1, stage)
    forward((4, 1))

    ssum[...] = jnp.zeros_like(ssum)
    ssum[8:12] = norm_ref[0:4]

    def row_loads(r, slot):
        pairs = [(own_hbm, ownb), (left_hbm, leftb), (right_hbm, rightb)]
        return [
            pltpu.make_async_copy(src.at[r], dst.at[slot], own_sem.at[n, slot])
            for n, (src, dst) in enumerate(pairs)
        ]

    def out_store(r, slot):
        return pltpu.make_async_copy(
            outb.at[slot, : shard - edge], out_hbm.at[r, : shard - edge], out_sem.at[slot]
        )

    for copy in row_loads(0, 0):
        copy.start()
    between = {1: [(0, 3), (2, 2)], 3: [(1, 3)], 4: [(3, 2)], 6: [(2, 3)]}

    def pool_step(r, carry):
        slot = r % 2

        @pl.when(r + 1 < rows)
        def _():
            for copy in row_loads(r + 1, (r + 1) % 2):
                copy.start()

        for t, pairs in between.items():

            @pl.when(r == t)
            def _():
                forward(*pairs)

        select = tap_select(seg_ref[r, :, half - edge : half + shard], edge, pooled_local)
        picked = dot(select, tok_ref[r, half - edge : half + shard])
        grad = dpool_own[r]
        terms, sums = [], []
        for t in range(KER):
            terms.append((grad * ker_ref[t : t + 1]).astype(BF))
            sums.append(jnp.sum(grad * picked[t * pooled_local : (t + 1) * pooled_local], axis=0, keepdims=True))
        ssum[0:KER] += jnp.concatenate(sums, axis=0)
        spread = dot(select, jnp.concatenate(terms, axis=0), 0, 0)
        rim_out[r] = spread[:edge].astype(BF)
        for copy in row_loads(r, slot):
            copy.wait()

        @pl.when(r >= 2)
        def _():
            out_store(r - 2, slot).wait()

        outb[slot] = ownb[slot] + spread[edge:]

        @pl.when(has_prev)
        def _():
            outb[slot, :half] += leftb[slot].astype(F32)

        @pl.when(has_next)
        def _():
            outb[slot, shard - half :] += rightb[slot].astype(F32)

        edgeb[r] = outb[slot, shard - edge :]
        out_store(r, slot).start()
        return carry

    lax.fori_loop(0, rows, pool_step, 0)

    @pl.when(has_prev)
    def _():
        rim.start()

    def small_copy(stage):
        return pltpu.make_async_remote_copy(
            src_ref=ssum, dst_ref=srecv.at[stage], send_sem=small_sem.at[stage, 0], recv_sem=small_sem.at[stage, 1],
            device_id={"seq": red.bit(bits - 1 - stage)[1]}, device_id_type=MESH,
        )

    def small_row(k):
        other = (red.row + k) % row_count
        return pltpu.make_async_remote_copy(
            src_ref=ssum, dst_ref=zsum.at[row_count - k], send_sem=zsmall_sem.at[k, 0],
            recv_sem=zsmall_sem.at[row_count - k, 1], device_id={"row": other}, device_id_type=MESH,
        )

    def small_add(stage):
        small_copy(stage).wait()
        ssum[...] += srecv[stage]

    small_copy(0).start()
    if small:
        forward((4, 2))
    else:
        for stage in range(1, bits):
            for u in range(units):
                red.advance(u, stage)
    small_add(0)
    small_copy(1).start()

    @pl.when(has_next)
    def _():
        rim.wait_recv()
        edgeb[...] += rim_in[...].astype(F32)

    edge_store = pltpu.make_async_copy(edgeb, out_hbm.at[:, shard - edge :], own_sem.at[0, 0])
    edge_store.start()
    forward((3, 3))
    small_add(1)
    small_copy(2).start()
    if small:
        forward((4, 3))
    else:
        for u in range(units):
            red.advance(u, bits)
    small_add(2)
    for stage in range(3, bits):
        small_copy(stage).start()
        small_add(stage)
    for k in range(1, row_count):
        small_row(k).start()
    zsum[0] = ssum[...]
    cols = width // row_count
    for n in range(5):
        g = red.row * 5 + n
        block, i = g // row_count, g % row_count
        unit = (block + 2) % 5
        win_ref[:, n * cols : (n + 1) * cols] = red.arrived(n, unit, i)
    for k in range(1, row_count):
        small_row(row_count - k).wait_recv()
    total = None
    for owner in range(row_count):
        term = zsum[(owner - red.row + row_count) % row_count]
        total = term if total is None else total + term
    conv_ref[...] = total[:KER]
    gain_ref[...] = total[8:10]
    bias_ref[...] = total[10:12]
    for k in range(1, row_count):
        small_row(k).wait_send()
    red.sent()
    edge_store.wait()
    for n in range(2):
        out_store(rows - 2 + n, n).wait()

    @pl.when(has_prev)
    def _():
        rim.wait_send()


def body(tokens, segment_ids, w_in, w_out, w_up, w_down, conv_kernel, norm_gain, norm_bias, cotangent):
    rows, shard, width = tokens.shape
    half = WIN // 2
    pooled_local = shard // STR
    near = shard + 2 * half
    count = rows * shard
    hidden = w_up.shape[1]
    seq_count = lax.axis_size("seq")
    row_count = lax.axis_size("row")
    seq_start = lax.axis_index("seq") * shard
    keys = near + pooled_local * seq_count

    own_seg = lax.dynamic_slice_in_dim(segment_ids, seq_start, shard, 1)
    padded_seg = jnp.pad(segment_ids, ((0, 0), (half, half)), constant_values=-1)
    window_seg = lax.dynamic_slice_in_dim(padded_seg, seq_start, near, 1)
    key_seg = jnp.concatenate([window_seg, segment_ids[:, ::STR]], axis=1)
    own_seg = own_seg[:, None]
    key_seg = key_seg[:, None]
    window_seg = window_seg[:, None]

    def row_spec(*tail):
        return pl.BlockSpec((1,) + tail, lambda r: (r,) + (0,) * len(tail))

    def whole_spec(*dims):
        return pl.BlockSpec(dims, lambda r: (0,) * len(dims), pipeline_mode=pl.Buffered(1))

    def struct(*dims, dtype=BF):
        return jax.ShapeDtypeStruct(dims, dtype)

    def params(limit):
        return pltpu.CompilerParams(dimension_semantics=("arbitrary",), vmem_limit_bytes=limit * MB)

    bits = seq_count.bit_length() - 1
    far = keys - near
    buffers = 2 if keys <= 2 * near else 1
    vmem = pl.BlockSpec(memory_space=pltpu.VMEM)
    hbm = pl.BlockSpec(memory_space=pl.ANY)
    dma = pltpu.SemaphoreType.DMA

    def scratch(*dims, dtype=BF):
        return pltpu.VMEM(dims, dtype)

    tok_ext, pooled_all, q, k_all, v_all, prob, attended = pl.pallas_call(
        functools.partial(front_kernel, seq_count, half, buffers),
        out_shape=(
            struct(rows, near, width), struct(rows, far, width), struct(rows, shard, width),
            struct(rows, keys, width), struct(rows, keys, width), struct(rows, PAIRS, keys, 2 * shard),
            struct(rows, shard, width),
        ),
        in_specs=[hbm] * 2 + [vmem] * 4,
        out_specs=(hbm,) * 7,
        scratch_shapes=[
            scratch(rows, near, width), scratch(rows, 16, width),
            scratch(*((2,) * bits + (rows, pooled_local, width))), scratch(*w_in.shape),
            scratch(rows, shard, width), scratch(rows, near, width), scratch(rows, near, width),
            scratch(buffers, far, width), scratch(buffers, far, width),
            scratch(buffers, PAIRS, keys, 2 * shard), scratch(buffers, shard, width),
            dma((2,)), dma((3, 2)), dma((2, bits, 2)), dma((3, rows)), dma((4, buffers)), dma, dma((seq_count,)),
        ],
        compiler_params=pltpu.CompilerParams(collective_id=2, has_side_effects=True, vmem_limit_bytes=60 * MB),
        name="front",
    )(tokens, w_in, window_seg, own_seg, key_seg, conv_kernel)

    block = 256
    flat_tokens = tokens.reshape(count, width)
    att_flat = attended.reshape(count, width)
    cot_flat = cotangent.reshape(count, width)

    def tok_spec(cols):
        return pl.BlockSpec((block, cols), lambda i: (i, 0))

    layer_out, act, upg, n1, r2, g1, g1b, att_grad, dsum, norm_sums = pl.pallas_call(
        mlp_kernel,
        out_shape=(
            struct(count, width), struct(count, hidden), struct(count, hidden), struct(count, width),
            struct(count, width), struct(count, width, dtype=F32), struct(count, width), struct(count, width),
            struct(16, count, dtype=F32), struct(8, width, dtype=F32),
        ),
        grid=(count // block,),
        in_specs=[
            tok_spec(width), tok_spec(width), tok_spec(width), whole_spec(*w_out.shape),
            whole_spec(*w_up.shape), whole_spec(*w_down.shape), whole_spec(2, width), whole_spec(2, width),
        ],
        out_specs=(
            tok_spec(width), tok_spec(hidden), tok_spec(hidden), tok_spec(width), tok_spec(width),
            tok_spec(width), tok_spec(width), tok_spec(width),
            pl.BlockSpec((16, block), lambda i: (0, i)), pl.BlockSpec((8, width), lambda i: (0, 0)),
        ),
        scratch_shapes=[pltpu.VMEM((block, hidden), F32)],
        compiler_params=params(56),
        name="mlp",
    )(flat_tokens, att_flat, cot_flat, w_out, w_up, w_down, norm_gain, norm_bias)

    def deep(x):
        return x.reshape(rows, shard, -1)

    part = width // seq_count
    up_units = hidden // width
    cols = width // row_count

    def halves(units, *tail, dtype=BF):
        return [pltpu.VMEM((units,) + (2,) * (bits - i) + tail, dtype) for i in range(bits + 1)]

    units = 2 * up_units + 1
    (
        w_out_grad, w_up_grad, w_down_grad, dq, dk, dv, dpool, own_grad, left_grad, right_grad,
    ) = pl.pallas_call(
        functools.partial(mid_kernel, seq_count, row_count, half, buffers),
        out_shape=(
            struct(part, cols, dtype=F32), struct(part, up_units * cols, dtype=F32),
            struct(up_units * part, cols, dtype=F32),
            struct(rows, shard, width), struct(rows, keys, width), struct(rows, keys, width),
            struct(rows, far, width), struct(rows, shard, width, dtype=F32),
            struct(rows, half, width), struct(rows, half, width),
        ),
        in_specs=[hbm] * 7 + [vmem] + [hbm] * 6,
        out_specs=(vmem,) * 3 + (hbm,) * 7,
        scratch_shapes=halves(units, part, width)
        + [scratch(units, row_count, part, cols), scratch(units, row_count, part, cols)]
        + [scratch(2, rows, shard, width)] + [scratch(rows, shard, width)] * 4 + [scratch(*w_in.shape)]
        + [
            scratch(buffers, shard, width), scratch(buffers, keys, width), scratch(buffers, keys, width),
            scratch(buffers, PAIRS, keys, 2 * shard), scratch(buffers, shard, width),
            scratch(buffers, shard, width, dtype=F32),
            scratch(buffers, shard, width), scratch(buffers, keys, width), scratch(buffers, keys, width),
            scratch(buffers, far, width), scratch(buffers, shard, width, dtype=F32),
            scratch(buffers, half, width), scratch(buffers, half, width),
        ]
        + [
            dma((units, bits)), dma((units, bits)), dma((units, row_count)), dma((units, row_count)),
            dma((2,)), dma((5,)), dma((6, buffers)), dma((5, buffers)), dma((2, buffers)), dma((2, rows)),
        ],
        compiler_params=pltpu.CompilerParams(collective_id=0, has_side_effects=True, vmem_limit_bytes=60 * MB),
        name="mid",
    )(
        deep(n1), deep(r2), attended, deep(g1b), deep(upg), deep(act), w_in, dsum,
        q, k_all, v_all, prob, deep(att_grad), deep(g1),
    )

    w_in_grad, token_grad, conv_grad, gain_grad, bias_grad = pl.pallas_call(
        functools.partial(tail_kernel, seq_count, row_count, half),
        out_shape=(
            struct(part, 5 * cols, dtype=F32), struct(rows, shard, width, dtype=F32),
            struct(KER, width, dtype=F32), struct(2, width, dtype=F32), struct(2, width, dtype=F32),
        ),
        in_specs=[hbm] * 9 + [vmem] * 3,
        out_specs=(vmem, hbm) + (vmem,) * 3,
        scratch_shapes=halves(5, part, width) + halves(2, rows, pooled_local, width // 2)
        + [scratch(5, row_count, part, cols), scratch(5, row_count, part, cols)]
        + [
            scratch(2, rows, near, width), scratch(rows, near, width), scratch(rows, min(near, far), width),
            scratch(*((2, width // 2, width) if far > near else (8, 128)), dtype=F32),
            scratch(rows, pooled_local, width, dtype=F32),
            scratch(rows, 16, width), scratch(rows, 16, width),
            scratch(2, shard, width, dtype=F32), scratch(2, half, width), scratch(2, half, width),
            scratch(2, shard, width, dtype=F32), scratch(rows, 16, width, dtype=F32),
            scratch(16, width, dtype=F32), scratch(bits, 16, width, dtype=F32), scratch(row_count, 16, width, dtype=F32),
        ]
        + [
            dma((5, bits)), dma((5, bits)), dma((5, row_count)), dma((5, row_count)), dma((2, bits)), dma((2, bits)),
            dma((2,)), dma((2,)), dma((2, seq_count)), dma((2,)), dma((3, 2)), dma((2,)), dma((bits, 2)), dma((row_count, 2)),
        ],
        compiler_params=pltpu.CompilerParams(collective_id=1, has_side_effects=True, vmem_limit_bytes=60 * MB),
        name="tail",
    )(
        tok_ext, pooled_all, dq, dk, dv, dpool, own_grad, left_grad, right_grad,
        window_seg, conv_kernel, norm_sums,
    )
    return (
        layer_out.reshape(rows, shard, width),
        token_grad,
        w_in_grad,
        w_out_grad,
        w_up_grad,
        w_down_grad,
        conv_grad,
        gain_grad,
        bias_grad,
    )


def solution(mesh):
    placed = (
        P("row", "seq", None), P("row", None), P(), P(), P(), P(), P(), P(), P(), P("row", "seq", None),
    )
    return jax.shard_map(
        body,
        mesh=mesh,
        in_specs=placed,
        out_specs=(
            P("row", "seq", None), P("row", "seq", None), P("seq", "row"), P("seq", "row"),
            P("seq", "row"), P("seq", "row"), P(), P(), P(),
        ),
        check_vma=False,
    )
```

```python
import functools

import jax
import jax.numpy as jnp
from jax import lax
from jax.experimental import pallas as pl
from jax.experimental.pallas import tpu as pltpu
from jax.sharding import PartitionSpec as P

HEADS = 12
HEAD = 64
WIN = 128
KER = 5
STR = 4
PAIRS = HEADS // 2

EPSILON = 1e-05
ROOT_HALF = 0.7071067811865476
INV_ROOT_2PI = 0.3989422804014327
NEG_LARGE = -1e30
BF = jnp.bfloat16
F32 = jnp.float32
MB = 1 << 20
MESH = pl.DeviceIdType.MESH


def dot(a, b, ca=1, cb=0):
    return lax.dot_general(a, b, (((ca,), (cb,)), ((), ())), preferred_element_type=F32)


def tap_select(seg_row, half, pooled_local):
    width = seg_row.shape[1]
    shape = (KER * pooled_local, width)
    rows = lax.broadcasted_iota(jnp.int32, shape, 0)
    cols = lax.broadcasted_iota(jnp.int32, shape, 1)
    tap = rows // pooled_local
    centre = half + STR * (rows - tap * pooled_local)
    seg = jnp.broadcast_to(seg_row, shape)
    centre_seg = jnp.sum(jnp.where(cols == centre, seg, 0), axis=1, keepdims=True)
    hit = (cols == centre + tap - KER // 2) & (seg == centre_seg)
    return jnp.where(hit, 1.0, 0.0).astype(BF)


def front_kernel(
    seq_count, half, buffers,
    tok_hbm, w_hbm, wseg_ref, qseg_ref, kseg_ref, ker_ref,
    ext_hbm, pool_hbm, q_hbm, k_hbm, v_hbm, p_hbm, att_hbm,
    tokx, rim_in, pool_ref, w_ref, qb, knb, vnb, kfb, vfb, pb, attb,
    load_sem, line_sem, gather_sem, near_sem, far_sem, ext_sem, pool_sem,
):
    bits = seq_count.bit_length() - 1
    rows, near, width = tokx.shape
    shard = near - 2 * half
    keys = k_hbm.shape[1]
    pooled_local = pool_ref.shape[bits + 1]
    seq = lax.axis_index("seq")
    has_prev = seq > 0
    has_next = seq < seq_count - 1
    edge = 16

    def flipped(dim):
        weight = 1 << (bits - 1 - dim)
        return seq + (1 - 2 * ((seq // weight) % 2)) * weight

    def line(n, src, dst, step):
        return pltpu.make_async_remote_copy(
            src_ref=src, dst_ref=dst, send_sem=line_sem.at[n, 0], recv_sem=line_sem.at[n, 1],
            device_id={"seq": seq + step}, device_id_type=MESH,
        )

    rim = line(0, tok_hbm.at[:, shard - edge :], rim_in, 1)
    to_next = line(1, tok_hbm.at[:, shard - half :], tokx.at[:, :half], 1)
    to_prev = line(2, tok_hbm.at[:, :half], tokx.at[:, half + shard :], -1)

    rest = list(range(bits - 1))
    cut = len(rest) // 2
    orders = (rest[::-1] + [bits - 1], rest[:cut][::-1] + rest[cut:][::-1] + [bits - 1])

    def gather(part, stage):
        order = orders[part]
        done = order[:stage]
        index = tuple(
            slice(None) if d in done else (seq // (1 << (bits - 1 - d))) % 2 for d in range(bits)
        )
        cols = slice(part * (width // 2), (part + 1) * (width // 2))
        block = pool_ref.at[index + (slice(None), slice(None), cols)]
        return pltpu.make_async_remote_copy(
            src_ref=block, dst_ref=block, send_sem=gather_sem.at[part, stage, 0],
            recv_sem=gather_sem.at[part, stage, 1],
            device_id={"seq": flipped(order[stage])}, device_id_type=MESH,
        )

    own = slice(half, half + shard)
    own_load = pltpu.make_async_copy(tok_hbm, tokx.at[:, own], load_sem.at[0])
    w_load = pltpu.make_async_copy(w_hbm, w_ref, load_sem.at[1])
    own_load.start()
    w_load.start()
    sem = pltpu.get_barrier_semaphore()
    peers = [flipped(d) for d in range(bits)] + [(seq + 1) % seq_count, (seq + seq_count - 1) % seq_count]
    for peer in peers:
        pl.semaphore_signal(sem, inc=1, device_id={"seq": peer}, device_id_type=MESH)
    pl.semaphore_wait(sem, len(peers))

    @pl.when(has_next)
    def _():
        rim.start()

    @pl.when(jnp.logical_not(has_prev))
    def _():
        rim_in[...] = jnp.zeros_like(rim_in)
        tokx[:, :half] = jnp.zeros((rows, half, width), BF)

    @pl.when(jnp.logical_not(has_next))
    def _():
        tokx[:, half + shard :] = jnp.zeros((rows, half, width), BF)

    own_load.wait()

    @pl.when(has_prev)
    def _():
        rim.wait_recv()

    mine = tuple((seq // (1 << (bits - 1 - d))) % 2 for d in range(bits))

    def pool_step(r, carry):
        stretch = jnp.concatenate([rim_in[r], tokx[r, own]], axis=0)
        picked = dot(tap_select(wseg_ref[r, :, half - edge : half + shard], edge, pooled_local), stretch)
        total = picked[:pooled_local] * ker_ref[0:1]
        for t in range(1, KER):
            total = total + picked[t * pooled_local : (t + 1) * pooled_local] * ker_ref[t : t + 1]
        pool_ref[mine + (r,)] = total.astype(BF)
        return carry

    lax.fori_loop(0, rows, pool_step, 0)
    for part in range(2):
        gather(part, 0).start()

    @pl.when(has_next)
    def _():
        to_next.start()

    @pl.when(has_prev)
    def _():
        to_prev.start()

    w_load.wait()
    scale = HEAD ** (-0.5)

    def own_step(r, carry):
        x = tokx[pl.ds(2 * r, 2), own].reshape(2 * shard, width)
        qb[pl.ds(2 * r, 2)] = (dot(x, w_ref[:, :width]) * scale).astype(BF).reshape(2, shard, width)
        knb[pl.ds(2 * r, 2), own] = dot(x, w_ref[:, width : 2 * width]).astype(BF).reshape(2, shard, width)
        vnb[pl.ds(2 * r, 2), own] = dot(x, w_ref[:, 2 * width : 3 * width]).astype(BF).reshape(2, shard, width)
        return carry

    lax.fori_loop(0, rows // 2, own_step, 0)
    for stage in range(1, bits):
        for part in range(2):
            gather(part, stage - 1).wait()
            gather(part, stage).start()
        if stage > 1:
            continue

        @pl.when(has_prev)
        def _():
            to_next.wait_recv()

        @pl.when(has_next)
        def _():
            to_prev.wait_recv()

        def halo_step(r, carry):
            x = tokx[pl.ds(2 * r, 2), :half].reshape(2 * half, width)
            y = tokx[pl.ds(2 * r, 2), half + shard :].reshape(2 * half, width)
            x = jnp.concatenate([x, y], axis=0)
            for ref, first in ((knb, width), (vnb, 2 * width)):
                both = dot(x, w_ref[:, first : first + width]).astype(BF)
                ref[pl.ds(2 * r, 2), :half] = both[: 2 * half].reshape(2, half, width)
                ref[pl.ds(2 * r, 2), half + shard :] = both[2 * half :].reshape(2, half, width)
            return carry

        lax.fori_loop(0, rows // 2, halo_step, 0)
    ext_store = pltpu.make_async_copy(tokx, ext_hbm, ext_sem)
    ext_store.start()
    for part in range(2):
        gather(part, bits - 1).wait()

    def pool_store(block):
        index = tuple((block >> (bits - 1 - d)) & 1 for d in range(bits))
        dst = pool_hbm.at[:, block * pooled_local : (block + 1) * pooled_local]
        return pltpu.make_async_copy(pool_ref.at[index], dst, pool_sem.at[block])

    for block in range(seq_count):
        pool_store(block).start()

    def near_stores(r):
        pairs = [(qb.at[r], q_hbm.at[r]), (knb.at[r], k_hbm.at[r, :near]), (vnb.at[r], v_hbm.at[r, :near])]
        return [pltpu.make_async_copy(src, dst, near_sem.at[n, r]) for n, (src, dst) in enumerate(pairs)]

    def far_stores(r, slot):
        pairs = [
            (kfb.at[slot], k_hbm.at[r, near:]), (vfb.at[slot], v_hbm.at[r, near:]),
            (pb.at[slot], p_hbm.at[r]), (attb.at[slot], att_hbm.at[r]),
        ]
        return [pltpu.make_async_copy(src, dst, far_sem.at[n, slot]) for n, (src, dst) in enumerate(pairs)]

    lane = lax.broadcasted_iota(jnp.int32, (shard, 2 * HEAD), 1)
    even = lane < HEAD

    def row_step(r, carry):
        slot = r % buffers
        for copy in near_stores(r):
            copy.start()

        @pl.when(r >= buffers)
        def _():
            for copy in far_stores(r - buffers, slot):
                copy.wait()

        pooled = pool_ref[(slice(None),) * bits + (r,)].reshape(keys - near, width)
        kfb[slot] = dot(pooled, w_ref[:, 3 * width : 4 * width]).astype(BF)
        vfb[slot] = dot(pooled, w_ref[:, 4 * width :]).astype(BF)
        key_seg = jnp.transpose(jnp.broadcast_to(kseg_ref[r], (shard, keys)))
        shape = (keys, shard)
        row = lax.broadcasted_iota(jnp.int32, shape, 0)
        col = lax.broadcasted_iota(jnp.int32, shape, 1)
        inside = (row >= near) | ((row >= col) & (row - col <= 2 * half))
        kept = inside & (key_seg == jnp.broadcast_to(qseg_ref[r], shape))
        bias = jnp.where(kept, 0.0, NEG_LARGE)
        bias = jnp.concatenate([bias, bias], axis=1)
        for j in range(PAIRS):
            cols = slice(2 * HEAD * j, 2 * HEAD * (j + 1))
            qp = qb[r, :, cols]
            zero = jnp.zeros_like(qp)
            stacked = jnp.concatenate([jnp.where(even, qp, zero), jnp.where(even, zero, qp)], axis=0)
            close = dot(knb[r, :, cols], stacked, 1, 1) + bias[:near]
            wide = dot(kfb[slot, :, cols], stacked, 1, 1) + bias[near:]
            top = jnp.maximum(jnp.max(close, axis=0, keepdims=True), jnp.max(wide, axis=0, keepdims=True))
            close = jnp.exp(close - top)
            wide = jnp.exp(wide - top)
            share = 1.0 / (jnp.sum(close, axis=0, keepdims=True) + jnp.sum(wide, axis=0, keepdims=True))
            close = (close * share).astype(BF)
            wide = (wide * share).astype(BF)
            pb[slot, j, :near] = close
            pb[slot, j, near:] = wide
            mixed = dot(vnb[r, :, cols], close, 0, 0) + dot(vfb[slot, :, cols], wide, 0, 0)
            mixed = jnp.concatenate([mixed[:HEAD, :shard], mixed[HEAD:, shard:]], axis=0)
            attb[slot, :, cols] = jnp.transpose(mixed).astype(BF)
        for copy in far_stores(r, slot):
            copy.start()
        return carry

    lax.fori_loop(0, rows, row_step, 0)
    for n in range(buffers):
        r = rows - buffers + n
        for copy in far_stores(r, r % buffers):
            copy.wait()
    for r in range(rows):
        for copy in near_stores(r):
            copy.wait()
    for block in range(seq_count):
        pool_store(block).wait()
    ext_store.wait()

    @pl.when(has_next)
    def _():
        rim.wait_send()
        to_next.wait_send()

    @pl.when(has_prev)
    def _():
        to_prev.wait_send()


def stage_orders(bits):
    rest = list(range(bits - 1))
    cut = len(rest) // 2
    return (
        [bits - 1] + rest[::-1],
        [bits - 1] + rest[:cut][::-1] + rest[cut:][::-1],
    )


class Reducer:
    def __init__(self, seq_count, row_count, units, dest, held, bufs, zsend, zrecv, sems, take=None, flip=0):
        self.take = take
        self.flip = flip
        self.bits = seq_count.bit_length() - 1
        self.row_count = row_count
        self.units = units
        self.dest = dest
        self.held, self.bufs, self.zsend, self.zrecv = held, bufs, zsend, zrecv
        self.send_sem, self.recv_sem, self.zsend_sem, self.zrecv_sem = sems
        self.seq = lax.axis_index("seq")
        self.row = lax.axis_index("row")
        self.orders = stage_orders(self.bits)

    def bit(self, dim):
        weight = 1 << (self.bits - 1 - dim)
        value = (self.seq // weight) % 2
        return value, self.seq + (1 - 2 * value) * weight

    def barrier(self, line=False):
        sem = pltpu.get_barrier_semaphore()
        count = 1 << self.bits
        peers = [{"seq": self.bit(dim)[1]} for dim in range(self.bits)]
        peers += [{"row": (self.row + k) % self.row_count} for k in range(1, self.row_count)]
        if line:
            peers += [{"seq": (self.seq + 1) % count}, {"seq": (self.seq + count - 1) % count}]
        for peer in peers:
            pl.semaphore_signal(sem, inc=1, device_id=peer, device_id_type=MESH)
        pl.semaphore_wait(sem, len(peers))

    def position(self, unit, stage):
        order = self.orders[(unit + self.flip) % 2]
        left = sorted(order[stage:])
        return order[stage], left.index(order[stage])

    def source(self, unit, stage, value):
        pos = self.position(unit, stage)[1]
        base, slot = (self.held, unit % self.held.shape[0]) if stage == 0 else (self.bufs[stage - 1], unit)
        return base, (slot,) + (slice(None),) * pos + (value,)

    def copy(self, unit, stage):
        value, partner = self.bit(self.position(unit, stage)[0])
        base, index = self.source(unit, stage, 1 - value)
        return pltpu.make_async_remote_copy(
            src_ref=base.at[index],
            dst_ref=self.bufs[stage].at[unit],
            send_sem=self.send_sem.at[unit, stage],
            recv_sem=self.recv_sem.at[unit, stage],
            device_id={"seq": partner},
            device_id_type=MESH,
        )

    def start(self, unit):
        self.copy(unit, 0).start()

    def advance(self, unit, stage):
        self.copy(unit, stage - 1).wait()
        dim, pos = self.position(unit, stage - 1)
        value = self.bit(dim)[0]
        buf = self.bufs[stage - 1]
        base, _ = self.source(unit, stage - 1, value)
        slot = unit % self.held.shape[0] if stage == 1 else unit
        lead = self.bits - stage
        total = None
        for flat in range(1 << lead):
            index = tuple((flat >> (lead - 1 - d)) & 1 for d in range(lead))
            own = base[(slot,) + index[:pos] + (value,) + index[pos:]]
            total = own.astype(F32) + buf[(unit,) + index].astype(F32)
            if stage < self.bits:
                buf[(unit,) + index] = total.astype(BF)
        if stage < self.bits:
            self.copy(unit, stage).start()
            return
        if self.take is not None:
            self.take(unit, total)
            return
        cols = total.shape[1] // self.row_count
        for i in range(self.row_count):
            self.zsend[unit, i] = total[:, i * cols : (i + 1) * cols].astype(BF)
        for i in range(self.row_count):
            target, slot = self.dest(unit, i)

            @pl.when(self.row != target)
            def _():
                self.row_copy(unit, i, target, slot).start()

    def row_copy(self, unit, i, target, slot):
        return pltpu.make_async_remote_copy(
            src_ref=self.zsend.at[unit, i],
            dst_ref=self.zrecv.at[slot, self.row],
            send_sem=self.zsend_sem.at[unit, i],
            recv_sem=self.zrecv_sem.at[slot, self.row],
            device_id={"row": target},
            device_id_type=MESH,
        )

    def finish_plan(self, plan):
        if not plan:
            for stage in range(1, self.bits + 1):
                for unit in range(self.units):
                    self.advance(unit, stage)

    def follow(self, plan, *place):
        for unit, stage in plan.get(place, ()):
            self.advance(unit, stage)

    def arrived(self, slot, unit, i):
        total = self.zsend[unit, i].astype(F32)
        for k in range(1, self.row_count):
            other = (self.row + k) % self.row_count
            pltpu.make_async_remote_copy(
                src_ref=self.zsend.at[0, 0],
                dst_ref=self.zrecv.at[slot, other],
                send_sem=self.zsend_sem.at[0, 0],
                recv_sem=self.zrecv_sem.at[slot, other],
                device_id={"row": other},
                device_id_type=MESH,
            ).wait_recv()
            total = total + self.zrecv[slot, other].astype(F32)
        return total

    def sent(self):
        for unit in range(self.units):
            for i in range(self.row_count):
                target, slot = self.dest(unit, i)

                @pl.when(self.row != target)
                def _():
                    self.row_copy(unit, i, target, slot).wait_send()


def split_index(flat, bits):
    return tuple((flat >> (bits - 1 - d)) & 1 for d in range(bits))


def mlp_kernel(
    seq_count, row_count,
    tok_hbm, att_hbm, cot_hbm, wo_hbm, wu_hbm, wd_hbm, gain_ref, bias_ref,
    out_hbm, upg_hbm, n1_hbm, g1_hbm, g1b_hbm, da_hbm, dsum_ref, small_ref, wdown_ref,
    held, *rest,
):
    bits = seq_count.bit_length() - 1
    bufs = rest[:bits]
    (
        zsend, zrecv, wo_ref, wu_ref, wd_ref, tokw, attw, cotw, actw, slopew, r2w, gradw, hatw, rstdw, outw, n1w,
        send_sem, recv_sem, zsend_sem, zrecv_sem, w_sem, in_sem, out_sem,
    ) = rest[bits:]
    rows, shard, width = tokw.shape
    hidden = wu_ref.shape[1]
    units = hidden // width
    part = width // seq_count
    tall = width // 2
    chunk = 512
    block = 2 * shard
    blocks = rows // 2
    gain_a, gain_b = gain_ref[0:1], gain_ref[1:2]

    red = Reducer(
        seq_count, row_count, units, lambda unit, i: (i, unit), held, bufs, zsend, zrecv,
        (send_sem, recv_sem, zsend_sem, zrecv_sem),
    )
    plan = {}
    if bits == 3 and units == 4 and blocks == 4:
        plan = {
            (0, 0): [(0, 1), (1, 1)], (0, 1): [(2, 1), (3, 1)], (1, 1): [(0, 2), (1, 2)],
            (2, 1): [(2, 2), (3, 2), (0, 3), (1, 3)], (3, 1): [(2, 3), (3, 3)],
        }

    def mean(x):
        return jnp.mean(x, axis=-1, keepdims=True)

    weights = [
        pltpu.make_async_copy(src, dst, w_sem.at[n])
        for n, (src, dst) in enumerate([(wo_hbm, wo_ref), (wu_hbm, wu_ref), (wd_hbm, wd_ref)])
    ]

    def loads(b):
        pairs = [(tok_hbm, tokw), (att_hbm, attw), (cot_hbm, cotw)]
        return [
            pltpu.make_async_copy(src.at[pl.ds(2 * b, 2)], dst.at[pl.ds(2 * b, 2)], in_sem.at[n, b])
            for n, (src, dst) in enumerate(pairs)
        ]

    def stores(b, first):
        pairs = [(outw, out_hbm), (n1w, n1_hbm), (actw, upg_hbm), (gradw, g1_hbm), (r2w, g1b_hbm), (tokw, da_hbm)]
        return [
            pltpu.make_async_copy(pairs[n][0].at[pl.ds(2 * b, 2)], pairs[n][1].at[pl.ds(2 * b, 2)], out_sem.at[n, b])
            for n in (range(2) if first else range(2, 6))
        ]

    weights[0].start()
    for copy in loads(0):
        copy.start()
    weights[1].start()
    weights[2].start()
    for b in range(1, blocks):
        for copy in loads(b):
            copy.start()
    red.barrier()
    small_ref[...] = jnp.zeros_like(small_ref)

    def flat(ref, b):
        return ref[pl.ds(2 * b, 2)].reshape(block, ref.shape[2])

    def put(ref, b, value):
        ref[pl.ds(2 * b, 2)] = value.reshape(2, shard, ref.shape[2])

    def forward_step(b, carry):
        for copy in loads(b):
            copy.wait()

        @pl.when(b == 0)
        def _():
            for copy in weights:
                copy.wait()

        rows_b = pl.ds(2 * b, 2)
        resid = flat(tokw, b).astype(F32) + dot(flat(attw, b), wo_ref[...])
        centred = resid - mean(resid)
        rstd_a = lax.rsqrt(mean(centred * centred) + EPSILON)
        hat_a = centred * rstd_a
        put(hatw, b, hat_a)
        rstdw[rows_b] = rstd_a.reshape(2, shard, 1)
        normed = hat_a * gain_a + bias_ref[0:1]
        low = normed.astype(BF)
        put(n1w, b, low)
        total = normed
        for c in range(0, hidden, chunk):
            up = dot(low, wu_ref[:, c : c + chunk])
            half_cdf = 0.5 * (1.0 + lax.erf(up * ROOT_HALF))
            act = (up * half_cdf).astype(BF)
            actw[rows_b, :, c : c + chunk] = act.reshape(2, shard, chunk)
            slope = half_cdf + up * (INV_ROOT_2PI * jnp.exp(-0.5 * up * up))
            slopew[rows_b, :, c : c + chunk] = slope.astype(BF).reshape(2, shard, chunk)
            total = total + dot(act, wd_ref[c : c + chunk, :])
        centred = total - mean(total)
        rstd_b = lax.rsqrt(mean(centred * centred) + EPSILON)
        hat_b = centred * rstd_b
        put(outw, b, (hat_b * gain_b + bias_ref[1:2]).astype(BF))
        for copy in stores(b, True):
            copy.start()
        g = flat(cotw, b).astype(F32)
        small_ref[1:2] += jnp.sum(g * hat_b, axis=0, keepdims=True)
        small_ref[3:4] += jnp.sum(g, axis=0, keepdims=True)
        e = g * gain_b
        grad = rstd_b * (e - mean(e) - hat_b * mean(e * hat_b))
        put(gradw, b, grad)
        put(r2w, b, grad.astype(BF))
        return carry

    lax.fori_loop(0, blocks, forward_step, 0)

    for c in range(hidden // tall):
        left = actw[:, :, tall * c : tall * (c + 1)].reshape(-1, tall)
        total = dot(left, r2w[...].reshape(-1, width), 0, 0)
        blocked = total.reshape(tall // part, part, width).astype(BF)
        for n in range(tall // part):
            place = (c * tall + n * part) // part
            held[(place % units,) + split_index(place // units, bits)] = blocked[n]
    for u in range(units):
        red.start(u)

    def backward_step(b, carry):
        rows_b = pl.ds(2 * b, 2)

        def advance(half_step):
            for t in range(blocks):
                if (t, half_step) in plan:

                    @pl.when(b == t)
                    def _():
                        red.follow(plan, t, half_step)

        advance(0)
        grad = flat(gradw, b)
        grad_low = flat(r2w, b)
        for c in range(0, hidden, chunk):
            if c == hidden // 2:
                advance(1)
            slope = slopew[rows_b, :, c : c + chunk].reshape(block, chunk).astype(F32)
            up_grad = (dot(grad_low, wd_ref[c : c + chunk, :], 1, 1) * slope).astype(BF)
            actw[rows_b, :, c : c + chunk] = up_grad.reshape(2, shard, chunk)
            grad = grad + dot(up_grad, wu_ref[:, c : c + chunk], 1, 1)
        hat_a = flat(hatw, b)
        small_ref[0:1] += jnp.sum(grad * hat_a, axis=0, keepdims=True)
        small_ref[2:3] += jnp.sum(grad, axis=0, keepdims=True)
        e = grad * gain_a
        resid_grad = rstdw[rows_b].reshape(block, 1) * (e - mean(e) - hat_a * mean(e * hat_a))
        put(gradw, b, resid_grad)
        resid_low = resid_grad.astype(BF)
        put(r2w, b, resid_low)
        att_grad = dot(resid_low, wo_ref[...], 1, 1).astype(BF)
        put(tokw, b, att_grad)
        for copy in stores(b, False):
            copy.start()
        prod = att_grad.astype(F32) * flat(attw, b).astype(F32)
        high = prod.astype(BF)
        rest = (prod - high.astype(F32)).astype(BF)
        heads = dsum_ref.shape[0]
        head_row = lax.broadcasted_iota(jnp.int32, (heads, width), 0)
        head_col = lax.broadcasted_iota(jnp.int32, (heads, width), 1) // HEAD
        pick = jnp.where(head_row == head_col, 1.0, 0.0).astype(BF)
        dsum_ref[:, pl.ds(pl.multiple_of(b * block, block), block)] = dot(pick, high, 1, 1) + dot(pick, rest, 1, 1)
        return carry

    lax.fori_loop(0, blocks, backward_step, 0)
    red.finish_plan(plan)
    for u in range(units):
        wdown_ref[u * part : (u + 1) * part] = red.arrived(u, u, red.row)
    red.sent()
    for b in range(blocks):
        for copy in stores(b, True) + stores(b, False):
            copy.wait()


def mid_kernel(
    seq_count, row_count, half, buffers,
    n1_hbm, att_hbm, g1b_hbm, upg_hbm, w_hbm, dsum_ref,
    q_hbm, k_hbm, v_hbm, p_hbm, da_hbm, g1_hbm,
    wout_ref, wup_ref, pown_ref, dq_hbm, dk_hbm, dv_hbm, dpool_hbm, own_hbm, left_hbm, right_hbm,
    held, *rest,
):
    bits = seq_count.bit_length() - 1
    bufs, rest = rest[:bits], rest[bits:]
    pheld, pbufs, rest = rest[0], rest[1 : 1 + bits], rest[1 + bits :]
    (
        zsend, zrecv, psend_sem, precv_sem, slots, n1_ref, att_ref, g1b_ref, w_ref,
        qb, kb, vb, pb, dab, g1_buf, dqb, dkb, dvb, dpb, owb, lfb, rtb,
        send_sem, recv_sem, zsend_sem, zrecv_sem, load_sem, once_sem, in_sem, out_sem, line_send, line_recv,
    ) = rest
    rows, shard, width = n1_ref.shape
    near = shard + 2 * half
    part = width // seq_count
    up_units = upg_hbm.shape[2] // width
    units = up_units + 1
    tall = width // 2
    steps = up_units
    first_rows, pooled_local = pown_ref.shape[:2]

    def dest(unit, i):
        if unit < up_units:
            g = unit * row_count + i
            return g // up_units, g % up_units
        return i, unit

    red = Reducer(
        seq_count, row_count, units, dest, held, bufs, zsend, zrecv, (send_sem, recv_sem, zsend_sem, zrecv_sem)
    )
    def take(unit, total):
        pown_ref[...] = total

    pred = Reducer(
        seq_count, row_count, 1, None, pheld, pbufs, None, None, (psend_sem, precv_sem, None, None), take
    )
    once = [
        pltpu.make_async_copy(src, dst, once_sem.at[n])
        for n, (src, dst) in enumerate([(n1_hbm, n1_ref), (att_hbm, att_ref), (g1b_hbm, g1b_ref), (w_hbm, w_ref)])
    ]

    def load(k):
        return pltpu.make_async_copy(
            upg_hbm.at[:, :, width * k : width * (k + 1)], slots.at[k % 2], load_sem.at[k % 2]
        )

    def taken(k):
        load(k).wait()
        if k + 1 < steps:
            load(k + 1).start()

    def row_loads(r, slot):
        pairs = [(q_hbm, qb), (k_hbm, kb), (v_hbm, vb), (p_hbm, pb), (da_hbm, dab), (g1_hbm, g1_buf)]
        return [
            pltpu.make_async_copy(src.at[r], dst.at[slot], in_sem.at[n, slot])
            for n, (src, dst) in enumerate(pairs)
        ]

    def row_stores(r, slot):
        pairs = [(dqb, dq_hbm), (dkb, dk_hbm), (dvb, dv_hbm), (dpb, dpool_hbm), (owb, own_hbm)]
        return [
            pltpu.make_async_copy(src.at[slot], dst.at[r], out_sem.at[n, slot])
            for n, (src, dst) in enumerate(pairs)
        ]

    has_prev = red.seq > 0
    has_next = red.seq < seq_count - 1

    def line(n, r, slot):
        src, dst = ((lfb, right_hbm), (rtb, left_hbm))[n]
        return pltpu.make_async_remote_copy(
            src_ref=src.at[slot], dst_ref=dst.at[r], send_sem=line_send.at[n, slot], recv_sem=line_recv.at[n, r],
            device_id={"seq": red.seq + 2 * n - 1}, device_id_type=MESH,
        )

    sides = ((0, has_prev, has_next), (1, has_next, has_prev))

    once[0].start()
    load(0).start()
    for copy in once[1:]:
        copy.start()
    if buffers > 1:
        for copy in row_loads(0, 0):
            copy.start()
    red.barrier(line=True)
    lead = (2,) * (bits - 1)
    plan, pool_plan = {}, {}
    if bits == 3 and up_units == 4 and rows == 8:
        plan = {
            ("up", 1): [(0, 1)], ("up", 2): [(1, 1)], ("up", 4): [(2, 1)],
            ("row", 0): [(3, 1), (0, 2)], ("row", 1): [(4, 1), (1, 2)], ("row", 2): [(2, 2), (0, 3)],
            ("row", 3): [(3, 2), (1, 3)], ("row", 4): [(4, 2), (2, 3)], ("row", 5): [(3, 3)], ("row", 6): [(4, 3)],
        }
        pool_plan = {("row", 5): [(0, 1)], ("row", 7): [(0, 2)], ("end",): [(0, 3)]}

    def product(unit, left_ref, right):
        for m in range(2):
            left = left_ref[:, :, tall * m : tall * (m + 1)].reshape(-1, tall)
            held[unit, m] = dot(left, right, 0, 0).reshape(lead + (part, width)).astype(BF)

    once[0].wait()
    for u in range(up_units):
        taken(u)
        product(u, n1_ref, slots[u % 2].reshape(-1, width))
        red.start(u)
        red.follow(plan, "up", u)
    once[1].wait()
    once[2].wait()
    product(up_units, att_ref, g1b_ref[...].reshape(-1, width))
    red.start(up_units)
    red.follow(plan, "up", up_units)
    once[3].wait()

    lane = lax.broadcasted_iota(jnp.int32, (shard, 2 * HEAD), 1)
    even = lane < HEAD

    def stack(pair):
        zero = jnp.zeros_like(pair)
        return jnp.concatenate([jnp.where(even, pair, zero), jnp.where(even, zero, pair)], axis=0)

    def row_step(r, carry):
        slot = r % buffers
        if buffers > 1:

            @pl.when(r + 1 < rows)
            def _():
                for copy in row_loads(r + 1, (r + 1) % buffers):
                    copy.start()

        else:
            for copy in row_loads(r, slot):
                copy.start()
        for t in range(rows):
            if ("row", t) in plan or ("row", t) in pool_plan or t == first_rows:

                @pl.when(r == t)
                def _():
                    if t == first_rows:
                        pred.start(0)
                    red.follow(plan, "row", t)
                    pred.follow(pool_plan, "row", t)

        for copy in row_loads(r, slot):
            copy.wait()

        @pl.when(r >= buffers)
        def _():
            for copy in row_stores(r - buffers, slot):
                copy.wait()

        for n, sends, _ in sides:

            @pl.when((r >= buffers) & sends)
            def _():
                line(n, r - buffers, slot).wait_send()

        row_sums = dsum_ref[:, pl.ds(pl.multiple_of(r * shard, shard), shard)]
        for j in range(PAIRS):
            cols = slice(2 * HEAD * j, 2 * HEAD * (j + 1))
            queries = stack(qb[slot, :, cols])
            grads = stack(dab[slot, :, cols])
            prob = pb[slot, j]
            dprob = dot(vb[slot, :, cols], grads, 1, 1)
            row_dot = jnp.concatenate([row_sums[2 * j : 2 * j + 1], row_sums[2 * j + 1 : 2 * j + 2]], axis=1)
            dscore = (prob.astype(F32) * (dprob - row_dot)).astype(BF)
            dvb[slot, :, cols] = dot(prob, grads).astype(BF)
            dkb[slot, :, cols] = dot(dscore, queries).astype(BF)
            mixed = dot(kb[slot, :, cols], dscore, 0, 0)
            mixed = jnp.concatenate([mixed[:HEAD, :shard], mixed[HEAD:, shard:]], axis=0)
            dqb[slot, :, cols] = (jnp.transpose(mixed) * HEAD ** (-0.5)).astype(BF)
        back = dot(dkb[slot, :near], w_ref[:, width : 2 * width], 1, 1) + dot(
            dvb[slot, :near], w_ref[:, 2 * width : 3 * width], 1, 1
        )
        lfb[slot] = back[:half].astype(BF)
        rtb[slot] = back[half + shard :].astype(BF)
        owb[slot] = g1_buf[slot] + back[half : half + shard] + dot(dqb[slot], w_ref[:, :width], 1, 1)
        pooled = (
            dot(dkb[slot, near:], w_ref[:, 3 * width : 4 * width], 1, 1)
            + dot(dvb[slot, near:], w_ref[:, 4 * width :], 1, 1)
        ).astype(BF)
        dpb[slot] = pooled

        @pl.when(r < first_rows)
        def _():
            index = (0,) + (slice(None),) * bits + (r,)
            pheld[index] = pooled.reshape((2,) * bits + (pooled_local, width))

        for copy in row_stores(r, slot):
            copy.start()
        for n, sends, _ in sides:

            @pl.when(sends)
            def _():
                line(n, r, slot).start()

        return carry

    lax.fori_loop(0, rows, row_step, 0)
    red.finish_plan(plan)
    pred.finish_plan(pool_plan)
    pred.follow(pool_plan, "end")
    for k in range(buffers):
        r = rows - buffers + k
        for copy in row_stores(r, r % buffers):
            copy.wait()
    for n, sends, takes in sides:

        @pl.when(sends)
        def _():
            for k in range(buffers):
                r = rows - buffers + k
                line(n, r, r % buffers).wait_send()

        @pl.when(takes)
        def _():
            for r in range(rows):
                line(n, r, r % buffers).wait_recv()

    row = red.row
    cols = width // row_count
    for n in range(up_units):
        g = row * up_units + n
        wup_ref[:, n * cols : (n + 1) * cols] = red.arrived(n, g // row_count, g % row_count)
    wout_ref[...] = red.arrived(up_units, up_units, row)
    red.sent()


def tail_kernel(
    seq_count, row_count, half,
    tok_hbm, pool_hbm, dq_hbm, dk_hbm, dv_hbm, dpool_hbm, pown_hbm, own_hbm, left_hbm, right_hbm,
    seg_ref, ker_ref, norm_ref,
    win_ref, out_hbm, conv_ref, gain_ref, bias_ref,
    held, *rest,
):
    bits = seq_count.bit_length() - 1
    bufs, rest = rest[:bits], rest[bits:]
    pheld, pbufs, rest = rest[0], rest[1 : 1 + bits], rest[1 + bits :]
    (
        zsend, zrecv, slots, tok_ref, pool_ref, partial, dpool_own, rim_out, rim_in, ownb, leftb, rightb, outb, edgeb,
        ssum, srecv, zsum,
        send_sem, recv_sem, zsend_sem, zrecv_sem, psend_sem, precv_sem, load_sem, pool_sem, ploads_sem,
        line_sem, own_sem, out_sem, small_sem, zsmall_sem,
    ) = rest
    rows, near, width = tok_ref.shape
    shard = near - 2 * half
    part = width // seq_count
    units = 5
    tall = width // 2
    piece = pool_ref.shape[1]
    pieces = (dk_hbm.shape[1] - near) // piece
    pooled_local = dpool_own.shape[1]
    late_rows = rows - pown_hbm.shape[0]
    edge = 16
    order = (0, 3, 4, 1, 2)

    def dest(unit, i):
        g = order[unit] * row_count + i
        return g // 5, g % 5

    red = Reducer(
        seq_count, row_count, units, dest, held, bufs, zsend, zrecv, (send_sem, recv_sem, zsend_sem, zrecv_sem)
    )

    def take(unit, total):
        dpool_own[rows - late_rows :] = total

    pred = Reducer(
        seq_count, row_count, 1, None, pheld, pbufs, None, None, (psend_sem, precv_sem, None, None), take, 1
    )
    steps = 2 * pieces + 3

    def load(k):
        buf = slots.at[k % 2]
        if k == 0:
            src, dst = dq_hbm, buf.at[:, :shard]
        elif k <= 2 * pieces:
            first = near + ((k - 1) % pieces) * piece
            src, dst = (dk_hbm, dv_hbm)[(k - 1) // pieces].at[:, first : first + piece], buf.at[:, :piece]
        else:
            src, dst = (dk_hbm, dv_hbm)[k - 2 * pieces - 1].at[:, :near], buf
        return pltpu.make_async_copy(src, dst, load_sem.at[k % 2])

    def taken(k):
        load(k).wait()
        if k + 1 < steps:
            load(k + 1).start()

    def pool_load(n):
        return pltpu.make_async_copy(pool_hbm.at[:, n * piece : (n + 1) * piece], pool_ref, pool_sem.at[0])

    tok_load = pltpu.make_async_copy(tok_hbm, tok_ref, pool_sem.at[1])

    def grad_load(owner):
        src = dpool_hbm.at[rows - late_rows :, owner * pooled_local : (owner + 1) * pooled_local]
        return pltpu.make_async_copy(src, pheld.at[(0,) + split_index(owner, bits)], ploads_sem.at[owner])

    own_pool = pltpu.make_async_copy(pown_hbm, dpool_own.at[: rows - late_rows], pool_sem.at[2])

    rim = pltpu.make_async_remote_copy(
        src_ref=rim_out, dst_ref=rim_in, send_sem=line_sem.at[0], recv_sem=line_sem.at[1],
        device_id={"seq": red.seq - 1}, device_id_type=MESH,
    )
    has_prev = red.seq > 0
    has_next = red.seq < seq_count - 1

    for owner in range(seq_count):
        grad_load(owner).start()
    load(0).start()
    tok_load.start()
    pool_load(0).start()
    own_pool.start()
    red.barrier(line=True)
    for owner in range(seq_count):
        grad_load(owner).wait()
    pred.start(0)

    lead = (2,) * (bits - 1)

    def product(unit, left, right, first=True, last=True):
        for m in range(2):
            total = dot(left(m), right, 0, 0)
            if m == 0 and first:
                step("half", unit)
            if not first:
                total = total + partial[m]
            if not last:
                partial[m] = total
                continue
            held[unit, m] = total.reshape(lead + (part, width)).astype(BF)

    def columns(ref, keep=slice(None)):
        return lambda m: ref[:, keep, tall * m : tall * (m + 1)].reshape(-1, tall)

    def whole(k, length):
        return slots[k % 2, :, :length].reshape(-1, width)

    plan, pool_plan = {}, {}
    if bits == 3 and rows == 8:
        plan = {
            ("half", 1): [(0, 1)], ("half", 2): [(1, 1)], ("half", 3): [(2, 1)], ("half", 4): [(3, 1), (0, 2)],
            ("row", 1): [(4, 1), (1, 2)], ("row", 2): [(0, 3), (2, 2)], ("row", 6): [(3, 2)],
            ("end", 0): [(1, 3), (2, 3)], ("end", 1): [(4, 2)], ("end", 2): [(3, 3)], ("end", 3): [(4, 3)],
        }
        pool_plan = {("done", 0): [(0, 1)], ("half", 3): [(0, 2)], ("row", 3): [(0, 3)]}

    def step(*place):
        red.follow(plan, *place)
        pred.follow(pool_plan, *place)

    own = slice(half, half + shard)
    tok_load.wait()
    taken(0)
    product(0, columns(tok_ref, own), whole(0, shard))
    red.start(0)
    step("done", 0)
    for n in range(2):
        for c in range(pieces):
            k = 1 + n * pieces + c
            if pieces > 1 and (n or c):
                pool_load(c).start()
            if pieces > 1 or n == 0:
                pool_load(c).wait()
            taken(k)
            product(1 + n, columns(pool_ref), whole(k, piece), c == 0, c == pieces - 1)
        red.start(1 + n)
    for n in range(2):
        k = 1 + 2 * pieces + n
        taken(k)
        product(3 + n, columns(tok_ref), whole(k, near))
        red.start(3 + n)
    own_pool.wait()
    pred.finish_plan(pool_plan)

    ssum[...] = jnp.zeros_like(ssum)
    ssum[8:12] = norm_ref[0:4]

    def row_loads(r, slot):
        pairs = [(own_hbm, ownb), (left_hbm, leftb), (right_hbm, rightb)]
        return [
            pltpu.make_async_copy(src.at[r], dst.at[slot], own_sem.at[n, slot])
            for n, (src, dst) in enumerate(pairs)
        ]

    def out_store(r, slot):
        return pltpu.make_async_copy(
            outb.at[slot, : shard - edge], out_hbm.at[r, : shard - edge], out_sem.at[slot]
        )

    for copy in row_loads(0, 0):
        copy.start()

    def pool_step(r, carry):
        slot = r % 2

        @pl.when(r + 1 < rows)
        def _():
            for copy in row_loads(r + 1, (r + 1) % 2):
                copy.start()

        for t in range(rows):
            if ("row", t) in plan or ("row", t) in pool_plan:

                @pl.when(r == t)
                def _():
                    step("row", t)

        select = tap_select(seg_ref[r, :, half - edge : half + shard], edge, pooled_local)
        picked = dot(select, tok_ref[r, half - edge : half + shard])
        grad = dpool_own[r]
        terms, sums = [], []
        for t in range(KER):
            terms.append((grad * ker_ref[t : t + 1]).astype(BF))
            sums.append(jnp.sum(grad * picked[t * pooled_local : (t + 1) * pooled_local], axis=0, keepdims=True))
        ssum[0:KER] += jnp.concatenate(sums, axis=0)
        spread = dot(select, jnp.concatenate(terms, axis=0), 0, 0)
        rim_out[r] = spread[:edge].astype(BF)
        for copy in row_loads(r, slot):
            copy.wait()

        @pl.when(r >= 2)
        def _():
            out_store(r - 2, slot).wait()

        outb[slot] = ownb[slot] + spread[edge:]

        @pl.when(has_prev)
        def _():
            outb[slot, :half] += leftb[slot].astype(F32)

        @pl.when(has_next)
        def _():
            outb[slot, shard - half :] += rightb[slot].astype(F32)

        edgeb[r] = outb[slot, shard - edge :]
        out_store(r, slot).start()
        return carry

    lax.fori_loop(0, rows, pool_step, 0)

    @pl.when(has_prev)
    def _():
        rim.start()

    def small_copy(stage):
        return pltpu.make_async_remote_copy(
            src_ref=ssum, dst_ref=srecv.at[stage], send_sem=small_sem.at[stage, 0], recv_sem=small_sem.at[stage, 1],
            device_id={"seq": red.bit(bits - 1 - stage)[1]}, device_id_type=MESH,
        )

    def small_row(k):
        other = (red.row + k) % row_count
        return pltpu.make_async_remote_copy(
            src_ref=ssum, dst_ref=zsum.at[row_count - k], send_sem=zsmall_sem.at[k, 0],
            recv_sem=zsmall_sem.at[row_count - k, 1], device_id={"row": other}, device_id_type=MESH,
        )

    def small_add(stage):
        small_copy(stage).wait()
        ssum[...] += srecv[stage]

    small_copy(0).start()
    step("end", 0)
    small_add(0)
    small_copy(1).start()

    @pl.when(has_next)
    def _():
        rim.wait_recv()
        edgeb[...] += rim_in[...].astype(F32)

    edge_store = pltpu.make_async_copy(edgeb, out_hbm.at[:, shard - edge :], own_sem.at[0, 0])
    edge_store.start()
    step("end", 1)
    small_add(1)
    small_copy(2).start()
    step("end", 2)
    step("end", 3)
    red.finish_plan(plan)
    small_add(2)
    for stage in range(3, bits):
        small_copy(stage).start()
        small_add(stage)
    for k in range(1, row_count):
        small_row(k).start()
    zsum[0] = ssum[...]
    cols = width // row_count
    for n in range(5):
        g = red.row * 5 + n
        block, i = g // row_count, g % row_count
        unit = block + 2 * ((block + 4) // 5) - 4 * (block // 3)
        win_ref[:, n * cols : (n + 1) * cols] = red.arrived(n, unit, i)
    for k in range(1, row_count):
        small_row(row_count - k).wait_recv()
    total = None
    for owner in range(row_count):
        term = zsum[(owner - red.row + row_count) % row_count]
        total = term if total is None else total + term
    conv_ref[...] = total[:KER]
    gain_ref[...] = total[8:10]
    bias_ref[...] = total[10:12]
    for k in range(1, row_count):
        small_row(k).wait_send()
    red.sent()
    edge_store.wait()
    for n in range(2):
        out_store(rows - 2 + n, n).wait()

    @pl.when(has_prev)
    def _():
        rim.wait_send()


def body(tokens, segment_ids, w_in, w_out, w_up, w_down, conv_kernel, norm_gain, norm_bias, cotangent):
    rows, shard, width = tokens.shape
    half = WIN // 2
    pooled_local = shard // STR
    near = shard + 2 * half
    count = rows * shard
    hidden = w_up.shape[1]
    seq_count = lax.axis_size("seq")
    row_count = lax.axis_size("row")
    seq_start = lax.axis_index("seq") * shard
    keys = near + pooled_local * seq_count

    own_seg = lax.dynamic_slice_in_dim(segment_ids, seq_start, shard, 1)
    padded_seg = jnp.pad(segment_ids, ((0, 0), (half, half)), constant_values=-1)
    window_seg = lax.dynamic_slice_in_dim(padded_seg, seq_start, near, 1)
    key_seg = jnp.concatenate([window_seg, segment_ids[:, ::STR]], axis=1)
    own_seg = own_seg[:, None]
    key_seg = key_seg[:, None]
    window_seg = window_seg[:, None]

    def struct(*dims, dtype=BF):
        return jax.ShapeDtypeStruct(dims, dtype)

    bits = seq_count.bit_length() - 1
    far = keys - near
    buffers = 2 if keys <= 2 * near else 1
    vmem = pl.BlockSpec(memory_space=pltpu.VMEM)
    hbm = pl.BlockSpec(memory_space=pl.ANY)
    dma = pltpu.SemaphoreType.DMA

    def scratch(*dims, dtype=BF):
        return pltpu.VMEM(dims, dtype)

    tok_ext, pooled_all, q, k_all, v_all, prob, attended = pl.pallas_call(
        functools.partial(front_kernel, seq_count, half, buffers),
        out_shape=(
            struct(rows, near, width), struct(rows, far, width), struct(rows, shard, width),
            struct(rows, keys, width), struct(rows, keys, width), struct(rows, PAIRS, keys, 2 * shard),
            struct(rows, shard, width),
        ),
        in_specs=[hbm] * 2 + [vmem] * 4,
        out_specs=(hbm,) * 7,
        scratch_shapes=[
            scratch(rows, near, width), scratch(rows, 16, width),
            scratch(*((2,) * bits + (rows, pooled_local, width))), scratch(*w_in.shape),
            scratch(rows, shard, width), scratch(rows, near, width), scratch(rows, near, width),
            scratch(buffers, far, width), scratch(buffers, far, width),
            scratch(buffers, PAIRS, keys, 2 * shard), scratch(buffers, shard, width),
            dma((2,)), dma((3, 2)), dma((2, bits, 2)), dma((3, rows)), dma((4, buffers)), dma, dma((seq_count,)),
        ],
        compiler_params=pltpu.CompilerParams(collective_id=2, has_side_effects=True, vmem_limit_bytes=60 * MB),
        name="front",
    )(tokens, w_in, window_seg, own_seg, key_seg, conv_kernel)

    part = width // seq_count
    up_units = hidden // width
    cols = width // row_count
    first_rows = rows // 2

    def halves(units, *tail):
        return [pltpu.VMEM((units,) + (2,) * (bits - i) + tail, BF) for i in range(bits + 1)]

    def mesh_params(collective_id):
        return pltpu.CompilerParams(
            collective_id=collective_id, has_side_effects=True, vmem_limit_bytes=60 * MB
        )

    def reduce_sems(units, tail=True):
        sems = [dma((units, bits)), dma((units, bits))]
        return sems + [dma((units, row_count)), dma((units, row_count))] if tail else sems

    layer_out, upg, n1, g1, g1b, att_grad, dsum, norm_sums, w_down_grad = pl.pallas_call(
        functools.partial(mlp_kernel, seq_count, row_count),
        out_shape=(
            struct(rows, shard, width), struct(rows, shard, hidden), struct(rows, shard, width),
            struct(rows, shard, width, dtype=F32), struct(rows, shard, width), struct(rows, shard, width),
            struct(16, count, dtype=F32), struct(8, width, dtype=F32), struct(up_units * part, cols, dtype=F32),
        ),
        in_specs=[hbm] * 6 + [vmem] * 2,
        out_specs=(hbm,) * 6 + (vmem,) * 3,
        scratch_shapes=halves(up_units, part, width)
        + [scratch(up_units, row_count, part, cols), scratch(up_units, row_count, part, cols)]
        + [scratch(*w_out.shape), scratch(*w_up.shape), scratch(*w_down.shape)]
        + [scratch(rows, shard, width)] * 3 + [scratch(rows, shard, hidden)] * 2
        + [
            scratch(rows, shard, width), scratch(rows, shard, width, dtype=F32), scratch(rows, shard, width, dtype=F32),
            scratch(rows, shard, 1, dtype=F32), scratch(rows, shard, width), scratch(rows, shard, width),
        ]
        + reduce_sems(up_units) + [dma((3,)), dma((3, rows // 2)), dma((6, rows // 2))],
        compiler_params=mesh_params(3),
        name="mlp",
    )(tokens, attended, cotangent, w_out, w_up, w_down, norm_gain, norm_bias)

    units = up_units + 1
    (
        w_out_grad, w_up_grad, pool_own, dq, dk, dv, dpool, own_grad, left_grad, right_grad,
    ) = pl.pallas_call(
        functools.partial(mid_kernel, seq_count, row_count, half, buffers),
        out_shape=(
            struct(part, cols, dtype=F32), struct(part, up_units * cols, dtype=F32),
            struct(first_rows, pooled_local, width, dtype=F32),
            struct(rows, shard, width), struct(rows, keys, width), struct(rows, keys, width),
            struct(rows, far, width), struct(rows, shard, width, dtype=F32),
            struct(rows, half, width), struct(rows, half, width),
        ),
        in_specs=[hbm] * 5 + [vmem] + [hbm] * 6,
        out_specs=(vmem,) * 3 + (hbm,) * 7,
        scratch_shapes=halves(units, part, width) + halves(1, first_rows, pooled_local, width)
        + [scratch(units, row_count, part, cols), scratch(units, row_count, part, cols)]
        + reduce_sems(1, False)
        + [scratch(2, rows, shard, width)] + [scratch(rows, shard, width)] * 3 + [scratch(*w_in.shape)]
        + [
            scratch(buffers, shard, width), scratch(buffers, keys, width), scratch(buffers, keys, width),
            scratch(buffers, PAIRS, keys, 2 * shard), scratch(buffers, shard, width),
            scratch(buffers, shard, width, dtype=F32),
            scratch(buffers, shard, width), scratch(buffers, keys, width), scratch(buffers, keys, width),
            scratch(buffers, far, width), scratch(buffers, shard, width, dtype=F32),
            scratch(buffers, half, width), scratch(buffers, half, width),
        ]
        + reduce_sems(units)
        + [dma((2,)), dma((4,)), dma((6, buffers)), dma((5, buffers)), dma((2, buffers)), dma((2, rows))],
        compiler_params=mesh_params(0),
        name="mid",
    )(n1, attended, g1b, upg, w_in, dsum, q, k_all, v_all, prob, att_grad, g1)

    w_in_grad, token_grad, conv_grad, gain_grad, bias_grad = pl.pallas_call(
        functools.partial(tail_kernel, seq_count, row_count, half),
        out_shape=(
            struct(part, 5 * cols, dtype=F32), struct(rows, shard, width, dtype=F32),
            struct(KER, width, dtype=F32), struct(2, width, dtype=F32), struct(2, width, dtype=F32),
        ),
        in_specs=[hbm] * 10 + [vmem] * 3,
        out_specs=(vmem, hbm) + (vmem,) * 3,
        scratch_shapes=halves(5, part, width) + halves(1, rows - first_rows, pooled_local, width)
        + [scratch(5, row_count, part, cols), scratch(5, row_count, part, cols)]
        + [
            scratch(2, rows, near, width), scratch(rows, near, width), scratch(rows, min(near, far), width),
            scratch(*((2, width // 2, width) if far > near else (8, 128)), dtype=F32),
            scratch(rows, pooled_local, width, dtype=F32),
            scratch(rows, 16, width), scratch(rows, 16, width),
            scratch(2, shard, width, dtype=F32), scratch(2, half, width), scratch(2, half, width),
            scratch(2, shard, width, dtype=F32), scratch(rows, 16, width, dtype=F32),
            scratch(16, width, dtype=F32), scratch(bits, 16, width, dtype=F32), scratch(row_count, 16, width, dtype=F32),
        ]
        + reduce_sems(5) + reduce_sems(1, False)
        + [
            dma((2,)), dma((3,)), dma((seq_count,)), dma((2,)), dma((3, 2)), dma((2,)), dma((bits, 2)), dma((row_count, 2)),
        ],
        compiler_params=mesh_params(1),
        name="tail",
    )(
        tok_ext, pooled_all, dq, dk, dv, dpool, pool_own, own_grad, left_grad, right_grad,
        window_seg, conv_kernel, norm_sums,
    )
    return (
        layer_out, token_grad, w_in_grad, w_out_grad, w_up_grad, w_down_grad, conv_grad, gain_grad, bias_grad,
    )


def solution(mesh):
    placed = (
        P("row", "seq", None), P("row", None), P(), P(), P(), P(), P(), P(), P(), P("row", "seq", None),
    )
    return jax.shard_map(
        body,
        mesh=mesh,
        in_specs=placed,
        out_specs=(
            P("row", "seq", None), P("row", "seq", None), P("seq", "row"), P("seq", "row"),
            P("seq", "row"), P("seq", "row"), P(), P(), P(),
        ),
        check_vma=False,
    )
```

```python
import functools

import jax
import jax.numpy as jnp
from jax import lax
from jax.experimental import pallas as pl
from jax.experimental.pallas import tpu as pltpu
from jax.sharding import PartitionSpec as P

HEADS = 12
HEAD = 64
WIN = 128
KER = 5
STR = 4
PAIRS = HEADS // 2

EPSILON = 1e-05
ROOT_HALF = 0.7071067811865476
INV_ROOT_2PI = 0.3989422804014327
NEG_LARGE = -1e30
BF = jnp.bfloat16
F32 = jnp.float32
MB = 1 << 20
MESH = pl.DeviceIdType.MESH


def dot(a, b, ca=1, cb=0):
    return lax.dot_general(a, b, (((ca,), (cb,)), ((), ())), preferred_element_type=F32)


def tap_select(seg_row, half, pooled_local):
    width = seg_row.shape[1]
    shape = (KER * pooled_local, width)
    rows = lax.broadcasted_iota(jnp.int32, shape, 0)
    cols = lax.broadcasted_iota(jnp.int32, shape, 1)
    tap = rows // pooled_local
    centre = half + STR * (rows - tap * pooled_local)
    seg = jnp.broadcast_to(seg_row, shape)
    centre_seg = jnp.sum(jnp.where(cols == centre, seg, 0), axis=1, keepdims=True)
    hit = (cols == centre + tap - KER // 2) & (seg == centre_seg)
    return jnp.where(hit, 1.0, 0.0).astype(BF)


def front_kernel(
    seq_count, half, buffers,
    tok_hbm, w_hbm, wseg_ref, qseg_ref, kseg_ref, ker_ref,
    ext_hbm, pool_hbm, q_hbm, k_hbm, v_hbm, p_hbm, att_hbm,
    tokx, rim_in, pool_ref, w_ref, qb, knb, vnb, kfb, vfb, pb, attb,
    load_sem, line_sem, gather_sem, near_sem, far_sem, ext_sem, pool_sem,
):
    bits = seq_count.bit_length() - 1
    rows, near, width = tokx.shape
    shard = near - 2 * half
    keys = k_hbm.shape[1]
    pooled_local = pool_ref.shape[bits + 1]
    seq = lax.axis_index("seq")
    has_prev = seq > 0
    has_next = seq < seq_count - 1
    edge = 16

    def flipped(dim):
        weight = 1 << (bits - 1 - dim)
        return seq + (1 - 2 * ((seq // weight) % 2)) * weight

    def line(n, src, dst, step):
        return pltpu.make_async_remote_copy(
            src_ref=src, dst_ref=dst, send_sem=line_sem.at[n, 0], recv_sem=line_sem.at[n, 1],
            device_id={"seq": seq + step}, device_id_type=MESH,
        )

    rim = line(0, tok_hbm.at[:, shard - edge :], rim_in, 1)
    to_next = line(1, tok_hbm.at[:, shard - half :], tokx.at[:, :half], 1)
    to_prev = line(2, tok_hbm.at[:, :half], tokx.at[:, half + shard :], -1)

    rest = list(range(bits - 1))
    cut = len(rest) // 2
    orders = (rest[::-1] + [bits - 1], rest[:cut][::-1] + rest[cut:][::-1] + [bits - 1])

    def gather(part, stage, group):
        order = orders[part]
        done = order[:stage]
        index = tuple(
            slice(None) if d in done else (seq // (1 << (bits - 1 - d))) % 2 for d in range(bits)
        )
        cols = slice(part * (width // 2), (part + 1) * (width // 2))
        some = slice(group * rows // 2, (group + 1) * rows // 2)
        block = pool_ref.at[index + (some, slice(None), cols)]
        return pltpu.make_async_remote_copy(
            src_ref=block, dst_ref=block, send_sem=gather_sem.at[part, stage, 2 * group],
            recv_sem=gather_sem.at[part, stage, 2 * group + 1],
            device_id={"seq": flipped(order[stage])}, device_id_type=MESH,
        )

    own = slice(half, half + shard)
    own_load = pltpu.make_async_copy(tok_hbm, tokx.at[:, own], load_sem.at[0])
    w_load = pltpu.make_async_copy(w_hbm, w_ref, load_sem.at[1])
    own_load.start()
    w_load.start()
    sem = pltpu.get_barrier_semaphore()
    peers = [flipped(d) for d in range(bits)] + [(seq + 1) % seq_count, (seq + seq_count - 1) % seq_count]
    for peer in peers:
        pl.semaphore_signal(sem, inc=1, device_id={"seq": peer}, device_id_type=MESH)
    pl.semaphore_wait(sem, len(peers))

    @pl.when(has_next)
    def _():
        rim.start()
        to_next.start()

    @pl.when(has_prev)
    def _():
        to_prev.start()

    @pl.when(jnp.logical_not(has_prev))
    def _():
        rim_in[...] = jnp.zeros_like(rim_in)
        tokx[:, :half] = jnp.zeros((rows, half, width), BF)

    @pl.when(jnp.logical_not(has_next))
    def _():
        tokx[:, half + shard :] = jnp.zeros((rows, half, width), BF)

    own_load.wait()

    @pl.when(has_prev)
    def _():
        rim.wait_recv()

    mine = tuple((seq // (1 << (bits - 1 - d))) % 2 for d in range(bits))

    def pool_step(r, carry):
        stretch = jnp.concatenate([rim_in[r], tokx[r, own]], axis=0)
        picked = dot(tap_select(wseg_ref[r, :, half - edge : half + shard], edge, pooled_local), stretch)
        total = picked[:pooled_local] * ker_ref[0:1]
        for t in range(1, KER):
            total = total + picked[t * pooled_local : (t + 1) * pooled_local] * ker_ref[t : t + 1]
        pool_ref[mine + (r,)] = total.astype(BF)
        return carry

    def onward(group, stage):
        for part in range(2):
            if stage:
                gather(part, stage - 1, group).wait()
            if stage < bits:
                gather(part, stage, group).start()

    for group in range(2):
        lax.fori_loop(group * rows // 2, (group + 1) * rows // 2, pool_step, 0)
        onward(group, 0)
    w_load.wait()
    scale = HEAD ** (-0.5)

    def own_step(r, carry):
        x = tokx[pl.ds(2 * r, 2), own].reshape(2 * shard, width)
        qb[pl.ds(2 * r, 2)] = (dot(x, w_ref[:, :width]) * scale).astype(BF).reshape(2, shard, width)
        knb[pl.ds(2 * r, 2), own] = dot(x, w_ref[:, width : 2 * width]).astype(BF).reshape(2, shard, width)
        vnb[pl.ds(2 * r, 2), own] = dot(x, w_ref[:, 2 * width : 3 * width]).astype(BF).reshape(2, shard, width)
        return carry

    lax.fori_loop(0, rows // 2, own_step, 0)
    onward(0, 1)
    onward(1, 1)

    @pl.when(has_prev)
    def _():
        to_next.wait_recv()

    @pl.when(has_next)
    def _():
        to_prev.wait_recv()

    def halo_step(r, carry):
        x = tokx[pl.ds(2 * r, 2), :half].reshape(2 * half, width)
        y = tokx[pl.ds(2 * r, 2), half + shard :].reshape(2 * half, width)
        x = jnp.concatenate([x, y], axis=0)
        for ref, first in ((knb, width), (vnb, 2 * width)):
            both = dot(x, w_ref[:, first : first + width]).astype(BF)
            ref[pl.ds(2 * r, 2), :half] = both[: 2 * half].reshape(2, half, width)
            ref[pl.ds(2 * r, 2), half + shard :] = both[2 * half :].reshape(2, half, width)
        return carry

    lax.fori_loop(0, rows // 2, halo_step, 0)
    for stage in range(2, bits + 1):
        onward(0, stage)
    ext_store = pltpu.make_async_copy(tokx, ext_hbm, ext_sem)
    ext_store.start()

    def pool_store(block):
        index = tuple((block >> (bits - 1 - d)) & 1 for d in range(bits))
        dst = pool_hbm.at[:, block * pooled_local : (block + 1) * pooled_local]
        return pltpu.make_async_copy(pool_ref.at[index], dst, pool_sem.at[block])

    def near_stores(r):
        pairs = [(qb.at[r], q_hbm.at[r]), (knb.at[r], k_hbm.at[r, :near]), (vnb.at[r], v_hbm.at[r, :near])]
        return [pltpu.make_async_copy(src, dst, near_sem.at[n, r]) for n, (src, dst) in enumerate(pairs)]

    def far_stores(r, slot):
        pairs = [
            (kfb.at[slot], k_hbm.at[r, near:]), (vfb.at[slot], v_hbm.at[r, near:]),
            (pb.at[slot], p_hbm.at[r]), (attb.at[slot], att_hbm.at[r]),
        ]
        return [pltpu.make_async_copy(src, dst, far_sem.at[n, slot]) for n, (src, dst) in enumerate(pairs)]

    lane = lax.broadcasted_iota(jnp.int32, (shard, 2 * HEAD), 1)
    even = lane < HEAD

    def row_step(r, carry):
        slot = r % buffers

        @pl.when(r == 1)
        def _():
            for stage in range(2, bits):
                onward(1, stage)

        @pl.when(r == rows // 2)
        def _():
            onward(1, bits)
            for block in range(seq_count):
                pool_store(block).start()

        for copy in near_stores(r):
            copy.start()

        @pl.when(r >= buffers)
        def _():
            for copy in far_stores(r - buffers, slot):
                copy.wait()

        pooled = pool_ref[(slice(None),) * bits + (r,)].reshape(keys - near, width)
        kfb[slot] = dot(pooled, w_ref[:, 3 * width : 4 * width]).astype(BF)
        vfb[slot] = dot(pooled, w_ref[:, 4 * width :]).astype(BF)
        key_seg = jnp.transpose(jnp.broadcast_to(kseg_ref[r], (shard, keys)))
        shape = (keys, shard)
        row = lax.broadcasted_iota(jnp.int32, shape, 0)
        col = lax.broadcasted_iota(jnp.int32, shape, 1)
        inside = (row >= near) | ((row >= col) & (row - col <= 2 * half))
        kept = inside & (key_seg == jnp.broadcast_to(qseg_ref[r], shape))
        bias = jnp.where(kept, 0.0, NEG_LARGE)
        bias = jnp.concatenate([bias, bias], axis=1)
        for j in range(PAIRS):
            cols = slice(2 * HEAD * j, 2 * HEAD * (j + 1))
            qp = qb[r, :, cols]
            zero = jnp.zeros_like(qp)
            stacked = jnp.concatenate([jnp.where(even, qp, zero), jnp.where(even, zero, qp)], axis=0)
            close = dot(knb[r, :, cols], stacked, 1, 1) + bias[:near]
            wide = dot(kfb[slot, :, cols], stacked, 1, 1) + bias[near:]
            top = jnp.maximum(jnp.max(close, axis=0, keepdims=True), jnp.max(wide, axis=0, keepdims=True))
            close = jnp.exp(close - top)
            wide = jnp.exp(wide - top)
            share = 1.0 / (jnp.sum(close, axis=0, keepdims=True) + jnp.sum(wide, axis=0, keepdims=True))
            close = (close * share).astype(BF)
            wide = (wide * share).astype(BF)
            pb[slot, j, :near] = close
            pb[slot, j, near:] = wide
            mixed = dot(vnb[r, :, cols], close, 0, 0) + dot(vfb[slot, :, cols], wide, 0, 0)
            mixed = jnp.concatenate([mixed[:HEAD, :shard], mixed[HEAD:, shard:]], axis=0)
            attb[slot, :, cols] = jnp.transpose(mixed).astype(BF)
        for copy in far_stores(r, slot):
            copy.start()
        return carry

    lax.fori_loop(0, rows, row_step, 0)
    for n in range(buffers):
        r = rows - buffers + n
        for copy in far_stores(r, r % buffers):
            copy.wait()
    for r in range(rows):
        for copy in near_stores(r):
            copy.wait()
    for block in range(seq_count):
        pool_store(block).wait()
    ext_store.wait()

    @pl.when(has_next)
    def _():
        rim.wait_send()
        to_next.wait_send()

    @pl.when(has_prev)
    def _():
        to_prev.wait_send()


def stage_orders(bits):
    rest = list(range(bits - 1))
    cut = len(rest) // 2
    return (
        [bits - 1] + rest[::-1],
        [bits - 1] + rest[:cut][::-1] + rest[cut:][::-1],
    )


def packed_shape(part, cols):
    return (part + part // 2, 128) if cols == 192 and part % 32 == 0 else (part, cols)


def packed(x):
    part, cols = x.shape
    if packed_shape(part, cols) == x.shape:
        return x
    rest = jnp.concatenate([x[: part // 2, 128:], x[part // 2 :, 128:]], axis=1)
    return jnp.concatenate([x[:, :128], rest], axis=0)


def unpacked(x, part, cols):
    if x.shape == (part, cols):
        return x
    rest = jnp.concatenate([x[part:, :64], x[part:, 64:]], axis=0)
    return jnp.concatenate([x[:part], rest], axis=1)


class RowSum:
    def __init__(self, row_count, units, blocks, cols, dest, zsend, zrecv, send_sem, recv_sem):
        self.row = lax.axis_index("row")
        self.row_count, self.units, self.blocks, self.cols, self.dest = row_count, units, blocks, cols, dest
        self.zsend, self.zrecv, self.send_sem, self.recv_sem = zsend, zrecv, send_sem, recv_sem

    def copy(self, unit, i, target, slot):
        return pltpu.make_async_remote_copy(
            src_ref=self.zsend.at[unit, i],
            dst_ref=self.zrecv.at[slot, self.row],
            send_sem=self.send_sem.at[unit, i],
            recv_sem=self.recv_sem.at[slot, self.row],
            device_id={"row": target},
            device_id_type=MESH,
        )

    def send(self, unit, total):
        for i in range(self.blocks):
            self.zsend[unit, i] = packed(total[:, i * self.cols : (i + 1) * self.cols].astype(BF))
        for i in range(self.blocks):
            target, slot = self.dest(unit, i)

            @pl.when(self.row != target)
            def _():
                self.copy(unit, i, target, slot).start()

    def arrived(self, slot, unit, i, part):
        total = self.zsend[unit, i].astype(F32)
        for k in range(1, self.row_count):
            other = (self.row + k) % self.row_count
            pltpu.make_async_remote_copy(
                src_ref=self.zsend.at[0, 0],
                dst_ref=self.zrecv.at[slot, other],
                send_sem=self.send_sem.at[0, 0],
                recv_sem=self.recv_sem.at[slot, other],
                device_id={"row": other},
                device_id_type=MESH,
            ).wait_recv()
            total = total + self.zrecv[slot, other].astype(F32)
        return unpacked(total, part, self.cols)

    def sent(self):
        for unit in range(self.units):
            for i in range(self.blocks):
                target, slot = self.dest(unit, i)

                @pl.when(self.row != target)
                def _():
                    self.copy(unit, i, target, slot).wait_send()


class Reducer:
    def __init__(self, seq_count, units, held, bufs, send_sem, recv_sem, take, flip=0):
        self.take = take
        self.flip = flip
        self.bits = seq_count.bit_length() - 1
        self.units = units
        self.held, self.bufs = held, bufs
        self.send_sem, self.recv_sem = send_sem, recv_sem
        self.seq = lax.axis_index("seq")
        self.orders = stage_orders(self.bits)

    def bit(self, dim):
        weight = 1 << (self.bits - 1 - dim)
        value = (self.seq // weight) % 2
        return value, self.seq + (1 - 2 * value) * weight

    def barrier(self, line=False, row_count=1):
        sem = pltpu.get_barrier_semaphore()
        count = 1 << self.bits
        row = lax.axis_index("row")
        peers = [{"seq": self.bit(dim)[1]} for dim in range(self.bits)]
        peers += [{"row": (row + k) % row_count} for k in range(1, row_count)]
        if line:
            peers += [{"seq": (self.seq + 1) % count}, {"seq": (self.seq + count - 1) % count}]
        for peer in peers:
            pl.semaphore_signal(sem, inc=1, device_id=peer, device_id_type=MESH)
        pl.semaphore_wait(sem, len(peers))

    def position(self, unit, stage):
        order = self.orders[(unit + self.flip) % 2]
        left = sorted(order[stage:])
        return order[stage], left.index(order[stage])

    def source(self, unit, stage, value):
        pos = self.position(unit, stage)[1]
        base, slot = (self.held, unit % self.held.shape[0]) if stage == 0 else (self.bufs[stage - 1], unit)
        return base, (slot,) + (slice(None),) * pos + (value,)

    def copy(self, unit, stage):
        value, partner = self.bit(self.position(unit, stage)[0])
        base, index = self.source(unit, stage, 1 - value)
        return pltpu.make_async_remote_copy(
            src_ref=base.at[index],
            dst_ref=self.bufs[stage].at[unit],
            send_sem=self.send_sem.at[unit, stage],
            recv_sem=self.recv_sem.at[unit, stage],
            device_id={"seq": partner},
            device_id_type=MESH,
        )

    def start(self, unit):
        self.copy(unit, 0).start()

    def advance(self, unit, stage):
        self.copy(unit, stage - 1).wait()
        dim, pos = self.position(unit, stage - 1)
        value = self.bit(dim)[0]
        buf = self.bufs[stage - 1]
        base, _ = self.source(unit, stage - 1, value)
        slot = unit % self.held.shape[0] if stage == 1 else unit
        lead = self.bits - stage
        total = None
        for flat in range(1 << lead):
            index = tuple((flat >> (lead - 1 - d)) & 1 for d in range(lead))
            own = base[(slot,) + index[:pos] + (value,) + index[pos:]]
            total = own.astype(F32) + buf[(unit,) + index].astype(F32)
            if stage < self.bits:
                buf[(unit,) + index] = total.astype(BF)
        if stage < self.bits:
            self.copy(unit, stage).start()
            return
        self.take(unit, total)

    def finish_plan(self, plan):
        if not plan:
            for stage in range(1, self.bits + 1):
                for unit in range(self.units):
                    self.advance(unit, stage)

    def follow(self, plan, *place):
        for unit, stage in plan.get(place, ()):
            self.advance(unit, stage)


def split_index(flat, bits):
    return tuple((flat >> (bits - 1 - d)) & 1 for d in range(bits))


def mlp_kernel(
    seq_count,
    tok_hbm, att_hbm, cot_hbm, wo_hbm, wu_hbm, wd_hbm, gain_ref, bias_ref,
    out_hbm, upg_hbm, n1_hbm, g1_hbm, g1b_hbm, da_hbm, dsum_ref, small_ref, down_ref,
    held, *rest,
):
    bits = seq_count.bit_length() - 1
    bufs = rest[:bits]
    (
        wo_ref, wu_ref, wd_ref, tokw, attw, cotw, actw, slopew, r2w, gradw, hatw, rstdw, outw, n1w,
        send_sem, recv_sem, w_sem, in_sem, out_sem,
    ) = rest[bits:]
    rows, shard, width = tokw.shape
    hidden = wu_ref.shape[1]
    units = hidden // width
    part = width // seq_count
    tall = width // 2
    chunk = 512
    block = 2 * shard
    blocks = rows // 2
    gain_a, gain_b = gain_ref[0:1], gain_ref[1:2]

    def take(unit, total):
        down_ref[unit] = total.astype(BF)

    red = Reducer(seq_count, units, held, bufs, send_sem, recv_sem, take)
    plan = {}
    if bits == 3 and units == 4 and blocks == 4:
        plan = {
            (0, 0): [(0, 1), (1, 1)], (0, 1): [(2, 1), (3, 1)], (1, 1): [(0, 2), (1, 2)],
            (2, 1): [(2, 2), (3, 2)], (3, 0): [(0, 3), (1, 3)], ("end",): [(2, 3), (3, 3)],
        }

    def mean(x):
        return jnp.mean(x, axis=-1, keepdims=True)

    weights = [
        pltpu.make_async_copy(src, dst, w_sem.at[n])
        for n, (src, dst) in enumerate([(wo_hbm, wo_ref), (wu_hbm, wu_ref), (wd_hbm, wd_ref)])
    ]

    def loads(b):
        pairs = [(tok_hbm, tokw), (att_hbm, attw), (cot_hbm, cotw)]
        return [
            pltpu.make_async_copy(src.at[pl.ds(2 * b, 2)], dst.at[pl.ds(2 * b, 2)], in_sem.at[n, b])
            for n, (src, dst) in enumerate(pairs)
        ]

    def stores(b, first):
        pairs = [(outw, out_hbm), (n1w, n1_hbm), (actw, upg_hbm), (gradw, g1_hbm), (r2w, g1b_hbm), (tokw, da_hbm)]
        return [
            pltpu.make_async_copy(pairs[n][0].at[pl.ds(2 * b, 2)], pairs[n][1].at[pl.ds(2 * b, 2)], out_sem.at[n, b])
            for n in (range(2) if first else range(2, 6))
        ]

    weights[0].start()
    for copy in loads(0):
        copy.start()
    weights[1].start()
    weights[2].start()
    for b in range(1, blocks):
        for copy in loads(b):
            copy.start()
    red.barrier()
    small_ref[...] = jnp.zeros_like(small_ref)

    def flat(ref, b):
        return ref[pl.ds(2 * b, 2)].reshape(block, ref.shape[2])

    def put(ref, b, value):
        ref[pl.ds(2 * b, 2)] = value.reshape(2, shard, ref.shape[2])

    def forward_step(b, carry):
        for copy in loads(b):
            copy.wait()

        @pl.when(b == 0)
        def _():
            for copy in weights:
                copy.wait()

        rows_b = pl.ds(2 * b, 2)
        resid = flat(tokw, b).astype(F32) + dot(flat(attw, b), wo_ref[...])
        centred = resid - mean(resid)
        rstd_a = lax.rsqrt(mean(centred * centred) + EPSILON)
        hat_a = centred * rstd_a
        put(hatw, b, hat_a)
        rstdw[rows_b] = rstd_a.reshape(2, shard, 1)
        normed = hat_a * gain_a + bias_ref[0:1]
        low = normed.astype(BF)
        put(n1w, b, low)
        total = normed
        for c in range(0, hidden, chunk):
            up = dot(low, wu_ref[:, c : c + chunk])
            half_cdf = 0.5 * (1.0 + lax.erf(up * ROOT_HALF))
            act = (up * half_cdf).astype(BF)
            actw[rows_b, :, c : c + chunk] = act.reshape(2, shard, chunk)
            slope = half_cdf + up * (INV_ROOT_2PI * jnp.exp(-0.5 * up * up))
            slopew[rows_b, :, c : c + chunk] = slope.astype(BF).reshape(2, shard, chunk)
            total = total + dot(act, wd_ref[c : c + chunk, :])
        centred = total - mean(total)
        rstd_b = lax.rsqrt(mean(centred * centred) + EPSILON)
        hat_b = centred * rstd_b
        put(outw, b, (hat_b * gain_b + bias_ref[1:2]).astype(BF))
        for copy in stores(b, True):
            copy.start()
        g = flat(cotw, b).astype(F32)
        small_ref[1:2] += jnp.sum(g * hat_b, axis=0, keepdims=True)
        small_ref[3:4] += jnp.sum(g, axis=0, keepdims=True)
        e = g * gain_b
        grad = rstd_b * (e - mean(e) - hat_b * mean(e * hat_b))
        put(gradw, b, grad)
        put(r2w, b, grad.astype(BF))
        return carry

    lax.fori_loop(0, blocks, forward_step, 0)

    for c in range(hidden // tall):
        left = actw[:, :, tall * c : tall * (c + 1)].reshape(-1, tall)
        total = dot(left, r2w[...].reshape(-1, width), 0, 0)
        blocked = total.reshape(tall // part, part, width).astype(BF)
        for n in range(tall // part):
            place = (c * tall + n * part) // part
            held[(place % units,) + split_index(place // units, bits)] = blocked[n]
    for u in range(units):
        red.start(u)

    def backward_step(b, carry):
        rows_b = pl.ds(2 * b, 2)

        def advance(half_step):
            for t in range(blocks):
                if (t, half_step) in plan:

                    @pl.when(b == t)
                    def _():
                        red.follow(plan, t, half_step)

        advance(0)
        grad = flat(gradw, b)
        grad_low = flat(r2w, b)
        for c in range(0, hidden, chunk):
            if c == hidden // 2:
                advance(1)
            slope = slopew[rows_b, :, c : c + chunk].reshape(block, chunk).astype(F32)
            up_grad = (dot(grad_low, wd_ref[c : c + chunk, :], 1, 1) * slope).astype(BF)
            actw[rows_b, :, c : c + chunk] = up_grad.reshape(2, shard, chunk)
            grad = grad + dot(up_grad, wu_ref[:, c : c + chunk], 1, 1)
        hat_a = flat(hatw, b)
        small_ref[0:1] += jnp.sum(grad * hat_a, axis=0, keepdims=True)
        small_ref[2:3] += jnp.sum(grad, axis=0, keepdims=True)
        e = grad * gain_a
        resid_grad = rstdw[rows_b].reshape(block, 1) * (e - mean(e) - hat_a * mean(e * hat_a))
        put(gradw, b, resid_grad)
        resid_low = resid_grad.astype(BF)
        put(r2w, b, resid_low)
        att_grad = dot(resid_low, wo_ref[...], 1, 1).astype(BF)
        put(tokw, b, att_grad)
        for copy in stores(b, False):
            copy.start()
        prod = att_grad.astype(F32) * flat(attw, b).astype(F32)
        high = prod.astype(BF)
        rest = (prod - high.astype(F32)).astype(BF)
        heads = dsum_ref.shape[0]
        head_row = lax.broadcasted_iota(jnp.int32, (heads, width), 0)
        head_col = lax.broadcasted_iota(jnp.int32, (heads, width), 1) // HEAD
        pick = jnp.where(head_row == head_col, 1.0, 0.0).astype(BF)
        dsum_ref[:, pl.ds(pl.multiple_of(b * block, block), block)] = dot(pick, high, 1, 1) + dot(pick, rest, 1, 1)
        return carry

    lax.fori_loop(0, blocks, backward_step, 0)
    red.finish_plan(plan)
    red.follow(plan, "end")
    for b in range(blocks):
        for copy in stores(b, True) + stores(b, False):
            copy.wait()


def mid_kernel(
    seq_count, row_count, half, buffers,
    n1_hbm, att_hbm, g1b_hbm, upg_hbm, w_hbm, dsum_ref,
    q_hbm, k_hbm, v_hbm, p_hbm, da_hbm, g1_hbm, down_ref,
    wout_ref, wup_ref, wdown_ref, pown_ref, dq_hbm, dk_hbm, dv_hbm, dpool_hbm, own_hbm, left_hbm, right_hbm,
    held, *rest,
):
    bits = seq_count.bit_length() - 1
    bufs, rest = rest[:bits], rest[bits:]
    pheld, pbufs, rest = rest[0], rest[1 : 1 + bits], rest[1 + bits :]
    (
        zsend, zrecv, psend_sem, precv_sem, slots, n1_ref, att_ref, g1b_ref, w_ref,
        qb, kb, vb, pb, dab, g1_buf, dqb, dkb, dvb, dpb, owb, lfb, rtb,
        send_sem, recv_sem, zsend_sem, zrecv_sem, load_sem, once_sem, in_sem, out_sem, line_send, line_recv,
    ) = rest
    rows, shard, width = n1_ref.shape
    near = shard + 2 * half
    part = width // seq_count
    up_units = upg_hbm.shape[2] // width
    units = up_units + 1
    tall = width // 2
    steps = up_units
    first_rows, pooled_local = pown_ref.shape[:2]

    def dest(unit, i):
        if unit < up_units:
            g = unit * row_count + i
            return g // up_units, g % up_units
        return i, unit

    cols = width // row_count
    down_units = down_ref.shape[0]
    sums = RowSum(row_count, units + down_units, row_count, cols, dest, zsend, zrecv, zsend_sem, zrecv_sem)
    red = Reducer(seq_count, units, held, bufs, send_sem, recv_sem, sums.send)

    def take(unit, total):
        pown_ref[...] = total

    pred = Reducer(seq_count, 1, pheld, pbufs, psend_sem, precv_sem, take)
    once = [
        pltpu.make_async_copy(src, dst, once_sem.at[n])
        for n, (src, dst) in enumerate([(n1_hbm, n1_ref), (att_hbm, att_ref), (g1b_hbm, g1b_ref), (w_hbm, w_ref)])
    ]

    def load(k):
        return pltpu.make_async_copy(
            upg_hbm.at[:, :, width * k : width * (k + 1)], slots.at[k % 2], load_sem.at[k % 2]
        )

    def taken(k):
        load(k).wait()
        if k + 1 < steps:
            load(k + 1).start()

    def row_loads(r, slot):
        pairs = [(q_hbm, qb), (k_hbm, kb), (v_hbm, vb), (p_hbm, pb), (da_hbm, dab), (g1_hbm, g1_buf)]
        return [
            pltpu.make_async_copy(src.at[r], dst.at[slot], in_sem.at[n, slot])
            for n, (src, dst) in enumerate(pairs)
        ]

    def row_stores(r, slot):
        pairs = [(dqb, dq_hbm), (dkb, dk_hbm), (dvb, dv_hbm), (dpb, dpool_hbm), (owb, own_hbm)]
        return [
            pltpu.make_async_copy(src.at[slot], dst.at[r], out_sem.at[n, slot])
            for n, (src, dst) in enumerate(pairs)
        ]

    has_prev = red.seq > 0
    has_next = red.seq < seq_count - 1

    def line(n, r, slot):
        src, dst = ((lfb, right_hbm), (rtb, left_hbm))[n]
        return pltpu.make_async_remote_copy(
            src_ref=src.at[slot], dst_ref=dst.at[r], send_sem=line_send.at[n, slot], recv_sem=line_recv.at[n, r],
            device_id={"seq": red.seq + 2 * n - 1}, device_id_type=MESH,
        )

    sides = ((0, has_prev, has_next), (1, has_next, has_prev))

    once[0].start()
    load(0).start()
    for copy in once[1:]:
        copy.start()
    if buffers > 1:
        for copy in row_loads(0, 0):
            copy.start()
    red.barrier(line=True, row_count=row_count)
    lead = (2,) * (bits - 1)
    plan, pool_plan = {}, {}
    if bits == 3 and up_units == 4 and rows == 8:
        plan = {
            ("up", 1): [(0, 1)], ("up", 2): [(1, 1)], ("up", 4): [(2, 1)],
            ("row", 0): [(3, 1)], ("row", 1): [(0, 2), (4, 1)], ("row", 2): [(1, 2)],
            ("row", 3): [(2, 2), (0, 3)], ("row", 4): [(3, 2), (1, 3)], ("row", 5): [(4, 2), (2, 3)],
            ("row", 6): [(3, 3)], ("row", 7): [(4, 3)],
        }
        pool_plan = {("row", 5): [(0, 1)], ("row", 7): [(0, 2)], ("end",): [(0, 3)]}

    def product(unit, left_ref, right):
        for m in range(2):
            left = left_ref[:, :, tall * m : tall * (m + 1)].reshape(-1, tall)
            held[unit, m] = dot(left, right, 0, 0).reshape(lead + (part, width)).astype(BF)

    once[0].wait()
    for u in range(up_units):
        taken(u)
        if u == 0:
            for n in range(down_units):
                sums.send(units + n, down_ref[n])
        product(u, n1_ref, slots[u % 2].reshape(-1, width))
        red.start(u)
        red.follow(plan, "up", u)
    once[1].wait()
    once[2].wait()
    product(up_units, att_ref, g1b_ref[...].reshape(-1, width))
    red.start(up_units)
    red.follow(plan, "up", up_units)
    once[3].wait()

    lane = lax.broadcasted_iota(jnp.int32, (shard, 2 * HEAD), 1)
    even = lane < HEAD

    def stack(pair):
        zero = jnp.zeros_like(pair)
        return jnp.concatenate([jnp.where(even, pair, zero), jnp.where(even, zero, pair)], axis=0)

    def row_step(r, carry):
        slot = r % buffers
        if buffers > 1:

            @pl.when(r + 1 < rows)
            def _():
                for copy in row_loads(r + 1, (r + 1) % buffers):
                    copy.start()

        else:
            for copy in row_loads(r, slot):
                copy.start()
        for t in range(rows):
            if ("row", t) in plan or ("row", t) in pool_plan or t == first_rows:

                @pl.when(r == t)
                def _():
                    if t == first_rows:
                        pred.start(0)
                    red.follow(plan, "row", t)
                    pred.follow(pool_plan, "row", t)

        for copy in row_loads(r, slot):
            copy.wait()

        @pl.when(r >= buffers)
        def _():
            for copy in row_stores(r - buffers, slot):
                copy.wait()

        for n, sends, _ in sides:

            @pl.when((r >= buffers) & sends)
            def _():
                line(n, r - buffers, slot).wait_send()

        row_sums = dsum_ref[:, pl.ds(pl.multiple_of(r * shard, shard), shard)]
        for j in range(PAIRS):
            cols = slice(2 * HEAD * j, 2 * HEAD * (j + 1))
            queries = stack(qb[slot, :, cols])
            grads = stack(dab[slot, :, cols])
            prob = pb[slot, j]
            dprob = dot(vb[slot, :, cols], grads, 1, 1)
            row_dot = jnp.concatenate([row_sums[2 * j : 2 * j + 1], row_sums[2 * j + 1 : 2 * j + 2]], axis=1)
            dscore = (prob.astype(F32) * (dprob - row_dot)).astype(BF)
            dvb[slot, :, cols] = dot(prob, grads).astype(BF)
            dkb[slot, :, cols] = dot(dscore, queries).astype(BF)
            mixed = dot(kb[slot, :, cols], dscore, 0, 0)
            mixed = jnp.concatenate([mixed[:HEAD, :shard], mixed[HEAD:, shard:]], axis=0)
            dqb[slot, :, cols] = (jnp.transpose(mixed) * HEAD ** (-0.5)).astype(BF)
        back = dot(dkb[slot, :near], w_ref[:, width : 2 * width], 1, 1) + dot(
            dvb[slot, :near], w_ref[:, 2 * width : 3 * width], 1, 1
        )
        lfb[slot] = back[:half].astype(BF)
        rtb[slot] = back[half + shard :].astype(BF)
        owb[slot] = g1_buf[slot] + back[half : half + shard] + dot(dqb[slot], w_ref[:, :width], 1, 1)
        pooled = (
            dot(dkb[slot, near:], w_ref[:, 3 * width : 4 * width], 1, 1)
            + dot(dvb[slot, near:], w_ref[:, 4 * width :], 1, 1)
        ).astype(BF)
        dpb[slot] = pooled

        @pl.when(r < first_rows)
        def _():
            index = (0,) + (slice(None),) * bits + (r,)
            pheld[index] = pooled.reshape((2,) * bits + (pooled_local, width))

        for copy in row_stores(r, slot):
            copy.start()
        for n, sends, _ in sides:

            @pl.when(sends)
            def _():
                line(n, r, slot).start()

        return carry

    lax.fori_loop(0, rows, row_step, 0)
    red.finish_plan(plan)
    pred.finish_plan(pool_plan)
    pred.follow(pool_plan, "end")
    for k in range(buffers):
        r = rows - buffers + k
        for copy in row_stores(r, r % buffers):
            copy.wait()
    for n, sends, takes in sides:

        @pl.when(sends)
        def _():
            for k in range(buffers):
                r = rows - buffers + k
                line(n, r, r % buffers).wait_send()

        @pl.when(takes)
        def _():
            for r in range(rows):
                line(n, r, r % buffers).wait_recv()

    row = sums.row
    for n in range(down_units):
        wdown_ref[n * part : (n + 1) * part] = sums.arrived(units + n, units + n, row, part)
    for n in range(up_units):
        g = row * up_units + n
        wup_ref[:, n * cols : (n + 1) * cols] = sums.arrived(n, g // row_count, g % row_count, part)
    wout_ref[...] = sums.arrived(up_units, up_units, row, part)
    sums.sent()


def tail_kernel(
    seq_count, row_count, half,
    tok_hbm, pool_hbm, dq_hbm, dk_hbm, dv_hbm, dpool_hbm, pown_hbm, own_hbm, left_hbm, right_hbm,
    seg_ref, ker_ref, norm_ref,
    win_ref, out_hbm, conv_ref, gain_ref, bias_ref,
    held, *rest,
):
    bits = seq_count.bit_length() - 1
    bufs, rest = rest[:bits], rest[bits:]
    pheld, pbufs, rest = rest[0], rest[1 : 1 + bits], rest[1 + bits :]
    (
        zsend, zrecv, slots, tok_ref, pool_ref, partial, dpool_own, rim_out, rim_in, ownb, leftb, rightb, outb, edgeb,
        ssum, srecv, zsum,
        send_sem, recv_sem, zsend_sem, zrecv_sem, psend_sem, precv_sem, load_sem, pool_sem, ploads_sem,
        line_sem, own_sem, out_sem, small_sem, zsmall_sem,
    ) = rest
    rows, near, width = tok_ref.shape
    shard = near - 2 * half
    part = width // seq_count
    units = 10
    tall = width // 2
    piece = pool_ref.shape[1]
    pieces = (dk_hbm.shape[1] - near) // piece
    pooled_local = dpool_own.shape[1]
    late_rows = rows - pown_hbm.shape[0]
    edge = 16
    order = (0, 3, 4, 1, 2)

    blocks = row_count // 2

    def dest(unit, i):
        g = order[unit // 2] * row_count + (unit % 2) * blocks + i
        return g // 5, g % 5

    cols = width // row_count
    sums = RowSum(row_count, units, blocks, cols, dest, zsend, zrecv, zsend_sem, zrecv_sem)
    red = Reducer(seq_count, units, held, bufs, send_sem, recv_sem, sums.send)

    def take(unit, total):
        dpool_own[rows - late_rows :] = total

    pred = Reducer(seq_count, 1, pheld, pbufs, psend_sem, precv_sem, take, 1)
    steps = 2 * pieces + 3

    def load(k):
        buf = slots.at[k % 2]
        if k == 0:
            src, dst = dq_hbm, buf.at[:, :shard]
        elif k <= 2 * pieces:
            first = near + ((k - 1) % pieces) * piece
            src, dst = (dk_hbm, dv_hbm)[(k - 1) // pieces].at[:, first : first + piece], buf.at[:, :piece]
        else:
            src, dst = (dk_hbm, dv_hbm)[k - 2 * pieces - 1].at[:, :near], buf
        return pltpu.make_async_copy(src, dst, load_sem.at[k % 2])

    def taken(k):
        load(k).wait()
        if k + 1 < steps:
            load(k + 1).start()

    def pool_load(n):
        return pltpu.make_async_copy(pool_hbm.at[:, n * piece : (n + 1) * piece], pool_ref, pool_sem.at[0])

    tok_load = pltpu.make_async_copy(tok_hbm, tok_ref, pool_sem.at[1])

    def grad_load(owner):
        src = dpool_hbm.at[rows - late_rows :, owner * pooled_local : (owner + 1) * pooled_local]
        return pltpu.make_async_copy(src, pheld.at[(0,) + split_index(owner, bits)], ploads_sem.at[owner])

    own_pool = pltpu.make_async_copy(pown_hbm, dpool_own.at[: rows - late_rows], pool_sem.at[2])

    rim = pltpu.make_async_remote_copy(
        src_ref=rim_out, dst_ref=rim_in, send_sem=line_sem.at[0], recv_sem=line_sem.at[1],
        device_id={"seq": red.seq - 1}, device_id_type=MESH,
    )
    has_prev = red.seq > 0
    has_next = red.seq < seq_count - 1

    for owner in range(seq_count):
        grad_load(owner).start()
    load(0).start()
    tok_load.start()
    pool_load(0).start()
    own_pool.start()
    red.barrier(line=True, row_count=row_count)
    for owner in range(seq_count):
        grad_load(owner).wait()
    pred.start(0)

    lead = (2,) * (bits - 1)

    def product(unit, left, right, first=True, last=True):
        for m in range(2):
            total = dot(left(m), right, 0, 0)
            if m == 0 and first:
                step("half", unit)
            if not first:
                total = total + partial[m]
            if not last:
                partial[m] = total
                continue
            total = total.reshape(lead + (part, width)).astype(BF)
            for h in range(2):
                held[2 * unit + h, m] = total[..., tall * h : tall * (h + 1)]

    def begin(unit):
        red.start(2 * unit)
        red.start(2 * unit + 1)

    def columns(ref, keep=slice(None)):
        return lambda m: ref[:, keep, tall * m : tall * (m + 1)].reshape(-1, tall)

    def whole(k, length):
        return slots[k % 2, :, :length].reshape(-1, width)

    plan, pool_plan = {}, {}
    if bits == 3 and rows == 8:
        plan = {
            ("half", 1): [(0, 1), (1, 1)], ("half", 2): [(2, 1), (3, 1)], ("half", 3): [(4, 1), (5, 1), (0, 2), (1, 2)],
            ("half", 4): [(6, 1), (7, 1), (2, 2), (3, 2)], ("row", 0): [(0, 3), (1, 3)],
            ("row", 1): [(8, 1), (9, 1)], ("row", 2): [(4, 2), (5, 2)], ("row", 4): [(2, 3), (3, 3)],
            ("row", 6): [(6, 2), (7, 2)], ("end", 0): [(4, 3), (5, 3)], ("end", 1): [(8, 2), (9, 2)],
            ("end", 2): [(6, 3), (7, 3)], ("end", 3): [(8, 3), (9, 3)],
        }
        pool_plan = {("done", 0): [(0, 1)], ("half", 3): [(0, 2)], ("row", 3): [(0, 3)]}

    def step(*place):
        red.follow(plan, *place)
        pred.follow(pool_plan, *place)

    own = slice(half, half + shard)
    tok_load.wait()
    taken(0)
    product(0, columns(tok_ref, own), whole(0, shard))
    begin(0)
    step("done", 0)
    for n in range(2):
        for c in range(pieces):
            k = 1 + n * pieces + c
            if pieces > 1 and (n or c):
                pool_load(c).start()
            if pieces > 1 or n == 0:
                pool_load(c).wait()
            taken(k)
            product(1 + n, columns(pool_ref), whole(k, piece), c == 0, c == pieces - 1)
        begin(1 + n)
    for n in range(2):
        k = 1 + 2 * pieces + n
        taken(k)
        product(3 + n, columns(tok_ref), whole(k, near))
        begin(3 + n)
    own_pool.wait()
    pred.finish_plan(pool_plan)

    ssum[...] = jnp.zeros_like(ssum)
    ssum[8:12] = norm_ref[0:4]

    def row_loads(r, slot):
        pairs = [(own_hbm, ownb), (left_hbm, leftb), (right_hbm, rightb)]
        return [
            pltpu.make_async_copy(src.at[r], dst.at[slot], own_sem.at[n, slot])
            for n, (src, dst) in enumerate(pairs)
        ]

    def out_store(r, slot):
        return pltpu.make_async_copy(
            outb.at[slot, : shard - edge], out_hbm.at[r, : shard - edge], out_sem.at[slot]
        )

    for copy in row_loads(0, 0):
        copy.start()

    def pool_step(r, carry):
        slot = r % 2

        @pl.when(r + 1 < rows)
        def _():
            for copy in row_loads(r + 1, (r + 1) % 2):
                copy.start()

        for t in range(rows):
            if ("row", t) in plan or ("row", t) in pool_plan:

                @pl.when(r == t)
                def _():
                    step("row", t)

        select = tap_select(seg_ref[r, :, half - edge : half + shard], edge, pooled_local)
        picked = dot(select, tok_ref[r, half - edge : half + shard])
        grad = dpool_own[r]
        terms, sums = [], []
        for t in range(KER):
            terms.append((grad * ker_ref[t : t + 1]).astype(BF))
            sums.append(jnp.sum(grad * picked[t * pooled_local : (t + 1) * pooled_local], axis=0, keepdims=True))
        ssum[0:KER] += jnp.concatenate(sums, axis=0)
        spread = dot(select, jnp.concatenate(terms, axis=0), 0, 0)
        rim_out[r] = spread[:edge].astype(BF)
        for copy in row_loads(r, slot):
            copy.wait()

        @pl.when(r >= 2)
        def _():
            out_store(r - 2, slot).wait()

        outb[slot] = ownb[slot] + spread[edge:]

        @pl.when(has_prev)
        def _():
            outb[slot, :half] += leftb[slot].astype(F32)

        @pl.when(has_next)
        def _():
            outb[slot, shard - half :] += rightb[slot].astype(F32)

        edgeb[r] = outb[slot, shard - edge :]
        out_store(r, slot).start()
        return carry

    lax.fori_loop(0, rows, pool_step, 0)

    @pl.when(has_prev)
    def _():
        rim.start()

    def small_copy(stage):
        return pltpu.make_async_remote_copy(
            src_ref=ssum, dst_ref=srecv.at[stage], send_sem=small_sem.at[stage, 0], recv_sem=small_sem.at[stage, 1],
            device_id={"seq": red.bit(bits - 1 - stage)[1]}, device_id_type=MESH,
        )

    def small_row(k):
        other = (sums.row + k) % row_count
        return pltpu.make_async_remote_copy(
            src_ref=ssum, dst_ref=zsum.at[row_count - k], send_sem=zsmall_sem.at[k, 0],
            recv_sem=zsmall_sem.at[row_count - k, 1], device_id={"row": other}, device_id_type=MESH,
        )

    def small_add(stage):
        small_copy(stage).wait()
        ssum[...] += srecv[stage]

    small_copy(0).start()
    step("end", 0)
    small_add(0)
    small_copy(1).start()

    @pl.when(has_next)
    def _():
        rim.wait_recv()
        edgeb[...] += rim_in[...].astype(F32)

    edge_store = pltpu.make_async_copy(edgeb, out_hbm.at[:, shard - edge :], own_sem.at[0, 0])
    edge_store.start()
    step("end", 1)
    small_add(1)
    small_copy(2).start()
    step("end", 2)
    step("end", 3)
    red.finish_plan(plan)
    small_add(2)
    for stage in range(3, bits):
        small_copy(stage).start()
        small_add(stage)
    for k in range(1, row_count):
        small_row(k).start()
    zsum[0] = ssum[...]
    for n in range(5):
        g = sums.row * 5 + n
        block, i = g // row_count, g % row_count
        place = block + 2 * ((block + 4) // 5) - 4 * (block // 3)
        win_ref[:, n * cols : (n + 1) * cols] = sums.arrived(n, 2 * place + i // blocks, i % blocks, part)
    for k in range(1, row_count):
        small_row(row_count - k).wait_recv()
    total = None
    for owner in range(row_count):
        term = zsum[(owner - sums.row + row_count) % row_count]
        total = term if total is None else total + term
    conv_ref[...] = total[:KER]
    gain_ref[...] = total[8:10]
    bias_ref[...] = total[10:12]
    for k in range(1, row_count):
        small_row(k).wait_send()
    sums.sent()
    edge_store.wait()
    for n in range(2):
        out_store(rows - 2 + n, n).wait()

    @pl.when(has_prev)
    def _():
        rim.wait_send()


def body(tokens, segment_ids, w_in, w_out, w_up, w_down, conv_kernel, norm_gain, norm_bias, cotangent):
    rows, shard, width = tokens.shape
    half = WIN // 2
    pooled_local = shard // STR
    near = shard + 2 * half
    count = rows * shard
    hidden = w_up.shape[1]
    seq_count = lax.axis_size("seq")
    row_count = lax.axis_size("row")
    seq_start = lax.axis_index("seq") * shard
    keys = near + pooled_local * seq_count

    own_seg = lax.dynamic_slice_in_dim(segment_ids, seq_start, shard, 1)
    padded_seg = jnp.pad(segment_ids, ((0, 0), (half, half)), constant_values=-1)
    window_seg = lax.dynamic_slice_in_dim(padded_seg, seq_start, near, 1)
    key_seg = jnp.concatenate([window_seg, segment_ids[:, ::STR]], axis=1)
    own_seg = own_seg[:, None]
    key_seg = key_seg[:, None]
    window_seg = window_seg[:, None]

    def struct(*dims, dtype=BF):
        return jax.ShapeDtypeStruct(dims, dtype)

    bits = seq_count.bit_length() - 1
    far = keys - near
    buffers = 2 if keys <= 2 * near else 1
    vmem = pl.BlockSpec(memory_space=pltpu.VMEM)
    hbm = pl.BlockSpec(memory_space=pl.ANY)
    dma = pltpu.SemaphoreType.DMA

    def scratch(*dims, dtype=BF):
        return pltpu.VMEM(dims, dtype)

    tok_ext, pooled_all, q, k_all, v_all, prob, attended = pl.pallas_call(
        functools.partial(front_kernel, seq_count, half, buffers),
        out_shape=(
            struct(rows, near, width), struct(rows, far, width), struct(rows, shard, width),
            struct(rows, keys, width), struct(rows, keys, width), struct(rows, PAIRS, keys, 2 * shard),
            struct(rows, shard, width),
        ),
        in_specs=[hbm] * 2 + [vmem] * 4,
        out_specs=(hbm,) * 7,
        scratch_shapes=[
            scratch(rows, near, width), scratch(rows, 16, width),
            scratch(*((2,) * bits + (rows, pooled_local, width))), scratch(*w_in.shape),
            scratch(rows, shard, width), scratch(rows, near, width), scratch(rows, near, width),
            scratch(buffers, far, width), scratch(buffers, far, width),
            scratch(buffers, PAIRS, keys, 2 * shard), scratch(buffers, shard, width),
            dma((2,)), dma((3, 2)), dma((2, bits, 4)), dma((3, rows)), dma((4, buffers)), dma, dma((seq_count,)),
        ],
        compiler_params=pltpu.CompilerParams(collective_id=2, has_side_effects=True, vmem_limit_bytes=60 * MB),
        name="front",
    )(tokens, w_in, window_seg, own_seg, key_seg, conv_kernel)

    part = width // seq_count
    up_units = hidden // width
    cols = width // row_count
    first_rows = rows // 2

    def halves(units, *tail):
        return [pltpu.VMEM((units,) + (2,) * (bits - i) + tail, BF) for i in range(bits + 1)]

    def mesh_params(collective_id):
        return pltpu.CompilerParams(
            collective_id=collective_id, has_side_effects=True, vmem_limit_bytes=60 * MB
        )

    def seq_sems(units):
        return [dma((units, bits)), dma((units, bits))]

    packing = packed_shape(part, cols)

    layer_out, upg, n1, g1, g1b, att_grad, dsum, norm_sums, down = pl.pallas_call(
        functools.partial(mlp_kernel, seq_count),
        out_shape=(
            struct(rows, shard, width), struct(rows, shard, hidden), struct(rows, shard, width),
            struct(rows, shard, width, dtype=F32), struct(rows, shard, width), struct(rows, shard, width),
            struct(16, count, dtype=F32), struct(8, width, dtype=F32), struct(up_units, part, width),
        ),
        in_specs=[hbm] * 6 + [vmem] * 2,
        out_specs=(hbm,) * 6 + (vmem,) * 3,
        scratch_shapes=halves(up_units, part, width)
        + [scratch(*w_out.shape), scratch(*w_up.shape), scratch(*w_down.shape)]
        + [scratch(rows, shard, width)] * 3 + [scratch(rows, shard, hidden)] * 2
        + [
            scratch(rows, shard, width), scratch(rows, shard, width, dtype=F32), scratch(rows, shard, width, dtype=F32),
            scratch(rows, shard, 1, dtype=F32), scratch(rows, shard, width), scratch(rows, shard, width),
        ]
        + seq_sems(up_units) + [dma((3,)), dma((3, rows // 2)), dma((6, rows // 2))],
        compiler_params=mesh_params(3),
        name="mlp",
    )(tokens, attended, cotangent, w_out, w_up, w_down, norm_gain, norm_bias)

    units = up_units + 1
    (
        w_out_grad, w_up_grad, w_down_grad, pool_own, dq, dk, dv, dpool, own_grad, left_grad, right_grad,
    ) = pl.pallas_call(
        functools.partial(mid_kernel, seq_count, row_count, half, buffers),
        out_shape=(
            struct(part, cols, dtype=F32), struct(part, up_units * cols, dtype=F32),
            struct(up_units * part, cols, dtype=F32), struct(first_rows, pooled_local, width, dtype=F32),
            struct(rows, shard, width), struct(rows, keys, width), struct(rows, keys, width),
            struct(rows, far, width), struct(rows, shard, width, dtype=F32),
            struct(rows, half, width), struct(rows, half, width),
        ),
        in_specs=[hbm] * 5 + [vmem] + [hbm] * 6 + [vmem],
        out_specs=(vmem,) * 4 + (hbm,) * 7,
        scratch_shapes=halves(units, part, width) + halves(1, first_rows, pooled_local, width)
        + [scratch(units + up_units, row_count, *packing), scratch(units + up_units, row_count, *packing)]
        + seq_sems(1)
        + [scratch(2, rows, shard, width)] + [scratch(rows, shard, width)] * 3 + [scratch(*w_in.shape)]
        + [
            scratch(buffers, shard, width), scratch(buffers, keys, width), scratch(buffers, keys, width),
            scratch(buffers, PAIRS, keys, 2 * shard), scratch(buffers, shard, width),
            scratch(buffers, shard, width, dtype=F32),
            scratch(buffers, shard, width), scratch(buffers, keys, width), scratch(buffers, keys, width),
            scratch(buffers, far, width), scratch(buffers, shard, width, dtype=F32),
            scratch(buffers, half, width), scratch(buffers, half, width),
        ]
        + seq_sems(units) + [dma((units + up_units, row_count)), dma((units + up_units, row_count))]
        + [dma((2,)), dma((4,)), dma((6, buffers)), dma((5, buffers)), dma((2, buffers)), dma((2, rows))],
        compiler_params=mesh_params(0),
        name="mid",
    )(n1, attended, g1b, upg, w_in, dsum, q, k_all, v_all, prob, att_grad, g1, down)

    w_in_grad, token_grad, conv_grad, gain_grad, bias_grad = pl.pallas_call(
        functools.partial(tail_kernel, seq_count, row_count, half),
        out_shape=(
            struct(part, 5 * cols, dtype=F32), struct(rows, shard, width, dtype=F32),
            struct(KER, width, dtype=F32), struct(2, width, dtype=F32), struct(2, width, dtype=F32),
        ),
        in_specs=[hbm] * 10 + [vmem] * 3,
        out_specs=(vmem, hbm) + (vmem,) * 3,
        scratch_shapes=halves(10, part, width // 2) + halves(1, rows - first_rows, pooled_local, width)
        + [scratch(10, row_count // 2, *packing), scratch(5, row_count, *packing)]
        + [
            scratch(2, rows, near, width), scratch(rows, near, width), scratch(rows, min(near, far), width),
            scratch(*((2, width // 2, width) if far > near else (8, 128)), dtype=F32),
            scratch(rows, pooled_local, width, dtype=F32),
            scratch(rows, 16, width), scratch(rows, 16, width),
            scratch(2, shard, width, dtype=F32), scratch(2, half, width), scratch(2, half, width),
            scratch(2, shard, width, dtype=F32), scratch(rows, 16, width, dtype=F32),
            scratch(16, width, dtype=F32), scratch(bits, 16, width, dtype=F32), scratch(row_count, 16, width, dtype=F32),
        ]
        + seq_sems(10) + [dma((10, row_count // 2)), dma((5, row_count))] + seq_sems(1)
        + [
            dma((2,)), dma((3,)), dma((seq_count,)), dma((2,)), dma((3, 2)), dma((2,)), dma((bits, 2)), dma((row_count, 2)),
        ],
        compiler_params=mesh_params(1),
        name="tail",
    )(
        tok_ext, pooled_all, dq, dk, dv, dpool, pool_own, own_grad, left_grad, right_grad,
        window_seg, conv_kernel, norm_sums,
    )
    return (
        layer_out, token_grad, w_in_grad, w_out_grad, w_up_grad, w_down_grad, conv_grad, gain_grad, bias_grad,
    )


def solution(mesh):
    placed = (
        P("row", "seq", None), P("row", None), P(), P(), P(), P(), P(), P(), P(), P("row", "seq", None),
    )
    return jax.shard_map(
        body,
        mesh=mesh,
        in_specs=placed,
        out_specs=(
            P("row", "seq", None), P("row", "seq", None), P("seq", "row"), P("seq", "row"),
            P("seq", "row"), P("seq", "row"), P(), P(), P(),
        ),
        check_vma=False,
    )
```

```python
import functools

import jax
import jax.numpy as jnp
from jax import lax
from jax.experimental import pallas as pl
from jax.experimental.pallas import tpu as pltpu
from jax.sharding import PartitionSpec as P

HEADS = 12
HEAD = 64
WIN = 128
KER = 5
STR = 4
PAIRS = HEADS // 2

EPSILON = 1e-05
ROOT_HALF = 0.7071067811865476
INV_ROOT_2PI = 0.3989422804014327
NEG_LARGE = -1e30
BF = jnp.bfloat16
F32 = jnp.float32
MB = 1 << 20
MESH = pl.DeviceIdType.MESH


def dot(a, b, ca=1, cb=0):
    return lax.dot_general(a, b, (((ca,), (cb,)), ((), ())), preferred_element_type=F32)


def tap_select(seg_row, half, pooled_local):
    width = seg_row.shape[1]
    shape = (KER * pooled_local, width)
    rows = lax.broadcasted_iota(jnp.int32, shape, 0)
    cols = lax.broadcasted_iota(jnp.int32, shape, 1)
    tap = rows // pooled_local
    centre = half + STR * (rows - tap * pooled_local)
    seg = jnp.broadcast_to(seg_row, shape)
    centre_seg = jnp.sum(jnp.where(cols == centre, seg, 0), axis=1, keepdims=True)
    hit = (cols == centre + tap - KER // 2) & (seg == centre_seg)
    return jnp.where(hit, 1.0, 0.0).astype(BF)


def front_kernel(
    seq_count, half, buffers,
    tok_hbm, w_hbm, wseg_ref, fseg_ref, ker_ref,
    ext_hbm, pool_hbm, q_hbm, k_hbm, v_hbm, p_hbm, att_hbm,
    tokx, rim_in, pool_ref, w_ref, qb, knb, vnb, kfb, vfb, pb, attb,
    load_sem, line_sem, gather_sem, near_sem, far_sem, ext_sem, pool_sem,
):
    bits = seq_count.bit_length() - 1
    rows, near, width = tokx.shape
    shard = near - 2 * half
    keys = k_hbm.shape[1]
    pooled_local = pool_ref.shape[bits + 1]
    seq = lax.axis_index("seq")
    has_prev = seq > 0
    has_next = seq < seq_count - 1
    edge = 16

    def flipped(dim):
        weight = 1 << (bits - 1 - dim)
        return seq + (1 - 2 * ((seq // weight) % 2)) * weight

    def line(n, src, dst, step):
        return pltpu.make_async_remote_copy(
            src_ref=src, dst_ref=dst, send_sem=line_sem.at[n, 0], recv_sem=line_sem.at[n, 1],
            device_id={"seq": seq + step}, device_id_type=MESH,
        )

    rim = line(0, tok_hbm.at[:, shard - edge :], rim_in, 1)
    to_next = line(1, tok_hbm.at[:, shard - half :], tokx.at[:, :half], 1)
    to_prev = line(2, tok_hbm.at[:, :half], tokx.at[:, half + shard :], -1)

    rest = list(range(bits - 1))
    cut = len(rest) // 2
    orders = (rest[::-1] + [bits - 1], rest[:cut][::-1] + rest[cut:][::-1] + [bits - 1])

    def gather(part, stage, group):
        order = orders[part]
        done = order[:stage]
        index = tuple(
            slice(None) if d in done else (seq // (1 << (bits - 1 - d))) % 2 for d in range(bits)
        )
        cols = slice(part * (width // 2), (part + 1) * (width // 2))
        some = slice(group * rows // 2, (group + 1) * rows // 2)
        block = pool_ref.at[index + (some, slice(None), cols)]
        return pltpu.make_async_remote_copy(
            src_ref=block, dst_ref=block, send_sem=gather_sem.at[part, stage, 2 * group],
            recv_sem=gather_sem.at[part, stage, 2 * group + 1],
            device_id={"seq": flipped(order[stage])}, device_id_type=MESH,
        )

    own = slice(half, half + shard)
    own_load = pltpu.make_async_copy(tok_hbm, tokx.at[:, own], load_sem.at[0])
    w_load = pltpu.make_async_copy(w_hbm, w_ref, load_sem.at[1])
    own_load.start()
    w_load.start()
    sem = pltpu.get_barrier_semaphore()
    peers = [flipped(d) for d in range(bits)] + [(seq + 1) % seq_count, (seq + seq_count - 1) % seq_count]
    for peer in peers:
        pl.semaphore_signal(sem, inc=1, device_id={"seq": peer}, device_id_type=MESH)
    pl.semaphore_wait(sem, len(peers))

    @pl.when(has_next)
    def _():
        rim.start()
        to_next.start()

    @pl.when(has_prev)
    def _():
        to_prev.start()

    @pl.when(jnp.logical_not(has_prev))
    def _():
        rim_in[...] = jnp.zeros_like(rim_in)
        tokx[:, :half] = jnp.zeros((rows, half, width), BF)

    @pl.when(jnp.logical_not(has_next))
    def _():
        tokx[:, half + shard :] = jnp.zeros((rows, half, width), BF)

    own_load.wait()

    @pl.when(has_prev)
    def _():
        rim.wait_recv()

    mine = tuple((seq // (1 << (bits - 1 - d))) % 2 for d in range(bits))

    def pool_step(r, carry):
        stretch = jnp.concatenate([rim_in[r], tokx[r, own]], axis=0)
        picked = dot(tap_select(wseg_ref[pl.ds(r, 1), half - edge : half + shard], edge, pooled_local), stretch)
        total = picked[:pooled_local] * ker_ref[0:1]
        for t in range(1, KER):
            total = total + picked[t * pooled_local : (t + 1) * pooled_local] * ker_ref[t : t + 1]
        pool_ref[mine + (r,)] = total.astype(BF)
        return carry

    def onward(group, stage):
        for part in range(2):
            if stage:
                gather(part, stage - 1, group).wait()
            if stage < bits:
                gather(part, stage, group).start()

    for group in range(2):
        lax.fori_loop(group * rows // 2, (group + 1) * rows // 2, pool_step, 0)
        onward(group, 0)
    w_load.wait()
    scale = HEAD ** (-0.5)

    def own_step(r, carry):
        x = tokx[pl.ds(2 * r, 2), own].reshape(2 * shard, width)
        qb[pl.ds(2 * r, 2)] = (dot(x, w_ref[:, :width]) * scale).astype(BF).reshape(2, shard, width)
        knb[pl.ds(2 * r, 2), own] = dot(x, w_ref[:, width : 2 * width]).astype(BF).reshape(2, shard, width)
        vnb[pl.ds(2 * r, 2), own] = dot(x, w_ref[:, 2 * width : 3 * width]).astype(BF).reshape(2, shard, width)
        return carry

    lax.fori_loop(0, rows // 2, own_step, 0)
    onward(0, 1)
    onward(1, 1)

    @pl.when(has_prev)
    def _():
        to_next.wait_recv()

    @pl.when(has_next)
    def _():
        to_prev.wait_recv()

    def halo_step(r, carry):
        x = tokx[pl.ds(2 * r, 2), :half].reshape(2 * half, width)
        y = tokx[pl.ds(2 * r, 2), half + shard :].reshape(2 * half, width)
        x = jnp.concatenate([x, y], axis=0)
        for ref, first in ((knb, width), (vnb, 2 * width)):
            both = dot(x, w_ref[:, first : first + width]).astype(BF)
            ref[pl.ds(2 * r, 2), :half] = both[: 2 * half].reshape(2, half, width)
            ref[pl.ds(2 * r, 2), half + shard :] = both[2 * half :].reshape(2, half, width)
        return carry

    lax.fori_loop(0, rows // 2, halo_step, 0)
    for stage in range(2, bits + 1):
        onward(0, stage)
    ext_store = pltpu.make_async_copy(tokx, ext_hbm, ext_sem)
    ext_store.start()

    def pool_store(block):
        index = tuple((block >> (bits - 1 - d)) & 1 for d in range(bits))
        dst = pool_hbm.at[:, block * pooled_local : (block + 1) * pooled_local]
        return pltpu.make_async_copy(pool_ref.at[index], dst, pool_sem.at[block])

    def near_stores(r):
        pairs = [(qb.at[r], q_hbm.at[r]), (knb.at[r], k_hbm.at[r, :near]), (vnb.at[r], v_hbm.at[r, :near])]
        return [pltpu.make_async_copy(src, dst, near_sem.at[n, r]) for n, (src, dst) in enumerate(pairs)]

    def far_stores(r, slot):
        pairs = [
            (kfb.at[slot], k_hbm.at[r, near:]), (vfb.at[slot], v_hbm.at[r, near:]),
            (pb.at[slot], p_hbm.at[r]), (attb.at[slot], att_hbm.at[r]),
        ]
        return [pltpu.make_async_copy(src, dst, far_sem.at[n, slot]) for n, (src, dst) in enumerate(pairs)]

    lane = lax.broadcasted_iota(jnp.int32, (shard, 2 * HEAD), 1)
    even = lane < HEAD

    def row_step(r, carry):
        slot = r % buffers

        @pl.when(r == 1)
        def _():
            for stage in range(2, bits):
                onward(1, stage)

        @pl.when(r == rows // 2)
        def _():
            onward(1, bits)
            for block in range(seq_count):
                pool_store(block).start()

        for copy in near_stores(r):
            copy.start()

        @pl.when(r >= buffers)
        def _():
            for copy in far_stores(r - buffers, slot):
                copy.wait()

        pooled = pool_ref[(slice(None),) * bits + (r,)].reshape(keys - near, width)
        kfb[slot] = dot(pooled, w_ref[:, 3 * width : 4 * width]).astype(BF)
        vfb[slot] = dot(pooled, w_ref[:, 4 * width :]).astype(BF)
        window = wseg_ref[pl.ds(r, 1), :]
        key_seg = jnp.concatenate([window, fseg_ref[pl.ds(r, 1), :]], axis=1)
        key_seg = jnp.transpose(jnp.broadcast_to(key_seg, (shard, keys)))
        shape = (keys, shard)
        row = lax.broadcasted_iota(jnp.int32, shape, 0)
        col = lax.broadcasted_iota(jnp.int32, shape, 1)
        inside = (row >= near) | ((row >= col) & (row - col <= 2 * half))
        kept = inside & (key_seg == jnp.broadcast_to(window[:, half : half + shard], shape))
        bias = jnp.where(kept, 0.0, NEG_LARGE)
        bias = jnp.concatenate([bias, bias], axis=1)

        def lanes(j):
            return slice(2 * HEAD * j, 2 * HEAD * (j + 1))

        def scores(j):
            qp = qb[r, :, lanes(j)]
            zero = jnp.zeros_like(qp)
            stacked = jnp.concatenate([jnp.where(even, qp, zero), jnp.where(even, zero, qp)], axis=0)
            return (
                dot(knb[r, :, lanes(j)], stacked, 1, 1) + bias[:near],
                dot(kfb[slot, :, lanes(j)], stacked, 1, 1) + bias[near:],
            )

        def softmax(close, wide):
            top = jnp.maximum(jnp.max(close, axis=0, keepdims=True), jnp.max(wide, axis=0, keepdims=True))
            close = jnp.exp(close - top)
            wide = jnp.exp(wide - top)
            share = 1.0 / (jnp.sum(close, axis=0, keepdims=True) + jnp.sum(wide, axis=0, keepdims=True))
            return (close * share).astype(BF), (wide * share).astype(BF)

        def mix(j, close, wide):
            pb[slot, j, :near] = close
            pb[slot, j, near:] = wide
            mixed = dot(vnb[r, :, lanes(j)], close, 0, 0) + dot(vfb[slot, :, lanes(j)], wide, 0, 0)
            mixed = jnp.concatenate([mixed[:HEAD, :shard], mixed[HEAD:, shard:]], axis=0)
            attb[slot, :, lanes(j)] = jnp.transpose(mixed).astype(BF)

        current, ready = scores(0), None
        for j in range(PAIRS):
            after = scores(j + 1) if j + 1 < PAIRS else None
            if ready is not None:
                mix(j - 1, *ready)
            ready, current = softmax(*current), after
        mix(PAIRS - 1, *ready)
        for copy in far_stores(r, slot):
            copy.start()
        return carry

    lax.fori_loop(0, rows, row_step, 0)
    for n in range(buffers):
        r = rows - buffers + n
        for copy in far_stores(r, r % buffers):
            copy.wait()
    for r in range(rows):
        for copy in near_stores(r):
            copy.wait()
    for block in range(seq_count):
        pool_store(block).wait()
    ext_store.wait()

    @pl.when(has_next)
    def _():
        rim.wait_send()
        to_next.wait_send()

    @pl.when(has_prev)
    def _():
        to_prev.wait_send()


def stage_orders(bits):
    rest = list(range(bits - 1))
    cut = len(rest) // 2
    return (
        [bits - 1] + rest[::-1],
        [bits - 1] + rest[:cut][::-1] + rest[cut:][::-1],
    )


def packed_shape(part, cols):
    return (part + part // 2, 128) if cols == 192 and part % 32 == 0 else (part, cols)


def packed(x):
    part, cols = x.shape
    if packed_shape(part, cols) == x.shape:
        return x
    rest = jnp.concatenate([x[: part // 2, 128:], x[part // 2 :, 128:]], axis=1)
    return jnp.concatenate([x[:, :128], rest], axis=0)


def unpacked(x, part, cols):
    if x.shape == (part, cols):
        return x
    rest = jnp.concatenate([x[part:, :64], x[part:, 64:]], axis=0)
    return jnp.concatenate([x[:part], rest], axis=1)


class RowSum:
    def __init__(self, row_count, units, blocks, cols, dest, zsend, zrecv, send_sem, recv_sem):
        self.row = lax.axis_index("row")
        self.row_count, self.units, self.blocks, self.cols, self.dest = row_count, units, blocks, cols, dest
        self.zsend, self.zrecv, self.send_sem, self.recv_sem = zsend, zrecv, send_sem, recv_sem

    def copy(self, unit, i, target, slot):
        return pltpu.make_async_remote_copy(
            src_ref=self.zsend.at[unit, i],
            dst_ref=self.zrecv.at[slot, self.row],
            send_sem=self.send_sem.at[unit, i],
            recv_sem=self.recv_sem.at[slot, self.row],
            device_id={"row": target},
            device_id_type=MESH,
        )

    def send(self, unit, total):
        for i in range(self.blocks):
            self.zsend[unit, i] = packed(total[:, i * self.cols : (i + 1) * self.cols].astype(BF))
        for i in range(self.blocks):
            target, slot = self.dest(unit, i)

            @pl.when(self.row != target)
            def _():
                self.copy(unit, i, target, slot).start()

    def arrived(self, slot, unit, i, part):
        total = self.zsend[unit, i].astype(F32)
        for k in range(1, self.row_count):
            other = (self.row + k) % self.row_count
            pltpu.make_async_remote_copy(
                src_ref=self.zsend.at[0, 0],
                dst_ref=self.zrecv.at[slot, other],
                send_sem=self.send_sem.at[0, 0],
                recv_sem=self.recv_sem.at[slot, other],
                device_id={"row": other},
                device_id_type=MESH,
            ).wait_recv()
            total = total + self.zrecv[slot, other].astype(F32)
        return unpacked(total, part, self.cols)

    def sent(self):
        for unit in range(self.units):
            for i in range(self.blocks):
                target, slot = self.dest(unit, i)

                @pl.when(self.row != target)
                def _():
                    self.copy(unit, i, target, slot).wait_send()


class Reducer:
    def __init__(self, seq_count, units, held, bufs, send_sem, recv_sem, take, flip=0):
        self.take = take
        self.flip = flip
        self.bits = seq_count.bit_length() - 1
        self.units = units
        self.held, self.bufs = held, bufs
        self.send_sem, self.recv_sem = send_sem, recv_sem
        self.seq = lax.axis_index("seq")
        self.orders = stage_orders(self.bits)

    def bit(self, dim):
        weight = 1 << (self.bits - 1 - dim)
        value = (self.seq // weight) % 2
        return value, self.seq + (1 - 2 * value) * weight

    def barrier(self, line=False, row_count=1):
        sem = pltpu.get_barrier_semaphore()
        count = 1 << self.bits
        row = lax.axis_index("row")
        peers = [{"seq": self.bit(dim)[1]} for dim in range(self.bits)]
        peers += [{"row": (row + k) % row_count} for k in range(1, row_count)]
        if line:
            peers += [{"seq": (self.seq + 1) % count}, {"seq": (self.seq + count - 1) % count}]
        for peer in peers:
            pl.semaphore_signal(sem, inc=1, device_id=peer, device_id_type=MESH)
        pl.semaphore_wait(sem, len(peers))

    def position(self, unit, stage):
        order = self.orders[(unit + self.flip) % 2]
        left = sorted(order[stage:])
        return order[stage], left.index(order[stage])

    def source(self, unit, stage, value):
        pos = self.position(unit, stage)[1]
        base, slot = (self.held, unit % self.held.shape[0]) if stage == 0 else (self.bufs[stage - 1], unit)
        return base, (slot,) + (slice(None),) * pos + (value,)

    def copy(self, unit, stage):
        value, partner = self.bit(self.position(unit, stage)[0])
        base, index = self.source(unit, stage, 1 - value)
        return pltpu.make_async_remote_copy(
            src_ref=base.at[index],
            dst_ref=self.bufs[stage].at[unit],
            send_sem=self.send_sem.at[unit, stage],
            recv_sem=self.recv_sem.at[unit, stage],
            device_id={"seq": partner},
            device_id_type=MESH,
        )

    def start(self, unit):
        self.copy(unit, 0).start()

    def advance(self, unit, stage):
        self.copy(unit, stage - 1).wait()
        dim, pos = self.position(unit, stage - 1)
        value = self.bit(dim)[0]
        buf = self.bufs[stage - 1]
        base, _ = self.source(unit, stage - 1, value)
        slot = unit % self.held.shape[0] if stage == 1 else unit
        lead = self.bits - stage
        total = None
        for flat in range(1 << lead):
            index = tuple((flat >> (lead - 1 - d)) & 1 for d in range(lead))
            own = base[(slot,) + index[:pos] + (value,) + index[pos:]]
            if stage < self.bits:
                buf[(unit,) + index] = own + buf[(unit,) + index]
            else:
                total = own.astype(F32) + buf[(unit,) + index].astype(F32)
        if stage < self.bits:
            self.copy(unit, stage).start()
            return
        self.take(unit, total)

    def finish_plan(self, plan):
        if not plan:
            for stage in range(1, self.bits + 1):
                for unit in range(self.units):
                    self.advance(unit, stage)

    def follow(self, plan, *place):
        for unit, stage in plan.get(place, ()):
            self.advance(unit, stage)


def split_index(flat, bits):
    return tuple((flat >> (bits - 1 - d)) & 1 for d in range(bits))


def mlp_kernel(
    seq_count,
    tok_hbm, att_hbm, cot_hbm, wo_hbm, wu_hbm, wd_hbm, gain_ref, bias_ref,
    out_hbm, upg_hbm, n1_hbm, g1_hbm, g1b_hbm, da_hbm, dsum_ref, small_ref, down_ref,
    held, *rest,
):
    bits = seq_count.bit_length() - 1
    bufs = rest[:bits]
    (
        wo_ref, wu_ref, wd_ref, tokw, attw, cotw, actw, slopew, r2w, gradw, hatw, rstdw, outw, n1w,
        send_sem, recv_sem, w_sem, in_sem, out_sem,
    ) = rest[bits:]
    rows, shard, width = tokw.shape
    hidden = wu_ref.shape[1]
    units = hidden // width
    part = width // seq_count
    tall = width // 2
    chunk = 512
    block = 2 * shard
    blocks = rows // 2
    gain_a, gain_b = gain_ref[0:1], gain_ref[1:2]

    def take(unit, total):
        down_ref[unit] = total.astype(BF)

    red = Reducer(seq_count, units, held, bufs, send_sem, recv_sem, take)
    plan = {}
    if bits == 3 and units == 4 and blocks == 4:
        plan = {
            (0, 0): [(0, 1), (1, 1)], (1, 0): [(2, 1), (3, 1), (0, 2), (1, 2)],
            (3, 0): [(2, 2), (3, 2), (0, 3), (1, 3)], ("end",): [(2, 3), (3, 3)],
        }

    def mean(x):
        return jnp.mean(x, axis=-1, keepdims=True)

    chunks = hidden // chunk

    def up_load(c):
        cols = slice(c * chunk, (c + 1) * chunk)
        return pltpu.make_async_copy(wu_hbm.at[:, cols], wu_ref.at[:, cols], w_sem.at[1 + c])

    def down_load(c):
        part_rows = slice(c * chunk, (c + 1) * chunk)
        return pltpu.make_async_copy(wd_hbm.at[part_rows], wd_ref.at[part_rows], w_sem.at[1 + chunks + c])

    out_load = pltpu.make_async_copy(wo_hbm, wo_ref, w_sem.at[0])

    def loads(b):
        pairs = [(tok_hbm, tokw), (att_hbm, attw), (cot_hbm, cotw)]
        return [
            pltpu.make_async_copy(src.at[pl.ds(2 * b, 2)], dst.at[pl.ds(2 * b, 2)], in_sem.at[n, b])
            for n, (src, dst) in enumerate(pairs)
        ]

    def stores(b, first):
        pairs = [(outw, out_hbm), (n1w, n1_hbm), (actw, upg_hbm), (gradw, g1_hbm), (r2w, g1b_hbm), (tokw, da_hbm)]
        return [
            pltpu.make_async_copy(pairs[n][0].at[pl.ds(2 * b, 2)], pairs[n][1].at[pl.ds(2 * b, 2)], out_sem.at[n, b])
            for n in (range(2) if first else range(2, 6))
        ]

    out_load.start()
    for copy in loads(0):
        copy.start()
    for c in range(chunks):
        up_load(c).start()
        down_load(c).start()
    for b in range(1, blocks):
        for copy in loads(b):
            copy.start()
    red.barrier()
    small_ref[...] = jnp.zeros_like(small_ref)

    def flat(ref, b):
        return ref[pl.ds(2 * b, 2)].reshape(block, ref.shape[2])

    def put(ref, b, value):
        ref[pl.ds(2 * b, 2)] = value.reshape(2, shard, ref.shape[2])

    def forward_step(b, carry):
        for copy in loads(b):
            copy.wait()

        rows_b = pl.ds(2 * b, 2)
        resid = flat(tokw, b).astype(F32) + dot(flat(attw, b), wo_ref[...])
        centred = resid - mean(resid)
        rstd_a = lax.rsqrt(mean(centred * centred) + EPSILON)
        hat_a = centred * rstd_a
        put(hatw, b, hat_a)
        rstdw[rows_b] = rstd_a.reshape(2, shard, 1)
        normed = hat_a * gain_a + bias_ref[0:1]
        low = normed.astype(BF)
        put(n1w, b, low)
        total = normed

        def raised(c):
            return dot(low, wu_ref[:, c * chunk : (c + 1) * chunk])

        def lowered(c, act):
            return dot(act, wd_ref[c * chunk : (c + 1) * chunk, :])

        for c in range(chunks):
            up = raised(c)
            half_cdf = 0.5 * (1.0 + lax.erf(up * ROOT_HALF))
            ready = (up * half_cdf).astype(BF)
            cols = slice(c * chunk, (c + 1) * chunk)
            actw[rows_b, :, cols] = ready.reshape(2, shard, chunk)
            slope = half_cdf + up * (INV_ROOT_2PI * jnp.exp(-0.5 * up * up))
            slopew[rows_b, :, cols] = slope.astype(BF).reshape(2, shard, chunk)
            total = total + lowered(c, ready)
        centred = total - mean(total)
        rstd_b = lax.rsqrt(mean(centred * centred) + EPSILON)
        hat_b = centred * rstd_b
        put(outw, b, (hat_b * gain_b + bias_ref[1:2]).astype(BF))
        for copy in stores(b, True):
            copy.start()
        g = flat(cotw, b).astype(F32)
        small_ref[1:2] += jnp.sum(g * hat_b, axis=0, keepdims=True)
        small_ref[3:4] += jnp.sum(g, axis=0, keepdims=True)
        e = g * gain_b
        grad = rstd_b * (e - mean(e) - hat_b * mean(e * hat_b))
        put(gradw, b, grad)
        put(r2w, b, grad.astype(BF))
        return carry

    out_load.wait()
    for c in range(chunks):
        up_load(c).wait()
        down_load(c).wait()
    lax.fori_loop(0, blocks, forward_step, 0)

    for c in range(hidden // tall):
        left = actw[:, :, tall * c : tall * (c + 1)].reshape(-1, tall)
        total = dot(left, r2w[...].reshape(-1, width), 0, 0)
        blocked = total.reshape(tall // part, part, width).astype(BF)
        for n in range(tall // part):
            place = (c * tall + n * part) // part
            held[(place % units,) + split_index(place // units, bits)] = blocked[n]
    for u in range(units):
        red.start(u)

    def backward_step(b, carry):
        rows_b = pl.ds(2 * b, 2)

        def advance(half_step):
            for t in range(blocks):
                if (t, half_step) in plan:

                    @pl.when(b == t)
                    def _():
                        red.follow(plan, t, half_step)

        advance(0)
        grad = flat(gradw, b)
        grad_low = flat(r2w, b)

        def raised(c):
            return dot(grad_low, wd_ref[c * chunk : (c + 1) * chunk, :], 1, 1)

        def lowered(c, up_grad):
            return dot(up_grad, wu_ref[:, c * chunk : (c + 1) * chunk], 1, 1)

        current, ready = raised(0), None
        for c in range(chunks):
            after = raised(c + 1) if c + 1 < chunks else None
            if ready is not None:
                grad = grad + lowered(c - 1, ready)
            cols = slice(c * chunk, (c + 1) * chunk)
            slope = slopew[rows_b, :, cols].reshape(block, chunk).astype(F32)
            ready = (current * slope).astype(BF)
            actw[rows_b, :, cols] = ready.reshape(2, shard, chunk)
            current = after
        grad = grad + lowered(chunks - 1, ready)
        hat_a = flat(hatw, b)
        small_ref[0:1] += jnp.sum(grad * hat_a, axis=0, keepdims=True)
        small_ref[2:3] += jnp.sum(grad, axis=0, keepdims=True)
        e = grad * gain_a
        resid_grad = rstdw[rows_b].reshape(block, 1) * (e - mean(e) - hat_a * mean(e * hat_a))
        put(gradw, b, resid_grad)
        resid_low = resid_grad.astype(BF)
        put(r2w, b, resid_low)
        att_grad = dot(resid_low, wo_ref[...], 1, 1).astype(BF)
        put(tokw, b, att_grad)
        for copy in stores(b, False):
            copy.start()
        prod = att_grad.astype(F32) * flat(attw, b).astype(F32)
        high = prod.astype(BF)
        rest = (prod - high.astype(F32)).astype(BF)
        heads = dsum_ref.shape[0]
        head_row = lax.broadcasted_iota(jnp.int32, (heads, width), 0)
        head_col = lax.broadcasted_iota(jnp.int32, (heads, width), 1) // HEAD
        pick = jnp.where(head_row == head_col, 1.0, 0.0).astype(BF)
        dsum_ref[:, pl.ds(pl.multiple_of(b * block, block), block)] = dot(pick, high, 1, 1) + dot(pick, rest, 1, 1)
        return carry

    lax.fori_loop(0, blocks, backward_step, 0)
    red.finish_plan(plan)
    red.follow(plan, "end")
    for b in range(blocks):
        for copy in stores(b, True) + stores(b, False):
            copy.wait()


def mid_kernel(
    seq_count, row_count, half, buffers,
    n1_hbm, att_hbm, g1b_hbm, upg_hbm, w_hbm, dsum_ref,
    q_hbm, k_hbm, v_hbm, p_hbm, da_hbm, g1_hbm, down_ref,
    wout_ref, wup_ref, wdown_ref, pown_ref, dq_hbm, dk_hbm, dv_hbm, dpool_hbm, own_hbm, left_hbm, right_hbm,
    held, *rest,
):
    bits = seq_count.bit_length() - 1
    bufs, rest = rest[:bits], rest[bits:]
    pheld, pbufs, rest = rest[0], rest[1 : 1 + bits], rest[1 + bits :]
    (
        zsend, zrecv, psend_sem, precv_sem, slots, n1_ref, att_ref, g1b_ref, w_ref,
        qb, kb, vb, pb, dab, g1_buf, dqb, dkb, dvb, dpb, owb, lfb, rtb,
        send_sem, recv_sem, zsend_sem, zrecv_sem, load_sem, once_sem, in_sem, out_sem, line_send, line_recv,
    ) = rest
    rows, shard, width = n1_ref.shape
    near = shard + 2 * half
    part = width // seq_count
    up_units = upg_hbm.shape[2] // width
    units = up_units + 1
    tall = width // 2
    steps = up_units
    first_rows, pooled_local = pown_ref.shape[:2]

    def dest(unit, i):
        if unit < up_units:
            g = unit * row_count + i
            return g // up_units, g % up_units
        return i, unit

    cols = width // row_count
    down_units = down_ref.shape[0]
    sums = RowSum(row_count, units + down_units, row_count, cols, dest, zsend, zrecv, zsend_sem, zrecv_sem)
    red = Reducer(seq_count, units, held, bufs, send_sem, recv_sem, sums.send)

    def take(unit, total):
        pown_ref[...] = total

    pred = Reducer(seq_count, 1, pheld, pbufs, psend_sem, precv_sem, take)
    once = [
        pltpu.make_async_copy(src, dst, once_sem.at[n])
        for n, (src, dst) in enumerate([(n1_hbm, n1_ref), (att_hbm, att_ref), (g1b_hbm, g1b_ref), (w_hbm, w_ref)])
    ]

    def load(k):
        return pltpu.make_async_copy(
            upg_hbm.at[:, :, width * k : width * (k + 1)], slots.at[k % 2], load_sem.at[k % 2]
        )

    def taken(k):
        load(k).wait()
        if k + 1 < steps:
            load(k + 1).start()

    def row_loads(r, slot):
        pairs = [(q_hbm, qb), (k_hbm, kb), (v_hbm, vb), (p_hbm, pb), (da_hbm, dab), (g1_hbm, g1_buf)]
        return [
            pltpu.make_async_copy(src.at[r], dst.at[slot], in_sem.at[n, slot])
            for n, (src, dst) in enumerate(pairs)
        ]

    def row_stores(r, slot):
        pairs = [(dqb, dq_hbm), (dkb, dk_hbm), (dvb, dv_hbm), (dpb, dpool_hbm), (owb, own_hbm)]
        return [
            pltpu.make_async_copy(src.at[slot], dst.at[r], out_sem.at[n, slot])
            for n, (src, dst) in enumerate(pairs)
        ]

    has_prev = red.seq > 0
    has_next = red.seq < seq_count - 1

    def line(n, r, slot):
        src, dst = ((lfb, right_hbm), (rtb, left_hbm))[n]
        return pltpu.make_async_remote_copy(
            src_ref=src.at[slot], dst_ref=dst.at[r], send_sem=line_send.at[n, slot], recv_sem=line_recv.at[n, r],
            device_id={"seq": red.seq + 2 * n - 1}, device_id_type=MESH,
        )

    sides = ((0, has_prev, has_next), (1, has_next, has_prev))

    once[0].start()
    load(0).start()
    for copy in once[1:]:
        copy.start()
    if buffers > 1:
        for copy in row_loads(0, 0):
            copy.start()
    red.barrier(line=True, row_count=row_count)
    lead = (2,) * (bits - 1)
    plan, pool_plan = {}, {}
    if bits == 3 and up_units == 4 and rows == 8:
        plan = {
            ("up", 1): [(0, 1)], ("up", 2): [(1, 1)], ("up", 4): [(2, 1)],
            ("row", 0): [(3, 1)], ("row", 1): [(0, 2), (4, 1)], ("row", 2): [(1, 2)],
            ("row", 3): [(2, 2), (0, 3)], ("row", 4): [(3, 2), (1, 3)], ("row", 5): [(4, 2), (2, 3)],
            ("row", 6): [(3, 3)], ("row", 7): [(4, 3)],
        }
        pool_plan = {("row", 4): [(0, 1)], ("row", 6): [(0, 2)], ("row", 7): [(0, 3)]}

    def product(unit, left_ref, right):
        for m in range(2):
            left = left_ref[:, :, tall * m : tall * (m + 1)].reshape(-1, tall)
            held[unit, m] = dot(left, right, 0, 0).reshape(lead + (part, width)).astype(BF)

    once[0].wait()
    for u in range(up_units):
        taken(u)
        if u == 0:
            for n in range(down_units):
                sums.send(units + n, down_ref[n])
        product(u, n1_ref, slots[u % 2].reshape(-1, width))
        red.start(u)
        red.follow(plan, "up", u)
    once[1].wait()
    once[2].wait()
    product(up_units, att_ref, g1b_ref[...].reshape(-1, width))
    red.start(up_units)
    red.follow(plan, "up", up_units)
    once[3].wait()

    lane = lax.broadcasted_iota(jnp.int32, (shard, 2 * HEAD), 1)
    even = lane < HEAD

    def stack(pair):
        zero = jnp.zeros_like(pair)
        return jnp.concatenate([jnp.where(even, pair, zero), jnp.where(even, zero, pair)], axis=0)

    def hooks(r, place):
        for t in range(rows):
            begins = place == "row" and t == first_rows
            if (place, t) in plan or (place, t) in pool_plan or begins:

                @pl.when(r == t)
                def _():
                    if begins:
                        pred.start(0)
                    red.follow(plan, place, t)
                    pred.follow(pool_plan, place, t)

    def row_step(r, carry):
        slot = r % buffers
        if buffers > 1:

            @pl.when(r + 1 < rows)
            def _():
                for copy in row_loads(r + 1, (r + 1) % buffers):
                    copy.start()

        else:
            for copy in row_loads(r, slot):
                copy.start()
        hooks(r, "row")
        for copy in row_loads(r, slot):
            copy.wait()

        @pl.when(r >= buffers)
        def _():
            for copy in row_stores(r - buffers, slot):
                copy.wait()

        for n, sends, _ in sides:

            @pl.when((r >= buffers) & sends)
            def _():
                line(n, r - buffers, slot).wait_send()

        row_sums = dsum_ref[:, pl.ds(pl.multiple_of(r * shard, shard), shard)]

        def lanes(j):
            return slice(2 * HEAD * j, 2 * HEAD * (j + 1))

        def dprobs(j):
            return dot(vb[slot, :, lanes(j)], stack(dab[slot, :, lanes(j)]), 1, 1)

        def dscores(j, dprob):
            row_dot = jnp.concatenate([row_sums[2 * j : 2 * j + 1], row_sums[2 * j + 1 : 2 * j + 2]], axis=1)
            return (pb[slot, j].astype(F32) * (dprob - row_dot)).astype(BF)

        def products(j, dscore):
            dvb[slot, :, lanes(j)] = dot(pb[slot, j], stack(dab[slot, :, lanes(j)])).astype(BF)
            dkb[slot, :, lanes(j)] = dot(dscore, stack(qb[slot, :, lanes(j)])).astype(BF)
            mixed = dot(kb[slot, :, lanes(j)], dscore, 0, 0)
            mixed = jnp.concatenate([mixed[:HEAD, :shard], mixed[HEAD:, shard:]], axis=0)
            dqb[slot, :, lanes(j)] = (jnp.transpose(mixed) * HEAD ** (-0.5)).astype(BF)

        current, ready = dprobs(0), None
        for j in range(PAIRS):
            after = dprobs(j + 1) if j + 1 < PAIRS else None
            if ready is not None:
                products(j - 1, ready)
            ready, current = dscores(j, current), after
        products(PAIRS - 1, ready)
        back = dot(dkb[slot, :near], w_ref[:, width : 2 * width], 1, 1) + dot(
            dvb[slot, :near], w_ref[:, 2 * width : 3 * width], 1, 1
        )
        lfb[slot] = back[:half].astype(BF)
        rtb[slot] = back[half + shard :].astype(BF)
        owb[slot] = g1_buf[slot] + back[half : half + shard] + dot(dqb[slot], w_ref[:, :width], 1, 1)
        pooled = (
            dot(dkb[slot, near:], w_ref[:, 3 * width : 4 * width], 1, 1)
            + dot(dvb[slot, near:], w_ref[:, 4 * width :], 1, 1)
        ).astype(BF)
        dpb[slot] = pooled

        @pl.when(r < first_rows)
        def _():
            index = (0,) + (slice(None),) * bits + (r,)
            pheld[index] = pooled.reshape((2,) * bits + (pooled_local, width))

        for copy in row_stores(r, slot):
            copy.start()
        for n, sends, _ in sides:

            @pl.when(sends)
            def _():
                line(n, r, slot).start()

        return carry

    lax.fori_loop(0, rows, row_step, 0)
    red.finish_plan(plan)
    pred.finish_plan(pool_plan)
    pred.follow(pool_plan, "end")
    for k in range(buffers):
        r = rows - buffers + k
        for copy in row_stores(r, r % buffers):
            copy.wait()
    for n, sends, takes in sides:

        @pl.when(sends)
        def _():
            for k in range(buffers):
                r = rows - buffers + k
                line(n, r, r % buffers).wait_send()

        @pl.when(takes)
        def _():
            for r in range(rows):
                line(n, r, r % buffers).wait_recv()

    row = sums.row
    down = [sums.arrived(units + n, units + n, row, part) for n in range(down_units)]
    wdown_ref[...] = jnp.transpose(jnp.concatenate(down, axis=0))
    for n in range(up_units):
        g = row * up_units + n
        wup_ref[:, n * cols : (n + 1) * cols] = sums.arrived(n, g // row_count, g % row_count, part)
    wout_ref[...] = sums.arrived(up_units, up_units, row, part)
    sums.sent()


def tail_kernel(
    seq_count, row_count, half,
    tok_hbm, pool_hbm, dq_hbm, dk_hbm, dv_hbm, dpool_hbm, pown_hbm, own_hbm, left_hbm, right_hbm,
    seg_ref, ker_ref, norm_ref,
    win_ref, out_hbm, conv_ref, gain_ref, bias_ref,
    held, *rest,
):
    bits = seq_count.bit_length() - 1
    bufs, rest = rest[:bits], rest[bits:]
    pheld, pbufs, rest = rest[0], rest[1 : 1 + bits], rest[1 + bits :]
    (
        zsend, zrecv, slots, tok_ref, pool_ref, partial, dpool_own, rim_out, rim_in, ownb, leftb, rightb, outb, edgeb,
        ssum, srecv, zsum,
        send_sem, recv_sem, zsend_sem, zrecv_sem, psend_sem, precv_sem, load_sem, pool_sem, ploads_sem,
        line_sem, own_sem, out_sem, small_sem, zsmall_sem,
    ) = rest
    rows, near, width = tok_ref.shape
    shard = near - 2 * half
    part = width // seq_count
    units = 10
    tall = width // 2
    piece = pool_ref.shape[1]
    pieces = (dk_hbm.shape[1] - near) // piece
    pooled_local = dpool_own.shape[1]
    late_rows = rows - pown_hbm.shape[0]
    edge = 16
    order = (0, 3, 4, 1, 2)

    blocks = row_count // 2

    def dest(unit, i):
        g = order[unit // 2] * row_count + (unit % 2) * blocks + i
        return g // 5, g % 5

    cols = width // row_count
    sums = RowSum(row_count, units, blocks, cols, dest, zsend, zrecv, zsend_sem, zrecv_sem)
    red = Reducer(seq_count, units, held, bufs, send_sem, recv_sem, sums.send)

    def take(unit, total):
        dpool_own[rows - late_rows :] = total

    pred = Reducer(seq_count, 1, pheld, pbufs, psend_sem, precv_sem, take, 1)
    steps = 2 * pieces + 3

    def load(k):
        buf = slots.at[k % 2]
        if k == 0:
            src, dst = dq_hbm, buf.at[:, :shard]
        elif k <= 2 * pieces:
            first = near + ((k - 1) % pieces) * piece
            src, dst = (dk_hbm, dv_hbm)[(k - 1) // pieces].at[:, first : first + piece], buf.at[:, :piece]
        else:
            src, dst = (dk_hbm, dv_hbm)[k - 2 * pieces - 1].at[:, :near], buf
        return pltpu.make_async_copy(src, dst, load_sem.at[k % 2])

    def taken(k):
        load(k).wait()
        if k + 1 < steps:
            load(k + 1).start()

    def pool_load(n):
        return pltpu.make_async_copy(pool_hbm.at[:, n * piece : (n + 1) * piece], pool_ref, pool_sem.at[0])

    tok_load = pltpu.make_async_copy(tok_hbm, tok_ref, pool_sem.at[1])

    def grad_load(owner):
        src = dpool_hbm.at[rows - late_rows :, owner * pooled_local : (owner + 1) * pooled_local]
        return pltpu.make_async_copy(src, pheld.at[(0,) + split_index(owner, bits)], ploads_sem.at[owner])

    own_pool = pltpu.make_async_copy(pown_hbm, dpool_own.at[: rows - late_rows], pool_sem.at[2])

    rim = pltpu.make_async_remote_copy(
        src_ref=rim_out, dst_ref=rim_in, send_sem=line_sem.at[0], recv_sem=line_sem.at[1],
        device_id={"seq": red.seq - 1}, device_id_type=MESH,
    )
    has_prev = red.seq > 0
    has_next = red.seq < seq_count - 1

    for owner in range(seq_count):
        grad_load(owner).start()
    load(0).start()
    tok_load.start()
    pool_load(0).start()
    own_pool.start()
    red.barrier(line=True, row_count=row_count)
    for owner in range(seq_count):
        grad_load(owner).wait()
    pred.start(0)

    lead = (2,) * (bits - 1)

    def product(unit, left, right, first=True, last=True):
        for m in range(2):
            total = dot(left(m), right, 0, 0)
            if m == 0 and first:
                step("half", unit)
            if not first:
                total = total + partial[m]
            if not last:
                partial[m] = total
                continue
            total = total.reshape(lead + (part, width)).astype(BF)
            for h in range(2):
                held[2 * unit + h, m] = total[..., tall * h : tall * (h + 1)]

    def begin(unit):
        red.start(2 * unit)
        red.start(2 * unit + 1)

    def columns(ref, keep=slice(None)):
        return lambda m: ref[:, keep, tall * m : tall * (m + 1)].reshape(-1, tall)

    def whole(k, length):
        return slots[k % 2, :, :length].reshape(-1, width)

    plan, pool_plan = {}, {}
    if bits == 3 and rows == 8:
        plan = {
            ("half", 1): [(0, 1), (1, 1)], ("half", 2): [(2, 1), (3, 1)], ("half", 3): [(4, 1), (5, 1), (0, 2), (1, 2)],
            ("half", 4): [(6, 1), (7, 1), (2, 2), (3, 2)], ("row", 0): [(0, 3), (1, 3)],
            ("row", 1): [(8, 1), (9, 1)], ("row", 2): [(4, 2), (5, 2)], ("row", 3): [(2, 3), (3, 3)],
            ("row", 5): [(6, 2), (7, 2)], ("row", 7): [(4, 3), (5, 3)], ("end", 0): [(6, 3), (7, 3)],
            ("end", 1): [(8, 2), (9, 2)], ("end", 3): [(8, 3), (9, 3)],
        }
        pool_plan = {("done", 0): [(0, 1)], ("half", 3): [(0, 2)], ("row", 3): [(0, 3)]}

    def step(*place):
        red.follow(plan, *place)
        pred.follow(pool_plan, *place)

    own = slice(half, half + shard)
    tok_load.wait()
    taken(0)
    product(0, columns(tok_ref, own), whole(0, shard))
    begin(0)
    step("done", 0)
    for n in range(2):
        for c in range(pieces):
            k = 1 + n * pieces + c
            if pieces > 1 and (n or c):
                pool_load(c).start()
            if pieces > 1 or n == 0:
                pool_load(c).wait()
            taken(k)
            product(1 + n, columns(pool_ref), whole(k, piece), c == 0, c == pieces - 1)
        begin(1 + n)
    for n in range(2):
        k = 1 + 2 * pieces + n
        taken(k)
        product(3 + n, columns(tok_ref), whole(k, near))
        begin(3 + n)
    own_pool.wait()
    pred.finish_plan(pool_plan)

    ssum[...] = jnp.zeros_like(ssum)
    ssum[8:12] = norm_ref[0:4]

    def row_loads(r, slot):
        pairs = [(own_hbm, ownb), (left_hbm, leftb), (right_hbm, rightb)]
        return [
            pltpu.make_async_copy(src.at[r], dst.at[slot], own_sem.at[n, slot])
            for n, (src, dst) in enumerate(pairs)
        ]

    def out_store(r, slot):
        return pltpu.make_async_copy(
            outb.at[slot, : shard - edge], out_hbm.at[r, : shard - edge], out_sem.at[slot]
        )

    for copy in row_loads(0, 0):
        copy.start()

    def pool_step(r, carry):
        slot = r % 2

        @pl.when(r + 1 < rows)
        def _():
            for copy in row_loads(r + 1, (r + 1) % 2):
                copy.start()

        for t in range(rows):
            if ("row", t) in plan or ("row", t) in pool_plan:

                @pl.when(r == t)
                def _():
                    step("row", t)

        select = tap_select(seg_ref[pl.ds(r, 1), half - edge : half + shard], edge, pooled_local)
        picked = dot(select, tok_ref[r, half - edge : half + shard])
        grad = dpool_own[r]
        terms, sums = [], []
        for t in range(KER):
            terms.append((grad * ker_ref[t : t + 1]).astype(BF))
            sums.append(jnp.sum(grad * picked[t * pooled_local : (t + 1) * pooled_local], axis=0, keepdims=True))
        ssum[0:KER] += jnp.concatenate(sums, axis=0)
        spread = dot(select, jnp.concatenate(terms, axis=0), 0, 0)
        rim_out[r] = spread[:edge].astype(BF)
        for copy in row_loads(r, slot):
            copy.wait()

        @pl.when(r >= 2)
        def _():
            out_store(r - 2, slot).wait()

        outb[slot] = ownb[slot] + spread[edge:]

        @pl.when(has_prev)
        def _():
            outb[slot, :half] += leftb[slot].astype(F32)

        @pl.when(has_next)
        def _():
            outb[slot, shard - half :] += rightb[slot].astype(F32)

        edgeb[r] = outb[slot, shard - edge :]
        out_store(r, slot).start()
        return carry

    lax.fori_loop(0, rows, pool_step, 0)

    @pl.when(has_prev)
    def _():
        rim.start()

    def small_copy(stage):
        return pltpu.make_async_remote_copy(
            src_ref=ssum, dst_ref=srecv.at[stage], send_sem=small_sem.at[stage, 0], recv_sem=small_sem.at[stage, 1],
            device_id={"seq": red.bit(bits - 1 - stage)[1]}, device_id_type=MESH,
        )

    def small_row(k):
        other = (sums.row + k) % row_count
        return pltpu.make_async_remote_copy(
            src_ref=ssum, dst_ref=zsum.at[row_count - k], send_sem=zsmall_sem.at[k, 0],
            recv_sem=zsmall_sem.at[row_count - k, 1], device_id={"row": other}, device_id_type=MESH,
        )

    def small_add(stage):
        small_copy(stage).wait()
        ssum[...] += srecv[stage]

    small_copy(0).start()
    step("end", 0)
    small_add(0)
    small_copy(1).start()

    @pl.when(has_next)
    def _():
        rim.wait_recv()
        edgeb[...] += rim_in[...].astype(F32)

    edge_store = pltpu.make_async_copy(edgeb, out_hbm.at[:, shard - edge :], own_sem.at[0, 0])
    edge_store.start()
    step("end", 1)
    small_add(1)
    small_copy(2).start()
    step("end", 2)
    step("end", 3)
    red.finish_plan(plan)
    small_add(2)
    for stage in range(3, bits):
        small_copy(stage).start()
        small_add(stage)
    for k in range(1, row_count):
        small_row(k).start()
    zsum[0] = ssum[...]
    for n in range(5):
        g = sums.row * 5 + n
        block, i = g // row_count, g % row_count
        place = block + 2 * ((block + 4) // 5) - 4 * (block // 3)
        win_ref[:, n * cols : (n + 1) * cols] = sums.arrived(n, 2 * place + i // blocks, i % blocks, part)
    for k in range(1, row_count):
        small_row(row_count - k).wait_recv()
    total = None
    for owner in range(row_count):
        term = zsum[(owner - sums.row + row_count) % row_count]
        total = term if total is None else total + term
    conv_ref[...] = total[:KER]
    gain_ref[...] = total[8:10]
    bias_ref[...] = total[10:12]
    for k in range(1, row_count):
        small_row(k).wait_send()
    sums.sent()
    edge_store.wait()
    for n in range(2):
        out_store(rows - 2 + n, n).wait()

    @pl.when(has_prev)
    def _():
        rim.wait_send()


def finish_kernel(splits, *refs):
    count = len(splits)
    ins, outs, bufs = refs[:count], refs[count : 2 * count], refs[2 * count : 3 * count]
    sem_in, sem_out = refs[3 * count :]
    loads, stores = [], []
    for src, dst, buf, split in zip(ins, outs, bufs, splits):
        length = src.shape[0] // split
        for n in range(split):
            piece = slice(n * length, (n + 1) * length)
            loads.append(pltpu.make_async_copy(src.at[piece], buf.at[piece], sem_in.at[len(loads)]))
            stores.append(pltpu.make_async_copy(buf.at[piece], dst.at[piece], sem_out.at[len(stores)]))
    for copy in loads:
        copy.start()
    for load, store in zip(loads, stores):
        load.wait()
        store.start()
    for copy in stores:
        copy.wait()


def body(tokens, segment_ids, w_in, w_out, w_up, w_down, conv_kernel, norm_gain, norm_bias, cotangent):
    rows, shard, width = tokens.shape
    half = WIN // 2
    pooled_local = shard // STR
    near = shard + 2 * half
    count = rows * shard
    hidden = w_up.shape[1]
    seq_count = lax.axis_size("seq")
    row_count = lax.axis_size("row")
    seq_start = lax.axis_index("seq") * shard
    keys = near + pooled_local * seq_count

    padded_seg = jnp.pad(segment_ids, ((0, 0), (half, half)), constant_values=-1)
    window_seg = lax.dynamic_slice_in_dim(padded_seg, seq_start, near, 1)
    far_seg = segment_ids[:, ::STR]

    def struct(*dims, dtype=BF):
        return jax.ShapeDtypeStruct(dims, dtype)

    bits = seq_count.bit_length() - 1
    far = keys - near
    buffers = 2 if keys <= 2 * near else 1
    vmem = pl.BlockSpec(memory_space=pltpu.VMEM)
    hbm = pl.BlockSpec(memory_space=pl.ANY)
    dma = pltpu.SemaphoreType.DMA

    def scratch(*dims, dtype=BF):
        return pltpu.VMEM(dims, dtype)

    tok_ext, pooled_all, q, k_all, v_all, prob, attended = pl.pallas_call(
        functools.partial(front_kernel, seq_count, half, buffers),
        out_shape=(
            struct(rows, near, width), struct(rows, far, width), struct(rows, shard, width),
            struct(rows, keys, width), struct(rows, keys, width), struct(rows, PAIRS, keys, 2 * shard),
            struct(rows, shard, width),
        ),
        in_specs=[hbm] * 2 + [vmem] * 3,
        out_specs=(hbm,) * 7,
        scratch_shapes=[
            scratch(rows, near, width), scratch(rows, 16, width),
            scratch(*((2,) * bits + (rows, pooled_local, width))), scratch(*w_in.shape),
            scratch(rows, shard, width), scratch(rows, near, width), scratch(rows, near, width),
            scratch(buffers, far, width), scratch(buffers, far, width),
            scratch(buffers, PAIRS, keys, 2 * shard), scratch(buffers, shard, width),
            dma((2,)), dma((3, 2)), dma((2, bits, 4)), dma((3, rows)), dma((4, buffers)), dma, dma((seq_count,)),
        ],
        compiler_params=pltpu.CompilerParams(collective_id=2, has_side_effects=True, vmem_limit_bytes=60 * MB),
        name="front",
    )(tokens, w_in, window_seg, far_seg, conv_kernel)

    part = width // seq_count
    up_units = hidden // width
    cols = width // row_count
    first_rows = 3 * rows // 8

    def halves(units, *tail):
        return [pltpu.VMEM((units,) + (2,) * (bits - i) + tail, BF) for i in range(bits + 1)]

    def mesh_params(collective_id):
        return pltpu.CompilerParams(
            collective_id=collective_id, has_side_effects=True, vmem_limit_bytes=60 * MB
        )

    def seq_sems(units):
        return [dma((units, bits)), dma((units, bits))]

    packing = packed_shape(part, cols)

    layer_out, upg, n1, g1, g1b, att_grad, dsum, norm_sums, down = pl.pallas_call(
        functools.partial(mlp_kernel, seq_count),
        out_shape=(
            struct(rows, shard, width), struct(rows, shard, hidden), struct(rows, shard, width),
            struct(rows, shard, width, dtype=F32), struct(rows, shard, width), struct(rows, shard, width),
            struct(16, count, dtype=F32), struct(8, width, dtype=F32), struct(up_units, part, width),
        ),
        in_specs=[hbm] * 6 + [vmem] * 2,
        out_specs=(hbm,) * 6 + (vmem,) * 3,
        scratch_shapes=halves(up_units, part, width)
        + [scratch(*w_out.shape), scratch(*w_up.shape), scratch(*w_down.shape)]
        + [scratch(rows, shard, width)] * 3 + [scratch(rows, shard, hidden)] * 2
        + [
            scratch(rows, shard, width), scratch(rows, shard, width, dtype=F32), scratch(rows, shard, width, dtype=F32),
            scratch(rows, shard, 1, dtype=F32), scratch(rows, shard, width), scratch(rows, shard, width),
        ]
        + seq_sems(up_units) + [dma((1 + hidden // 256,)), dma((3, rows // 2)), dma((6, rows // 2))],
        compiler_params=mesh_params(3),
        name="mlp",
    )(tokens, attended, cotangent, w_out, w_up, w_down, norm_gain, norm_bias)

    units = up_units + 1
    (
        w_out_grad, w_up_grad, w_down_grad, pool_own, dq, dk, dv, dpool, own_grad, left_grad, right_grad,
    ) = pl.pallas_call(
        functools.partial(mid_kernel, seq_count, row_count, half, buffers),
        out_shape=(
            struct(part, cols, dtype=F32), struct(part, up_units * cols, dtype=F32),
            struct(cols, up_units * part, dtype=F32), struct(first_rows, pooled_local, width, dtype=F32),
            struct(rows, shard, width), struct(rows, keys, width), struct(rows, keys, width),
            struct(rows, far, width), struct(rows, shard, width, dtype=F32),
            struct(rows, half, width), struct(rows, half, width),
        ),
        in_specs=[hbm] * 5 + [vmem] + [hbm] * 6 + [vmem],
        out_specs=(vmem,) * 4 + (hbm,) * 7,
        scratch_shapes=halves(units, part, width) + halves(1, first_rows, pooled_local, width)
        + [scratch(units + up_units, row_count, *packing), scratch(units + up_units, row_count, *packing)]
        + seq_sems(1)
        + [scratch(2, rows, shard, width)] + [scratch(rows, shard, width)] * 3 + [scratch(*w_in.shape)]
        + [
            scratch(buffers, shard, width), scratch(buffers, keys, width), scratch(buffers, keys, width),
            scratch(buffers, PAIRS, keys, 2 * shard), scratch(buffers, shard, width),
            scratch(buffers, shard, width, dtype=F32),
            scratch(buffers, shard, width), scratch(buffers, keys, width), scratch(buffers, keys, width),
            scratch(buffers, far, width), scratch(buffers, shard, width, dtype=F32),
            scratch(buffers, half, width), scratch(buffers, half, width),
        ]
        + seq_sems(units) + [dma((units + up_units, row_count)), dma((units + up_units, row_count))]
        + [dma((2,)), dma((4,)), dma((6, buffers)), dma((5, buffers)), dma((2, buffers)), dma((2, rows))],
        compiler_params=mesh_params(0),
        name="mid",
    )(n1, attended, g1b, upg, w_in, dsum, q, k_all, v_all, prob, att_grad, g1, down)

    w_in_grad, token_grad, conv_grad, gain_grad, bias_grad = pl.pallas_call(
        functools.partial(tail_kernel, seq_count, row_count, half),
        out_shape=(
            struct(part, 5 * cols, dtype=F32), struct(rows, shard, width, dtype=F32),
            struct(KER, width, dtype=F32), struct(2, width, dtype=F32), struct(2, width, dtype=F32),
        ),
        in_specs=[hbm] * 10 + [vmem] * 3,
        out_specs=(vmem, hbm) + (vmem,) * 3,
        scratch_shapes=halves(10, part, width // 2) + halves(1, rows - first_rows, pooled_local, width)
        + [scratch(10, row_count // 2, *packing), scratch(5, row_count, *packing)]
        + [
            scratch(2, rows, near, width), scratch(rows, near, width), scratch(rows, min(near, far), width),
            scratch(*((2, width // 2, width) if far > near else (8, 128)), dtype=F32),
            scratch(rows, pooled_local, width, dtype=F32),
            scratch(rows, 16, width), scratch(rows, 16, width),
            scratch(2, shard, width, dtype=F32), scratch(2, half, width), scratch(2, half, width),
            scratch(2, shard, width, dtype=F32), scratch(rows, 16, width, dtype=F32),
            scratch(16, width, dtype=F32), scratch(bits, 16, width, dtype=F32), scratch(row_count, 16, width, dtype=F32),
        ]
        + seq_sems(10) + [dma((10, row_count // 2)), dma((5, row_count))] + seq_sems(1)
        + [
            dma((2,)), dma((3,)), dma((seq_count,)), dma((2,)), dma((3, 2)), dma((2,)), dma((bits, 2)), dma((row_count, 2)),
        ],
        compiler_params=mesh_params(1),
        name="tail",
    )(
        tok_ext, pooled_all, dq, dk, dv, dpool, pool_own, own_grad, left_grad, right_grad,
        window_seg, conv_kernel, norm_sums,
    )
    results = (
        layer_out, token_grad, w_in_grad, w_out_grad, w_up_grad, w_down_grad, conv_grad, gain_grad, bias_grad,
    )
    splits = tuple(4 if x.ndim == 3 else 1 for x in results)
    done = pl.pallas_call(
        functools.partial(finish_kernel, splits),
        out_shape=tuple(struct(*x.shape, dtype=x.dtype) for x in results),
        in_specs=[hbm] * 9,
        out_specs=(hbm,) * 9,
        scratch_shapes=[scratch(*x.shape, dtype=x.dtype) for x in results] + [dma((sum(splits),)), dma((sum(splits),))],
        compiler_params=pltpu.CompilerParams(vmem_limit_bytes=60 * MB),
        name="finish",
    )(*results)
    return done[:5] + (done[5].T,) + done[6:]


def solution(mesh):
    placed = (
        P("row", "seq", None), P("row", None), P(), P(), P(), P(), P(), P(), P(), P("row", "seq", None),
    )
    return jax.shard_map(
        body,
        mesh=mesh,
        in_specs=placed,
        out_specs=(
            P("row", "seq", None), P("row", "seq", None), P("seq", "row"), P("seq", "row"),
            P("seq", "row"), P("seq", "row"), P(), P(), P(),
        ),
        check_vma=False,
    )
```

```python
import functools

import jax
import jax.numpy as jnp
from jax import lax
from jax.experimental import pallas as pl
from jax.experimental.pallas import tpu as pltpu
from jax.sharding import PartitionSpec as P

HEADS = 12
HEAD = 64
WIN = 128
KER = 5
STR = 4
PAIRS = HEADS // 2

EPSILON = 1e-05
ROOT_HALF = 0.7071067811865476
INV_ROOT_2PI = 0.3989422804014327
NEG_LARGE = -1e30
BF = jnp.bfloat16
F32 = jnp.float32
MB = 1 << 20
MESH = pl.DeviceIdType.MESH


def dot(a, b, ca=1, cb=0):
    return lax.dot_general(a, b, (((ca,), (cb,)), ((), ())), preferred_element_type=F32)


def tap_select(seg_row, half, pooled_local):
    width = seg_row.shape[1]
    shape = (KER * pooled_local, width)
    rows = lax.broadcasted_iota(jnp.int32, shape, 0)
    cols = lax.broadcasted_iota(jnp.int32, shape, 1)
    tap = rows // pooled_local
    centre = half + STR * (rows - tap * pooled_local)
    seg = jnp.broadcast_to(seg_row, shape)
    centre_seg = jnp.sum(jnp.where(cols == centre, seg, 0), axis=1, keepdims=True)
    hit = (cols == centre + tap - KER // 2) & (seg == centre_seg)
    return jnp.where(hit, 1.0, 0.0).astype(BF)


def front_kernel(
    seq_count, half, buffers,
    tok_hbm, w_hbm, wseg_ref, fseg_ref, ker_ref,
    ext_hbm, pool_hbm, q_hbm, k_hbm, v_hbm, p_hbm, att_hbm,
    tokx, rim_in, pool_ref, w_ref, qb, knb, vnb, kfb, vfb, pb, attb,
    load_sem, line_sem, gather_sem, near_sem, far_sem, ext_sem, pool_sem,
):
    bits = seq_count.bit_length() - 1
    rows, near, width = tokx.shape
    shard = near - 2 * half
    keys = k_hbm.shape[1]
    pooled_local = pool_ref.shape[bits + 1]
    seq = lax.axis_index("seq")
    has_prev = seq > 0
    has_next = seq < seq_count - 1
    edge = 16

    def flipped(dim):
        weight = 1 << (bits - 1 - dim)
        return seq + (1 - 2 * ((seq // weight) % 2)) * weight

    def line(n, src, dst, step):
        return pltpu.make_async_remote_copy(
            src_ref=src, dst_ref=dst, send_sem=line_sem.at[n, 0], recv_sem=line_sem.at[n, 1],
            device_id={"seq": seq + step}, device_id_type=MESH,
        )

    rim = line(0, tok_hbm.at[:, shard - edge :], rim_in, 1)
    to_next = line(1, tok_hbm.at[:, shard - half :], tokx.at[:, :half], 1)
    to_prev = line(2, tok_hbm.at[:, :half], tokx.at[:, half + shard :], -1)

    rest = list(range(bits - 1))
    cut = len(rest) // 2
    orders = (rest[::-1] + [bits - 1], rest[:cut][::-1] + rest[cut:][::-1] + [bits - 1])

    def gather(part, stage, group):
        order = orders[part]
        done = order[:stage]
        index = tuple(
            slice(None) if d in done else (seq // (1 << (bits - 1 - d))) % 2 for d in range(bits)
        )
        cols = slice(part * (width // 2), (part + 1) * (width // 2))
        some = slice(group * rows // 2, (group + 1) * rows // 2)
        block = pool_ref.at[index + (some, slice(None), cols)]
        return pltpu.make_async_remote_copy(
            src_ref=block, dst_ref=block, send_sem=gather_sem.at[part, stage, 2 * group],
            recv_sem=gather_sem.at[part, stage, 2 * group + 1],
            device_id={"seq": flipped(order[stage])}, device_id_type=MESH,
        )

    own = slice(half, half + shard)
    own_load = pltpu.make_async_copy(tok_hbm, tokx.at[:, own], load_sem.at[0])
    w_load = pltpu.make_async_copy(w_hbm, w_ref, load_sem.at[1])
    own_load.start()
    w_load.start()
    sem = pltpu.get_barrier_semaphore()
    peers = [flipped(d) for d in range(bits)] + [(seq + 1) % seq_count, (seq + seq_count - 1) % seq_count]
    for peer in peers:
        pl.semaphore_signal(sem, inc=1, device_id={"seq": peer}, device_id_type=MESH)
    pl.semaphore_wait(sem, len(peers))

    @pl.when(has_next)
    def _():
        rim.start()
        to_next.start()

    @pl.when(has_prev)
    def _():
        to_prev.start()

    @pl.when(jnp.logical_not(has_prev))
    def _():
        rim_in[...] = jnp.zeros_like(rim_in)
        tokx[:, :half] = jnp.zeros((rows, half, width), BF)

    @pl.when(jnp.logical_not(has_next))
    def _():
        tokx[:, half + shard :] = jnp.zeros((rows, half, width), BF)

    own_load.wait()

    @pl.when(has_prev)
    def _():
        rim.wait_recv()

    mine = tuple((seq // (1 << (bits - 1 - d))) % 2 for d in range(bits))

    def pool_step(r, carry):
        stretch = jnp.concatenate([rim_in[r], tokx[r, own]], axis=0)
        picked = dot(tap_select(wseg_ref[pl.ds(r, 1), half - edge : half + shard], edge, pooled_local), stretch)
        total = picked[:pooled_local] * ker_ref[0:1]
        for t in range(1, KER):
            total = total + picked[t * pooled_local : (t + 1) * pooled_local] * ker_ref[t : t + 1]
        pool_ref[mine + (r,)] = total.astype(BF)
        return carry

    def onward(group, stage):
        for part in range(2):
            if stage:
                gather(part, stage - 1, group).wait()
            if stage < bits:
                gather(part, stage, group).start()

    for group in range(2):
        lax.fori_loop(group * rows // 2, (group + 1) * rows // 2, pool_step, 0)
        onward(group, 0)
    w_load.wait()
    scale = HEAD ** (-0.5)

    def own_step(r, carry):
        x = tokx[pl.ds(2 * r, 2), own].reshape(2 * shard, width)
        qb[pl.ds(2 * r, 2)] = (dot(x, w_ref[:, :width]) * scale).astype(BF).reshape(2, shard, width)
        knb[pl.ds(2 * r, 2), own] = dot(x, w_ref[:, width : 2 * width]).astype(BF).reshape(2, shard, width)
        vnb[pl.ds(2 * r, 2), own] = dot(x, w_ref[:, 2 * width : 3 * width]).astype(BF).reshape(2, shard, width)
        return carry

    lax.fori_loop(0, rows // 2, own_step, 0)
    onward(0, 1)
    onward(1, 1)

    @pl.when(has_prev)
    def _():
        to_next.wait_recv()

    @pl.when(has_next)
    def _():
        to_prev.wait_recv()

    def halo_step(r, carry):
        x = tokx[pl.ds(2 * r, 2), :half].reshape(2 * half, width)
        y = tokx[pl.ds(2 * r, 2), half + shard :].reshape(2 * half, width)
        x = jnp.concatenate([x, y], axis=0)
        for ref, first in ((knb, width), (vnb, 2 * width)):
            both = dot(x, w_ref[:, first : first + width]).astype(BF)
            ref[pl.ds(2 * r, 2), :half] = both[: 2 * half].reshape(2, half, width)
            ref[pl.ds(2 * r, 2), half + shard :] = both[2 * half :].reshape(2, half, width)
        return carry

    lax.fori_loop(0, rows // 2, halo_step, 0)
    for stage in range(2, bits + 1):
        onward(0, stage)
    ext_store = pltpu.make_async_copy(tokx, ext_hbm, ext_sem)
    ext_store.start()

    def pool_store(block):
        index = tuple((block >> (bits - 1 - d)) & 1 for d in range(bits))
        dst = pool_hbm.at[:, block * pooled_local : (block + 1) * pooled_local]
        return pltpu.make_async_copy(pool_ref.at[index], dst, pool_sem.at[block])

    def near_stores(r):
        pairs = [(qb.at[r], q_hbm.at[r]), (knb.at[r], k_hbm.at[r, :near]), (vnb.at[r], v_hbm.at[r, :near])]
        return [pltpu.make_async_copy(src, dst, near_sem.at[n, r]) for n, (src, dst) in enumerate(pairs)]

    def far_stores(r, slot):
        pairs = [
            (kfb.at[slot], k_hbm.at[r, near:]), (vfb.at[slot], v_hbm.at[r, near:]),
            (pb.at[slot], p_hbm.at[r]), (attb.at[slot], att_hbm.at[r]),
        ]
        return [pltpu.make_async_copy(src, dst, far_sem.at[n, slot]) for n, (src, dst) in enumerate(pairs)]

    lane = lax.broadcasted_iota(jnp.int32, (shard, 2 * HEAD), 1)
    even = lane < HEAD

    def row_step(r, carry):
        slot = r % buffers

        @pl.when(r == 1)
        def _():
            for stage in range(2, bits):
                onward(1, stage)

        @pl.when(r == rows // 2)
        def _():
            onward(1, bits)
            for block in range(seq_count):
                pool_store(block).start()

        for copy in near_stores(r):
            copy.start()

        @pl.when(r >= buffers)
        def _():
            for copy in far_stores(r - buffers, slot):
                copy.wait()

        pooled = pool_ref[(slice(None),) * bits + (r,)].reshape(keys - near, width)
        kfb[slot] = dot(pooled, w_ref[:, 3 * width : 4 * width]).astype(BF)
        vfb[slot] = dot(pooled, w_ref[:, 4 * width :]).astype(BF)
        window = wseg_ref[pl.ds(r, 1), :]
        key_seg = jnp.concatenate([window, fseg_ref[pl.ds(r, 1), :]], axis=1)
        key_seg = jnp.transpose(jnp.broadcast_to(key_seg, (shard, keys)))
        shape = (keys, shard)
        row = lax.broadcasted_iota(jnp.int32, shape, 0)
        col = lax.broadcasted_iota(jnp.int32, shape, 1)
        inside = (row >= near) | ((row >= col) & (row - col <= 2 * half))
        kept = inside & (key_seg == jnp.broadcast_to(window[:, half : half + shard], shape))
        bias = jnp.where(kept, 0.0, NEG_LARGE)
        bias = jnp.concatenate([bias, bias], axis=1)

        def lanes(j):
            return slice(2 * HEAD * j, 2 * HEAD * (j + 1))

        def scores(j):
            qp = qb[r, :, lanes(j)]
            zero = jnp.zeros_like(qp)
            stacked = jnp.concatenate([jnp.where(even, qp, zero), jnp.where(even, zero, qp)], axis=0)
            return (
                dot(knb[r, :, lanes(j)], stacked, 1, 1) + bias[:near],
                dot(kfb[slot, :, lanes(j)], stacked, 1, 1) + bias[near:],
            )

        def softmax(close, wide):
            top = jnp.maximum(jnp.max(close, axis=0, keepdims=True), jnp.max(wide, axis=0, keepdims=True))
            close = jnp.exp(close - top)
            wide = jnp.exp(wide - top)
            share = 1.0 / (jnp.sum(close, axis=0, keepdims=True) + jnp.sum(wide, axis=0, keepdims=True))
            return (close * share).astype(BF), (wide * share).astype(BF)

        def mix(j, close, wide):
            pb[slot, j, :near] = close
            pb[slot, j, near:] = wide
            mixed = dot(vnb[r, :, lanes(j)], close, 0, 0) + dot(vfb[slot, :, lanes(j)], wide, 0, 0)
            mixed = jnp.concatenate([mixed[:HEAD, :shard], mixed[HEAD:, shard:]], axis=0)
            attb[slot, :, lanes(j)] = jnp.transpose(mixed).astype(BF)

        current, ready = scores(0), None
        for j in range(PAIRS):
            after = scores(j + 1) if j + 1 < PAIRS else None
            if ready is not None:
                mix(j - 1, *ready)
            ready, current = softmax(*current), after
        mix(PAIRS - 1, *ready)
        for copy in far_stores(r, slot):
            copy.start()
        return carry

    lax.fori_loop(0, rows, row_step, 0)
    for n in range(buffers):
        r = rows - buffers + n
        for copy in far_stores(r, r % buffers):
            copy.wait()
    for r in range(rows):
        for copy in near_stores(r):
            copy.wait()
    for block in range(seq_count):
        pool_store(block).wait()
    ext_store.wait()

    @pl.when(has_next)
    def _():
        rim.wait_send()
        to_next.wait_send()

    @pl.when(has_prev)
    def _():
        to_prev.wait_send()


def stage_orders(bits):
    rest = list(range(bits - 1))
    cut = len(rest) // 2
    return (
        [bits - 1] + rest[::-1],
        [bits - 1] + rest[:cut][::-1] + rest[cut:][::-1],
    )


def packed_shape(part, cols):
    return (part + part // 2, 128) if cols == 192 and part % 32 == 0 else (part, cols)


def packed(x):
    part, cols = x.shape
    if packed_shape(part, cols) == x.shape:
        return x
    rest = jnp.concatenate([x[: part // 2, 128:], x[part // 2 :, 128:]], axis=1)
    return jnp.concatenate([x[:, :128], rest], axis=0)


def unpacked(x, part, cols):
    if x.shape == (part, cols):
        return x
    rest = jnp.concatenate([x[part:, :64], x[part:, 64:]], axis=0)
    return jnp.concatenate([x[:part], rest], axis=1)


class RowSum:
    def __init__(self, row_count, units, blocks, cols, dest, zsend, zrecv, send_sem, recv_sem):
        self.row = lax.axis_index("row")
        self.row_count, self.units, self.blocks, self.cols, self.dest = row_count, units, blocks, cols, dest
        self.zsend, self.zrecv, self.send_sem, self.recv_sem = zsend, zrecv, send_sem, recv_sem

    def copy(self, unit, i, target, slot):
        return pltpu.make_async_remote_copy(
            src_ref=self.zsend.at[unit, i],
            dst_ref=self.zrecv.at[slot, self.row],
            send_sem=self.send_sem.at[unit, i],
            recv_sem=self.recv_sem.at[slot, self.row],
            device_id={"row": target},
            device_id_type=MESH,
        )

    def send(self, unit, total):
        for i in range(self.blocks):
            self.zsend[unit, i] = packed(total[:, i * self.cols : (i + 1) * self.cols].astype(BF))
        for i in range(self.blocks):
            target, slot = self.dest(unit, i)

            @pl.when(self.row != target)
            def _():
                self.copy(unit, i, target, slot).start()

    def arrived(self, slot, unit, i, part):
        total = self.zsend[unit, i].astype(F32)
        for k in range(1, self.row_count):
            other = (self.row + k) % self.row_count
            pltpu.make_async_remote_copy(
                src_ref=self.zsend.at[0, 0],
                dst_ref=self.zrecv.at[slot, other],
                send_sem=self.send_sem.at[0, 0],
                recv_sem=self.recv_sem.at[slot, other],
                device_id={"row": other},
                device_id_type=MESH,
            ).wait_recv()
            total = total + self.zrecv[slot, other].astype(F32)
        return unpacked(total, part, self.cols)

    def sent(self):
        for unit in range(self.units):
            for i in range(self.blocks):
                target, slot = self.dest(unit, i)

                @pl.when(self.row != target)
                def _():
                    self.copy(unit, i, target, slot).wait_send()


class Reducer:
    def __init__(self, seq_count, units, held, bufs, send_sem, recv_sem, take, flip=0):
        self.take = take
        self.flip = flip
        self.bits = seq_count.bit_length() - 1
        self.units = units
        self.held, self.bufs = held, bufs
        self.send_sem, self.recv_sem = send_sem, recv_sem
        self.seq = lax.axis_index("seq")
        self.orders = stage_orders(self.bits)

    def bit(self, dim):
        weight = 1 << (self.bits - 1 - dim)
        value = (self.seq // weight) % 2
        return value, self.seq + (1 - 2 * value) * weight

    def barrier(self, line=False, row_count=1):
        sem = pltpu.get_barrier_semaphore()
        count = 1 << self.bits
        row = lax.axis_index("row")
        peers = [{"seq": self.bit(dim)[1]} for dim in range(self.bits)]
        peers += [{"row": (row + k) % row_count} for k in range(1, row_count)]
        if line:
            peers += [{"seq": (self.seq + 1) % count}, {"seq": (self.seq + count - 1) % count}]
        for peer in peers:
            pl.semaphore_signal(sem, inc=1, device_id=peer, device_id_type=MESH)
        pl.semaphore_wait(sem, len(peers))

    def position(self, unit, stage):
        order = self.orders[(unit + self.flip) % 2]
        left = sorted(order[stage:])
        return order[stage], left.index(order[stage])

    def source(self, unit, stage, value):
        pos = self.position(unit, stage)[1]
        base, slot = (self.held, unit % self.held.shape[0]) if stage == 0 else (self.bufs[stage - 1], unit)
        return base, (slot,) + (slice(None),) * pos + (value,)

    def copy(self, unit, stage):
        value, partner = self.bit(self.position(unit, stage)[0])
        base, index = self.source(unit, stage, 1 - value)
        return pltpu.make_async_remote_copy(
            src_ref=base.at[index],
            dst_ref=self.bufs[stage].at[unit],
            send_sem=self.send_sem.at[unit, stage],
            recv_sem=self.recv_sem.at[unit, stage],
            device_id={"seq": partner},
            device_id_type=MESH,
        )

    def start(self, unit):
        self.copy(unit, 0).start()

    def advance(self, unit, stage):
        self.copy(unit, stage - 1).wait()
        dim, pos = self.position(unit, stage - 1)
        value = self.bit(dim)[0]
        buf = self.bufs[stage - 1]
        base, _ = self.source(unit, stage - 1, value)
        slot = unit % self.held.shape[0] if stage == 1 else unit
        lead = self.bits - stage
        total = None
        for flat in range(1 << lead):
            index = tuple((flat >> (lead - 1 - d)) & 1 for d in range(lead))
            own = base[(slot,) + index[:pos] + (value,) + index[pos:]]
            if stage < self.bits:
                buf[(unit,) + index] = own + buf[(unit,) + index]
            else:
                total = own.astype(F32) + buf[(unit,) + index].astype(F32)
        if stage < self.bits:
            self.copy(unit, stage).start()
            return
        self.take(unit, total)

    def finish_plan(self, plan):
        if not plan:
            for stage in range(1, self.bits + 1):
                for unit in range(self.units):
                    self.advance(unit, stage)

    def follow(self, plan, *place):
        for unit, stage in plan.get(place, ()):
            self.advance(unit, stage)


def split_index(flat, bits):
    return tuple((flat >> (bits - 1 - d)) & 1 for d in range(bits))


def mlp_kernel(
    seq_count,
    tok_hbm, att_hbm, cot_hbm, wo_hbm, wu_hbm, wd_hbm, gain_ref, bias_ref,
    out_hbm, upg_hbm, n1_hbm, g1b_hbm, da_hbm, dsum_ref, small_ref, down_ref,
    held, *rest,
):
    bits = seq_count.bit_length() - 1
    bufs = rest[:bits]
    (
        wo_ref, wu_ref, wd_ref, tokw, attw, cotw, actw, slopew, r2w, gradw, hatw, rstdw, outw, n1w,
        send_sem, recv_sem, w_sem, in_sem, out_sem,
    ) = rest[bits:]
    rows, shard, width = tokw.shape
    hidden = wu_ref.shape[1]
    units = hidden // width
    part = width // seq_count
    tall = width // 2
    chunk = 512
    block = 2 * shard
    blocks = rows // 2
    gain_a, gain_b = gain_ref[0:1], gain_ref[1:2]

    def take(unit, total):
        down_ref[unit] = total.astype(BF)

    red = Reducer(seq_count, units, held, bufs, send_sem, recv_sem, take)
    plan = {}
    if bits == 3 and units == 4 and blocks == 4:
        plan = {
            (0, 0): [(0, 1), (1, 1)], (1, 0): [(2, 1), (3, 1), (0, 2), (1, 2)],
            (3, 0): [(2, 2), (3, 2), (0, 3), (1, 3)], ("end",): [(2, 3), (3, 3)],
        }

    def mean(x):
        return jnp.mean(x, axis=-1, keepdims=True)

    chunks = hidden // chunk

    def up_load(c):
        cols = slice(c * chunk, (c + 1) * chunk)
        return pltpu.make_async_copy(wu_hbm.at[:, cols], wu_ref.at[:, cols], w_sem.at[1 + c])

    def down_load(c):
        part_rows = slice(c * chunk, (c + 1) * chunk)
        return pltpu.make_async_copy(wd_hbm.at[part_rows], wd_ref.at[part_rows], w_sem.at[1 + chunks + c])

    out_load = pltpu.make_async_copy(wo_hbm, wo_ref, w_sem.at[0])

    def loads(b):
        pairs = [(tok_hbm, tokw), (att_hbm, attw), (cot_hbm, cotw)]
        return [
            pltpu.make_async_copy(src.at[pl.ds(2 * b, 2)], dst.at[pl.ds(2 * b, 2)], in_sem.at[n, b])
            for n, (src, dst) in enumerate(pairs)
        ]

    def stores(b, first):
        pairs = [(outw, out_hbm), (n1w, n1_hbm), (actw, upg_hbm), (r2w, g1b_hbm), (tokw, da_hbm)]
        return [
            pltpu.make_async_copy(pairs[n][0].at[pl.ds(2 * b, 2)], pairs[n][1].at[pl.ds(2 * b, 2)], out_sem.at[n, b])
            for n in (range(2) if first else range(2, 5))
        ]

    out_load.start()
    for copy in loads(0):
        copy.start()
    for c in range(chunks):
        up_load(c).start()
        down_load(c).start()
    for b in range(1, blocks):
        for copy in loads(b):
            copy.start()
    red.barrier()
    small_ref[...] = jnp.zeros_like(small_ref)

    def flat(ref, b):
        return ref[pl.ds(2 * b, 2)].reshape(block, ref.shape[2])

    def put(ref, b, value):
        ref[pl.ds(2 * b, 2)] = value.reshape(2, shard, ref.shape[2])

    def forward_step(b, carry):
        for copy in loads(b):
            copy.wait()

        rows_b = pl.ds(2 * b, 2)
        resid = flat(tokw, b).astype(F32) + dot(flat(attw, b), wo_ref[...])
        centred = resid - mean(resid)
        rstd_a = lax.rsqrt(mean(centred * centred) + EPSILON)
        hat_a = centred * rstd_a
        put(hatw, b, hat_a)
        rstdw[rows_b] = rstd_a.reshape(2, shard, 1)
        normed = hat_a * gain_a + bias_ref[0:1]
        low = normed.astype(BF)
        put(n1w, b, low)
        total = normed

        def raised(c):
            return dot(low, wu_ref[:, c * chunk : (c + 1) * chunk])

        def lowered(c, act):
            return dot(act, wd_ref[c * chunk : (c + 1) * chunk, :])

        for c in range(chunks):
            up = raised(c)
            half_cdf = 0.5 * (1.0 + lax.erf(up * ROOT_HALF))
            ready = (up * half_cdf).astype(BF)
            cols = slice(c * chunk, (c + 1) * chunk)
            actw[rows_b, :, cols] = ready.reshape(2, shard, chunk)
            slope = half_cdf + up * (INV_ROOT_2PI * jnp.exp(-0.5 * up * up))
            slopew[rows_b, :, cols] = slope.astype(BF).reshape(2, shard, chunk)
            total = total + lowered(c, ready)
        centred = total - mean(total)
        rstd_b = lax.rsqrt(mean(centred * centred) + EPSILON)
        hat_b = centred * rstd_b
        put(outw, b, (hat_b * gain_b + bias_ref[1:2]).astype(BF))
        for copy in stores(b, True):
            copy.start()
        g = flat(cotw, b).astype(F32)
        small_ref[1:2] += jnp.sum(g * hat_b, axis=0, keepdims=True)
        small_ref[3:4] += jnp.sum(g, axis=0, keepdims=True)
        e = g * gain_b
        grad = rstd_b * (e - mean(e) - hat_b * mean(e * hat_b))
        put(gradw, b, grad)
        put(r2w, b, grad.astype(BF))
        return carry

    out_load.wait()
    for c in range(chunks):
        up_load(c).wait()
        down_load(c).wait()
    lax.fori_loop(0, blocks, forward_step, 0)

    for c in range(hidden // tall):
        left = actw[:, :, tall * c : tall * (c + 1)].reshape(-1, tall)
        total = dot(left, r2w[...].reshape(-1, width), 0, 0)
        blocked = total.reshape(tall // part, part, width).astype(BF)
        for n in range(tall // part):
            place = (c * tall + n * part) // part
            held[(place % units,) + split_index(place // units, bits)] = blocked[n]
    for u in range(units):
        red.start(u)

    def backward_step(b, carry):
        rows_b = pl.ds(2 * b, 2)

        def advance(half_step):
            for t in range(blocks):
                if (t, half_step) in plan:

                    @pl.when(b == t)
                    def _():
                        red.follow(plan, t, half_step)

        advance(0)
        grad = flat(gradw, b)
        grad_low = flat(r2w, b)

        def raised(c):
            return dot(grad_low, wd_ref[c * chunk : (c + 1) * chunk, :], 1, 1)

        def lowered(c, up_grad):
            return dot(up_grad, wu_ref[:, c * chunk : (c + 1) * chunk], 1, 1)

        current, ready = raised(0), None
        for c in range(chunks):
            after = raised(c + 1) if c + 1 < chunks else None
            if ready is not None:
                grad = grad + lowered(c - 1, ready)
            cols = slice(c * chunk, (c + 1) * chunk)
            slope = slopew[rows_b, :, cols].reshape(block, chunk).astype(F32)
            ready = (current * slope).astype(BF)
            actw[rows_b, :, cols] = ready.reshape(2, shard, chunk)
            current = after
        grad = grad + lowered(chunks - 1, ready)
        hat_a = flat(hatw, b)
        small_ref[0:1] += jnp.sum(grad * hat_a, axis=0, keepdims=True)
        small_ref[2:3] += jnp.sum(grad, axis=0, keepdims=True)
        e = grad * gain_a
        resid_grad = rstdw[rows_b].reshape(block, 1) * (e - mean(e) - hat_a * mean(e * hat_a))
        resid_low = resid_grad.astype(BF)
        put(r2w, b, resid_low)
        att_grad = dot(resid_low, wo_ref[...], 1, 1).astype(BF)
        put(tokw, b, att_grad)
        for copy in stores(b, False):
            copy.start()
        prod = att_grad.astype(F32) * flat(attw, b).astype(F32)
        high = prod.astype(BF)
        rest = (prod - high.astype(F32)).astype(BF)
        heads = dsum_ref.shape[0]
        head_row = lax.broadcasted_iota(jnp.int32, (heads, width), 0)
        head_col = lax.broadcasted_iota(jnp.int32, (heads, width), 1) // HEAD
        pick = jnp.where(head_row == head_col, 1.0, 0.0).astype(BF)
        dsum_ref[:, pl.ds(pl.multiple_of(b * block, block), block)] = dot(pick, high, 1, 1) + dot(pick, rest, 1, 1)
        return carry

    lax.fori_loop(0, blocks, backward_step, 0)
    red.finish_plan(plan)
    red.follow(plan, "end")
    for b in range(blocks):
        for copy in stores(b, True) + stores(b, False):
            copy.wait()


def mid_kernel(
    seq_count, row_count, half, buffers,
    n1_hbm, att_hbm, g1b_hbm, upg_hbm, w_hbm, dsum_ref,
    q_hbm, k_hbm, v_hbm, p_hbm, da_hbm, down_ref,
    wout_ref, wup_ref, wdown_ref, pown_ref, dq_hbm, dk_hbm, dv_hbm, dpool_hbm, own_hbm, left_hbm, right_hbm,
    held, *rest,
):
    bits = seq_count.bit_length() - 1
    bufs, rest = rest[:bits], rest[bits:]
    pheld, pbufs, rest = rest[0], rest[1 : 1 + bits], rest[1 + bits :]
    (
        zsend, zrecv, psend_sem, precv_sem, slots, n1_ref, att_ref, g1b_ref, w_ref,
        qb, kb, vb, pb, dab, dqb, dkb, dvb, dpb, owb, lfb, rtb,
        send_sem, recv_sem, zsend_sem, zrecv_sem, load_sem, once_sem, in_sem, out_sem, line_send, line_recv,
    ) = rest
    rows, shard, width = n1_ref.shape
    near = shard + 2 * half
    part = width // seq_count
    up_units = upg_hbm.shape[2] // width
    units = up_units + 1
    tall = width // 2
    steps = up_units
    first_rows, pooled_local = pown_ref.shape[:2]

    def dest(unit, i):
        if unit < up_units:
            g = unit * row_count + i
            return g // up_units, g % up_units
        return i, unit

    cols = width // row_count
    down_units = down_ref.shape[0]
    sums = RowSum(row_count, units + down_units, row_count, cols, dest, zsend, zrecv, zsend_sem, zrecv_sem)
    red = Reducer(seq_count, units, held, bufs, send_sem, recv_sem, sums.send, 1)

    def take(unit, total):
        pown_ref[...] = total

    pred = Reducer(seq_count, 1, pheld, pbufs, psend_sem, precv_sem, take, 1)
    once = [
        pltpu.make_async_copy(src, dst, once_sem.at[n])
        for n, (src, dst) in enumerate([(n1_hbm, n1_ref), (att_hbm, att_ref), (g1b_hbm, g1b_ref), (w_hbm, w_ref)])
    ]

    def load(k):
        return pltpu.make_async_copy(
            upg_hbm.at[:, :, width * k : width * (k + 1)], slots.at[k % 2], load_sem.at[k % 2]
        )

    def taken(k):
        load(k).wait()
        if k + 1 < steps:
            load(k + 1).start()

    def row_loads(r, slot):
        pairs = [(p_hbm, pb), (k_hbm, kb), (v_hbm, vb), (q_hbm, qb), (da_hbm, dab)]
        return [
            pltpu.make_async_copy(src.at[r], dst.at[slot], in_sem.at[n, slot])
            for n, (src, dst) in enumerate(pairs)
        ]

    def row_stores(r, slot):
        pairs = [(dqb, dq_hbm), (dkb, dk_hbm), (dvb, dv_hbm), (owb, own_hbm)]
        return [
            pltpu.make_async_copy(src.at[slot], dst.at[r], out_sem.at[n, slot])
            for n, (src, dst) in enumerate(pairs)
        ]

    def pool_store(r, slot):
        return pltpu.make_async_copy(dpb.at[slot], dpool_hbm.at[r - first_rows], out_sem.at[4, slot])

    has_prev = red.seq > 0
    has_next = red.seq < seq_count - 1

    def line(n, r):
        src, dst = ((lfb, right_hbm), (rtb, left_hbm))[n]
        return pltpu.make_async_remote_copy(
            src_ref=src.at[r], dst_ref=dst.at[r], send_sem=line_send.at[n, r], recv_sem=line_recv.at[n, r],
            device_id={"seq": red.seq + 2 * n - 1}, device_id_type=MESH,
        )

    sides = ((0, has_prev, has_next), (1, has_next, has_prev))

    once[0].start()
    load(0).start()
    for copy in once[1:]:
        copy.start()
    if buffers > 1:
        for copy in row_loads(0, 0):
            copy.start()
    red.barrier(line=True, row_count=row_count)
    lead = (2,) * (bits - 1)
    plan, pool_plan = {}, {}
    if bits == 3 and up_units == 4 and rows == 8:
        plan = {
            ("up", 1): [(0, 1)], ("up", 2): [(1, 1)], ("up", 4): [(2, 1)],
            ("row", 0): [(3, 1)], ("row", 1): [(0, 2), (4, 1)], ("row", 2): [(1, 2)],
            ("row", 3): [(2, 2), (0, 3)], ("row", 4): [(3, 2), (1, 3)], ("row", 5): [(4, 2), (2, 3)],
            ("row", 6): [(3, 3)], ("row", 7): [(4, 3)],
        }
        pool_plan = {("row", 4): [(0, 1)], ("row", 6): [(0, 2)], ("row", 7): [(0, 3)]}

    def product(unit, left_ref, right):
        for m in range(2):
            left = left_ref[:, :, tall * m : tall * (m + 1)].reshape(-1, tall)
            held[unit, m] = dot(left, right, 0, 0).reshape(lead + (part, width)).astype(BF)

    once[0].wait()
    for u in range(up_units):
        taken(u)
        if u == 0:
            for n in range(down_units):
                sums.send(units + n, down_ref[n])
        product(u, n1_ref, slots[u % 2].reshape(-1, width))
        red.start(u)
        red.follow(plan, "up", u)
    once[1].wait()
    once[2].wait()
    product(up_units, att_ref, g1b_ref[...].reshape(-1, width))
    red.start(up_units)
    red.follow(plan, "up", up_units)
    once[3].wait()

    lane = lax.broadcasted_iota(jnp.int32, (shard, 2 * HEAD), 1)
    even = lane < HEAD

    def stack(pair):
        zero = jnp.zeros_like(pair)
        return jnp.concatenate([jnp.where(even, pair, zero), jnp.where(even, zero, pair)], axis=0)

    def hooks(r, place):
        for t in range(rows):
            begins = place == "row" and t == first_rows
            if (place, t) in plan or (place, t) in pool_plan or begins:

                @pl.when(r == t)
                def _():
                    if begins:
                        pred.start(0)
                    red.follow(plan, place, t)
                    pred.follow(pool_plan, place, t)

    def row_step(r, carry):
        slot = r % buffers
        if buffers > 1:

            @pl.when(r + 1 < rows)
            def _():
                for copy in row_loads(r + 1, (r + 1) % buffers):
                    copy.start()

        else:
            for copy in row_loads(r, slot):
                copy.start()
        hooks(r, "row")
        for copy in row_loads(r, slot):
            copy.wait()

        @pl.when(r >= buffers)
        def _():
            for copy in row_stores(r - buffers, slot):
                copy.wait()

        @pl.when(r >= buffers + first_rows)
        def _():
            pool_store(r - buffers, slot).wait()

        row_sums = dsum_ref[:, pl.ds(pl.multiple_of(r * shard, shard), shard)]

        def lanes(j):
            return slice(2 * HEAD * j, 2 * HEAD * (j + 1))

        def dprobs(j):
            return dot(vb[slot, :, lanes(j)], stack(dab[slot, :, lanes(j)]), 1, 1)

        def dscores(j, dprob):
            row_dot = jnp.concatenate([row_sums[2 * j : 2 * j + 1], row_sums[2 * j + 1 : 2 * j + 2]], axis=1)
            return (pb[slot, j].astype(F32) * (dprob - row_dot)).astype(BF)

        def products(j, dscore):
            dvb[slot, :, lanes(j)] = dot(pb[slot, j], stack(dab[slot, :, lanes(j)])).astype(BF)
            dkb[slot, :, lanes(j)] = dot(dscore, stack(qb[slot, :, lanes(j)])).astype(BF)
            mixed = dot(kb[slot, :, lanes(j)], dscore, 0, 0)
            mixed = jnp.concatenate([mixed[:HEAD, :shard], mixed[HEAD:, shard:]], axis=0)
            dqb[slot, :, lanes(j)] = (jnp.transpose(mixed) * HEAD ** (-0.5)).astype(BF)

        current, ready = dprobs(0), None
        for j in range(PAIRS):
            after = dprobs(j + 1) if j + 1 < PAIRS else None
            if ready is not None:
                products(j - 1, ready)
            ready, current = dscores(j, current), after
        products(PAIRS - 1, ready)
        back = dot(dkb[slot, :near], w_ref[:, width : 2 * width], 1, 1) + dot(
            dvb[slot, :near], w_ref[:, 2 * width : 3 * width], 1, 1
        )
        lfb[r] = back[:half].astype(BF)
        rtb[r] = back[half + shard :].astype(BF)
        own = g1b_ref[r].astype(F32) + back[half : half + shard] + dot(dqb[slot], w_ref[:, :width], 1, 1)
        owb[slot] = own.astype(BF)
        pooled = (
            dot(dkb[slot, near:], w_ref[:, 3 * width : 4 * width], 1, 1)
            + dot(dvb[slot, near:], w_ref[:, 4 * width :], 1, 1)
        ).astype(BF)
        dpb[slot] = pooled

        @pl.when(r < first_rows)
        def _():
            index = (0,) + (slice(None),) * bits + (r,)
            pheld[index] = pooled.reshape((2,) * bits + (pooled_local, width))

        @pl.when(r >= first_rows)
        def _():
            pool_store(r, slot).start()

        for copy in row_stores(r, slot):
            copy.start()
        for n, sends, _ in sides:

            @pl.when(sends)
            def _():
                line(n, r).start()

        return carry

    lax.fori_loop(0, rows, row_step, 0)
    red.finish_plan(plan)
    pred.finish_plan(pool_plan)
    pred.follow(pool_plan, "end")
    for k in range(buffers):
        r = rows - buffers + k
        for copy in row_stores(r, r % buffers):
            copy.wait()
        pool_store(r, r % buffers).wait()
    for n, sends, takes in sides:

        @pl.when(sends)
        def _():
            for r in range(rows):
                line(n, r).wait_send()

        @pl.when(takes)
        def _():
            for r in range(rows):
                line(n, r).wait_recv()

    row = sums.row
    down = [sums.arrived(units + n, units + n, row, part) for n in range(down_units)]
    wdown_ref[...] = jnp.transpose(jnp.concatenate(down, axis=0))
    for n in range(up_units):
        g = row * up_units + n
        wup_ref[:, n * cols : (n + 1) * cols] = sums.arrived(n, g // row_count, g % row_count, part)
    wout_ref[...] = sums.arrived(up_units, up_units, row, part)
    sums.sent()


def tail_kernel(
    seq_count, row_count, half,
    tok_hbm, pool_hbm, dq_hbm, dk_hbm, dv_hbm, dpool_hbm, pown_hbm, own_hbm, left_hbm, right_hbm,
    seg_ref, ker_ref, norm_ref,
    win_ref, out_hbm, conv_ref, gain_ref, bias_ref,
    held, *rest,
):
    bits = seq_count.bit_length() - 1
    bufs, rest = rest[:bits], rest[bits:]
    pheld, pbufs, rest = rest[0], rest[1 : 1 + bits], rest[1 + bits :]
    (
        zsend, zrecv, slots, tok_ref, pool_ref, partial, dpool_own, rim_out, rim_in, ownb, leftb, rightb, outb, edgeb,
        ssum, srecv, zsum,
        send_sem, recv_sem, zsend_sem, zrecv_sem, psend_sem, precv_sem, load_sem, pool_sem, ploads_sem,
        line_sem, own_sem, out_sem, small_sem, zsmall_sem,
    ) = rest
    rows, near, width = tok_ref.shape
    shard = near - 2 * half
    part = width // seq_count
    units = 10
    tall = width // 2
    piece = pool_ref.shape[1]
    pieces = (dk_hbm.shape[1] - near) // piece
    pooled_local = dpool_own.shape[1]
    late_rows = rows - pown_hbm.shape[0]
    edge = 16
    order = (0, 3, 4, 1, 2)

    blocks = row_count // 2

    def dest(unit, i):
        g = order[unit // 2] * row_count + (unit % 2) * blocks + i
        return g // 5, g % 5

    cols = width // row_count
    sums = RowSum(row_count, units, blocks, cols, dest, zsend, zrecv, zsend_sem, zrecv_sem)
    red = Reducer(seq_count, units, held, bufs, send_sem, recv_sem, sums.send)

    def take(unit, total):
        dpool_own[rows - late_rows :] = total

    pred = Reducer(seq_count, 1, pheld, pbufs, psend_sem, precv_sem, take, 1)
    steps = 2 * pieces + 3

    def load(k):
        buf = slots.at[k % 2]
        if k == 0:
            src, dst = dq_hbm, buf.at[:, :shard]
        elif k <= 2 * pieces:
            first = near + ((k - 1) % pieces) * piece
            src, dst = (dk_hbm, dv_hbm)[(k - 1) // pieces].at[:, first : first + piece], buf.at[:, :piece]
        else:
            src, dst = (dk_hbm, dv_hbm)[k - 2 * pieces - 1].at[:, :near], buf
        group = rows // 4
        return [
            pltpu.make_async_copy(
                src.at[n * group : (n + 1) * group], dst.at[n * group : (n + 1) * group], load_sem.at[k % 2, n]
            )
            for n in range(4)
        ]

    def taken(k):
        for copy in load(k):
            copy.wait()
        if k + 1 < steps:
            for copy in load(k + 1):
                copy.start()

    def pool_load(n):
        return pltpu.make_async_copy(pool_hbm.at[:, n * piece : (n + 1) * piece], pool_ref, pool_sem.at[0])

    tok_load = pltpu.make_async_copy(tok_hbm, tok_ref, pool_sem.at[1])

    def grad_load(owner):
        src = dpool_hbm.at[:, owner * pooled_local : (owner + 1) * pooled_local]
        return pltpu.make_async_copy(src, pheld.at[(0,) + split_index(owner, bits)], ploads_sem.at[owner])

    own_pool = pltpu.make_async_copy(pown_hbm, dpool_own.at[: rows - late_rows], pool_sem.at[2])

    rim = pltpu.make_async_remote_copy(
        src_ref=rim_out, dst_ref=rim_in, send_sem=line_sem.at[0], recv_sem=line_sem.at[1],
        device_id={"seq": red.seq - 1}, device_id_type=MESH,
    )
    has_prev = red.seq > 0
    has_next = red.seq < seq_count - 1

    for owner in range(seq_count):
        grad_load(owner).start()
    for copy in load(0):
        copy.start()
    tok_load.start()
    pool_load(0).start()
    own_pool.start()
    red.barrier(line=True, row_count=row_count)
    for owner in range(seq_count):
        grad_load(owner).wait()
    pred.start(0)

    lead = (2,) * (bits - 1)

    def product(unit, left, right, first=True, last=True):
        for m in range(2):
            total = dot(left(m), right, 0, 0)
            if m == 0 and first:
                step("half", unit)
            if not first:
                total = total + partial[m]
            if not last:
                partial[m] = total
                continue
            total = total.reshape(lead + (part, width)).astype(BF)
            for h in range(2):
                held[2 * unit + h, m] = total[..., tall * h : tall * (h + 1)]

    def begin(unit):
        red.start(2 * unit)
        red.start(2 * unit + 1)

    def columns(ref, keep=slice(None)):
        return lambda m: ref[:, keep, tall * m : tall * (m + 1)].reshape(-1, tall)

    def whole(k, length):
        return slots[k % 2, :, :length].reshape(-1, width)

    plan, pool_plan = {}, {}
    if bits == 3 and rows == 8:
        plan = {
            ("half", 1): [(0, 1), (1, 1)], ("half", 2): [(2, 1), (3, 1)], ("half", 3): [(4, 1), (5, 1), (0, 2), (1, 2)],
            ("half", 4): [(6, 1), (7, 1), (2, 2), (3, 2)], ("row", 0): [(0, 3), (1, 3)],
            ("row", 1): [(8, 1), (9, 1)], ("row", 2): [(4, 2), (5, 2)], ("row", 3): [(2, 3), (3, 3)],
            ("row", 5): [(6, 2), (7, 2)], ("row", 7): [(4, 3), (5, 3)], ("end", 0): [(6, 3), (7, 3)],
            ("end", 1): [(8, 2), (9, 2)], ("end", 3): [(8, 3), (9, 3)],
        }
        pool_plan = {("done", 0): [(0, 1)], ("half", 3): [(0, 2)], ("row", 3): [(0, 3)]}

    def step(*place):
        red.follow(plan, *place)
        pred.follow(pool_plan, *place)

    own = slice(half, half + shard)
    tok_load.wait()
    taken(0)
    product(0, columns(tok_ref, own), whole(0, shard))
    begin(0)
    step("done", 0)
    for n in range(2):
        for c in range(pieces):
            k = 1 + n * pieces + c
            if pieces > 1 and (n or c):
                pool_load(c).start()
            if pieces > 1 or n == 0:
                pool_load(c).wait()
            taken(k)
            product(1 + n, columns(pool_ref), whole(k, piece), c == 0, c == pieces - 1)
        begin(1 + n)
    for n in range(2):
        k = 1 + 2 * pieces + n
        taken(k)
        product(3 + n, columns(tok_ref), whole(k, near))
        begin(3 + n)
    own_pool.wait()
    pred.finish_plan(pool_plan)

    ssum[...] = jnp.zeros_like(ssum)
    ssum[8:12] = norm_ref[0:4]

    def row_loads(r, slot):
        pairs = [(own_hbm, ownb), (left_hbm, leftb), (right_hbm, rightb)]
        return [
            pltpu.make_async_copy(src.at[r], dst.at[slot], own_sem.at[n, slot])
            for n, (src, dst) in enumerate(pairs)
        ]

    def out_store(r, slot):
        return pltpu.make_async_copy(
            outb.at[slot, : shard - edge], out_hbm.at[r, : shard - edge], out_sem.at[slot]
        )

    for copy in row_loads(0, 0):
        copy.start()

    def pool_step(r, carry):
        slot = r % 2

        @pl.when(r + 1 < rows)
        def _():
            for copy in row_loads(r + 1, (r + 1) % 2):
                copy.start()

        for t in range(rows):
            if ("row", t) in plan or ("row", t) in pool_plan:

                @pl.when(r == t)
                def _():
                    step("row", t)

        select = tap_select(seg_ref[pl.ds(r, 1), half - edge : half + shard], edge, pooled_local)
        picked = dot(select, tok_ref[r, half - edge : half + shard])
        grad = dpool_own[r]
        terms, sums = [], []
        for t in range(KER):
            terms.append((grad * ker_ref[t : t + 1]).astype(BF))
            sums.append(jnp.sum(grad * picked[t * pooled_local : (t + 1) * pooled_local], axis=0, keepdims=True))
        ssum[0:KER] += jnp.concatenate(sums, axis=0)
        spread = dot(select, jnp.concatenate(terms, axis=0), 0, 0)
        rim_out[r] = spread[:edge].astype(BF)
        for copy in row_loads(r, slot):
            copy.wait()

        @pl.when(r >= 2)
        def _():
            out_store(r - 2, slot).wait()

        outb[slot] = ownb[slot].astype(F32) + spread[edge:]

        @pl.when(has_prev)
        def _():
            outb[slot, :half] += leftb[slot].astype(F32)

        @pl.when(has_next)
        def _():
            outb[slot, shard - half :] += rightb[slot].astype(F32)

        edgeb[r] = outb[slot, shard - edge :]
        out_store(r, slot).start()
        return carry

    lax.fori_loop(0, rows, pool_step, 0)

    @pl.when(has_prev)
    def _():
        rim.start()

    def small_copy(stage):
        return pltpu.make_async_remote_copy(
            src_ref=ssum, dst_ref=srecv.at[stage], send_sem=small_sem.at[stage, 0], recv_sem=small_sem.at[stage, 1],
            device_id={"seq": red.bit(bits - 1 - stage)[1]}, device_id_type=MESH,
        )

    def small_row(k):
        other = (sums.row + k) % row_count
        return pltpu.make_async_remote_copy(
            src_ref=ssum, dst_ref=zsum.at[row_count - k], send_sem=zsmall_sem.at[k, 0],
            recv_sem=zsmall_sem.at[row_count - k, 1], device_id={"row": other}, device_id_type=MESH,
        )

    def small_add(stage):
        small_copy(stage).wait()
        ssum[...] += srecv[stage]

    small_copy(0).start()
    step("end", 0)
    small_add(0)
    small_copy(1).start()

    @pl.when(has_next)
    def _():
        rim.wait_recv()
        edgeb[...] += rim_in[...].astype(F32)

    edge_store = pltpu.make_async_copy(edgeb, out_hbm.at[:, shard - edge :], own_sem.at[0, 0])
    edge_store.start()
    step("end", 1)
    small_add(1)
    small_copy(2).start()
    step("end", 2)
    step("end", 3)
    red.finish_plan(plan)
    small_add(2)
    for stage in range(3, bits):
        small_copy(stage).start()
        small_add(stage)
    for k in range(1, row_count):
        small_row(k).start()
    zsum[0] = ssum[...]
    for n in range(5):
        g = sums.row * 5 + n
        block, i = g // row_count, g % row_count
        place = block + 2 * ((block + 4) // 5) - 4 * (block // 3)
        win_ref[:, n * cols : (n + 1) * cols] = sums.arrived(n, 2 * place + i // blocks, i % blocks, part)
    for k in range(1, row_count):
        small_row(row_count - k).wait_recv()
    total = None
    for owner in range(row_count):
        term = zsum[(owner - sums.row + row_count) % row_count]
        total = term if total is None else total + term
    conv_ref[...] = total[:KER]
    gain_ref[...] = total[8:10]
    bias_ref[...] = total[10:12]
    for k in range(1, row_count):
        small_row(k).wait_send()
    sums.sent()
    edge_store.wait()
    for n in range(2):
        out_store(rows - 2 + n, n).wait()

    @pl.when(has_prev)
    def _():
        rim.wait_send()


def finish_kernel(splits, *refs):
    count = len(splits)
    ins, outs, bufs = refs[:count], refs[count : 2 * count], refs[2 * count : 3 * count]
    sem_in, sem_out = refs[3 * count :]
    loads, stores = [], []
    for src, dst, buf, split in zip(ins, outs, bufs, splits):
        length = src.shape[0] // split
        for n in range(split):
            piece = slice(n * length, (n + 1) * length)
            loads.append(pltpu.make_async_copy(src.at[piece], buf.at[piece], sem_in.at[len(loads)]))
            stores.append(pltpu.make_async_copy(buf.at[piece], dst.at[piece], sem_out.at[len(stores)]))
    for copy in loads:
        copy.start()
    for load, store in zip(loads, stores):
        load.wait()
        store.start()
    for copy in stores:
        copy.wait()


def body(tokens, segment_ids, w_in, w_out, w_up, w_down, conv_kernel, norm_gain, norm_bias, cotangent):
    rows, shard, width = tokens.shape
    half = WIN // 2
    pooled_local = shard // STR
    near = shard + 2 * half
    count = rows * shard
    hidden = w_up.shape[1]
    seq_count = lax.axis_size("seq")
    row_count = lax.axis_size("row")
    seq_start = lax.axis_index("seq") * shard
    keys = near + pooled_local * seq_count

    padded_seg = jnp.pad(segment_ids, ((0, 0), (half, half)), constant_values=-1)
    window_seg = lax.dynamic_slice_in_dim(padded_seg, seq_start, near, 1)
    far_seg = segment_ids[:, ::STR]

    def struct(*dims, dtype=BF):
        return jax.ShapeDtypeStruct(dims, dtype)

    bits = seq_count.bit_length() - 1
    far = keys - near
    buffers = 2 if keys <= 2 * near else 1
    vmem = pl.BlockSpec(memory_space=pltpu.VMEM)
    hbm = pl.BlockSpec(memory_space=pl.ANY)
    dma = pltpu.SemaphoreType.DMA

    def scratch(*dims, dtype=BF):
        return pltpu.VMEM(dims, dtype)

    tok_ext, pooled_all, q, k_all, v_all, prob, attended = pl.pallas_call(
        functools.partial(front_kernel, seq_count, half, buffers),
        out_shape=(
            struct(rows, near, width), struct(rows, far, width), struct(rows, shard, width),
            struct(rows, keys, width), struct(rows, keys, width), struct(rows, PAIRS, keys, 2 * shard),
            struct(rows, shard, width),
        ),
        in_specs=[hbm] * 2 + [vmem] * 3,
        out_specs=(hbm,) * 7,
        scratch_shapes=[
            scratch(rows, near, width), scratch(rows, 16, width),
            scratch(*((2,) * bits + (rows, pooled_local, width))), scratch(*w_in.shape),
            scratch(rows, shard, width), scratch(rows, near, width), scratch(rows, near, width),
            scratch(buffers, far, width), scratch(buffers, far, width),
            scratch(buffers, PAIRS, keys, 2 * shard), scratch(buffers, shard, width),
            dma((2,)), dma((3, 2)), dma((2, bits, 4)), dma((3, rows)), dma((4, buffers)), dma, dma((seq_count,)),
        ],
        compiler_params=pltpu.CompilerParams(collective_id=2, has_side_effects=True, vmem_limit_bytes=60 * MB),
        name="front",
    )(tokens, w_in, window_seg, far_seg, conv_kernel)

    part = width // seq_count
    up_units = hidden // width
    cols = width // row_count
    first_rows = 3 * rows // 8

    def halves(units, *tail):
        return [pltpu.VMEM((units,) + (2,) * (bits - i) + tail, BF) for i in range(bits + 1)]

    def mesh_params(collective_id):
        return pltpu.CompilerParams(
            collective_id=collective_id, has_side_effects=True, vmem_limit_bytes=60 * MB
        )

    def seq_sems(units):
        return [dma((units, bits)), dma((units, bits))]

    packing = packed_shape(part, cols)

    layer_out, upg, n1, g1b, att_grad, dsum, norm_sums, down = pl.pallas_call(
        functools.partial(mlp_kernel, seq_count),
        out_shape=(
            struct(rows, shard, width), struct(rows, shard, hidden), struct(rows, shard, width),
            struct(rows, shard, width), struct(rows, shard, width),
            struct(16, count, dtype=F32), struct(8, width, dtype=F32), struct(up_units, part, width),
        ),
        in_specs=[hbm] * 6 + [vmem] * 2,
        out_specs=(hbm,) * 5 + (vmem,) * 3,
        scratch_shapes=halves(up_units, part, width)
        + [scratch(*w_out.shape), scratch(*w_up.shape), scratch(*w_down.shape)]
        + [scratch(rows, shard, width)] * 3 + [scratch(rows, shard, hidden)] * 2
        + [
            scratch(rows, shard, width), scratch(rows, shard, width, dtype=F32), scratch(rows, shard, width, dtype=F32),
            scratch(rows, shard, 1, dtype=F32), scratch(rows, shard, width), scratch(rows, shard, width),
        ]
        + seq_sems(up_units) + [dma((1 + hidden // 256,)), dma((3, rows // 2)), dma((5, rows // 2))],
        compiler_params=mesh_params(3),
        name="mlp",
    )(tokens, attended, cotangent, w_out, w_up, w_down, norm_gain, norm_bias)

    units = up_units + 1
    (
        w_out_grad, w_up_grad, w_down_grad, pool_own, dq, dk, dv, dpool, own_grad, left_grad, right_grad,
    ) = pl.pallas_call(
        functools.partial(mid_kernel, seq_count, row_count, half, buffers),
        out_shape=(
            struct(part, cols, dtype=F32), struct(part, up_units * cols, dtype=F32),
            struct(cols, up_units * part, dtype=F32), struct(first_rows, pooled_local, width, dtype=F32),
            struct(rows, shard, width), struct(rows, keys, width), struct(rows, keys, width),
            struct(rows - first_rows, far, width), struct(rows, shard, width),
            struct(rows, half, width), struct(rows, half, width),
        ),
        in_specs=[hbm] * 5 + [vmem] + [hbm] * 5 + [vmem],
        out_specs=(vmem,) * 4 + (hbm,) * 7,
        scratch_shapes=halves(units, part, width) + halves(1, first_rows, pooled_local, width)
        + [scratch(units + up_units, row_count, *packing), scratch(units + up_units, row_count, *packing)]
        + seq_sems(1)
        + [scratch(2, rows, shard, width)] + [scratch(rows, shard, width)] * 3 + [scratch(*w_in.shape)]
        + [
            scratch(buffers, shard, width), scratch(buffers, keys, width), scratch(buffers, keys, width),
            scratch(buffers, PAIRS, keys, 2 * shard), scratch(buffers, shard, width),
            scratch(buffers, shard, width), scratch(buffers, keys, width), scratch(buffers, keys, width),
            scratch(buffers, far, width), scratch(buffers, shard, width),
            scratch(rows, half, width), scratch(rows, half, width),
        ]
        + seq_sems(units) + [dma((units + up_units, row_count)), dma((units + up_units, row_count))]
        + [dma((2,)), dma((4,)), dma((6, buffers)), dma((5, buffers)), dma((2, rows)), dma((2, rows))],
        compiler_params=mesh_params(0),
        name="mid",
    )(n1, attended, g1b, upg, w_in, dsum, q, k_all, v_all, prob, att_grad, down)

    w_in_grad, token_grad, conv_grad, gain_grad, bias_grad = pl.pallas_call(
        functools.partial(tail_kernel, seq_count, row_count, half),
        out_shape=(
            struct(part, 5 * cols, dtype=F32), struct(rows, shard, width, dtype=F32),
            struct(KER, width, dtype=F32), struct(2, width, dtype=F32), struct(2, width, dtype=F32),
        ),
        in_specs=[hbm] * 10 + [vmem] * 3,
        out_specs=(vmem, hbm) + (vmem,) * 3,
        scratch_shapes=halves(10, part, width // 2) + halves(1, rows - first_rows, pooled_local, width)
        + [scratch(10, row_count // 2, *packing), scratch(5, row_count, *packing)]
        + [
            scratch(2, rows, near, width), scratch(rows, near, width), scratch(rows, min(near, far), width),
            scratch(*((2, width // 2, width) if far > near else (8, 128)), dtype=F32),
            scratch(rows, pooled_local, width, dtype=F32),
            scratch(rows, 16, width), scratch(rows, 16, width),
            scratch(2, shard, width), scratch(2, half, width), scratch(2, half, width),
            scratch(2, shard, width, dtype=F32), scratch(rows, 16, width, dtype=F32),
            scratch(16, width, dtype=F32), scratch(bits, 16, width, dtype=F32), scratch(row_count, 16, width, dtype=F32),
        ]
        + seq_sems(10) + [dma((10, row_count // 2)), dma((5, row_count))] + seq_sems(1)
        + [
            dma((2, 4)), dma((3,)), dma((seq_count,)), dma((2,)), dma((3, 2)), dma((2,)), dma((bits, 2)), dma((row_count, 2)),
        ],
        compiler_params=mesh_params(1),
        name="tail",
    )(
        tok_ext, pooled_all, dq, dk, dv, dpool, pool_own, own_grad, left_grad, right_grad,
        window_seg, conv_kernel, norm_sums,
    )
    results = (
        layer_out, token_grad, w_in_grad, w_out_grad, w_up_grad, w_down_grad, conv_grad, gain_grad, bias_grad,
    )
    splits = tuple(4 if x.ndim == 3 else 1 for x in results)
    done = pl.pallas_call(
        functools.partial(finish_kernel, splits),
        out_shape=tuple(struct(*x.shape, dtype=x.dtype) for x in results),
        in_specs=[hbm] * 9,
        out_specs=(hbm,) * 9,
        scratch_shapes=[scratch(*x.shape, dtype=x.dtype) for x in results] + [dma((sum(splits),)), dma((sum(splits),))],
        compiler_params=pltpu.CompilerParams(vmem_limit_bytes=60 * MB),
        name="finish",
    )(*results)
    return done[:5] + (done[5].T,) + done[6:]


def solution(mesh):
    placed = (
        P("row", "seq", None), P("row", None), P(), P(), P(), P(), P(), P(), P(), P("row", "seq", None),
    )
    return jax.shard_map(
        body,
        mesh=mesh,
        in_specs=placed,
        out_specs=(
            P("row", "seq", None), P("row", "seq", None), P("seq", "row"), P("seq", "row"),
            P("seq", "row"), P("seq", "row"), P(), P(), P(),
        ),
        check_vma=False,
    )
```

```python
import functools

import jax
import jax.numpy as jnp
from jax import lax
from jax.experimental import pallas as pl
from jax.experimental.pallas import tpu as pltpu
from jax.sharding import PartitionSpec as P

HEADS = 12
HEAD = 64
WIN = 128
KER = 5
STR = 4
PAIRS = HEADS // 2

EPSILON = 1e-05
ROOT_HALF = 0.7071067811865476
INV_ROOT_2PI = 0.3989422804014327
NEG_LARGE = -1e30
BF = jnp.bfloat16
F32 = jnp.float32
MB = 1 << 20
MESH = pl.DeviceIdType.MESH


def dot(a, b, ca=1, cb=0):
    return lax.dot_general(a, b, (((ca,), (cb,)), ((), ())), preferred_element_type=F32)


def tap_select(seg_row, half, pooled_local):
    width = seg_row.shape[1]
    shape = (KER * pooled_local, width)
    rows = lax.broadcasted_iota(jnp.int32, shape, 0)
    cols = lax.broadcasted_iota(jnp.int32, shape, 1)
    tap = rows // pooled_local
    centre = half + STR * (rows - tap * pooled_local)
    seg = jnp.broadcast_to(seg_row, shape)
    centre_seg = jnp.sum(jnp.where(cols == centre, seg, 0), axis=1, keepdims=True)
    hit = (cols == centre + tap - KER // 2) & (seg == centre_seg)
    return jnp.where(hit, 1.0, 0.0).astype(BF)


def front_kernel(
    seq_count, half, buffers,
    tok_hbm, w_hbm, wseg_ref, fseg_ref, ker_ref,
    ext_hbm, pool_hbm, q_hbm, k_hbm, v_hbm, p_hbm, att_hbm,
    tokx, rim_in, pool_ref, w_ref, qb, knb, vnb, kfb, vfb, pb, attb,
    load_sem, line_sem, gather_sem, near_sem, far_sem, ext_sem, pool_sem,
):
    bits = seq_count.bit_length() - 1
    rows, near, width = tokx.shape
    shard = near - 2 * half
    keys = k_hbm.shape[1]
    pooled_local = pool_ref.shape[bits + 1]
    seq = lax.axis_index("seq")
    has_prev = seq > 0
    has_next = seq < seq_count - 1
    edge = 16

    def flipped(dim):
        weight = 1 << (bits - 1 - dim)
        return seq + (1 - 2 * ((seq // weight) % 2)) * weight

    def line(n, src, dst, step):
        return pltpu.make_async_remote_copy(
            src_ref=src, dst_ref=dst, send_sem=line_sem.at[n, 0], recv_sem=line_sem.at[n, 1],
            device_id={"seq": seq + step}, device_id_type=MESH,
        )

    rim = line(0, tok_hbm.at[:, shard - edge :], rim_in, 1)
    to_next = line(1, tok_hbm.at[:, shard - half :], tokx.at[:, :half], 1)
    to_prev = line(2, tok_hbm.at[:, :half], tokx.at[:, half + shard :], -1)

    rest = list(range(bits - 1))
    cut = len(rest) // 2
    orders = (rest[::-1] + [bits - 1], rest[:cut][::-1] + rest[cut:][::-1] + [bits - 1])

    def gather(part, stage, group):
        order = orders[part]
        done = order[:stage]
        index = tuple(
            slice(None) if d in done else (seq // (1 << (bits - 1 - d))) % 2 for d in range(bits)
        )
        cols = slice(part * (width // 2), (part + 1) * (width // 2))
        some = slice(group * rows // 2, (group + 1) * rows // 2)
        block = pool_ref.at[index + (some, slice(None), cols)]
        return pltpu.make_async_remote_copy(
            src_ref=block, dst_ref=block, send_sem=gather_sem.at[part, stage, 2 * group],
            recv_sem=gather_sem.at[part, stage, 2 * group + 1],
            device_id={"seq": flipped(order[stage])}, device_id_type=MESH,
        )

    own = slice(half, half + shard)
    own_load = pltpu.make_async_copy(tok_hbm, tokx.at[:, own], load_sem.at[0])
    w_load = pltpu.make_async_copy(w_hbm, w_ref, load_sem.at[1])
    own_load.start()
    w_load.start()
    sem = pltpu.get_barrier_semaphore()
    peers = [flipped(d) for d in range(bits)] + [(seq + 1) % seq_count, (seq + seq_count - 1) % seq_count]
    for peer in peers:
        pl.semaphore_signal(sem, inc=1, device_id={"seq": peer}, device_id_type=MESH)
    pl.semaphore_wait(sem, len(peers))

    @pl.when(has_next)
    def _():
        rim.start()
        to_next.start()

    @pl.when(has_prev)
    def _():
        to_prev.start()

    @pl.when(jnp.logical_not(has_prev))
    def _():
        rim_in[...] = jnp.zeros_like(rim_in)
        tokx[:, :half] = jnp.zeros((rows, half, width), BF)

    @pl.when(jnp.logical_not(has_next))
    def _():
        tokx[:, half + shard :] = jnp.zeros((rows, half, width), BF)

    own_load.wait()

    @pl.when(has_prev)
    def _():
        rim.wait_recv()

    mine = tuple((seq // (1 << (bits - 1 - d))) % 2 for d in range(bits))

    def pool_step(r, carry):
        stretch = jnp.concatenate([rim_in[r], tokx[r, own]], axis=0)
        picked = dot(tap_select(wseg_ref[pl.ds(r, 1), half - edge : half + shard], edge, pooled_local), stretch)
        total = picked[:pooled_local] * ker_ref[0:1]
        for t in range(1, KER):
            total = total + picked[t * pooled_local : (t + 1) * pooled_local] * ker_ref[t : t + 1]
        pool_ref[mine + (r,)] = total.astype(BF)
        return carry

    def onward(group, stage):
        for part in range(2):
            if stage:
                gather(part, stage - 1, group).wait()
            if stage < bits:
                gather(part, stage, group).start()

    for group in range(2):
        lax.fori_loop(group * rows // 2, (group + 1) * rows // 2, pool_step, 0)
        onward(group, 0)
    w_load.wait()
    scale = HEAD ** (-0.5)

    def own_step(r, carry):
        x = tokx[pl.ds(2 * r, 2), own].reshape(2 * shard, width)
        qb[pl.ds(2 * r, 2)] = (dot(x, w_ref[:, :width]) * scale).astype(BF).reshape(2, shard, width)
        knb[pl.ds(2 * r, 2), own] = dot(x, w_ref[:, width : 2 * width]).astype(BF).reshape(2, shard, width)
        vnb[pl.ds(2 * r, 2), own] = dot(x, w_ref[:, 2 * width : 3 * width]).astype(BF).reshape(2, shard, width)
        return carry

    lax.fori_loop(0, rows // 2, own_step, 0)
    onward(0, 1)
    onward(1, 1)

    @pl.when(has_prev)
    def _():
        to_next.wait_recv()

    @pl.when(has_next)
    def _():
        to_prev.wait_recv()

    def halo_step(r, carry):
        x = tokx[pl.ds(2 * r, 2), :half].reshape(2 * half, width)
        y = tokx[pl.ds(2 * r, 2), half + shard :].reshape(2 * half, width)
        x = jnp.concatenate([x, y], axis=0)
        for ref, first in ((knb, width), (vnb, 2 * width)):
            both = dot(x, w_ref[:, first : first + width]).astype(BF)
            ref[pl.ds(2 * r, 2), :half] = both[: 2 * half].reshape(2, half, width)
            ref[pl.ds(2 * r, 2), half + shard :] = both[2 * half :].reshape(2, half, width)
        return carry

    lax.fori_loop(0, rows // 2, halo_step, 0)
    for stage in range(2, bits + 1):
        onward(0, stage)
    ext_store = pltpu.make_async_copy(tokx, ext_hbm, ext_sem)
    ext_store.start()

    def pool_store(block):
        index = tuple((block >> (bits - 1 - d)) & 1 for d in range(bits))
        dst = pool_hbm.at[:, block * pooled_local : (block + 1) * pooled_local]
        return pltpu.make_async_copy(pool_ref.at[index], dst, pool_sem.at[block])

    def near_stores(r):
        pairs = [(qb.at[r], q_hbm.at[r]), (knb.at[r], k_hbm.at[r, :near]), (vnb.at[r], v_hbm.at[r, :near])]
        return [pltpu.make_async_copy(src, dst, near_sem.at[n, r]) for n, (src, dst) in enumerate(pairs)]

    def far_stores(r, slot):
        pairs = [
            (kfb.at[slot], k_hbm.at[r, near:]), (vfb.at[slot], v_hbm.at[r, near:]),
            (pb.at[slot], p_hbm.at[r]), (attb.at[slot], att_hbm.at[r]),
        ]
        return [pltpu.make_async_copy(src, dst, far_sem.at[n, slot]) for n, (src, dst) in enumerate(pairs)]

    lane = lax.broadcasted_iota(jnp.int32, (shard, 2 * HEAD), 1)
    even = lane < HEAD

    def row_step(r, carry):
        slot = r % buffers

        @pl.when(r == 1)
        def _():
            for stage in range(2, bits):
                onward(1, stage)

        @pl.when(r == rows // 2)
        def _():
            onward(1, bits)
            for block in range(seq_count):
                pool_store(block).start()

        for copy in near_stores(r):
            copy.start()

        @pl.when(r >= buffers)
        def _():
            for copy in far_stores(r - buffers, slot):
                copy.wait()

        pooled = pool_ref[(slice(None),) * bits + (r,)].reshape(keys - near, width)
        kfb[slot] = dot(pooled, w_ref[:, 3 * width : 4 * width]).astype(BF)
        vfb[slot] = dot(pooled, w_ref[:, 4 * width :]).astype(BF)
        window = wseg_ref[pl.ds(r, 1), :]
        key_seg = jnp.concatenate([window, fseg_ref[pl.ds(r, 1), :]], axis=1)
        key_seg = jnp.transpose(jnp.broadcast_to(key_seg, (shard, keys)))
        shape = (keys, shard)
        row = lax.broadcasted_iota(jnp.int32, shape, 0)
        col = lax.broadcasted_iota(jnp.int32, shape, 1)
        inside = (row >= near) | ((row >= col) & (row - col <= 2 * half))
        kept = inside & (key_seg == jnp.broadcast_to(window[:, half : half + shard], shape))
        bias = jnp.where(kept, 0.0, NEG_LARGE)
        bias = jnp.concatenate([bias, bias], axis=1)

        def lanes(j):
            return slice(2 * HEAD * j, 2 * HEAD * (j + 1))

        def scores(j):
            qp = qb[r, :, lanes(j)]
            zero = jnp.zeros_like(qp)
            stacked = jnp.concatenate([jnp.where(even, qp, zero), jnp.where(even, zero, qp)], axis=0)
            return (
                dot(knb[r, :, lanes(j)], stacked, 1, 1) + bias[:near],
                dot(kfb[slot, :, lanes(j)], stacked, 1, 1) + bias[near:],
            )

        def softmax(close, wide):
            top = jnp.maximum(jnp.max(close, axis=0, keepdims=True), jnp.max(wide, axis=0, keepdims=True))
            close = jnp.exp(close - top)
            wide = jnp.exp(wide - top)
            share = 1.0 / (jnp.sum(close, axis=0, keepdims=True) + jnp.sum(wide, axis=0, keepdims=True))
            return (close * share).astype(BF), (wide * share).astype(BF)

        def mix(j, close, wide):
            pb[slot, j, :near] = close
            pb[slot, j, near:] = wide
            mixed = dot(vnb[r, :, lanes(j)], close, 0, 0) + dot(vfb[slot, :, lanes(j)], wide, 0, 0)
            mixed = jnp.concatenate([mixed[:HEAD, :shard], mixed[HEAD:, shard:]], axis=0)
            attb[slot, :, lanes(j)] = jnp.transpose(mixed).astype(BF)

        current, ready = scores(0), None
        for j in range(PAIRS):
            after = scores(j + 1) if j + 1 < PAIRS else None
            if ready is not None:
                mix(j - 1, *ready)
            ready, current = softmax(*current), after
        mix(PAIRS - 1, *ready)
        for copy in far_stores(r, slot):
            copy.start()
        return carry

    lax.fori_loop(0, rows, row_step, 0)
    for n in range(buffers):
        r = rows - buffers + n
        for copy in far_stores(r, r % buffers):
            copy.wait()
    for r in range(rows):
        for copy in near_stores(r):
            copy.wait()
    for block in range(seq_count):
        pool_store(block).wait()
    ext_store.wait()

    @pl.when(has_next)
    def _():
        rim.wait_send()
        to_next.wait_send()

    @pl.when(has_prev)
    def _():
        to_prev.wait_send()


def stage_orders(bits):
    rest = list(range(bits - 1))
    cut = len(rest) // 2
    return (
        [bits - 1] + rest[::-1],
        [bits - 1] + rest[:cut][::-1] + rest[cut:][::-1],
    )


def packed_shape(part, cols):
    return (part + part // 2, 128) if cols == 192 and part % 32 == 0 else (part, cols)


def packed(x):
    part, cols = x.shape
    if packed_shape(part, cols) == x.shape:
        return x
    rest = jnp.concatenate([x[: part // 2, 128:], x[part // 2 :, 128:]], axis=1)
    return jnp.concatenate([x[:, :128], rest], axis=0)


def unpacked(x, part, cols):
    if x.shape == (part, cols):
        return x
    rest = jnp.concatenate([x[part:, :64], x[part:, 64:]], axis=0)
    return jnp.concatenate([x[:part], rest], axis=1)


class RowSum:
    def __init__(self, row_count, units, blocks, cols, dest, zsend, zrecv, send_sem, recv_sem):
        self.row = lax.axis_index("row")
        self.row_count, self.units, self.blocks, self.cols, self.dest = row_count, units, blocks, cols, dest
        self.zsend, self.zrecv, self.send_sem, self.recv_sem = zsend, zrecv, send_sem, recv_sem

    def copy(self, unit, i, target, slot):
        return pltpu.make_async_remote_copy(
            src_ref=self.zsend.at[unit, i],
            dst_ref=self.zrecv.at[slot, self.row],
            send_sem=self.send_sem.at[unit, i],
            recv_sem=self.recv_sem.at[slot, self.row],
            device_id={"row": target},
            device_id_type=MESH,
        )

    def send(self, unit, total):
        for i in range(self.blocks):
            self.zsend[unit, i] = packed(total[:, i * self.cols : (i + 1) * self.cols].astype(BF))
        for i in range(self.blocks):
            target, slot = self.dest(unit, i)

            @pl.when(self.row != target)
            def _():
                self.copy(unit, i, target, slot).start()

    def arrived(self, slot, unit, i, part):
        total = self.zsend[unit, i].astype(F32)
        for k in range(1, self.row_count):
            other = (self.row + k) % self.row_count
            pltpu.make_async_remote_copy(
                src_ref=self.zsend.at[0, 0],
                dst_ref=self.zrecv.at[slot, other],
                send_sem=self.send_sem.at[0, 0],
                recv_sem=self.recv_sem.at[slot, other],
                device_id={"row": other},
                device_id_type=MESH,
            ).wait_recv()
            total = total + self.zrecv[slot, other].astype(F32)
        return unpacked(total, part, self.cols)

    def sent(self):
        for unit in range(self.units):
            for i in range(self.blocks):
                target, slot = self.dest(unit, i)

                @pl.when(self.row != target)
                def _():
                    self.copy(unit, i, target, slot).wait_send()


class Reducer:
    def __init__(self, seq_count, units, held, bufs, send_sem, recv_sem, take, flip=0):
        self.take = take
        self.flip = flip
        self.bits = seq_count.bit_length() - 1
        self.units = units
        self.held, self.bufs = held, bufs
        self.send_sem, self.recv_sem = send_sem, recv_sem
        self.seq = lax.axis_index("seq")
        self.orders = stage_orders(self.bits)

    def bit(self, dim):
        weight = 1 << (self.bits - 1 - dim)
        value = (self.seq // weight) % 2
        return value, self.seq + (1 - 2 * value) * weight

    def barrier(self, line=False, row_count=1):
        sem = pltpu.get_barrier_semaphore()
        count = 1 << self.bits
        row = lax.axis_index("row")
        peers = [{"seq": self.bit(dim)[1]} for dim in range(self.bits)]
        peers += [{"row": (row + k) % row_count} for k in range(1, row_count)]
        if line:
            peers += [{"seq": (self.seq + 1) % count}, {"seq": (self.seq + count - 1) % count}]
        for peer in peers:
            pl.semaphore_signal(sem, inc=1, device_id=peer, device_id_type=MESH)
        pl.semaphore_wait(sem, len(peers))

    def position(self, unit, stage):
        order = self.orders[(unit + self.flip) % 2]
        left = sorted(order[stage:])
        return order[stage], left.index(order[stage])

    def source(self, unit, stage, value):
        pos = self.position(unit, stage)[1]
        base, slot = (self.held, unit % self.held.shape[0]) if stage == 0 else (self.bufs[stage - 1], unit)
        return base, (slot,) + (slice(None),) * pos + (value,)

    def copy(self, unit, stage):
        value, partner = self.bit(self.position(unit, stage)[0])
        base, index = self.source(unit, stage, 1 - value)
        return pltpu.make_async_remote_copy(
            src_ref=base.at[index],
            dst_ref=self.bufs[stage].at[unit],
            send_sem=self.send_sem.at[unit, stage],
            recv_sem=self.recv_sem.at[unit, stage],
            device_id={"seq": partner},
            device_id_type=MESH,
        )

    def start(self, unit):
        self.copy(unit, 0).start()

    def advance(self, unit, stage):
        self.copy(unit, stage - 1).wait()
        dim, pos = self.position(unit, stage - 1)
        value = self.bit(dim)[0]
        buf = self.bufs[stage - 1]
        base, _ = self.source(unit, stage - 1, value)
        slot = unit % self.held.shape[0] if stage == 1 else unit
        lead = self.bits - stage
        total = None
        for flat in range(1 << lead):
            index = tuple((flat >> (lead - 1 - d)) & 1 for d in range(lead))
            own = base[(slot,) + index[:pos] + (value,) + index[pos:]]
            if stage < self.bits:
                buf[(unit,) + index] = own + buf[(unit,) + index]
            else:
                total = own.astype(F32) + buf[(unit,) + index].astype(F32)
        if stage < self.bits:
            self.copy(unit, stage).start()
            return
        self.take(unit, total)

    def finish_plan(self, plan):
        if not plan:
            for stage in range(1, self.bits + 1):
                for unit in range(self.units):
                    self.advance(unit, stage)

    def follow(self, plan, *place):
        for unit, stage in plan.get(place, ()):
            self.advance(unit, stage)


def split_index(flat, bits):
    return tuple((flat >> (bits - 1 - d)) & 1 for d in range(bits))


def mlp_kernel(
    seq_count,
    tok_hbm, att_hbm, cot_hbm, wo_hbm, wu_hbm, wd_hbm, gain_ref, bias_ref,
    out_hbm, upg_hbm, n1_hbm, g1b_hbm, da_hbm, dsum_ref, small_ref, down_ref,
    held, *rest,
):
    bits = seq_count.bit_length() - 1
    bufs = rest[:bits]
    (
        wo_ref, wu_ref, wd_ref, tokw, attw, cotw, actw, slopew, r2w, gradw, hatw, rstdw, outw, n1w,
        send_sem, recv_sem, w_sem, in_sem, out_sem,
    ) = rest[bits:]
    rows, shard, width = tokw.shape
    hidden = wu_ref.shape[1]
    units = hidden // width
    part = width // seq_count
    tall = width // 2
    chunk = 512
    block = 2 * shard
    blocks = rows // 2
    gain_a, gain_b = gain_ref[0:1], gain_ref[1:2]

    def take(unit, total):
        down_ref[unit] = total.astype(BF)

    red = Reducer(seq_count, units, held, bufs, send_sem, recv_sem, take)
    plan = {}
    if bits == 3 and units == 4 and blocks == 4:
        plan = {
            (0, 0): [(0, 1), (1, 1)], (1, 0): [(2, 1), (3, 1), (0, 2), (1, 2)],
            (3, 0): [(2, 2), (3, 2), (0, 3), (1, 3)], ("end",): [(2, 3), (3, 3)],
        }

    def mean(x):
        return jnp.mean(x, axis=-1, keepdims=True)

    chunks = hidden // chunk

    def up_load(c):
        cols = slice(c * chunk, (c + 1) * chunk)
        return pltpu.make_async_copy(wu_hbm.at[:, cols], wu_ref.at[:, cols], w_sem.at[1 + c])

    def down_load(c):
        part_rows = slice(c * chunk, (c + 1) * chunk)
        return pltpu.make_async_copy(wd_hbm.at[part_rows], wd_ref.at[part_rows], w_sem.at[1 + chunks + c])

    out_load = pltpu.make_async_copy(wo_hbm, wo_ref, w_sem.at[0])

    def loads(b):
        pairs = [(tok_hbm, tokw), (att_hbm, attw), (cot_hbm, cotw)]
        return [
            pltpu.make_async_copy(src.at[pl.ds(2 * b, 2)], dst.at[pl.ds(2 * b, 2)], in_sem.at[n, b])
            for n, (src, dst) in enumerate(pairs)
        ]

    def stores(b, first):
        pairs = [(outw, out_hbm), (n1w, n1_hbm), (actw, upg_hbm), (r2w, g1b_hbm), (tokw, da_hbm)]
        return [
            pltpu.make_async_copy(pairs[n][0].at[pl.ds(2 * b, 2)], pairs[n][1].at[pl.ds(2 * b, 2)], out_sem.at[n, b])
            for n in (range(2) if first else range(2, 5))
        ]

    out_load.start()
    for copy in loads(0):
        copy.start()
    for c in range(chunks):
        up_load(c).start()
        down_load(c).start()
    for b in range(1, blocks):
        for copy in loads(b):
            copy.start()
    red.barrier()
    small_ref[...] = jnp.zeros_like(small_ref)

    def flat(ref, b):
        return ref[pl.ds(2 * b, 2)].reshape(block, ref.shape[2])

    def put(ref, b, value):
        ref[pl.ds(2 * b, 2)] = value.reshape(2, shard, ref.shape[2])

    def forward_step(b, carry):
        for copy in loads(b):
            copy.wait()

        rows_b = pl.ds(2 * b, 2)
        resid = flat(tokw, b).astype(F32) + dot(flat(attw, b), wo_ref[...])
        centred = resid - mean(resid)
        rstd_a = lax.rsqrt(mean(centred * centred) + EPSILON)
        hat_a = centred * rstd_a
        put(hatw, b, hat_a)
        rstdw[rows_b] = rstd_a.reshape(2, shard, 1)
        normed = hat_a * gain_a + bias_ref[0:1]
        low = normed.astype(BF)
        put(n1w, b, low)
        total = normed

        def raised(c):
            return dot(low, wu_ref[:, c * chunk : (c + 1) * chunk])

        def lowered(c, act):
            return dot(act, wd_ref[c * chunk : (c + 1) * chunk, :])

        for c in range(chunks):
            up = raised(c)
            half_cdf = 0.5 * (1.0 + lax.erf(up * ROOT_HALF))
            ready = (up * half_cdf).astype(BF)
            cols = slice(c * chunk, (c + 1) * chunk)
            actw[rows_b, :, cols] = ready.reshape(2, shard, chunk)
            slope = half_cdf + up * (INV_ROOT_2PI * jnp.exp(-0.5 * up * up))
            slopew[rows_b, :, cols] = slope.astype(BF).reshape(2, shard, chunk)
            total = total + lowered(c, ready)
        centred = total - mean(total)
        rstd_b = lax.rsqrt(mean(centred * centred) + EPSILON)
        hat_b = centred * rstd_b
        put(outw, b, (hat_b * gain_b + bias_ref[1:2]).astype(BF))
        for copy in stores(b, True):
            copy.start()
        g = flat(cotw, b).astype(F32)
        small_ref[1:2] += jnp.sum(g * hat_b, axis=0, keepdims=True)
        small_ref[3:4] += jnp.sum(g, axis=0, keepdims=True)
        e = g * gain_b
        grad = rstd_b * (e - mean(e) - hat_b * mean(e * hat_b))
        put(gradw, b, grad)
        put(r2w, b, grad.astype(BF))
        return carry

    out_load.wait()
    for c in range(chunks):
        up_load(c).wait()
        down_load(c).wait()
    lax.fori_loop(0, blocks, forward_step, 0)

    for c in range(hidden // tall):
        left = actw[:, :, tall * c : tall * (c + 1)].reshape(-1, tall)
        total = dot(left, r2w[...].reshape(-1, width), 0, 0)
        blocked = total.reshape(tall // part, part, width).astype(BF)
        for n in range(tall // part):
            place = (c * tall + n * part) // part
            held[(place % units,) + split_index(place // units, bits)] = blocked[n]
    for u in range(units):
        red.start(u)

    def backward_step(b, carry):
        rows_b = pl.ds(2 * b, 2)

        def advance(half_step):
            for t in range(blocks):
                if (t, half_step) in plan:

                    @pl.when(b == t)
                    def _():
                        red.follow(plan, t, half_step)

        advance(0)
        grad = flat(gradw, b)
        grad_low = flat(r2w, b)

        def raised(c):
            return dot(grad_low, wd_ref[c * chunk : (c + 1) * chunk, :], 1, 1)

        def lowered(c, up_grad):
            return dot(up_grad, wu_ref[:, c * chunk : (c + 1) * chunk], 1, 1)

        current, ready = raised(0), None
        for c in range(chunks):
            after = raised(c + 1) if c + 1 < chunks else None
            if ready is not None:
                grad = grad + lowered(c - 1, ready)
            cols = slice(c * chunk, (c + 1) * chunk)
            slope = slopew[rows_b, :, cols].reshape(block, chunk).astype(F32)
            ready = (current * slope).astype(BF)
            actw[rows_b, :, cols] = ready.reshape(2, shard, chunk)
            current = after
        grad = grad + lowered(chunks - 1, ready)
        hat_a = flat(hatw, b)
        small_ref[0:1] += jnp.sum(grad * hat_a, axis=0, keepdims=True)
        small_ref[2:3] += jnp.sum(grad, axis=0, keepdims=True)
        e = grad * gain_a
        resid_grad = rstdw[rows_b].reshape(block, 1) * (e - mean(e) - hat_a * mean(e * hat_a))
        resid_low = resid_grad.astype(BF)
        put(r2w, b, resid_low)
        att_grad = dot(resid_low, wo_ref[...], 1, 1).astype(BF)
        put(tokw, b, att_grad)
        for copy in stores(b, False):
            copy.start()
        prod = att_grad.astype(F32) * flat(attw, b).astype(F32)
        high = prod.astype(BF)
        rest = (prod - high.astype(F32)).astype(BF)
        heads = dsum_ref.shape[0]
        head_row = lax.broadcasted_iota(jnp.int32, (heads, width), 0)
        head_col = lax.broadcasted_iota(jnp.int32, (heads, width), 1) // HEAD
        pick = jnp.where(head_row == head_col, 1.0, 0.0).astype(BF)
        dsum_ref[:, pl.ds(pl.multiple_of(b * block, block), block)] = dot(pick, high, 1, 1) + dot(pick, rest, 1, 1)
        return carry

    lax.fori_loop(0, blocks, backward_step, 0)
    red.finish_plan(plan)
    red.follow(plan, "end")
    for b in range(blocks):
        for copy in stores(b, True) + stores(b, False):
            copy.wait()


def mid_kernel(
    seq_count, row_count, half, buffers,
    n1_hbm, att_hbm, g1b_hbm, upg_hbm, w_hbm, dsum_ref,
    q_hbm, k_hbm, v_hbm, p_hbm, da_hbm, down_ref,
    wout_ref, wup_ref, wdown_ref, pown_ref, dq_hbm, dk_hbm, dv_hbm, dpool_hbm, own_hbm, left_hbm, right_hbm,
    held, *rest,
):
    bits = seq_count.bit_length() - 1
    bufs, rest = rest[:bits], rest[bits:]
    pheld, pbufs, rest = rest[0], rest[1 : 1 + bits], rest[1 + bits :]
    (
        zsend, zrecv, psend_sem, precv_sem, slots, n1_ref, att_ref, g1b_ref, w_ref,
        qb, kb, vb, pb, dab, dqb, dkb, dvb, dpb, owb, lfb, rtb,
        send_sem, recv_sem, zsend_sem, zrecv_sem, load_sem, once_sem, in_sem, out_sem, line_send, line_recv,
    ) = rest
    rows, shard, width = n1_ref.shape
    near = shard + 2 * half
    part = width // seq_count
    up_units = upg_hbm.shape[2] // width
    units = up_units + 1
    tall = width // 2
    steps = up_units
    first_rows, pooled_local = pown_ref.shape[:2]

    def dest(unit, i):
        if unit < up_units:
            g = unit * row_count + i
            return g // up_units, g % up_units
        return i, unit

    cols = width // row_count
    down_units = down_ref.shape[0]
    sums = RowSum(row_count, units + down_units, row_count, cols, dest, zsend, zrecv, zsend_sem, zrecv_sem)
    red = Reducer(seq_count, units, held, bufs, send_sem, recv_sem, sums.send, 1)

    def take(unit, total):
        pown_ref[...] = total

    pred = Reducer(seq_count, 1, pheld, pbufs, psend_sem, precv_sem, take, 1)
    once = [
        pltpu.make_async_copy(src, dst, once_sem.at[n])
        for n, (src, dst) in enumerate([(n1_hbm, n1_ref), (att_hbm, att_ref), (g1b_hbm, g1b_ref), (w_hbm, w_ref)])
    ]

    def load(k):
        return pltpu.make_async_copy(
            upg_hbm.at[:, :, width * k : width * (k + 1)], slots.at[k % 2], load_sem.at[k % 2]
        )

    def taken(k):
        load(k).wait()
        if k + 1 < steps:
            load(k + 1).start()

    def row_loads(r, slot):
        pairs = [(p_hbm, pb), (k_hbm, kb), (v_hbm, vb), (q_hbm, qb), (da_hbm, dab)]
        return [
            pltpu.make_async_copy(src.at[r], dst.at[slot], in_sem.at[n, slot])
            for n, (src, dst) in enumerate(pairs)
        ]

    def row_stores(r, slot):
        pairs = [(dqb, dq_hbm), (dkb, dk_hbm), (dvb, dv_hbm), (owb, own_hbm)]
        return [
            pltpu.make_async_copy(src.at[slot], dst.at[r], out_sem.at[n, slot])
            for n, (src, dst) in enumerate(pairs)
        ]

    def pool_store(r, slot):
        return pltpu.make_async_copy(dpb.at[slot], dpool_hbm.at[r - first_rows], out_sem.at[4, slot])

    has_prev = red.seq > 0
    has_next = red.seq < seq_count - 1

    def line(n, r):
        src, dst = ((lfb, right_hbm), (rtb, left_hbm))[n]
        return pltpu.make_async_remote_copy(
            src_ref=src.at[r], dst_ref=dst.at[r], send_sem=line_send.at[n, r], recv_sem=line_recv.at[n, r],
            device_id={"seq": red.seq + 2 * n - 1}, device_id_type=MESH,
        )

    sides = ((0, has_prev, has_next), (1, has_next, has_prev))

    once[0].start()
    load(0).start()
    for copy in once[1:]:
        copy.start()
    if buffers > 1:
        for copy in row_loads(0, 0):
            copy.start()
    red.barrier(line=True, row_count=row_count)
    lead = (2,) * (bits - 1)
    plan, pool_plan = {}, {}
    if bits == 3 and up_units == 4 and rows == 8:
        plan = {
            ("up", 1): [(0, 1)], ("up", 2): [(1, 1)], ("up", 4): [(2, 1)],
            ("row", 0): [(3, 1)], ("row", 1): [(0, 2), (4, 1)], ("row", 2): [(1, 2)],
            ("row", 3): [(2, 2), (0, 3)], ("row", 4): [(3, 2), (1, 3)], ("row", 5): [(4, 2), (2, 3)],
            ("row", 6): [(3, 3)], ("row", 7): [(4, 3)],
        }
        pool_plan = {("row", 5): [(0, 1)], ("row", 7): [(0, 2)], ("end",): [(0, 3)]}

    def product(unit, left_ref, right):
        for m in range(2):
            left = left_ref[:, :, tall * m : tall * (m + 1)].reshape(-1, tall)
            held[unit, m] = dot(left, right, 0, 0).reshape(lead + (part, width)).astype(BF)

    once[0].wait()
    for u in range(up_units):
        taken(u)
        if u == 0:
            for n in range(down_units):
                sums.send(units + n, down_ref[n])
        product(u, n1_ref, slots[u % 2].reshape(-1, width))
        red.start(u)
        red.follow(plan, "up", u)
    once[1].wait()
    once[2].wait()
    product(up_units, att_ref, g1b_ref[...].reshape(-1, width))
    red.start(up_units)
    red.follow(plan, "up", up_units)
    once[3].wait()

    lane = lax.broadcasted_iota(jnp.int32, (shard, 2 * HEAD), 1)
    even = lane < HEAD

    def stack(pair):
        zero = jnp.zeros_like(pair)
        return jnp.concatenate([jnp.where(even, pair, zero), jnp.where(even, zero, pair)], axis=0)

    def hooks(r, place):
        for t in range(rows):
            begins = place == "row" and t == first_rows
            if (place, t) in plan or (place, t) in pool_plan or begins:

                @pl.when(r == t)
                def _():
                    if begins:
                        pred.start(0)
                    red.follow(plan, place, t)
                    pred.follow(pool_plan, place, t)

    def row_step(r, carry):
        slot = r % buffers
        if buffers > 1:

            @pl.when(r + 1 < rows)
            def _():
                for copy in row_loads(r + 1, (r + 1) % buffers):
                    copy.start()

        else:
            for copy in row_loads(r, slot):
                copy.start()
        hooks(r, "row")
        for copy in row_loads(r, slot):
            copy.wait()

        @pl.when(r >= buffers)
        def _():
            for copy in row_stores(r - buffers, slot):
                copy.wait()

        @pl.when(r >= buffers + first_rows)
        def _():
            pool_store(r - buffers, slot).wait()

        row_sums = dsum_ref[:, pl.ds(pl.multiple_of(r * shard, shard), shard)]

        def lanes(j):
            return slice(2 * HEAD * j, 2 * HEAD * (j + 1))

        def dprobs(j):
            return dot(vb[slot, :, lanes(j)], stack(dab[slot, :, lanes(j)]), 1, 1)

        def dscores(j, dprob):
            row_dot = jnp.concatenate([row_sums[2 * j : 2 * j + 1], row_sums[2 * j + 1 : 2 * j + 2]], axis=1)
            return (pb[slot, j].astype(F32) * (dprob - row_dot)).astype(BF)

        def products(j, dscore):
            dvb[slot, :, lanes(j)] = dot(pb[slot, j], stack(dab[slot, :, lanes(j)])).astype(BF)
            dkb[slot, :, lanes(j)] = dot(dscore, stack(qb[slot, :, lanes(j)])).astype(BF)
            mixed = dot(kb[slot, :, lanes(j)], dscore, 0, 0)
            mixed = jnp.concatenate([mixed[:HEAD, :shard], mixed[HEAD:, shard:]], axis=0)
            dqb[slot, :, lanes(j)] = (jnp.transpose(mixed) * HEAD ** (-0.5)).astype(BF)

        current, ready = dprobs(0), None
        for j in range(PAIRS):
            after = dprobs(j + 1) if j + 1 < PAIRS else None
            if ready is not None:
                products(j - 1, ready)
            ready, current = dscores(j, current), after
        products(PAIRS - 1, ready)
        back = dot(dkb[slot, :near], w_ref[:, width : 2 * width], 1, 1) + dot(
            dvb[slot, :near], w_ref[:, 2 * width : 3 * width], 1, 1
        )
        lfb[r] = back[:half].astype(BF)
        rtb[r] = back[half + shard :].astype(BF)
        own = g1b_ref[r].astype(F32) + back[half : half + shard] + dot(dqb[slot], w_ref[:, :width], 1, 1)
        owb[slot] = own.astype(BF)
        pooled = (
            dot(dkb[slot, near:], w_ref[:, 3 * width : 4 * width], 1, 1)
            + dot(dvb[slot, near:], w_ref[:, 4 * width :], 1, 1)
        ).astype(BF)
        dpb[slot] = pooled

        @pl.when(r < first_rows)
        def _():
            index = (0,) + (slice(None),) * bits + (r,)
            pheld[index] = pooled.reshape((2,) * bits + (pooled_local, width))

        @pl.when(r >= first_rows)
        def _():
            pool_store(r, slot).start()

        for copy in row_stores(r, slot):
            copy.start()
        for n, sends, _ in sides:

            @pl.when(sends)
            def _():
                line(n, r).start()

        return carry

    lax.fori_loop(0, rows, row_step, 0)
    red.finish_plan(plan)
    pred.finish_plan(pool_plan)
    pred.follow(pool_plan, "end")
    for k in range(buffers):
        r = rows - buffers + k
        for copy in row_stores(r, r % buffers):
            copy.wait()
        pool_store(r, r % buffers).wait()
    for n, sends, takes in sides:

        @pl.when(sends)
        def _():
            for r in range(rows):
                line(n, r).wait_send()

        @pl.when(takes)
        def _():
            for r in range(rows):
                line(n, r).wait_recv()

    row = sums.row
    down = [sums.arrived(units + n, units + n, row, part) for n in range(down_units)]
    wdown_ref[...] = jnp.transpose(jnp.concatenate(down, axis=0))
    for n in range(up_units):
        g = row * up_units + n
        wup_ref[:, n * cols : (n + 1) * cols] = sums.arrived(n, g // row_count, g % row_count, part)
    wout_ref[...] = sums.arrived(up_units, up_units, row, part)
    sums.sent()


def tail_kernel(
    seq_count, row_count, half,
    tok_hbm, pool_hbm, dq_hbm, dk_hbm, dv_hbm, dpool_hbm, pown_hbm, own_hbm, left_hbm, right_hbm,
    seg_ref, ker_ref, norm_ref,
    win_ref, out_hbm, conv_ref, gain_ref, bias_ref,
    held, *rest,
):
    bits = seq_count.bit_length() - 1
    bufs, rest = rest[:bits], rest[bits:]
    pheld, pbufs, rest = rest[0], rest[1 : 1 + bits], rest[1 + bits :]
    (
        zsend, zrecv, slots, tok_ref, pool_ref, partial, dpool_own, rim_out, rim_in, ownb, leftb, rightb, outb, edgeb,
        ssum, srecv, zsum,
        send_sem, recv_sem, zsend_sem, zrecv_sem, psend_sem, precv_sem, load_sem, pool_sem, ploads_sem,
        line_sem, own_sem, out_sem, small_sem, zsmall_sem,
    ) = rest
    rows, near, width = tok_ref.shape
    shard = near - 2 * half
    part = width // seq_count
    units = 10
    tall = width // 2
    piece = pool_ref.shape[1]
    pieces = (dk_hbm.shape[1] - near) // piece
    pooled_local = dpool_own.shape[1]
    late_rows = rows - pown_hbm.shape[0]
    edge = 16
    order = (0, 3, 4, 1, 2)

    blocks = row_count // 2

    def dest(unit, i):
        g = order[unit // 2] * row_count + (unit % 2) * blocks + i
        return g // 5, g % 5

    cols = width // row_count
    sums = RowSum(row_count, units, blocks, cols, dest, zsend, zrecv, zsend_sem, zrecv_sem)
    red = Reducer(seq_count, units, held, bufs, send_sem, recv_sem, sums.send)

    def take(unit, total):
        dpool_own[rows - late_rows :] = total

    pred = Reducer(seq_count, 1, pheld, pbufs, psend_sem, precv_sem, take, 1)
    steps = 2 * pieces + 3

    def load(k):
        buf = slots.at[k % 2]
        if k == 0:
            src, dst = dq_hbm, buf.at[:, :shard]
        elif k <= 2 * pieces:
            first = near + ((k - 1) % pieces) * piece
            src, dst = (dk_hbm, dv_hbm)[(k - 1) // pieces].at[:, first : first + piece], buf.at[:, :piece]
        else:
            src, dst = (dk_hbm, dv_hbm)[k - 2 * pieces - 1].at[:, :near], buf
        group = rows // 4
        return [
            pltpu.make_async_copy(
                src.at[n * group : (n + 1) * group], dst.at[n * group : (n + 1) * group], load_sem.at[k % 2, n]
            )
            for n in range(4)
        ]

    def taken(k):
        for copy in load(k):
            copy.wait()
        if k + 1 < steps:
            for copy in load(k + 1):
                copy.start()

    def pool_load(n):
        return pltpu.make_async_copy(pool_hbm.at[:, n * piece : (n + 1) * piece], pool_ref, pool_sem.at[0])

    tok_load = pltpu.make_async_copy(tok_hbm, tok_ref, pool_sem.at[1])

    def grad_load(owner):
        src = dpool_hbm.at[:, owner * pooled_local : (owner + 1) * pooled_local]
        return pltpu.make_async_copy(src, pheld.at[(0,) + split_index(owner, bits)], ploads_sem.at[owner])

    own_pool = pltpu.make_async_copy(pown_hbm, dpool_own.at[: rows - late_rows], pool_sem.at[2])

    rim = pltpu.make_async_remote_copy(
        src_ref=rim_out, dst_ref=rim_in, send_sem=line_sem.at[0], recv_sem=line_sem.at[1],
        device_id={"seq": red.seq - 1}, device_id_type=MESH,
    )
    has_prev = red.seq > 0
    has_next = red.seq < seq_count - 1

    for owner in range(seq_count):
        grad_load(owner).start()
    for copy in load(0):
        copy.start()
    tok_load.start()
    pool_load(0).start()
    own_pool.start()
    red.barrier(line=True, row_count=row_count)
    for owner in range(seq_count):
        grad_load(owner).wait()
    pred.start(0)

    lead = (2,) * (bits - 1)

    def product(unit, left, right, first=True, last=True):
        for m in range(2):
            total = dot(left(m), right, 0, 0)
            if m == 0 and first:
                step("half", unit)
            if not first:
                total = total + partial[m]
            if not last:
                partial[m] = total
                continue
            total = total.reshape(lead + (part, width)).astype(BF)
            for h in range(2):
                held[2 * unit + h, m] = total[..., tall * h : tall * (h + 1)]

    def begin(unit):
        red.start(2 * unit)
        red.start(2 * unit + 1)

    def columns(ref, keep=slice(None)):
        return lambda m: ref[:, keep, tall * m : tall * (m + 1)].reshape(-1, tall)

    def whole(k, length):
        return slots[k % 2, :, :length].reshape(-1, width)

    plan, pool_plan = {}, {}
    if bits == 3 and rows == 8:
        plan = {
            ("half", 1): [(0, 1), (1, 1)], ("half", 2): [(2, 1), (3, 1)], ("half", 3): [(4, 1), (5, 1), (0, 2), (1, 2)],
            ("half", 4): [(6, 1), (7, 1), (2, 2), (3, 2)], ("row", 0): [(0, 3), (1, 3)],
            ("row", 1): [(8, 1), (9, 1)], ("row", 2): [(4, 2), (5, 2)], ("row", 3): [(2, 3), (3, 3)],
            ("row", 5): [(6, 2), (7, 2)], ("row", 7): [(4, 3), (5, 3)], ("end", 0): [(6, 3), (7, 3)],
            ("end", 1): [(8, 2), (9, 2)], ("end", 3): [(8, 3), (9, 3)],
        }
        pool_plan = {("done", 0): [(0, 1)], ("half", 3): [(0, 2)], ("row", 4): [(0, 3)]}

    def step(*place):
        red.follow(plan, *place)
        pred.follow(pool_plan, *place)

    own = slice(half, half + shard)
    tok_load.wait()
    taken(0)
    product(0, columns(tok_ref, own), whole(0, shard))
    begin(0)
    step("done", 0)
    for n in range(2):
        for c in range(pieces):
            k = 1 + n * pieces + c
            if pieces > 1 and (n or c):
                pool_load(c).start()
            if pieces > 1 or n == 0:
                pool_load(c).wait()
            taken(k)
            product(1 + n, columns(pool_ref), whole(k, piece), c == 0, c == pieces - 1)
        begin(1 + n)
    for n in range(2):
        k = 1 + 2 * pieces + n
        taken(k)
        product(3 + n, columns(tok_ref), whole(k, near))
        begin(3 + n)
    own_pool.wait()
    pred.finish_plan(pool_plan)

    ssum[...] = jnp.zeros_like(ssum)
    ssum[8:12] = norm_ref[0:4]

    def row_loads(r, slot):
        pairs = [(own_hbm, ownb), (left_hbm, leftb), (right_hbm, rightb)]
        return [
            pltpu.make_async_copy(src.at[r], dst.at[slot], own_sem.at[n, slot])
            for n, (src, dst) in enumerate(pairs)
        ]

    def out_store(r, slot):
        return pltpu.make_async_copy(
            outb.at[slot, : shard - edge], out_hbm.at[r, : shard - edge], out_sem.at[slot]
        )

    for copy in row_loads(0, 0):
        copy.start()

    def pool_step(r, carry):
        slot = r % 2

        @pl.when(r + 1 < rows)
        def _():
            for copy in row_loads(r + 1, (r + 1) % 2):
                copy.start()

        for t in range(rows):
            if ("row", t) in plan or ("row", t) in pool_plan:

                @pl.when(r == t)
                def _():
                    step("row", t)

        select = tap_select(seg_ref[pl.ds(r, 1), half - edge : half + shard], edge, pooled_local)
        picked = dot(select, tok_ref[r, half - edge : half + shard])
        grad = dpool_own[r]
        terms, sums = [], []
        for t in range(KER):
            terms.append((grad * ker_ref[t : t + 1]).astype(BF))
            sums.append(jnp.sum(grad * picked[t * pooled_local : (t + 1) * pooled_local], axis=0, keepdims=True))
        ssum[0:KER] += jnp.concatenate(sums, axis=0)
        spread = dot(select, jnp.concatenate(terms, axis=0), 0, 0)
        rim_out[r] = spread[:edge].astype(BF)
        for copy in row_loads(r, slot):
            copy.wait()

        @pl.when(r >= 2)
        def _():
            out_store(r - 2, slot).wait()

        outb[slot] = ownb[slot].astype(F32) + spread[edge:]

        @pl.when(has_prev)
        def _():
            outb[slot, :half] += leftb[slot].astype(F32)

        @pl.when(has_next)
        def _():
            outb[slot, shard - half :] += rightb[slot].astype(F32)

        edgeb[r] = outb[slot, shard - edge :]
        out_store(r, slot).start()
        return carry

    lax.fori_loop(0, rows, pool_step, 0)

    @pl.when(has_prev)
    def _():
        rim.start()

    def small_copy(stage):
        return pltpu.make_async_remote_copy(
            src_ref=ssum, dst_ref=srecv.at[stage], send_sem=small_sem.at[stage, 0], recv_sem=small_sem.at[stage, 1],
            device_id={"seq": red.bit(bits - 1 - stage)[1]}, device_id_type=MESH,
        )

    def small_row(k):
        other = (sums.row + k) % row_count
        return pltpu.make_async_remote_copy(
            src_ref=ssum, dst_ref=zsum.at[row_count - k], send_sem=zsmall_sem.at[k, 0],
            recv_sem=zsmall_sem.at[row_count - k, 1], device_id={"row": other}, device_id_type=MESH,
        )

    def small_add(stage):
        small_copy(stage).wait()
        ssum[...] += srecv[stage]

    small_copy(0).start()
    step("end", 0)
    small_add(0)
    small_copy(1).start()

    @pl.when(has_next)
    def _():
        rim.wait_recv()
        edgeb[...] += rim_in[...].astype(F32)

    edge_store = pltpu.make_async_copy(edgeb, out_hbm.at[:, shard - edge :], own_sem.at[0, 0])
    edge_store.start()
    step("end", 1)
    small_add(1)
    small_copy(2).start()
    step("end", 2)
    step("end", 3)
    red.finish_plan(plan)
    small_add(2)
    for stage in range(3, bits):
        small_copy(stage).start()
        small_add(stage)
    for k in range(1, row_count):
        small_row(k).start()
    zsum[0] = ssum[...]
    for n in range(5):
        g = sums.row * 5 + n
        block, i = g // row_count, g % row_count
        place = block + 2 * ((block + 4) // 5) - 4 * (block // 3)
        win_ref[:, n * cols : (n + 1) * cols] = sums.arrived(n, 2 * place + i // blocks, i % blocks, part)
    for k in range(1, row_count):
        small_row(row_count - k).wait_recv()
    total = None
    for owner in range(row_count):
        term = zsum[(owner - sums.row + row_count) % row_count]
        total = term if total is None else total + term
    conv_ref[...] = total[:KER]
    gain_ref[...] = total[8:10]
    bias_ref[...] = total[10:12]
    for k in range(1, row_count):
        small_row(k).wait_send()
    sums.sent()
    edge_store.wait()
    for n in range(2):
        out_store(rows - 2 + n, n).wait()

    @pl.when(has_prev)
    def _():
        rim.wait_send()


def finish_kernel(splits, *refs):
    count = len(splits)
    ins, outs, bufs = refs[:count], refs[count : 2 * count], refs[2 * count : 3 * count]
    sem_in, sem_out = refs[3 * count :]
    loads, stores = [], []
    for src, dst, buf, split in zip(ins, outs, bufs, splits):
        length = src.shape[0] // split
        for n in range(split):
            piece = slice(n * length, (n + 1) * length)
            loads.append(pltpu.make_async_copy(src.at[piece], buf.at[piece], sem_in.at[len(loads)]))
            stores.append(pltpu.make_async_copy(buf.at[piece], dst.at[piece], sem_out.at[len(stores)]))
    for copy in loads:
        copy.start()
    for load, store in zip(loads, stores):
        load.wait()
        store.start()
    for copy in stores:
        copy.wait()


def body(tokens, segment_ids, w_in, w_out, w_up, w_down, conv_kernel, norm_gain, norm_bias, cotangent):
    rows, shard, width = tokens.shape
    half = WIN // 2
    pooled_local = shard // STR
    near = shard + 2 * half
    count = rows * shard
    hidden = w_up.shape[1]
    seq_count = lax.axis_size("seq")
    row_count = lax.axis_size("row")
    seq_start = lax.axis_index("seq") * shard
    keys = near + pooled_local * seq_count

    padded_seg = jnp.pad(segment_ids, ((0, 0), (half, half)), constant_values=-1)
    window_seg = lax.dynamic_slice_in_dim(padded_seg, seq_start, near, 1)
    far_seg = segment_ids[:, ::STR]

    def struct(*dims, dtype=BF):
        return jax.ShapeDtypeStruct(dims, dtype)

    bits = seq_count.bit_length() - 1
    far = keys - near
    buffers = 2 if keys <= 2 * near else 1
    vmem = pl.BlockSpec(memory_space=pltpu.VMEM)
    hbm = pl.BlockSpec(memory_space=pl.ANY)
    dma = pltpu.SemaphoreType.DMA

    def scratch(*dims, dtype=BF):
        return pltpu.VMEM(dims, dtype)

    tok_ext, pooled_all, q, k_all, v_all, prob, attended = pl.pallas_call(
        functools.partial(front_kernel, seq_count, half, buffers),
        out_shape=(
            struct(rows, near, width), struct(rows, far, width), struct(rows, shard, width),
            struct(rows, keys, width), struct(rows, keys, width), struct(rows, PAIRS, keys, 2 * shard),
            struct(rows, shard, width),
        ),
        in_specs=[hbm] * 2 + [vmem] * 3,
        out_specs=(hbm,) * 7,
        scratch_shapes=[
            scratch(rows, near, width), scratch(rows, 16, width),
            scratch(*((2,) * bits + (rows, pooled_local, width))), scratch(*w_in.shape),
            scratch(rows, shard, width), scratch(rows, near, width), scratch(rows, near, width),
            scratch(buffers, far, width), scratch(buffers, far, width),
            scratch(buffers, PAIRS, keys, 2 * shard), scratch(buffers, shard, width),
            dma((2,)), dma((3, 2)), dma((2, bits, 4)), dma((3, rows)), dma((4, buffers)), dma, dma((seq_count,)),
        ],
        compiler_params=pltpu.CompilerParams(collective_id=2, has_side_effects=True, vmem_limit_bytes=60 * MB),
        name="front",
    )(tokens, w_in, window_seg, far_seg, conv_kernel)

    part = width // seq_count
    up_units = hidden // width
    cols = width // row_count
    first_rows = rows // 2

    def halves(units, *tail):
        return [pltpu.VMEM((units,) + (2,) * (bits - i) + tail, BF) for i in range(bits + 1)]

    def mesh_params(collective_id):
        return pltpu.CompilerParams(
            collective_id=collective_id, has_side_effects=True, vmem_limit_bytes=60 * MB
        )

    def seq_sems(units):
        return [dma((units, bits)), dma((units, bits))]

    packing = packed_shape(part, cols)

    layer_out, upg, n1, g1b, att_grad, dsum, norm_sums, down = pl.pallas_call(
        functools.partial(mlp_kernel, seq_count),
        out_shape=(
            struct(rows, shard, width), struct(rows, shard, hidden), struct(rows, shard, width),
            struct(rows, shard, width), struct(rows, shard, width),
            struct(16, count, dtype=F32), struct(8, width, dtype=F32), struct(up_units, part, width),
        ),
        in_specs=[hbm] * 6 + [vmem] * 2,
        out_specs=(hbm,) * 5 + (vmem,) * 3,
        scratch_shapes=halves(up_units, part, width)
        + [scratch(*w_out.shape), scratch(*w_up.shape), scratch(*w_down.shape)]
        + [scratch(rows, shard, width)] * 3 + [scratch(rows, shard, hidden)] * 2
        + [
            scratch(rows, shard, width), scratch(rows, shard, width, dtype=F32), scratch(rows, shard, width, dtype=F32),
            scratch(rows, shard, 1, dtype=F32), scratch(rows, shard, width), scratch(rows, shard, width),
        ]
        + seq_sems(up_units) + [dma((1 + hidden // 256,)), dma((3, rows // 2)), dma((5, rows // 2))],
        compiler_params=mesh_params(3),
        name="mlp",
    )(tokens, attended, cotangent, w_out, w_up, w_down, norm_gain, norm_bias)

    units = up_units + 1
    (
        w_out_grad, w_up_grad, w_down_grad, pool_own, dq, dk, dv, dpool, own_grad, left_grad, right_grad,
    ) = pl.pallas_call(
        functools.partial(mid_kernel, seq_count, row_count, half, buffers),
        out_shape=(
            struct(part, cols, dtype=F32), struct(part, up_units * cols, dtype=F32),
            struct(cols, up_units * part, dtype=F32), struct(first_rows, pooled_local, width, dtype=F32),
            struct(rows, shard, width), struct(rows, keys, width), struct(rows, keys, width),
            struct(rows - first_rows, far, width), struct(rows, shard, width),
            struct(rows, half, width), struct(rows, half, width),
        ),
        in_specs=[hbm] * 5 + [vmem] + [hbm] * 5 + [vmem],
        out_specs=(vmem,) * 4 + (hbm,) * 7,
        scratch_shapes=halves(units, part, width) + halves(1, first_rows, pooled_local, width)
        + [scratch(units + up_units, row_count, *packing), scratch(units + up_units, row_count, *packing)]
        + seq_sems(1)
        + [scratch(2, rows, shard, width)] + [scratch(rows, shard, width)] * 3 + [scratch(*w_in.shape)]
        + [
            scratch(buffers, shard, width), scratch(buffers, keys, width), scratch(buffers, keys, width),
            scratch(buffers, PAIRS, keys, 2 * shard), scratch(buffers, shard, width),
            scratch(buffers, shard, width), scratch(buffers, keys, width), scratch(buffers, keys, width),
            scratch(buffers, far, width), scratch(buffers, shard, width),
            scratch(rows, half, width), scratch(rows, half, width),
        ]
        + seq_sems(units) + [dma((units + up_units, row_count)), dma((units + up_units, row_count))]
        + [dma((2,)), dma((4,)), dma((6, buffers)), dma((5, buffers)), dma((2, rows)), dma((2, rows))],
        compiler_params=mesh_params(0),
        name="mid",
    )(n1, attended, g1b, upg, w_in, dsum, q, k_all, v_all, prob, att_grad, down)

    w_in_grad, token_grad, conv_grad, gain_grad, bias_grad = pl.pallas_call(
        functools.partial(tail_kernel, seq_count, row_count, half),
        out_shape=(
            struct(part, 5 * cols, dtype=F32), struct(rows, shard, width, dtype=F32),
            struct(KER, width, dtype=F32), struct(2, width, dtype=F32), struct(2, width, dtype=F32),
        ),
        in_specs=[hbm] * 10 + [vmem] * 3,
        out_specs=(vmem, hbm) + (vmem,) * 3,
        scratch_shapes=halves(10, part, width // 2) + halves(1, rows - first_rows, pooled_local, width)
        + [scratch(10, row_count // 2, *packing), scratch(5, row_count, *packing)]
        + [
            scratch(2, rows, near, width), scratch(rows, near, width), scratch(rows, min(near, far), width),
            scratch(*((2, width // 2, width) if far > near else (8, 128)), dtype=F32),
            scratch(rows, pooled_local, width, dtype=F32),
            scratch(rows, 16, width), scratch(rows, 16, width),
            scratch(2, shard, width), scratch(2, half, width), scratch(2, half, width),
            scratch(2, shard, width, dtype=F32), scratch(rows, 16, width, dtype=F32),
            scratch(16, width, dtype=F32), scratch(bits, 16, width, dtype=F32), scratch(row_count, 16, width, dtype=F32),
        ]
        + seq_sems(10) + [dma((10, row_count // 2)), dma((5, row_count))] + seq_sems(1)
        + [
            dma((2, 4)), dma((3,)), dma((seq_count,)), dma((2,)), dma((3, 2)), dma((2,)), dma((bits, 2)), dma((row_count, 2)),
        ],
        compiler_params=mesh_params(1),
        name="tail",
    )(
        tok_ext, pooled_all, dq, dk, dv, dpool, pool_own, own_grad, left_grad, right_grad,
        window_seg, conv_kernel, norm_sums,
    )
    results = (
        layer_out, token_grad, w_in_grad, w_out_grad, w_up_grad, w_down_grad, conv_grad, gain_grad, bias_grad,
    )
    splits = tuple(4 if x.ndim == 3 else 1 for x in results)
    done = pl.pallas_call(
        functools.partial(finish_kernel, splits),
        out_shape=tuple(struct(*x.shape, dtype=x.dtype) for x in results),
        in_specs=[hbm] * 9,
        out_specs=(hbm,) * 9,
        scratch_shapes=[scratch(*x.shape, dtype=x.dtype) for x in results] + [dma((sum(splits),)), dma((sum(splits),))],
        compiler_params=pltpu.CompilerParams(vmem_limit_bytes=60 * MB),
        name="finish",
    )(*results)
    return done[:5] + (done[5].T,) + done[6:]


def solution(mesh):
    placed = (
        P("row", "seq", None), P("row", None), P(), P(), P(), P(), P(), P(), P(), P("row", "seq", None),
    )
    return jax.shard_map(
        body,
        mesh=mesh,
        in_specs=placed,
        out_specs=(
            P("row", "seq", None), P("row", "seq", None), P("seq", "row"), P("seq", "row"),
            P("seq", "row"), P("seq", "row"), P(), P(), P(),
        ),
        check_vma=False,
    )
```

```python
import functools

import jax
import jax.numpy as jnp
from jax import lax
from jax.experimental import pallas as pl
from jax.experimental.pallas import tpu as pltpu
from jax.sharding import PartitionSpec as P

HEADS = 12
HEAD = 64
WIN = 128
KER = 5
STR = 4
PAIRS = HEADS // 2

EPSILON = 1e-05
ROOT_HALF = 0.7071067811865476
INV_ROOT_2PI = 0.3989422804014327
NEG_LARGE = -1e30
BF = jnp.bfloat16
F32 = jnp.float32
MB = 1 << 20
MESH = pl.DeviceIdType.MESH


def dot(a, b, ca=1, cb=0):
    return lax.dot_general(a, b, (((ca,), (cb,)), ((), ())), preferred_element_type=F32)


def tap_select(seg_row, half, pooled_local):
    width = seg_row.shape[1]
    shape = (KER * pooled_local, width)
    rows = lax.broadcasted_iota(jnp.int32, shape, 0)
    cols = lax.broadcasted_iota(jnp.int32, shape, 1)
    tap = rows // pooled_local
    centre = half + STR * (rows - tap * pooled_local)
    seg = jnp.broadcast_to(seg_row, shape)
    centre_seg = jnp.sum(jnp.where(cols == centre, seg, 0), axis=1, keepdims=True)
    hit = (cols == centre + tap - KER // 2) & (seg == centre_seg)
    return jnp.where(hit, 1.0, 0.0).astype(BF)


def front_kernel(
    seq_count, half, buffers,
    tok_hbm, w_hbm, wseg_ref, fseg_ref, ker_ref,
    ext_hbm, pool_hbm, q_hbm, k_hbm, v_hbm, p_hbm, att_hbm,
    tokx, rim_in, pool_ref, w_ref, qb, knb, vnb, kfb, vfb, pb, attb,
    load_sem, line_sem, gather_sem, near_sem, far_sem, ext_sem, pool_sem,
):
    bits = seq_count.bit_length() - 1
    rows, near, width = tokx.shape
    shard = near - 2 * half
    keys = k_hbm.shape[1]
    pooled_local = pool_ref.shape[bits + 1]
    seq = lax.axis_index("seq")
    has_prev = seq > 0
    has_next = seq < seq_count - 1
    edge = 16

    def flipped(dim):
        weight = 1 << (bits - 1 - dim)
        return seq + (1 - 2 * ((seq // weight) % 2)) * weight

    def line(n, src, dst, step):
        return pltpu.make_async_remote_copy(
            src_ref=src, dst_ref=dst, send_sem=line_sem.at[n, 0], recv_sem=line_sem.at[n, 1],
            device_id={"seq": seq + step}, device_id_type=MESH,
        )

    rim = line(0, tok_hbm.at[:, shard - edge :], rim_in, 1)
    to_next = line(1, tok_hbm.at[:, shard - half :], tokx.at[:, :half], 1)
    to_prev = line(2, tok_hbm.at[:, :half], tokx.at[:, half + shard :], -1)

    rest = list(range(bits - 1))
    cut = len(rest) // 2
    orders = (rest[::-1] + [bits - 1], rest[:cut][::-1] + rest[cut:][::-1] + [bits - 1])

    def gather(part, stage, group):
        order = orders[part]
        done = order[:stage]
        index = tuple(
            slice(None) if d in done else (seq // (1 << (bits - 1 - d))) % 2 for d in range(bits)
        )
        cols = slice(part * (width // 2), (part + 1) * (width // 2))
        some = slice(group * rows // 2, (group + 1) * rows // 2)
        block = pool_ref.at[index + (some, slice(None), cols)]
        return pltpu.make_async_remote_copy(
            src_ref=block, dst_ref=block, send_sem=gather_sem.at[part, stage, 2 * group],
            recv_sem=gather_sem.at[part, stage, 2 * group + 1],
            device_id={"seq": flipped(order[stage])}, device_id_type=MESH,
        )

    own = slice(half, half + shard)
    own_load = pltpu.make_async_copy(tok_hbm, tokx.at[:, own], load_sem.at[0])
    w_load = pltpu.make_async_copy(w_hbm, w_ref, load_sem.at[1])
    own_load.start()
    w_load.start()
    sem = pltpu.get_barrier_semaphore()
    peers = [flipped(d) for d in range(bits)] + [(seq + 1) % seq_count, (seq + seq_count - 1) % seq_count]
    for peer in peers:
        pl.semaphore_signal(sem, inc=1, device_id={"seq": peer}, device_id_type=MESH)
    pl.semaphore_wait(sem, len(peers))

    @pl.when(has_next)
    def _():
        rim.start()
        to_next.start()

    @pl.when(has_prev)
    def _():
        to_prev.start()

    @pl.when(jnp.logical_not(has_prev))
    def _():
        rim_in[...] = jnp.zeros_like(rim_in)
        tokx[:, :half] = jnp.zeros((rows, half, width), BF)

    @pl.when(jnp.logical_not(has_next))
    def _():
        tokx[:, half + shard :] = jnp.zeros((rows, half, width), BF)

    own_load.wait()

    @pl.when(has_prev)
    def _():
        rim.wait_recv()

    mine = tuple((seq // (1 << (bits - 1 - d))) % 2 for d in range(bits))

    def pool_step(r, carry):
        stretch = jnp.concatenate([rim_in[r], tokx[r, own]], axis=0)
        picked = dot(tap_select(wseg_ref[pl.ds(r, 1), half - edge : half + shard], edge, pooled_local), stretch)
        total = picked[:pooled_local] * ker_ref[0:1]
        for t in range(1, KER):
            total = total + picked[t * pooled_local : (t + 1) * pooled_local] * ker_ref[t : t + 1]
        pool_ref[mine + (r,)] = total.astype(BF)
        return carry

    def onward(group, stage):
        for part in range(2):
            if stage:
                gather(part, stage - 1, group).wait()
            if stage < bits:
                gather(part, stage, group).start()

    for group in range(2):
        lax.fori_loop(group * rows // 2, (group + 1) * rows // 2, pool_step, 0)
        onward(group, 0)
    w_load.wait()
    scale = HEAD ** (-0.5)

    def own_step(r, carry):
        x = tokx[pl.ds(2 * r, 2), own].reshape(2 * shard, width)
        qb[pl.ds(2 * r, 2)] = (dot(x, w_ref[:, :width]) * scale).astype(BF).reshape(2, shard, width)
        knb[pl.ds(2 * r, 2), own] = dot(x, w_ref[:, width : 2 * width]).astype(BF).reshape(2, shard, width)
        vnb[pl.ds(2 * r, 2), own] = dot(x, w_ref[:, 2 * width : 3 * width]).astype(BF).reshape(2, shard, width)
        return carry

    lax.fori_loop(0, rows // 2, own_step, 0)
    onward(0, 1)
    onward(1, 1)

    @pl.when(has_prev)
    def _():
        to_next.wait_recv()

    @pl.when(has_next)
    def _():
        to_prev.wait_recv()

    def halo_step(r, carry):
        x = tokx[pl.ds(2 * r, 2), :half].reshape(2 * half, width)
        y = tokx[pl.ds(2 * r, 2), half + shard :].reshape(2 * half, width)
        x = jnp.concatenate([x, y], axis=0)
        for ref, first in ((knb, width), (vnb, 2 * width)):
            both = dot(x, w_ref[:, first : first + width]).astype(BF)
            ref[pl.ds(2 * r, 2), :half] = both[: 2 * half].reshape(2, half, width)
            ref[pl.ds(2 * r, 2), half + shard :] = both[2 * half :].reshape(2, half, width)
        return carry

    lax.fori_loop(0, rows // 2, halo_step, 0)
    for stage in range(2, bits + 1):
        onward(0, stage)
    ext_store = pltpu.make_async_copy(tokx, ext_hbm, ext_sem)
    ext_store.start()

    def pool_store(block):
        index = tuple((block >> (bits - 1 - d)) & 1 for d in range(bits))
        dst = pool_hbm.at[:, block * pooled_local : (block + 1) * pooled_local]
        return pltpu.make_async_copy(pool_ref.at[index], dst, pool_sem.at[block])

    def near_stores(r):
        pairs = [(qb.at[r], q_hbm.at[r]), (knb.at[r], k_hbm.at[r, :near]), (vnb.at[r], v_hbm.at[r, :near])]
        return [pltpu.make_async_copy(src, dst, near_sem.at[n, r]) for n, (src, dst) in enumerate(pairs)]

    def far_stores(r, slot):
        pairs = [
            (kfb.at[slot], k_hbm.at[r, near:]), (vfb.at[slot], v_hbm.at[r, near:]),
            (pb.at[slot], p_hbm.at[r]), (attb.at[slot], att_hbm.at[r]),
        ]
        return [pltpu.make_async_copy(src, dst, far_sem.at[n, slot]) for n, (src, dst) in enumerate(pairs)]

    lane = lax.broadcasted_iota(jnp.int32, (shard, 2 * HEAD), 1)
    even = lane < HEAD

    def row_step(r, carry):
        slot = r % buffers

        @pl.when(r == 1)
        def _():
            for stage in range(2, bits):
                onward(1, stage)

        @pl.when(r == rows // 2)
        def _():
            onward(1, bits)
            for block in range(seq_count):
                pool_store(block).start()

        for copy in near_stores(r):
            copy.start()

        @pl.when(r >= buffers)
        def _():
            for copy in far_stores(r - buffers, slot):
                copy.wait()

        pooled = pool_ref[(slice(None),) * bits + (r,)].reshape(keys - near, width)
        kfb[slot] = dot(pooled, w_ref[:, 3 * width : 4 * width]).astype(BF)
        vfb[slot] = dot(pooled, w_ref[:, 4 * width :]).astype(BF)
        window = wseg_ref[pl.ds(r, 1), :]
        key_seg = jnp.concatenate([window, fseg_ref[pl.ds(r, 1), :]], axis=1)
        key_seg = jnp.transpose(jnp.broadcast_to(key_seg, (shard, keys)))
        shape = (keys, shard)
        row = lax.broadcasted_iota(jnp.int32, shape, 0)
        col = lax.broadcasted_iota(jnp.int32, shape, 1)
        inside = (row >= near) | ((row >= col) & (row - col <= 2 * half))
        kept = inside & (key_seg == jnp.broadcast_to(window[:, half : half + shard], shape))
        bias = jnp.where(kept, 0.0, NEG_LARGE)
        bias = jnp.concatenate([bias, bias], axis=1)

        def lanes(j):
            return slice(2 * HEAD * j, 2 * HEAD * (j + 1))

        def scores(j):
            qp = qb[r, :, lanes(j)]
            zero = jnp.zeros_like(qp)
            stacked = jnp.concatenate([jnp.where(even, qp, zero), jnp.where(even, zero, qp)], axis=0)
            return (
                dot(knb[r, :, lanes(j)], stacked, 1, 1) + bias[:near],
                dot(kfb[slot, :, lanes(j)], stacked, 1, 1) + bias[near:],
            )

        def softmax(close, wide):
            top = jnp.maximum(jnp.max(close, axis=0, keepdims=True), jnp.max(wide, axis=0, keepdims=True))
            close = jnp.exp(close - top)
            wide = jnp.exp(wide - top)
            share = 1.0 / (jnp.sum(close, axis=0, keepdims=True) + jnp.sum(wide, axis=0, keepdims=True))
            return (close * share).astype(BF), (wide * share).astype(BF)

        def mix(j, close, wide):
            pb[slot, j, :near] = close
            pb[slot, j, near:] = wide
            mixed = dot(vnb[r, :, lanes(j)], close, 0, 0) + dot(vfb[slot, :, lanes(j)], wide, 0, 0)
            mixed = jnp.concatenate([mixed[:HEAD, :shard], mixed[HEAD:, shard:]], axis=0)
            attb[slot, :, lanes(j)] = jnp.transpose(mixed).astype(BF)

        current, ready = scores(0), None
        for j in range(PAIRS):
            after = scores(j + 1) if j + 1 < PAIRS else None
            if ready is not None:
                mix(j - 1, *ready)
            ready, current = softmax(*current), after
        mix(PAIRS - 1, *ready)
        for copy in far_stores(r, slot):
            copy.start()
        return carry

    lax.fori_loop(0, rows, row_step, 0)
    for n in range(buffers):
        r = rows - buffers + n
        for copy in far_stores(r, r % buffers):
            copy.wait()
    for r in range(rows):
        for copy in near_stores(r):
            copy.wait()
    for block in range(seq_count):
        pool_store(block).wait()
    ext_store.wait()

    @pl.when(has_next)
    def _():
        rim.wait_send()
        to_next.wait_send()

    @pl.when(has_prev)
    def _():
        to_prev.wait_send()


def stage_orders(bits):
    rest = list(range(bits - 1))
    cut = len(rest) // 2
    return (
        [bits - 1] + rest[::-1],
        [bits - 1] + rest[:cut][::-1] + rest[cut:][::-1],
    )


def packed_shape(part, cols):
    return (part + part // 2, 128) if cols == 192 and part % 32 == 0 else (part, cols)


def packed(x):
    part, cols = x.shape
    if packed_shape(part, cols) == x.shape:
        return x
    rest = jnp.concatenate([x[: part // 2, 128:], x[part // 2 :, 128:]], axis=1)
    return jnp.concatenate([x[:, :128], rest], axis=0)


def unpacked(x, part, cols):
    if x.shape == (part, cols):
        return x
    rest = jnp.concatenate([x[part:, :64], x[part:, 64:]], axis=0)
    return jnp.concatenate([x[:part], rest], axis=1)


class RowSum:
    def __init__(self, row_count, units, blocks, cols, dest, zsend, zrecv, send_sem, recv_sem):
        self.row = lax.axis_index("row")
        self.row_count, self.units, self.blocks, self.cols, self.dest = row_count, units, blocks, cols, dest
        self.zsend, self.zrecv, self.send_sem, self.recv_sem = zsend, zrecv, send_sem, recv_sem

    def copy(self, unit, i, target, slot):
        return pltpu.make_async_remote_copy(
            src_ref=self.zsend.at[unit, i],
            dst_ref=self.zrecv.at[slot, self.row],
            send_sem=self.send_sem.at[unit, i],
            recv_sem=self.recv_sem.at[slot, self.row],
            device_id={"row": target},
            device_id_type=MESH,
        )

    def send(self, unit, total):
        for i in range(self.blocks):
            self.zsend[unit, i] = packed(total[:, i * self.cols : (i + 1) * self.cols].astype(BF))
        for i in range(self.blocks):
            target, slot = self.dest(unit, i)

            @pl.when(self.row != target)
            def _():
                self.copy(unit, i, target, slot).start()

    def arrived(self, slot, unit, i, part):
        total = self.zsend[unit, i].astype(F32)
        for k in range(1, self.row_count):
            other = (self.row + k) % self.row_count
            pltpu.make_async_remote_copy(
                src_ref=self.zsend.at[0, 0],
                dst_ref=self.zrecv.at[slot, other],
                send_sem=self.send_sem.at[0, 0],
                recv_sem=self.recv_sem.at[slot, other],
                device_id={"row": other},
                device_id_type=MESH,
            ).wait_recv()
            total = total + self.zrecv[slot, other].astype(F32)
        return unpacked(total, part, self.cols)

    def sent(self):
        for unit in range(self.units):
            for i in range(self.blocks):
                target, slot = self.dest(unit, i)

                @pl.when(self.row != target)
                def _():
                    self.copy(unit, i, target, slot).wait_send()


class Reducer:
    def __init__(self, seq_count, units, held, bufs, send_sem, recv_sem, take, flip=0):
        self.take = take
        self.flip = flip
        self.bits = seq_count.bit_length() - 1
        self.units = units
        self.held, self.bufs = held, bufs
        self.send_sem, self.recv_sem = send_sem, recv_sem
        self.seq = lax.axis_index("seq")
        self.orders = stage_orders(self.bits)

    def bit(self, dim):
        weight = 1 << (self.bits - 1 - dim)
        value = (self.seq // weight) % 2
        return value, self.seq + (1 - 2 * value) * weight

    def barrier(self, line=False, row_count=1):
        sem = pltpu.get_barrier_semaphore()
        count = 1 << self.bits
        row = lax.axis_index("row")
        peers = [{"seq": self.bit(dim)[1]} for dim in range(self.bits)]
        peers += [{"row": (row + k) % row_count} for k in range(1, row_count)]
        if line:
            peers += [{"seq": (self.seq + 1) % count}, {"seq": (self.seq + count - 1) % count}]
        for peer in peers:
            pl.semaphore_signal(sem, inc=1, device_id=peer, device_id_type=MESH)
        pl.semaphore_wait(sem, len(peers))

    def position(self, unit, stage):
        order = self.orders[(unit + self.flip) % 2]
        left = sorted(order[stage:])
        return order[stage], left.index(order[stage])

    def source(self, unit, stage, value):
        pos = self.position(unit, stage)[1]
        base, slot = (self.held, unit % self.held.shape[0]) if stage == 0 else (self.bufs[stage - 1], unit)
        return base, (slot,) + (slice(None),) * pos + (value,)

    def copy(self, unit, stage):
        value, partner = self.bit(self.position(unit, stage)[0])
        base, index = self.source(unit, stage, 1 - value)
        return pltpu.make_async_remote_copy(
            src_ref=base.at[index],
            dst_ref=self.bufs[stage].at[unit],
            send_sem=self.send_sem.at[unit, stage],
            recv_sem=self.recv_sem.at[unit, stage],
            device_id={"seq": partner},
            device_id_type=MESH,
        )

    def start(self, unit):
        self.copy(unit, 0).start()

    def advance(self, unit, stage):
        self.copy(unit, stage - 1).wait()
        dim, pos = self.position(unit, stage - 1)
        value = self.bit(dim)[0]
        buf = self.bufs[stage - 1]
        base, _ = self.source(unit, stage - 1, value)
        slot = unit % self.held.shape[0] if stage == 1 else unit
        lead = self.bits - stage
        total = None
        for flat in range(1 << lead):
            index = tuple((flat >> (lead - 1 - d)) & 1 for d in range(lead))
            own = base[(slot,) + index[:pos] + (value,) + index[pos:]]
            if stage < self.bits:
                buf[(unit,) + index] = own + buf[(unit,) + index]
            else:
                total = own.astype(F32) + buf[(unit,) + index].astype(F32)
        if stage < self.bits:
            self.copy(unit, stage).start()
            return
        self.take(unit, total)

    def finish_plan(self, plan):
        if not plan:
            for stage in range(1, self.bits + 1):
                for unit in range(self.units):
                    self.advance(unit, stage)

    def follow(self, plan, *place):
        for unit, stage in plan.get(place, ()):
            self.advance(unit, stage)


def split_index(flat, bits):
    return tuple((flat >> (bits - 1 - d)) & 1 for d in range(bits))


def mlp_kernel(
    seq_count,
    tok_hbm, att_hbm, cot_hbm, wo_hbm, wu_hbm, wd_hbm, gain_ref, bias_ref,
    out_hbm, upg_hbm, n1_hbm, g1b_hbm, da_hbm, dsum_ref, small_ref, down_ref,
    held, *rest,
):
    bits = seq_count.bit_length() - 1
    bufs = rest[:bits]
    (
        wo_ref, wu_ref, wd_ref, tokw, attw, cotw, actw, slopew, r2w, gradw, hatw, rstdw, outw, n1w,
        send_sem, recv_sem, w_sem, in_sem, out_sem,
    ) = rest[bits:]
    rows, shard, width = tokw.shape
    hidden = wu_ref.shape[1]
    units = hidden // width
    part = width // seq_count
    tall = width // 2
    chunk = 512
    block = 2 * shard
    blocks = rows // 2
    gain_a, gain_b = gain_ref[0:1], gain_ref[1:2]

    def take(unit, total):
        down_ref[unit] = total.astype(BF)

    red = Reducer(seq_count, units, held, bufs, send_sem, recv_sem, take)
    plan = {}
    if bits == 3 and units == 4 and blocks == 4:
        plan = {
            (0, 0): [(0, 1), (1, 1)], (1, 0): [(2, 1), (3, 1), (0, 2), (1, 2)],
            (3, 0): [(2, 2), (3, 2), (0, 3), (1, 3)], ("end",): [(2, 3), (3, 3)],
        }

    def mean(x):
        return jnp.mean(x, axis=-1, keepdims=True)

    chunks = hidden // chunk

    def up_load(c):
        cols = slice(c * chunk, (c + 1) * chunk)
        return pltpu.make_async_copy(wu_hbm.at[:, cols], wu_ref.at[:, cols], w_sem.at[1 + c])

    def down_load(c):
        part_rows = slice(c * chunk, (c + 1) * chunk)
        return pltpu.make_async_copy(wd_hbm.at[part_rows], wd_ref.at[part_rows], w_sem.at[1 + chunks + c])

    out_load = pltpu.make_async_copy(wo_hbm, wo_ref, w_sem.at[0])

    def loads(b):
        pairs = [(tok_hbm, tokw), (att_hbm, attw), (cot_hbm, cotw)]
        return [
            pltpu.make_async_copy(src.at[pl.ds(2 * b, 2)], dst.at[pl.ds(2 * b, 2)], in_sem.at[n, b])
            for n, (src, dst) in enumerate(pairs)
        ]

    def stores(b, first):
        pairs = [(outw, out_hbm), (n1w, n1_hbm), (actw, upg_hbm), (r2w, g1b_hbm), (tokw, da_hbm)]
        return [
            pltpu.make_async_copy(pairs[n][0].at[pl.ds(2 * b, 2)], pairs[n][1].at[pl.ds(2 * b, 2)], out_sem.at[n, b])
            for n in (range(2) if first else range(2, 5))
        ]

    out_load.start()
    for copy in loads(0):
        copy.start()
    for c in range(chunks):
        up_load(c).start()
        down_load(c).start()
    for b in range(1, blocks):
        for copy in loads(b):
            copy.start()
    red.barrier()
    small_ref[...] = jnp.zeros_like(small_ref)

    def flat(ref, b):
        return ref[pl.ds(2 * b, 2)].reshape(block, ref.shape[2])

    def put(ref, b, value):
        ref[pl.ds(2 * b, 2)] = value.reshape(2, shard, ref.shape[2])

    def forward_step(b, carry):
        for copy in loads(b):
            copy.wait()

        rows_b = pl.ds(2 * b, 2)
        resid = flat(tokw, b).astype(F32) + dot(flat(attw, b), wo_ref[...])
        centred = resid - mean(resid)
        rstd_a = lax.rsqrt(mean(centred * centred) + EPSILON)
        hat_a = centred * rstd_a
        put(hatw, b, hat_a)
        rstdw[rows_b] = rstd_a.reshape(2, shard, 1)
        normed = hat_a * gain_a + bias_ref[0:1]
        low = normed.astype(BF)
        put(n1w, b, low)
        total = normed

        def raised(c):
            return dot(low, wu_ref[:, c * chunk : (c + 1) * chunk])

        def lowered(c, act):
            return dot(act, wd_ref[c * chunk : (c + 1) * chunk, :])

        for c in range(chunks):
            up = raised(c)
            half_cdf = 0.5 * (1.0 + lax.erf(up * ROOT_HALF))
            ready = (up * half_cdf).astype(BF)
            cols = slice(c * chunk, (c + 1) * chunk)
            actw[rows_b, :, cols] = ready.reshape(2, shard, chunk)
            slope = half_cdf + up * (INV_ROOT_2PI * jnp.exp(-0.5 * up * up))
            slopew[rows_b, :, cols] = slope.astype(BF).reshape(2, shard, chunk)
            total = total + lowered(c, ready)
        centred = total - mean(total)
        rstd_b = lax.rsqrt(mean(centred * centred) + EPSILON)
        hat_b = centred * rstd_b
        put(outw, b, (hat_b * gain_b + bias_ref[1:2]).astype(BF))
        for copy in stores(b, True):
            copy.start()
        g = flat(cotw, b).astype(F32)
        small_ref[1:2] += jnp.sum(g * hat_b, axis=0, keepdims=True)
        small_ref[3:4] += jnp.sum(g, axis=0, keepdims=True)
        e = g * gain_b
        grad = rstd_b * (e - mean(e) - hat_b * mean(e * hat_b))
        put(gradw, b, grad)
        put(r2w, b, grad.astype(BF))
        return carry

    out_load.wait()
    for c in range(chunks):
        up_load(c).wait()
        down_load(c).wait()
    lax.fori_loop(0, blocks, forward_step, 0)

    for c in range(hidden // tall):
        left = actw[:, :, tall * c : tall * (c + 1)].reshape(-1, tall)
        total = dot(left, r2w[...].reshape(-1, width), 0, 0)
        blocked = total.reshape(tall // part, part, width).astype(BF)
        for n in range(tall // part):
            place = (c * tall + n * part) // part
            held[(place % units,) + split_index(place // units, bits)] = blocked[n]
    for u in range(units):
        red.start(u)

    def backward_step(b, carry):
        rows_b = pl.ds(2 * b, 2)

        def advance(half_step):
            for t in range(blocks):
                if (t, half_step) in plan:

                    @pl.when(b == t)
                    def _():
                        red.follow(plan, t, half_step)

        advance(0)
        grad = flat(gradw, b)
        grad_low = flat(r2w, b)

        def raised(c):
            return dot(grad_low, wd_ref[c * chunk : (c + 1) * chunk, :], 1, 1)

        def lowered(c, up_grad):
            return dot(up_grad, wu_ref[:, c * chunk : (c + 1) * chunk], 1, 1)

        current, ready = raised(0), None
        for c in range(chunks):
            after = raised(c + 1) if c + 1 < chunks else None
            if ready is not None:
                grad = grad + lowered(c - 1, ready)
            cols = slice(c * chunk, (c + 1) * chunk)
            slope = slopew[rows_b, :, cols].reshape(block, chunk).astype(F32)
            ready = (current * slope).astype(BF)
            actw[rows_b, :, cols] = ready.reshape(2, shard, chunk)
            current = after
        grad = grad + lowered(chunks - 1, ready)
        hat_a = flat(hatw, b)
        small_ref[0:1] += jnp.sum(grad * hat_a, axis=0, keepdims=True)
        small_ref[2:3] += jnp.sum(grad, axis=0, keepdims=True)
        e = grad * gain_a
        resid_grad = rstdw[rows_b].reshape(block, 1) * (e - mean(e) - hat_a * mean(e * hat_a))
        resid_low = resid_grad.astype(BF)
        put(r2w, b, resid_low)
        att_grad = dot(resid_low, wo_ref[...], 1, 1).astype(BF)
        put(tokw, b, att_grad)
        for copy in stores(b, False):
            copy.start()
        prod = att_grad.astype(F32) * flat(attw, b).astype(F32)
        high = prod.astype(BF)
        rest = (prod - high.astype(F32)).astype(BF)
        heads = dsum_ref.shape[0]
        head_row = lax.broadcasted_iota(jnp.int32, (heads, width), 0)
        head_col = lax.broadcasted_iota(jnp.int32, (heads, width), 1) // HEAD
        pick = jnp.where(head_row == head_col, 1.0, 0.0).astype(BF)
        dsum_ref[:, pl.ds(pl.multiple_of(b * block, block), block)] = dot(pick, high, 1, 1) + dot(pick, rest, 1, 1)
        return carry

    lax.fori_loop(0, blocks, backward_step, 0)
    red.finish_plan(plan)
    red.follow(plan, "end")
    for b in range(blocks):
        for copy in stores(b, True) + stores(b, False):
            copy.wait()


def mid_kernel(
    seq_count, row_count, half, buffers,
    n1_hbm, att_hbm, g1b_hbm, upg_hbm, w_hbm, dsum_ref,
    q_hbm, k_hbm, v_hbm, p_hbm, da_hbm, down_ref,
    wout_ref, wup_ref, wdown_ref, pown_ref, dq_hbm, dk_hbm, dv_hbm, dpool_hbm, own_hbm, left_hbm, right_hbm,
    held, *rest,
):
    bits = seq_count.bit_length() - 1
    bufs, rest = rest[:bits], rest[bits:]
    pheld, pbufs, rest = rest[0], rest[1 : 1 + bits], rest[1 + bits :]
    (
        zsend, zrecv, psend_sem, precv_sem, slots, n1_ref, att_ref, g1b_ref, w_ref,
        qb, kb, vb, pb, dab, dqb, dkb, dvb, dpb, owb, lfb, rtb,
        send_sem, recv_sem, zsend_sem, zrecv_sem, load_sem, once_sem, in_sem, out_sem, line_send, line_recv,
    ) = rest
    rows, shard, width = n1_ref.shape
    near = shard + 2 * half
    part = width // seq_count
    up_units = upg_hbm.shape[2] // width
    units = up_units + 1
    tall = width // 2
    steps = up_units
    first_rows, pooled_local = pown_ref.shape[:2]

    def dest(unit, i):
        if unit < up_units:
            g = unit * row_count + i
            return g // up_units, g % up_units
        return i, unit

    cols = width // row_count
    down_units = down_ref.shape[0]
    sums = RowSum(row_count, units + down_units, row_count, cols, dest, zsend, zrecv, zsend_sem, zrecv_sem)
    red = Reducer(seq_count, units, held, bufs, send_sem, recv_sem, sums.send, 1)

    def take(unit, total):
        pown_ref[...] = total

    pred = Reducer(seq_count, 1, pheld, pbufs, psend_sem, precv_sem, take, 1)
    once = [
        pltpu.make_async_copy(src, dst, once_sem.at[n])
        for n, (src, dst) in enumerate([(n1_hbm, n1_ref), (att_hbm, att_ref), (g1b_hbm, g1b_ref), (w_hbm, w_ref)])
    ]

    def load(k):
        return pltpu.make_async_copy(
            upg_hbm.at[:, :, width * k : width * (k + 1)], slots.at[k % 2], load_sem.at[k % 2]
        )

    def taken(k):
        load(k).wait()
        if k + 1 < steps:
            load(k + 1).start()

    def row_loads(r, slot):
        pairs = [(p_hbm, pb), (k_hbm, kb), (v_hbm, vb), (q_hbm, qb), (da_hbm, dab)]
        return [
            pltpu.make_async_copy(src.at[r], dst.at[slot], in_sem.at[n, slot])
            for n, (src, dst) in enumerate(pairs)
        ]

    def row_stores(r, slot):
        pairs = [(dqb, dq_hbm), (dkb, dk_hbm), (dvb, dv_hbm), (owb, own_hbm)]
        return [
            pltpu.make_async_copy(src.at[slot], dst.at[r], out_sem.at[n, slot])
            for n, (src, dst) in enumerate(pairs)
        ]

    def pool_store(r, slot):
        return pltpu.make_async_copy(dpb.at[slot], dpool_hbm.at[r - first_rows], out_sem.at[4, slot])

    has_prev = red.seq > 0
    has_next = red.seq < seq_count - 1

    def line(n, r):
        src, dst = ((lfb, right_hbm), (rtb, left_hbm))[n]
        return pltpu.make_async_remote_copy(
            src_ref=src.at[r], dst_ref=dst.at[r], send_sem=line_send.at[n, r], recv_sem=line_recv.at[n, r],
            device_id={"seq": red.seq + 2 * n - 1}, device_id_type=MESH,
        )

    sides = ((0, has_prev, has_next), (1, has_next, has_prev))

    once[0].start()
    load(0).start()
    for copy in once[1:]:
        copy.start()
    if buffers > 1:
        for copy in row_loads(0, 0):
            copy.start()
    red.barrier(line=True, row_count=row_count)
    lead = (2,) * (bits - 1)
    plan, pool_plan = {}, {}
    if bits == 3 and up_units == 4 and rows == 8:
        plan = {
            ("up", 1): [(0, 1)], ("up", 2): [(1, 1)], ("up", 4): [(2, 1)],
            ("row", 0): [(3, 1)], ("row", 1): [(0, 2), (4, 1)], ("row", 2): [(1, 2)],
            ("row", 3): [(2, 2), (0, 3)], ("row", 4): [(3, 2), (1, 3)], ("row", 5): [(4, 2), (2, 3)],
            ("row", 6): [(3, 3)], ("row", 7): [(4, 3)],
        }
        pool_plan = {("row", 4): [(0, 1)], ("row", 6): [(0, 2)], ("row", 7): [(0, 3)]}

    def product(unit, left_ref, right):
        for m in range(2):
            left = left_ref[:, :, tall * m : tall * (m + 1)].reshape(-1, tall)
            held[unit, m] = dot(left, right, 0, 0).reshape(lead + (part, width)).astype(BF)

    once[0].wait()
    for u in range(up_units):
        taken(u)
        if u == 0:
            for n in range(down_units):
                sums.send(units + n, down_ref[n])
        product(u, n1_ref, slots[u % 2].reshape(-1, width))
        red.start(u)
        red.follow(plan, "up", u)
    once[1].wait()
    once[2].wait()
    product(up_units, att_ref, g1b_ref[...].reshape(-1, width))
    red.start(up_units)
    red.follow(plan, "up", up_units)
    once[3].wait()

    lane = lax.broadcasted_iota(jnp.int32, (shard, 2 * HEAD), 1)
    even = lane < HEAD

    def stack(pair):
        zero = jnp.zeros_like(pair)
        return jnp.concatenate([jnp.where(even, pair, zero), jnp.where(even, zero, pair)], axis=0)

    def hooks(r, place):
        for t in range(rows):
            begins = place == "row" and t == first_rows
            if (place, t) in plan or (place, t) in pool_plan or begins:

                @pl.when(r == t)
                def _():
                    if begins:
                        pred.start(0)
                    red.follow(plan, place, t)
                    pred.follow(pool_plan, place, t)

    def row_step(r, carry):
        slot = r % buffers
        if buffers > 1:

            @pl.when(r + 1 < rows)
            def _():
                for copy in row_loads(r + 1, (r + 1) % buffers):
                    copy.start()

        else:
            for copy in row_loads(r, slot):
                copy.start()
        hooks(r, "row")
        for copy in row_loads(r, slot):
            copy.wait()

        @pl.when(r >= buffers)
        def _():
            for copy in row_stores(r - buffers, slot):
                copy.wait()

        @pl.when(r >= buffers + first_rows)
        def _():
            pool_store(r - buffers, slot).wait()

        row_sums = dsum_ref[:, pl.ds(pl.multiple_of(r * shard, shard), shard)]

        def lanes(j):
            return slice(2 * HEAD * j, 2 * HEAD * (j + 1))

        def dprobs(j):
            return dot(vb[slot, :, lanes(j)], stack(dab[slot, :, lanes(j)]), 1, 1)

        def dscores(j, dprob):
            row_dot = jnp.concatenate([row_sums[2 * j : 2 * j + 1], row_sums[2 * j + 1 : 2 * j + 2]], axis=1)
            return (pb[slot, j].astype(F32) * (dprob - row_dot)).astype(BF)

        def products(j, dscore):
            dvb[slot, :, lanes(j)] = dot(pb[slot, j], stack(dab[slot, :, lanes(j)])).astype(BF)
            dkb[slot, :, lanes(j)] = dot(dscore, stack(qb[slot, :, lanes(j)])).astype(BF)
            mixed = dot(kb[slot, :, lanes(j)], dscore, 0, 0)
            mixed = jnp.concatenate([mixed[:HEAD, :shard], mixed[HEAD:, shard:]], axis=0)
            dqb[slot, :, lanes(j)] = (jnp.transpose(mixed) * HEAD ** (-0.5)).astype(BF)

        current, ready = dprobs(0), None
        for j in range(PAIRS):
            after = dprobs(j + 1) if j + 1 < PAIRS else None
            if ready is not None:
                products(j - 1, ready)
            ready, current = dscores(j, current), after
        products(PAIRS - 1, ready)
        back = dot(dkb[slot, :near], w_ref[:, width : 2 * width], 1, 1) + dot(
            dvb[slot, :near], w_ref[:, 2 * width : 3 * width], 1, 1
        )
        lfb[r] = back[:half].astype(BF)
        rtb[r] = back[half + shard :].astype(BF)
        own = g1b_ref[r].astype(F32) + back[half : half + shard] + dot(dqb[slot], w_ref[:, :width], 1, 1)
        owb[slot] = own.astype(BF)
        pooled = (
            dot(dkb[slot, near:], w_ref[:, 3 * width : 4 * width], 1, 1)
            + dot(dvb[slot, near:], w_ref[:, 4 * width :], 1, 1)
        ).astype(BF)
        dpb[slot] = pooled

        @pl.when(r < first_rows)
        def _():
            index = (0,) + (slice(None),) * bits + (r,)
            pheld[index] = pooled.reshape((2,) * bits + (pooled_local, width))

        @pl.when(r >= first_rows)
        def _():
            pool_store(r, slot).start()

        for copy in row_stores(r, slot):
            copy.start()
        for n, sends, _ in sides:

            @pl.when(sends)
            def _():
                line(n, r).start()

        return carry

    lax.fori_loop(0, rows, row_step, 0)
    red.finish_plan(plan)
    pred.finish_plan(pool_plan)
    pred.follow(pool_plan, "end")
    for k in range(buffers):
        r = rows - buffers + k
        for copy in row_stores(r, r % buffers):
            copy.wait()
        pool_store(r, r % buffers).wait()
    for n, sends, takes in sides:

        @pl.when(sends)
        def _():
            for r in range(rows):
                line(n, r).wait_send()

        @pl.when(takes)
        def _():
            for r in range(rows):
                line(n, r).wait_recv()

    row = sums.row
    down = [sums.arrived(units + n, units + n, row, part) for n in range(down_units)]
    wdown_ref[...] = jnp.transpose(jnp.concatenate(down, axis=0))
    for n in range(up_units):
        g = row * up_units + n
        wup_ref[:, n * cols : (n + 1) * cols] = sums.arrived(n, g // row_count, g % row_count, part)
    wout_ref[...] = sums.arrived(up_units, up_units, row, part)
    sums.sent()


def tail_kernel(
    seq_count, row_count, half,
    tok_hbm, pool_hbm, dq_hbm, dk_hbm, dv_hbm, dpool_hbm, pown_hbm, own_hbm, left_hbm, right_hbm,
    seg_ref, ker_ref, norm_ref,
    win_ref, out_hbm, conv_ref, gain_ref, bias_ref,
    held, *rest,
):
    bits = seq_count.bit_length() - 1
    bufs, rest = rest[:bits], rest[bits:]
    pheld, pbufs, rest = rest[0], rest[1 : 1 + bits], rest[1 + bits :]
    (
        zsend, zrecv, slots, tok_ref, pool_ref, partial, dpool_own, rim_out, rim_in, ownb, leftb, rightb, outb, edgeb,
        ssum, srecv, zsum,
        send_sem, recv_sem, zsend_sem, zrecv_sem, psend_sem, precv_sem, load_sem, pool_sem, ploads_sem,
        line_sem, own_sem, out_sem, small_sem, zsmall_sem,
    ) = rest
    rows, near, width = tok_ref.shape
    shard = near - 2 * half
    part = width // seq_count
    units = 10
    tall = width // 2
    piece = pool_ref.shape[1]
    pieces = (dk_hbm.shape[1] - near) // piece
    pooled_local = dpool_own.shape[1]
    late_rows = rows - pown_hbm.shape[0]
    edge = 16
    order = (0, 3, 4, 1, 2)

    blocks = row_count // 2

    def dest(unit, i):
        g = order[unit // 2] * row_count + (unit % 2) * blocks + i
        return g // 5, g % 5

    cols = width // row_count
    sums = RowSum(row_count, units, blocks, cols, dest, zsend, zrecv, zsend_sem, zrecv_sem)
    red = Reducer(seq_count, units, held, bufs, send_sem, recv_sem, sums.send)

    def take(unit, total):
        dpool_own[rows - late_rows :] = total

    pred = Reducer(seq_count, 1, pheld, pbufs, psend_sem, precv_sem, take, 1)
    steps = 2 * pieces + 3

    def load(k):
        buf = slots.at[k % 2]
        if k == 0:
            src, dst = dq_hbm, buf.at[:, :shard]
        elif k <= 2 * pieces:
            first = near + ((k - 1) % pieces) * piece
            src, dst = (dk_hbm, dv_hbm)[(k - 1) // pieces].at[:, first : first + piece], buf.at[:, :piece]
        else:
            src, dst = (dk_hbm, dv_hbm)[k - 2 * pieces - 1].at[:, :near], buf
        group = rows // 4
        return [
            pltpu.make_async_copy(
                src.at[n * group : (n + 1) * group], dst.at[n * group : (n + 1) * group], load_sem.at[k % 2, n]
            )
            for n in range(4)
        ]

    def taken(k):
        for copy in load(k):
            copy.wait()
        if k + 1 < steps:
            for copy in load(k + 1):
                copy.start()

    def pool_load(n):
        return pltpu.make_async_copy(pool_hbm.at[:, n * piece : (n + 1) * piece], pool_ref, pool_sem.at[0])

    tok_load = pltpu.make_async_copy(tok_hbm, tok_ref, pool_sem.at[1])

    def grad_load(owner):
        src = dpool_hbm.at[:, owner * pooled_local : (owner + 1) * pooled_local]
        return pltpu.make_async_copy(src, pheld.at[(0,) + split_index(owner, bits)], ploads_sem.at[owner])

    own_pool = pltpu.make_async_copy(pown_hbm, dpool_own.at[: rows - late_rows], pool_sem.at[2])

    rim = pltpu.make_async_remote_copy(
        src_ref=rim_out, dst_ref=rim_in, send_sem=line_sem.at[0], recv_sem=line_sem.at[1],
        device_id={"seq": red.seq - 1}, device_id_type=MESH,
    )
    has_prev = red.seq > 0
    has_next = red.seq < seq_count - 1

    for owner in range(seq_count):
        grad_load(owner).start()
    for copy in load(0):
        copy.start()
    tok_load.start()
    pool_load(0).start()
    own_pool.start()
    red.barrier(line=True, row_count=row_count)
    for owner in range(seq_count):
        grad_load(owner).wait()
    pred.start(0)

    lead = (2,) * (bits - 1)

    def product(unit, left, right, first=True, last=True):
        for m in range(2):
            total = dot(left(m), right, 0, 0)
            if m == 0 and first:
                step("half", unit)
            if not first:
                total = total + partial[m]
            if not last:
                partial[m] = total
                continue
            total = total.reshape(lead + (part, width)).astype(BF)
            for h in range(2):
                held[2 * unit + h, m] = total[..., tall * h : tall * (h + 1)]

    def begin(unit):
        red.start(2 * unit)
        red.start(2 * unit + 1)

    def columns(ref, keep=slice(None)):
        return lambda m: ref[:, keep, tall * m : tall * (m + 1)].reshape(-1, tall)

    def whole(k, length):
        return slots[k % 2, :, :length].reshape(-1, width)

    plan, pool_plan = {}, {}
    if bits == 3 and rows == 8:
        plan = {
            ("half", 1): [(0, 1), (1, 1)], ("half", 2): [(2, 1), (3, 1)], ("half", 3): [(4, 1), (5, 1), (0, 2), (1, 2)],
            ("half", 4): [(6, 1), (7, 1), (2, 2), (3, 2)], ("row", 0): [(0, 3), (1, 3)],
            ("row", 1): [(8, 1), (9, 1)], ("row", 2): [(4, 2), (5, 2)], ("row", 3): [(2, 3), (3, 3)],
            ("row", 5): [(6, 2), (7, 2)], ("row", 7): [(4, 3), (5, 3)], ("end", 0): [(6, 3), (7, 3)],
            ("end", 1): [(8, 2), (9, 2)], ("end", 3): [(8, 3), (9, 3)],
        }
        pool_plan = {("done", 0): [(0, 1)], ("half", 3): [(0, 2)], ("row", 4): [(0, 3)]}

    def step(*place):
        red.follow(plan, *place)
        pred.follow(pool_plan, *place)

    own = slice(half, half + shard)
    tok_load.wait()
    taken(0)
    product(0, columns(tok_ref, own), whole(0, shard))
    begin(0)
    step("done", 0)
    for n in range(2):
        for c in range(pieces):
            k = 1 + n * pieces + c
            if pieces > 1 and (n or c):
                pool_load(c).start()
            if pieces > 1 or n == 0:
                pool_load(c).wait()
            taken(k)
            product(1 + n, columns(pool_ref), whole(k, piece), c == 0, c == pieces - 1)
        begin(1 + n)
    for n in range(2):
        k = 1 + 2 * pieces + n
        taken(k)
        product(3 + n, columns(tok_ref), whole(k, near))
        begin(3 + n)
    own_pool.wait()
    pred.finish_plan(pool_plan)

    ssum[...] = jnp.zeros_like(ssum)
    ssum[8:12] = norm_ref[0:4]

    def row_loads(r, slot):
        pairs = [(own_hbm, ownb), (left_hbm, leftb), (right_hbm, rightb)]
        return [
            pltpu.make_async_copy(src.at[r], dst.at[slot], own_sem.at[n, slot])
            for n, (src, dst) in enumerate(pairs)
        ]

    def out_store(r, slot):
        return pltpu.make_async_copy(
            outb.at[slot, : shard - edge], out_hbm.at[r, : shard - edge], out_sem.at[slot]
        )

    for copy in row_loads(0, 0):
        copy.start()

    def pool_step(r, carry):
        slot = r % 2

        @pl.when(r + 1 < rows)
        def _():
            for copy in row_loads(r + 1, (r + 1) % 2):
                copy.start()

        for t in range(rows):
            if ("row", t) in plan or ("row", t) in pool_plan:

                @pl.when(r == t)
                def _():
                    step("row", t)

        select = tap_select(seg_ref[pl.ds(r, 1), half - edge : half + shard], edge, pooled_local)
        picked = dot(select, tok_ref[r, half - edge : half + shard])
        grad = dpool_own[r]
        terms, sums = [], []
        for t in range(KER):
            terms.append((grad * ker_ref[t : t + 1]).astype(BF))
            sums.append(jnp.sum(grad * picked[t * pooled_local : (t + 1) * pooled_local], axis=0, keepdims=True))
        ssum[0:KER] += jnp.concatenate(sums, axis=0)
        spread = dot(select, jnp.concatenate(terms, axis=0), 0, 0)
        rim_out[r] = spread[:edge].astype(BF)
        for copy in row_loads(r, slot):
            copy.wait()

        @pl.when(r >= 2)
        def _():
            out_store(r - 2, slot).wait()

        outb[slot] = ownb[slot].astype(F32) + spread[edge:]

        @pl.when(has_prev)
        def _():
            outb[slot, :half] += leftb[slot].astype(F32)

        @pl.when(has_next)
        def _():
            outb[slot, shard - half :] += rightb[slot].astype(F32)

        edgeb[r] = outb[slot, shard - edge :]
        out_store(r, slot).start()
        return carry

    lax.fori_loop(0, rows, pool_step, 0)

    @pl.when(has_prev)
    def _():
        rim.start()

    def small_copy(stage):
        return pltpu.make_async_remote_copy(
            src_ref=ssum, dst_ref=srecv.at[stage], send_sem=small_sem.at[stage, 0], recv_sem=small_sem.at[stage, 1],
            device_id={"seq": red.bit(bits - 1 - stage)[1]}, device_id_type=MESH,
        )

    def small_row(k):
        other = (sums.row + k) % row_count
        return pltpu.make_async_remote_copy(
            src_ref=ssum, dst_ref=zsum.at[row_count - k], send_sem=zsmall_sem.at[k, 0],
            recv_sem=zsmall_sem.at[row_count - k, 1], device_id={"row": other}, device_id_type=MESH,
        )

    def small_add(stage):
        small_copy(stage).wait()
        ssum[...] += srecv[stage]

    small_copy(0).start()
    step("end", 0)
    small_add(0)
    small_copy(1).start()

    @pl.when(has_next)
    def _():
        rim.wait_recv()
        edgeb[...] += rim_in[...].astype(F32)

    edge_store = pltpu.make_async_copy(edgeb, out_hbm.at[:, shard - edge :], own_sem.at[0, 0])
    edge_store.start()
    step("end", 1)
    small_add(1)
    small_copy(2).start()
    step("end", 2)
    step("end", 3)
    red.finish_plan(plan)
    small_add(2)
    for stage in range(3, bits):
        small_copy(stage).start()
        small_add(stage)
    for k in range(1, row_count):
        small_row(k).start()
    zsum[0] = ssum[...]
    for n in range(5):
        g = sums.row * 5 + n
        block, i = g // row_count, g % row_count
        place = block + 2 * ((block + 4) // 5) - 4 * (block // 3)
        win_ref[:, n * cols : (n + 1) * cols] = sums.arrived(n, 2 * place + i // blocks, i % blocks, part)
    for k in range(1, row_count):
        small_row(row_count - k).wait_recv()
    total = None
    for owner in range(row_count):
        term = zsum[(owner - sums.row + row_count) % row_count]
        total = term if total is None else total + term
    conv_ref[...] = total[:KER]
    gain_ref[...] = total[8:10]
    bias_ref[...] = total[10:12]
    for k in range(1, row_count):
        small_row(k).wait_send()
    sums.sent()
    edge_store.wait()
    for n in range(2):
        out_store(rows - 2 + n, n).wait()

    @pl.when(has_prev)
    def _():
        rim.wait_send()


def finish_kernel(splits, *refs):
    count = len(splits)
    ins, outs, bufs = refs[:count], refs[count : 2 * count], refs[2 * count : 3 * count]
    sem_in, sem_out = refs[3 * count :]
    loads, stores = [], []
    for src, dst, buf, split in zip(ins, outs, bufs, splits):
        length = src.shape[0] // split
        for n in range(split):
            piece = slice(n * length, (n + 1) * length)
            loads.append(pltpu.make_async_copy(src.at[piece], buf.at[piece], sem_in.at[len(loads)]))
            stores.append(pltpu.make_async_copy(buf.at[piece], dst.at[piece], sem_out.at[len(stores)]))
    for copy in loads:
        copy.start()
    for load, store in zip(loads, stores):
        load.wait()
        store.start()
    for copy in stores:
        copy.wait()


def body(tokens, segment_ids, w_in, w_out, w_up, w_down, conv_kernel, norm_gain, norm_bias, cotangent):
    rows, shard, width = tokens.shape
    half = WIN // 2
    pooled_local = shard // STR
    near = shard + 2 * half
    count = rows * shard
    hidden = w_up.shape[1]
    seq_count = lax.axis_size("seq")
    row_count = lax.axis_size("row")
    seq_start = lax.axis_index("seq") * shard
    keys = near + pooled_local * seq_count

    padded_seg = jnp.pad(segment_ids, ((0, 0), (half, half)), constant_values=-1)
    window_seg = lax.dynamic_slice_in_dim(padded_seg, seq_start, near, 1)
    far_seg = segment_ids[:, ::STR]

    def struct(*dims, dtype=BF):
        return jax.ShapeDtypeStruct(dims, dtype)

    bits = seq_count.bit_length() - 1
    far = keys - near
    buffers = 2 if keys <= 2 * near else 1
    vmem = pl.BlockSpec(memory_space=pltpu.VMEM)
    hbm = pl.BlockSpec(memory_space=pl.ANY)
    dma = pltpu.SemaphoreType.DMA

    def scratch(*dims, dtype=BF):
        return pltpu.VMEM(dims, dtype)

    tok_ext, pooled_all, q, k_all, v_all, prob, attended = pl.pallas_call(
        functools.partial(front_kernel, seq_count, half, buffers),
        out_shape=(
            struct(rows, near, width), struct(rows, far, width), struct(rows, shard, width),
            struct(rows, keys, width), struct(rows, keys, width), struct(rows, PAIRS, keys, 2 * shard),
            struct(rows, shard, width),
        ),
        in_specs=[hbm] * 2 + [vmem] * 3,
        out_specs=(hbm,) * 7,
        scratch_shapes=[
            scratch(rows, near, width), scratch(rows, 16, width),
            scratch(*((2,) * bits + (rows, pooled_local, width))), scratch(*w_in.shape),
            scratch(rows, shard, width), scratch(rows, near, width), scratch(rows, near, width),
            scratch(buffers, far, width), scratch(buffers, far, width),
            scratch(buffers, PAIRS, keys, 2 * shard), scratch(buffers, shard, width),
            dma((2,)), dma((3, 2)), dma((2, bits, 4)), dma((3, rows)), dma((4, buffers)), dma, dma((seq_count,)),
        ],
        compiler_params=pltpu.CompilerParams(collective_id=2, has_side_effects=True, vmem_limit_bytes=60 * MB),
        name="front",
    )(tokens, w_in, window_seg, far_seg, conv_kernel)

    part = width // seq_count
    up_units = hidden // width
    cols = width // row_count
    first_rows = rows // 2

    def halves(units, *tail):
        return [pltpu.VMEM((units,) + (2,) * (bits - i) + tail, BF) for i in range(bits + 1)]

    def mesh_params(collective_id):
        return pltpu.CompilerParams(
            collective_id=collective_id, has_side_effects=True, vmem_limit_bytes=60 * MB
        )

    def seq_sems(units):
        return [dma((units, bits)), dma((units, bits))]

    packing = packed_shape(part, cols)

    layer_out, upg, n1, g1b, att_grad, dsum, norm_sums, down = pl.pallas_call(
        functools.partial(mlp_kernel, seq_count),
        out_shape=(
            struct(rows, shard, width), struct(rows, shard, hidden), struct(rows, shard, width),
            struct(rows, shard, width), struct(rows, shard, width),
            struct(16, count, dtype=F32), struct(8, width, dtype=F32), struct(up_units, part, width),
        ),
        in_specs=[hbm] * 6 + [vmem] * 2,
        out_specs=(hbm,) * 5 + (vmem,) * 3,
        scratch_shapes=halves(up_units, part, width)
        + [scratch(*w_out.shape), scratch(*w_up.shape), scratch(*w_down.shape)]
        + [scratch(rows, shard, width)] * 3 + [scratch(rows, shard, hidden)] * 2
        + [
            scratch(rows, shard, width), scratch(rows, shard, width, dtype=F32), scratch(rows, shard, width, dtype=F32),
            scratch(rows, shard, 1, dtype=F32), scratch(rows, shard, width), scratch(rows, shard, width),
        ]
        + seq_sems(up_units) + [dma((1 + hidden // 256,)), dma((3, rows // 2)), dma((5, rows // 2))],
        compiler_params=mesh_params(3),
        name="mlp",
    )(tokens, attended, cotangent, w_out, w_up, w_down, norm_gain, norm_bias)

    units = up_units + 1
    (
        w_out_grad, w_up_grad, w_down_grad, pool_own, dq, dk, dv, dpool, own_grad, left_grad, right_grad,
    ) = pl.pallas_call(
        functools.partial(mid_kernel, seq_count, row_count, half, buffers),
        out_shape=(
            struct(part, cols, dtype=F32), struct(part, up_units * cols, dtype=F32),
            struct(cols, up_units * part, dtype=F32), struct(first_rows, pooled_local, width, dtype=F32),
            struct(rows, shard, width), struct(rows, keys, width), struct(rows, keys, width),
            struct(rows - first_rows, far, width), struct(rows, shard, width),
            struct(rows, half, width), struct(rows, half, width),
        ),
        in_specs=[hbm] * 5 + [vmem] + [hbm] * 5 + [vmem],
        out_specs=(vmem,) * 4 + (hbm,) * 7,
        scratch_shapes=halves(units, part, width) + halves(1, first_rows, pooled_local, width)
        + [scratch(units + up_units, row_count, *packing), scratch(units + up_units, row_count, *packing)]
        + seq_sems(1)
        + [scratch(2, rows, shard, width)] + [scratch(rows, shard, width)] * 3 + [scratch(*w_in.shape)]
        + [
            scratch(buffers, shard, width), scratch(buffers, keys, width), scratch(buffers, keys, width),
            scratch(buffers, PAIRS, keys, 2 * shard), scratch(buffers, shard, width),
            scratch(buffers, shard, width), scratch(buffers, keys, width), scratch(buffers, keys, width),
            scratch(buffers, far, width), scratch(buffers, shard, width),
            scratch(rows, half, width), scratch(rows, half, width),
        ]
        + seq_sems(units) + [dma((units + up_units, row_count)), dma((units + up_units, row_count))]
        + [dma((2,)), dma((4,)), dma((6, buffers)), dma((5, buffers)), dma((2, rows)), dma((2, rows))],
        compiler_params=mesh_params(0),
        name="mid",
    )(n1, attended, g1b, upg, w_in, dsum, q, k_all, v_all, prob, att_grad, down)

    w_in_grad, token_grad, conv_grad, gain_grad, bias_grad = pl.pallas_call(
        functools.partial(tail_kernel, seq_count, row_count, half),
        out_shape=(
            struct(part, 5 * cols, dtype=F32), struct(rows, shard, width, dtype=F32),
            struct(KER, width, dtype=F32), struct(2, width, dtype=F32), struct(2, width, dtype=F32),
        ),
        in_specs=[hbm] * 10 + [vmem] * 3,
        out_specs=(vmem, hbm) + (vmem,) * 3,
        scratch_shapes=halves(10, part, width // 2) + halves(1, rows - first_rows, pooled_local, width)
        + [scratch(10, row_count // 2, *packing), scratch(5, row_count, *packing)]
        + [
            scratch(2, rows, near, width), scratch(rows, near, width), scratch(rows, min(near, far), width),
            scratch(*((2, width // 2, width) if far > near else (8, 128)), dtype=F32),
            scratch(rows, pooled_local, width, dtype=F32),
            scratch(rows, 16, width), scratch(rows, 16, width),
            scratch(2, shard, width), scratch(2, half, width), scratch(2, half, width),
            scratch(2, shard, width, dtype=F32), scratch(rows, 16, width, dtype=F32),
            scratch(16, width, dtype=F32), scratch(bits, 16, width, dtype=F32), scratch(row_count, 16, width, dtype=F32),
        ]
        + seq_sems(10) + [dma((10, row_count // 2)), dma((5, row_count))] + seq_sems(1)
        + [
            dma((2, 4)), dma((3,)), dma((seq_count,)), dma((2,)), dma((3, 2)), dma((2,)), dma((bits, 2)), dma((row_count, 2)),
        ],
        compiler_params=mesh_params(1),
        name="tail",
    )(
        tok_ext, pooled_all, dq, dk, dv, dpool, pool_own, own_grad, left_grad, right_grad,
        window_seg, conv_kernel, norm_sums,
    )
    results = (
        layer_out, token_grad, w_in_grad, w_out_grad, w_up_grad, w_down_grad, conv_grad, gain_grad, bias_grad,
    )
    splits = tuple(4 if x.ndim == 3 else 1 for x in results)
    done = pl.pallas_call(
        functools.partial(finish_kernel, splits),
        out_shape=tuple(struct(*x.shape, dtype=x.dtype) for x in results),
        in_specs=[hbm] * 9,
        out_specs=(hbm,) * 9,
        scratch_shapes=[scratch(*x.shape, dtype=x.dtype) for x in results] + [dma((sum(splits),)), dma((sum(splits),))],
        compiler_params=pltpu.CompilerParams(vmem_limit_bytes=60 * MB),
        name="finish",
    )(*results)
    return done[:5] + (done[5].T,) + done[6:]


def solution(mesh):
    placed = (
        P("row", "seq", None), P("row", None), P(), P(), P(), P(), P(), P(), P(), P("row", "seq", None),
    )
    return jax.shard_map(
        body,
        mesh=mesh,
        in_specs=placed,
        out_specs=(
            P("row", "seq", None), P("row", "seq", None), P("seq", "row"), P("seq", "row"),
            P("seq", "row"), P("seq", "row"), P(), P(), P(),
        ),
        check_vma=False,
    )
```
